32 devices in a mesh: seq: 8 (over z, y), head: 4 (over x, core).
Axes of the slice: x: 2, y: 2, z: 4, core: 2. Of those that a mesh axis runs over, the one named last changes fastest.
Arguments:
- tokens: bfloat16 [8192, 1024], P('seq'), may hold values from -6 to 6
- w_query: bfloat16 [1024, 1024], P(None, 'head'), may hold values from -0.375 to 0.375
- w_key: bfloat16 [1024, 1024], P(None, 'head'), may hold values from -0.1875 to 0.1875
- w_value: bfloat16 [1024, 1024], P(None, 'head'), may hold values from -0.1875 to 0.1875
- w_out: bfloat16 [1024, 1024], P(None, 'head'), may hold values from -0.1875 to 0.1875
- level_mix: float32 [4, 16], P(None, 'head'), may hold values from 0.25 to 2
- fine_blocks: int32 [64, 4], P('seq'), may hold values from 0 to 15, as said below
- order: int32 [8, 1024], P('seq'), may hold values from 0 to 1023, each once within a row
- mask_ids: int32 [8, 512], P('seq'), may hold values from 0 to 1023, as said below
Outputs:
- layer_out: bfloat16 [8192, 1024], P('seq', 'head')
The draws below stay inside these ranges and needn't reach their ends.
Inputs may be any that keep to these rules, and one draw needn't show every extreme that they name: `fine_blocks`: row g names 4 distinct blocks of a window of 16 blocks: ids below 8 stand for the previous time shard's blocks, ids from 8 up for the query block's own shard's blocks, and the first entry is always the query block's own block. `order`: each row is a permutation of the positions of one time shard. `mask_ids`: each row lists exactly 512 distinct positions of its time shard.
All inputs are finite; a program needn't handle non-finite values.
Results may differ from the reference program's by a relative error of at most 0.0098.
Values may be sent and summed in bfloat16 or wider, within the bound.
No kernel may reach another device: no remote copies, remote signals or barrier semaphores. Data moves between devices by JAX's collectives and lax.ppermute only.
A program may use at most 64 MiB of HBM per device.

```python
import math
import jax
import jax.numpy as jnp
from jax import lax

MODEL_DIMENSION = 1024
HEADS = 16
HEAD_DIM = 64
TOKENS_PER_PART = 1024
FBLK = 128
FINE_K = 4
POOL1 = 8
POOL2 = 64
POOL3 = 512
SLAB_COUNT = 8
PIECE_TOKENS = 128
TOKENS = 8192
BPD = 8
QBLOCKS = 64
MASK_DEV = 512


def draw_fine_blocks(key, part):
    row_keys = jax.random.split(key, QBLOCKS)
    own_ids = BPD + jnp.arange(QBLOCKS, dtype=jnp.int32) % BPD

    def one_row(row_key, own_id):
        others = jax.random.permutation(row_key, 2 * BPD - 1)[:FINE_K - 1].astype(jnp.int32)
        others = jnp.where(others >= own_id, others + 1, others)
        return jnp.concatenate([own_id[None], others])
    return jax.vmap(one_row)(row_keys, own_ids)


def draw_mask_ids(key, part):
    shard_keys = jax.random.split(key, SLAB_COUNT)

    def one_shard(shard_key):
        return jax.random.permutation(shard_key, TOKENS_PER_PART)[:MASK_DEV].astype(jnp.int32)
    return jax.vmap(one_shard)(shard_keys)


def steps_of(own_key, shape, cuts, least, top_value):
    loudness, own = 1.0, jax.random.fold_in(own_key, 6)
    for axis_at, blocks in cuts:
        draws = jnp.exp(jax.random.uniform(jax.random.fold_in(own, axis_at), (blocks,), jnp.float32, least / len(cuts), top_value / len(cuts)))
        loudness = loudness * jnp.repeat(draws, shape[axis_at] // blocks).reshape([-1 if axis == axis_at else 1 for axis in range(len(shape))])
    return loudness


def scatter_about(stream_key, extent, deviation, limit, shards=(), kind=jnp.bfloat16):
    result = deviation * jax.random.normal(stream_key, extent, jnp.float32)
    if shards:
        result = result * steps_of(stream_key, extent, shards, -0.22, 0.18)
    return jnp.clip(result, -limit, limit).astype(kind)


def setup_inputs(seed: int = 0) -> dict:
    arg_keys = jax.random.split(jax.random.key(seed), 10)
    tokens = scatter_about(arg_keys[0], (TOKENS, MODEL_DIMENSION), 1.0, 6.0, ((0, 8),))
    w_query = scatter_about(arg_keys[1], (MODEL_DIMENSION, MODEL_DIMENSION), (MODEL_DIMENSION // 4) ** -0.5, 0.375, ((1, 4),))
    w_key = scatter_about(arg_keys[2], (MODEL_DIMENSION, MODEL_DIMENSION), MODEL_DIMENSION ** -0.5, 0.1875, ((1, 4),))
    w_value = scatter_about(arg_keys[3], (MODEL_DIMENSION, MODEL_DIMENSION), MODEL_DIMENSION ** -0.5, 0.1875, ((1, 4),))
    w_out = scatter_about(arg_keys[4], (MODEL_DIMENSION, MODEL_DIMENSION), MODEL_DIMENSION ** -0.5, 0.1875, ((1, 4),))
    level_mix = jnp.clip(jnp.exp(math.log(2.0) - 2.0794415 * jax.random.uniform(arg_keys[5], (4, HEADS), jnp.float32) ** steps_of(arg_keys[5], (4, HEADS), ((1, 4),), -0.2, 0.2)), 0.25, 2.0)
    fine_blocks = draw_fine_blocks(jax.random.fold_in(arg_keys[9], 71), 0)
    order = jax.vmap(lambda own: jax.random.permutation(own, TOKENS_PER_PART))(jax.random.split(arg_keys[7], SLAB_COUNT)).reshape((SLAB_COUNT, TOKENS_PER_PART)).astype(jnp.int32)
    mask_ids = draw_mask_ids(jax.random.fold_in(arg_keys[9], 71), 0)
    return dict(tokens=tokens, w_query=w_query, w_key=w_key, w_value=w_value, w_out=w_out, level_mix=level_mix, fine_blocks=fine_blocks, order=order, mask_ids=mask_ids)


def time_order(tokens, order):
    sensor_grouped = tokens.reshape(SLAB_COUNT, SLAB_COUNT, PIECE_TOKENS, MODEL_DIMENSION)
    axes_exchanged = jnp.transpose(sensor_grouped, (1, 0, 2, 3)).reshape(SLAB_COUNT, TOKENS_PER_PART, MODEL_DIMENSION)
    picked = jnp.take_along_axis(axes_exchanged, order[:, :, None], axis=1)
    return picked.reshape(TOKENS, MODEL_DIMENSION)

def level_summaries(key_rows, value_rows, visible, pooling):
    groups = TOKENS // pooling
    weights = visible.reshape(groups, pooling, 1)
    key_sums = lax.optimization_barrier(jnp.sum(key_rows.astype(jnp.float32).reshape(groups, pooling, MODEL_DIMENSION) * weights, axis=1))
    value_sums = lax.optimization_barrier(jnp.sum(value_rows.astype(jnp.float32).reshape(groups, pooling, MODEL_DIMENSION) * weights, axis=1))
    counts = lax.optimization_barrier(jnp.sum(visible.reshape(groups, pooling), axis=1))
    factor = 1.0 / jnp.sqrt(jnp.maximum(counts, 1.0))
    return ((key_sums * factor[:, None]).astype(jnp.bfloat16), (value_sums * factor[:, None]).astype(jnp.bfloat16))

def rounded_weights(weights):
    return lax.optimization_barrier(weights.astype(jnp.bfloat16)).astype(jnp.float32)

def coarse_output(queries, key_rows, value_rows):
    scaling = 1.0 / math.sqrt(HEAD_DIM)
    scores = jnp.einsum('qhd,khd->hqk', queries.astype(jnp.float32), key_rows.astype(jnp.float32)) * scaling
    weights = jnp.exp(scores - lax.optimization_barrier(jnp.max(scores, axis=2, keepdims=True)))
    numerator = jnp.einsum('hqk,khd->qhd', rounded_weights(weights), value_rows.astype(jnp.float32))
    return numerator / jnp.transpose(lax.optimization_barrier(jnp.sum(weights, axis=2)))[:, :, None]

def reference(tokens, w_query, w_key, w_value, w_out, level_mix, fine_blocks, order, mask_ids):
    timed = time_order(tokens, order)
    queries = jnp.dot(timed, w_query, preferred_element_type=jnp.float32).astype(jnp.bfloat16)
    key_rows = jnp.dot(timed, w_key, preferred_element_type=jnp.float32).astype(jnp.bfloat16)
    value_rows = jnp.dot(timed, w_value, preferred_element_type=jnp.float32).astype(jnp.bfloat16)
    shard_index = jnp.arange(SLAB_COUNT, dtype=jnp.int32)[:, None]
    visible = jnp.ones((SLAB_COUNT, TOKENS_PER_PART), jnp.float32).at[shard_index, mask_ids].set(0.0).reshape(TOKENS)
    key_one, value_one = level_summaries(key_rows, value_rows, visible, POOL1)
    key_two, value_two = level_summaries(key_rows, value_rows, visible, POOL2)
    key_three, value_three = level_summaries(key_rows, value_rows, visible, POOL3)
    near_count = TOKENS_PER_PART // POOL1
    mid_count = TOKENS_PER_PART // POOL2
    near_keys = key_one.reshape(SLAB_COUNT, near_count, HEADS, HEAD_DIM)
    near_values = value_one.reshape(SLAB_COUNT, near_count, HEADS, HEAD_DIM)
    padded_keys = jnp.pad(key_two.reshape(SLAB_COUNT, mid_count, MODEL_DIMENSION), ((1, 1), (0, 0), (0, 0)))
    padded_values = jnp.pad(value_two.reshape(SLAB_COUNT, mid_count, MODEL_DIMENSION), ((1, 1), (0, 0), (0, 0)))
    mid_keys = jnp.concatenate([padded_keys[:-2], padded_keys[1:-1], padded_keys[2:]], axis=1)
    mid_values = jnp.concatenate([padded_values[:-2], padded_values[1:-1], padded_values[2:]], axis=1)
    mid_keys = mid_keys.reshape(SLAB_COUNT, 3 * mid_count, HEADS, HEAD_DIM)
    mid_values = mid_values.reshape(SLAB_COUNT, 3 * mid_count, HEADS, HEAD_DIM)
    far_keys = key_three.reshape(TOKENS // POOL3, HEADS, HEAD_DIM)
    far_values = value_three.reshape(TOKENS // POOL3, HEADS, HEAD_DIM)
    shard_queries = queries.reshape(SLAB_COUNT, BPD, FBLK, HEADS, HEAD_DIM)
    shard_keys = key_rows.reshape(SLAB_COUNT, BPD, FBLK, HEADS, HEAD_DIM)
    shard_values = value_rows.reshape(SLAB_COUNT, BPD, FBLK, HEADS, HEAD_DIM)
    shard_visible = visible.reshape(SLAB_COUNT, BPD, FBLK)
    prev_keys = jnp.concatenate([jnp.zeros_like(shard_keys[:1]), shard_keys[:-1]], axis=0)
    prev_values = jnp.concatenate([jnp.zeros_like(shard_values[:1]), shard_values[:-1]], axis=0)
    prev_visible = jnp.concatenate([jnp.zeros_like(shard_visible[:1]), shard_visible[:-1]], axis=0)
    block_lists = fine_blocks.reshape(SLAB_COUNT, BPD, FINE_K)
    scaling = 1.0 / math.sqrt(HEAD_DIM)
    inside = jnp.arange(FBLK, dtype=jnp.int32)
    same_row = inside[:, None] == inside[None, :]
    own_ids = (BPD + jnp.arange(BPD, dtype=jnp.int32))[:, None]

    def shard_attention(operands):
        block_queries, own_keys, own_values, last_keys, last_values, own_visible, last_visible, lists_here, near_k, near_v, mid_k, mid_v = operands
        window_keys = jnp.concatenate([last_keys, own_keys], axis=0)
        window_values = jnp.concatenate([last_values, own_values], axis=0)
        window_visible = jnp.concatenate([last_visible, own_visible], axis=0)
        chosen_keys = window_keys[lists_here].reshape(BPD, FINE_K * FBLK, HEADS, HEAD_DIM)
        chosen_values = window_values[lists_here].reshape(BPD, FINE_K * FBLK, HEADS, HEAD_DIM)
        selected_visible = window_visible[lists_here].reshape(BPD, FINE_K * FBLK)
        own_block = lists_here == own_ids
        is_self = (own_block[:, None, :, None] & same_row[None, :, None, :]).reshape(BPD, FBLK, FINE_K * FBLK)
        allowed = is_self | (selected_visible[:, None, :] > 0.5)
        scores = jnp.einsum('bqhd,bkhd->bhqk', block_queries.astype(jnp.float32), chosen_keys.astype(jnp.float32)) * scaling
        masked_scores = jnp.where(allowed[:, None], scores, -jnp.inf)
        top = lax.optimization_barrier(jnp.max(masked_scores, axis=3, keepdims=True))
        weights = jnp.where(allowed[:, None], jnp.exp(scores - top), 0.0)
        numerator = jnp.einsum('bhqk,bkhd->bqhd', rounded_weights(weights), chosen_values.astype(jnp.float32))
        denominator = jnp.transpose(lax.optimization_barrier(jnp.sum(weights, axis=3)), (0, 2, 1))
        fine_out = (numerator / denominator[..., None]).reshape(TOKENS_PER_PART, HEADS, HEAD_DIM)
        flat_queries = block_queries.reshape(TOKENS_PER_PART, HEADS, HEAD_DIM)
        out_one = coarse_output(flat_queries, near_k, near_v)
        out_two = coarse_output(flat_queries, mid_k, mid_v)
        out_three = coarse_output(flat_queries, far_keys, far_values)
        blended = level_mix[0][None, :, None] * fine_out + level_mix[1][None, :, None] * out_one + level_mix[2][None, :, None] * out_two + level_mix[3][None, :, None] * out_three
        return blended.reshape(TOKENS_PER_PART, MODEL_DIMENSION).astype(jnp.bfloat16)
    attended = lax.map(shard_attention, (shard_queries, shard_keys, shard_values, prev_keys, prev_values, shard_visible, prev_visible, block_lists, near_keys, near_values, mid_keys, mid_values))
    attended = attended.reshape(TOKENS, MODEL_DIMENSION)
    return jnp.dot(attended, w_out, preferred_element_type=jnp.float32).astype(jnp.bfloat16)
```

```python
import functools

import jax
import jax.numpy as jnp
from jax import lax
from jax.experimental import pallas as pl
from jax.experimental.pallas import tpu as pltpu
from jax.sharding import PartitionSpec as P

FBLK = 128
FINE_K = 4
POOL1 = 8
POOL2 = 64
POOL3 = 512
SUMM_ROWS = 32
BF = jnp.bfloat16
F32 = jnp.float32
HIDE = -1e30
VMEM_LIMIT = 56 * 1024 * 1024

X_PAIRS = [(0, 2), (2, 0), (1, 3), (3, 1)]
CORE_PAIRS = [(0, 1), (1, 0), (2, 3), (3, 2)]


def nn(a, b):
    return lax.dot_general(a, b, (((1,), (0,)), ((), ())), preferred_element_type=F32)


def nt(a, b):
    return lax.dot_general(a, b, (((1,), (1,)), ((), ())), preferred_element_type=F32)


def vmem_specs(count):
    return [pl.BlockSpec(memory_space=pltpu.VMEM)] * count


def over_head(block, pairs):
    return lax.ppermute(block, "head", pairs)


def exchange_tokens(tokens):
    tok_rows, width = tokens.shape
    slabs = lax.axis_size("seq")
    rows = tok_rows // slabs
    quarter = width // 4
    slab, head = lax.axis_index("seq"), lax.axis_index("head")
    split = tokens.reshape(slabs, rows, width)

    def columns(other):
        return lax.dynamic_slice_in_dim(split, (head ^ other) * quarter, quarter, axis=2)

    mine = columns(0)
    if slabs != 8:
        first = lax.all_to_all(mine, "seq", split_axis=0, concat_axis=0, tiled=True).reshape(
            tok_rows, quarter
        )
        third = over_head(first, X_PAIRS)
        second = over_head(first, CORE_PAIRS)
        fourth = over_head(third, CORE_PAIRS)
        return [(first, 0, 0), (third, 0, 1), (second, 0, 2), (fourth, 0, 3)], 0
    partner = columns(2)

    def to_peer(source, distance):
        block = lax.dynamic_index_in_dim(source, slab ^ distance, axis=0, keepdims=False)
        return lax.ppermute(block, "seq", [(i, i ^ distance) for i in range(slabs)])

    far = jnp.concatenate([to_peer(mine, d) for d in (7, 6, 5, 4)], axis=0)
    both = jnp.concatenate([mine, partner], axis=2)
    near = jnp.concatenate([to_peer(both, d) for d in (3, 2, 1)], axis=0)
    far_x = over_head(far, X_PAIRS)
    near_core = over_head(near, CORE_PAIRS)
    far_core = over_head(far, CORE_PAIRS)
    far_last = over_head(far_x, CORE_PAIRS)
    own = jnp.concatenate(
        [
            lax.dynamic_index_in_dim(part, slab, axis=0, keepdims=False)
            for part in (mine, partner, columns(1), columns(3))
        ],
        axis=1,
    )
    pieces = [(far, 0, 0), (far_x, 0, 1), (far_core, 0, 2), (far_last, 0, 3)]
    pieces += [(near, 4 * rows, 0), (near_core, 4 * rows, 2), (own, 7 * rows, 0)]
    return pieces, (slab ^ 7) * rows


def project_kernel(places, *refs):
    count = len(places)
    piece_refs, refs = refs[:count], refs[count:]
    wqv_ref, wk_ref, p_ref, pt_ref, ac_ref, fcol_ref, frow_ref = refs[:7]
    qt_ref, vt_ref, k_ref, nk_ref, nvt_ref, summ_ref, comp_ref, x_ref = refs[7:]
    quarter = x_ref.shape[1] // 4
    for piece, (row, column) in zip(piece_refs, places):
        height, width = piece.shape
        x_ref[row : row + height, column * quarter : column * quarter + width] = piece[...]
    group = wk_ref.shape[1]
    x = x_ref[...]
    qv = nt(wqv_ref[...], x).astype(BF)
    k0 = nn(x, wk_ref[...]).astype(BF)
    k = nn(p_ref[...], k0).astype(BF)
    k_ref[...] = k
    qvt = nn(qv, pt_ref[...]).astype(BF)
    qt_ref[...] = qvt[:group] * jnp.asarray(0.125, BF)
    vt = qvt[group:]
    vt_ref[...] = vt
    ac = ac_ref[...]
    near = nk_ref.shape[0]
    lead = near + SUMM_ROWS
    kl = nn(ac, k)
    vl = nt(vt, ac)
    kf = (kl[:lead] * fcol_ref[...]).astype(BF)
    vf = vl[:, :lead] * frow_ref[...]
    nk_ref[...] = kf[:near]
    nvt_ref[...] = vf[:, :near].astype(BF)
    summ_ref[:SUMM_ROWS] = kf[near:]
    summ_ref[SUMM_ROWS:] = jnp.transpose(vf[:, near:]).astype(BF)
    packed = kl.shape[0] - lead
    comp_ref[:packed] = kl[lead:].astype(BF)
    vc = vl[:, lead:].astype(BF)
    for part in range(packed // group):
        comp_ref[packed + part * group : packed + (part + 1) * group] = vc[
            :, part * group : (part + 1) * group
        ]


def attend_kernel(
    lists_ref, mix_ref, qt_ref, k_ref, vt_ref, comp_ref, e_ref, et_ref, bias_ref, nk_ref, nvt_ref,
    summ_ref, selk_ref, selv_ref, out_ref, kw_ref, vw_ref, kc_ref, vc_ref, q4_ref, p_ref,
):
    tok_rows, group = k_ref.shape
    heads = mix_ref.shape[1]
    width = group // heads
    fine = FINE_K * FBLK
    near = nk_ref.shape[0]
    mid_at = fine + near
    mid = 3 * (tok_rows // POOL2)
    far_at = mid_at + mid
    total = kc_ref.shape[0]
    packed = e_ref.shape[1]
    kw_ref[:tok_rows] = nn(e_ref[...], comp_ref[:packed]).astype(BF)
    kw_ref[tok_rows:] = k_ref[...]
    prev = None
    for part in range(packed // group):
        term = nn(
            comp_ref[packed + part * group : packed + (part + 1) * group],
            et_ref[part * group : (part + 1) * group],
        )
        prev = term if prev is None else prev + term
    vw_ref[:, :tok_rows] = prev.astype(BF)
    vw_ref[:, tok_rows:] = vt_ref[...]
    summ = summ_ref[...]
    kc_ref[fine:mid_at] = nk_ref[...]
    vc_ref[:, fine:mid_at] = nvt_ref[...]
    kc_ref[mid_at:] = nn(selk_ref[...], summ).astype(BF)
    vc_ref[:, mid_at:] = jnp.transpose(nn(selv_ref[...], summ)).astype(BF)
    q4_ref[...] = jnp.zeros_like(q4_ref)
    same = lax.broadcasted_iota(jnp.int32, (FBLK, FBLK), 0) == lax.broadcasted_iota(
        jnp.int32, (FBLK, FBLK), 1
    )

    def block(g, carry):
        at = pl.multiple_of(g * FBLK, FBLK)
        biases = []
        for entry in range(FINE_K):
            start = pl.multiple_of(lists_ref[g, entry] * FBLK, FBLK)
            kc_ref[entry * FBLK : (entry + 1) * FBLK] = kw_ref[pl.ds(start, FBLK)]
            vc_ref[:, entry * FBLK : (entry + 1) * FBLK] = vw_ref[:, pl.ds(start, FBLK)]
            bias = bias_ref[pl.ds(start, FBLK)]
            biases.append(jnp.where(same, 0.0, bias) if entry == 0 else bias)
        for h in range(heads):
            q4_ref[h * width : (h + 1) * width, h * FBLK : (h + 1) * FBLK] = qt_ref[
                h * width : (h + 1) * width, pl.ds(at, FBLK)
            ]
        scores = nn(kc_ref[...], q4_ref[...])
        scales = []
        for h in range(heads):
            lanes = slice(h * FBLK, (h + 1) * FBLK)
            parts = [scores[e * FBLK : (e + 1) * FBLK, lanes] + biases[e] for e in range(FINE_K)]
            top = functools.reduce(
                jnp.maximum, [jnp.max(part, axis=0, keepdims=True) for part in parts]
            )
            den = jnp.zeros_like(top)
            for e, part in enumerate(parts):
                weight = jnp.exp(part - top)
                den = den + jnp.sum(weight, axis=0, keepdims=True)
                p_ref[e * FBLK : (e + 1) * FBLK, lanes] = weight.astype(BF)
            scales.append(mix_ref[0, h] / den)
            for level, (low, high) in enumerate(((fine, mid_at), (mid_at, far_at), (far_at, total))):
                part = scores[low:high, lanes]
                weight = jnp.exp(part - jnp.max(part, axis=0, keepdims=True))
                scale = mix_ref[level + 1, h] / jnp.sum(weight, axis=0, keepdims=True)
                p_ref[low:high, lanes] = (weight * scale).astype(BF)
        fine_out = nn(vc_ref[:, :fine], p_ref[:fine])
        coarse_out = nn(vc_ref[:, fine:], p_ref[fine:])
        rows = []
        for h in range(heads):
            pick = (slice(h * width, (h + 1) * width), slice(h * FBLK, (h + 1) * FBLK))
            rows.append(fine_out[pick] * scales[h] + coarse_out[pick])
        out_ref[pl.ds(at, FBLK)] = jnp.transpose(jnp.concatenate(rows, axis=0)).astype(BF)
        return carry

    lax.fori_loop(0, tok_rows // FBLK, block, 0)


def output_kernel(a_ref, b_ref, c_ref, d_ref, w_ref, out_ref):
    group = a_ref.shape[1]
    total = None
    for index, part in enumerate((a_ref, b_ref, c_ref, d_ref)):
        term = nn(part[...], w_ref[index * group : (index + 1) * group])
        total = term if total is None else total + term
    out_ref[...] = total.astype(BF)


def visibility(mask_ids, tok_rows):
    position = jnp.arange(tok_rows, dtype=jnp.int32)
    hidden = jnp.sum((mask_ids[:, None] == position[None, :]).astype(jnp.int32), axis=0)
    before = jnp.sum((mask_ids[:, None] < position[None, :]).astype(jnp.int32), axis=0)
    return hidden == 0, position - before


def local(tokens, w_query, w_key, w_value, w_out, level_mix, fine_blocks, order, mask_ids):
    tok_rows, width = tokens.shape
    slabs = lax.axis_size("seq")
    slab, head = lax.axis_index("seq"), lax.axis_index("head")
    group = w_query.shape[1]
    heads = level_mix.shape[1]
    packed = tok_rows - mask_ids.shape[1]
    near, mids, fars = tok_rows // POOL1, tok_rows // POOL2, tok_rows // POOL3
    quarter = width // 4

    before_mask = lax.ppermute(mask_ids, "seq", [(i, i + 1) for i in range(slabs - 1)])
    pieces, flip = exchange_tokens(tokens)

    place = order[0] ^ flip
    index = jnp.arange(tok_rows, dtype=jnp.int32)
    permute = (place[:, None] == index[None, :]).astype(BF)
    permute_t = (index[:, None] == place[None, :]).astype(BF)
    seen, rank = visibility(mask_ids[0], tok_rows)
    lead = near + SUMM_ROWS
    row = jnp.arange(lead + packed, dtype=jnp.int32)[:, None]
    target = jnp.where(
        row < near,
        index // POOL1,
        jnp.where(
            row < near + mids,
            index // POOL2 + near,
            jnp.where(row < lead, index // POOL3 + near + mids, rank + lead),
        ),
    )
    member = (target == row) & seen[None, :]
    pool = member.astype(BF)
    counts = jnp.sum(member[:lead].astype(F32), axis=1)
    factor = 1.0 / jnp.sqrt(jnp.maximum(counts, 1.0))
    seen_before, rank_before = visibility(before_mask[0], tok_rows)
    seen_before = seen_before & (slab > 0)
    slot = jnp.arange(packed, dtype=jnp.int32)
    expand = ((rank_before[:, None] == slot[None, :]) & seen_before[:, None]).astype(BF)
    expand_t = ((slot[:, None] == rank_before[None, :]) & seen_before[None, :]).astype(BF)
    bias = jnp.where(jnp.concatenate([seen_before, seen]), 0.0, HIDE).astype(F32)
    bias = jnp.broadcast_to(bias[:, None], (2 * tok_rows, FBLK))
    line = jnp.arange(3 * mids + fars * slabs, dtype=jnp.int32)
    mid_shard = slab - 1 + line // mids
    far_line = line - 3 * mids
    step = 2 * SUMM_ROWS
    source = jnp.where(
        line < 3 * mids,
        mid_shard * step + line % mids,
        far_line // fars * step + mids + far_line % fars,
    )
    inside = (line >= 3 * mids) | ((mid_shard >= 0) & (mid_shard < slabs))
    column = jnp.arange(step * slabs, dtype=jnp.int32)[None, :]
    select_k = ((source[:, None] == column) & inside[:, None]).astype(BF)
    select_v = ((source[:, None] + SUMM_ROWS == column) & inside[:, None]).astype(BF)

    def by_quarter(weight):
        parts = [
            lax.dynamic_slice_in_dim(weight, (head ^ other) * quarter, quarter, axis=0)
            for other in (0, 2, 1, 3)
        ]
        return jnp.concatenate(parts, axis=0)

    wqv_t = by_quarter(jnp.concatenate([w_query, w_value], axis=1)).T
    wk = by_quarter(w_key)
    wo = by_quarter(w_out)

    shape = jax.ShapeDtypeStruct
    params = pltpu.CompilerParams(vmem_limit_bytes=VMEM_LIMIT)
    places = tuple((r, c) for _, r, c in pieces)
    q_t, v_t, keys, near_k, near_vt, summ, comp = pl.pallas_call(
        functools.partial(project_kernel, places),
        out_shape=(
            shape((group, tok_rows), BF),
            shape((group, tok_rows), BF),
            shape((tok_rows, group), BF),
            shape((near, group), BF),
            shape((group, near), BF),
            shape((step, group), BF),
            shape((2 * packed, group), BF),
        ),
        in_specs=vmem_specs(len(pieces) + 7),
        out_specs=vmem_specs(7),
        scratch_shapes=[pltpu.VMEM((tok_rows, width), BF)],
        compiler_params=params,
        name="project",
    )(
        *[piece for piece, _, _ in pieces],
        wqv_t,
        wk,
        permute,
        permute_t,
        pool,
        factor[:, None],
        factor[None, :],
    )
    comp_before = lax.ppermute(comp, "seq", [(i, i + 1) for i in range(slabs - 1)])
    summ_all = lax.all_to_all(
        jnp.broadcast_to(summ[None], (slabs, step, group)), "seq", split_axis=0, concat_axis=0, tiled=True
    ).reshape(slabs * step, group)

    total = FINE_K * FBLK + near + line.shape[0]
    smem = pl.BlockSpec(memory_space=pltpu.SMEM)
    attended = pl.pallas_call(
        attend_kernel,
        out_shape=shape((tok_rows, group), BF),
        in_specs=[smem, smem] + vmem_specs(12),
        out_specs=pl.BlockSpec(memory_space=pltpu.VMEM),
        scratch_shapes=[
            pltpu.VMEM((2 * tok_rows, group), BF),
            pltpu.VMEM((group, 2 * tok_rows), BF),
            pltpu.VMEM((total, group), BF),
            pltpu.VMEM((group, total), BF),
            pltpu.VMEM((group, heads * FBLK), BF),
            pltpu.VMEM((total, heads * FBLK), BF),
        ],
        compiler_params=params,
        name="attend",
    )(
        fine_blocks, level_mix, q_t, keys, v_t, comp_before, expand, expand_t, bias, near_k, near_vt,
        summ_all, select_k, select_v,
    )
    third = over_head(attended, X_PAIRS)
    second = over_head(attended, CORE_PAIRS)
    fourth = over_head(third, CORE_PAIRS)
    steps = 4
    tile = pl.BlockSpec((tok_rows // steps, group), lambda i: (i, 0))
    return pl.pallas_call(
        output_kernel,
        grid=(steps,),
        out_shape=shape((tok_rows, group), BF),
        in_specs=[tile] * 4 + [pl.BlockSpec((width, group), lambda i: (0, 0))],
        out_specs=tile,
        compiler_params=params,
        name="output",
    )(attended, third, second, fourth, wo)


def solution(mesh):
    placed = (
        P("seq", None),
        P(None, "head"),
        P(None, "head"),
        P(None, "head"),
        P(None, "head"),
        P(None, "head"),
        P("seq", None),
        P("seq", None),
        P("seq", None),
    )
    return jax.shard_map(
        local, mesh=mesh, in_specs=placed, out_specs=P("seq", "head"), check_vma=False
    )
```

```python
import functools

import jax
import jax.numpy as jnp
from jax import lax
from jax.experimental import pallas as pl
from jax.experimental.pallas import tpu as pltpu
from jax.sharding import PartitionSpec as P

FBLK = 128
FINE_K = 4
POOL1 = 8
POOL2 = 64
POOL3 = 512
SUMM_ROWS = 32
BF = jnp.bfloat16
F32 = jnp.float32
I32 = jnp.int32
HIDE = -1e30
VMEM_LIMIT = 24 * 1024 * 1024

X_PAIRS = [(0, 2), (2, 0), (1, 3), (3, 1)]
CORE_PAIRS = [(0, 1), (1, 0), (2, 3), (3, 2)]


def nn(a, b):
    return lax.dot_general(a, b, (((1,), (0,)), ((), ())), preferred_element_type=F32)


def nt(a, b):
    return lax.dot_general(a, b, (((1,), (1,)), ((), ())), preferred_element_type=F32)


def iota(shape, axis):
    return lax.broadcasted_iota(I32, shape, axis)


def ones_where(condition):
    return jnp.where(condition, 1.0, 0.0).astype(BF)


def vmem_specs(count):
    return [pl.BlockSpec(memory_space=pltpu.VMEM)] * count


def smem_specs(count):
    return [pl.BlockSpec(memory_space=pltpu.SMEM)] * count


def over_head(block, pairs):
    return lax.ppermute(block, "head", pairs)


def to_next(block):
    return lax.ppermute(block, "seq", [(i, i + 1) for i in range(lax.axis_size("seq") - 1)])


def exchange_tokens(tokens, head):
    tok_rows, width = tokens.shape
    slabs = lax.axis_size("seq")
    rows = tok_rows // slabs
    quarter = width // 4
    slab = lax.axis_index("seq")
    split = tokens.reshape(slabs, rows, width)

    def columns(other):
        return lax.dynamic_slice_in_dim(split, (head ^ other) * quarter, quarter, axis=2)

    mine = columns(0)
    if slabs != 8:
        first = lax.all_to_all(mine, "seq", split_axis=0, concat_axis=0, tiled=True).reshape(
            tok_rows, quarter
        )
        third = over_head(first, X_PAIRS)
        second = over_head(first, CORE_PAIRS)
        fourth = over_head(third, CORE_PAIRS)
        pieces = [(first, 0, (0,)), (third, 0, (2,)), (second, 0, (1,)), (fourth, 0, (3,))]
        return pieces, 0, first
    both = jnp.concatenate([mine, columns(2)], axis=2)

    def to_peer(source, distance):
        block = lax.dynamic_index_in_dim(source, slab ^ distance, axis=0, keepdims=False)
        return lax.ppermute(block, "seq", [(i, i ^ distance) for i in range(slabs)])

    far = jnp.concatenate([to_peer(mine, d) for d in (7, 6, 5, 4)], axis=0)
    near = jnp.concatenate([to_peer(both, d) for d in (3, 2, 1)], axis=0)
    far_x = over_head(far, X_PAIRS)
    near_core = over_head(near, CORE_PAIRS)
    far_core = over_head(far, CORE_PAIRS)
    far_last = over_head(far_x, CORE_PAIRS)
    own = lax.dynamic_index_in_dim(split, slab, axis=0, keepdims=False)
    pieces = [(far, 0, (0,)), (far_x, 0, (2,)), (far_core, 0, (1,)), (far_last, 0, (3,))]
    pieces += [(near, 4 * rows, (0, 2)), (near_core, 4 * rows, (1, 3)), (own, 7 * rows, None)]
    return pieces, (slab ^ 7) * rows, far


def prepare_kernel(
    place_ref, order_ref, mask_ref, before_ref, wq_ref, wv_ref,
    p_ref, pt_ref, sel_ref, fcol_ref, frow_ref, e_ref, et_ref, bias_ref, selk_ref, selv_ref, wt_ref,
):
    slab, flip, slabs = place_ref[0], place_ref[1], place_ref[2]
    tok_rows = order_ref.shape[1]
    packed = e_ref.shape[1]
    mids, fars = tok_rows // POOL2, tok_rows // POOL3
    group = wq_ref.shape[1]
    lanes = 128

    def column(row):
        return jnp.transpose(jnp.broadcast_to(row.astype(F32), (lanes, row.shape[1]))).astype(I32)

    def ranks(ids):
        hidden = column(ids)
        parts = []
        for at in range(0, tok_rows, lanes):
            time = iota((1, lanes), 1) + at
            count = jnp.sum(jnp.where(hidden < time, 1.0, 0.0), axis=0, keepdims=True)
            here = jnp.sum(jnp.where(hidden == time, 1.0, 0.0), axis=0, keepdims=True)
            parts.append(jnp.where(here == 0.0, time - count.astype(I32), -1))
        return jnp.concatenate(parts, axis=1)

    place = order_ref[...] ^ flip
    place_column = column(place)
    for at in range(0, tok_rows, lanes):
        p_ref[:, at : at + lanes] = ones_where(place_column == iota((tok_rows, lanes), 1) + at)
        pt_ref[at : at + lanes] = ones_where(iota((lanes, tok_rows), 0) + at == place)
    rank = ranks(mask_ref[...])
    rank_before = jnp.where(slab > 0, ranks(before_ref[...]), -1)
    time = jnp.where(rank >= 0, iota((1, tok_rows), 1), -1) + 1
    line = iota((16, tok_rows), 0)
    stack = jnp.where(
        line == 0,
        time >> 5,
        jnp.where(
            line == 1,
            time & 31,
            jnp.where(line == 2, (rank + 1) >> 5, jnp.where(line == 3, (rank + 1) & 31, 0)),
        ),
    )
    moved = nn(stack.astype(F32).astype(BF), p_ref[...]).astype(I32)
    time_here = (moved[0:1] << 5) + moved[1:2] - 1
    rank_here = (moved[2:3] << 5) + moved[3:4] - 1
    for at in range(0, packed, lanes):
        sel_ref[at : at + lanes] = ones_where(iota((lanes, tok_rows), 0) + at == rank_here)
    line = iota((SUMM_ROWS, tok_rows), 0)
    sel_ref[packed : packed + SUMM_ROWS] = ones_where(
        ((time_here >> 6) == line) | (((time_here >> 9) + mids == line) & (time_here >= 0))
    )
    lead = packed + SUMM_ROWS
    near = sel_ref.shape[0] - lead
    sel_ref[lead:] = ones_where((time_here >> 3) == iota((near, tok_rows), 0))
    pools = sel_ref[packed:]
    fcol_ref[...] = 1.0 / jnp.sqrt(jnp.maximum(nn(pools, jnp.ones((tok_rows, lanes), BF)), 1.0))
    frow_ref[...] = 1.0 / jnp.sqrt(jnp.maximum(nt(jnp.ones((16, tok_rows), BF), pools), 1.0))
    rank_column = column(rank_before)
    for at in range(0, packed, lanes):
        e_ref[:, at : at + lanes] = ones_where(rank_column == iota((tok_rows, lanes), 1) + at)
        et_ref[at : at + lanes] = ones_where(iota((lanes, tok_rows), 0) + at == rank_before)
    bias_ref[:tok_rows] = jnp.where(rank_column >= 0, 0.0, HIDE)
    bias_ref[tok_rows:] = jnp.where(column(rank) >= 0, 0.0, HIDE)
    shape = selk_ref.shape
    line = iota(shape, 0)
    step = 2 * SUMM_ROWS
    turn = line // mids
    far = line - 3 * mids
    shard = slab - 1 + turn
    source = jnp.where(
        line < 3 * mids, shard * step + line - turn * mids, far // fars * step + mids + far % fars
    )
    source = jnp.where((line >= 3 * mids) | ((shard >= 0) & (shard < slabs)), source, -step)
    selk_ref[...] = ones_where(source == iota(shape, 1))
    selv_ref[...] = ones_where(source + SUMM_ROWS == iota(shape, 1))
    wt_ref[:group] = jnp.transpose(wq_ref[...])
    wt_ref[group:] = jnp.transpose(wv_ref[...])


def project_kernel(places, *refs):
    count = len(places)
    place_ref, piece_refs, refs = refs[0], refs[1 : count + 1], refs[count + 1 :]
    wt_ref, wk_ref, sel_ref, fcol_ref, frow_ref, comp_ref, summ_ref, k_ref, qv_ref, x_ref = refs
    quarter = x_ref.shape[1] // 4
    head = place_ref[3]
    for piece, (row, distances) in zip(piece_refs, places):
        height = piece.shape[0]
        if distances is None:
            x_ref[row : row + height] = piece[...]
            continue
        for part, distance in enumerate(distances):
            start = pl.multiple_of((head ^ distance) * quarter, quarter)
            x_ref[row : row + height, pl.ds(start, quarter)] = piece[
                :, part * quarter : (part + 1) * quarter
            ]
    group = wk_ref.shape[1]
    packed = comp_ref.shape[0] // 2
    lead = packed + SUMM_ROWS
    x = x_ref[...]
    keys = nn(x, wk_ref[...]).astype(BF)
    k_ref[...] = keys
    vt = nt(wt_ref[group:], x).astype(BF)
    qv_ref[group:] = vt
    sel = sel_ref[:lead]
    kl = nn(sel, keys)
    vl = nt(vt, sel)
    comp_ref[:packed] = kl[:packed].astype(BF)
    vc = vl[:, :packed].astype(BF)
    for part in range(packed // group):
        comp_ref[packed + part * group : packed + (part + 1) * group] = vc[
            :, part * group : (part + 1) * group
        ]
    factor = fcol_ref[:SUMM_ROWS, :1]
    summ_k = (kl[packed:] * factor).astype(BF)
    tail = jnp.concatenate(
        [vl[:, packed:], jnp.zeros((group, 128 - SUMM_ROWS), F32)], axis=1
    )
    summ_v = (jnp.transpose(tail)[:SUMM_ROWS] * factor).astype(BF)
    step = 2 * SUMM_ROWS
    for shard in range(summ_ref.shape[0]):
        summ_ref[shard, :SUMM_ROWS] = summ_k
        summ_ref[shard, SUMM_ROWS:] = summ_v
    qv_ref[:group] = nt(wt_ref[:group], x).astype(BF)


def order_kernel(
    p_ref, pt_ref, sel_ref, fcol_ref, frow_ref, k0_ref, qv_ref, qt_ref, vt_ref, k_ref, nk_ref, nvt_ref
):
    group = k_ref.shape[1]
    near = nk_ref.shape[0]
    k0 = k0_ref[...]
    k_ref[...] = nn(p_ref[...], k0).astype(BF)
    qv = qv_ref[...]
    timed = nn(qv, pt_ref[...])
    qt_ref[...] = (timed[:group] * 0.125).astype(BF)
    vt_ref[...] = timed[group:].astype(BF)
    pool = sel_ref[sel_ref.shape[0] - near :]
    nk_ref[...] = (nn(pool, k0) * fcol_ref[SUMM_ROWS:, :1]).astype(BF)
    nvt_ref[...] = (nt(qv[group:], pool) * frow_ref[:1, SUMM_ROWS:]).astype(BF)


def spread_heads(q4_ref, qt_ref, at, heads):
    width = q4_ref.shape[0] // heads
    for h in range(heads):
        rows = slice(h * width, (h + 1) * width)
        q4_ref[rows, h * FBLK : (h + 1) * FBLK] = qt_ref[rows, at : at + FBLK]


def own_kernel(
    mix_ref, qt_ref, k_ref, vt_ref, bias_ref, nk_ref, nvt_ref, acc_ref, near_ref, top_ref, den_ref, q4_ref, p_ref
):
    tok_rows, group = k_ref.shape
    heads = mix_ref.shape[1]
    width = group // heads
    q4_ref[...] = jnp.zeros_like(q4_ref)
    same = iota((FBLK, FBLK), 0) == iota((FBLK, FBLK), 1)
    nk = nk_ref[...]
    nvt = nvt_ref[...]
    near = nk.shape[0]
    for g in range(tok_rows // FBLK):
        at = g * FBLK
        slot = g % 2
        spread_heads(q4_ref.at[slot], qt_ref, at, heads)
        q4 = q4_ref[slot]
        bias = jnp.where(same, 0.0, bias_ref[tok_rows + at : tok_rows + at + FBLK])
        own_scores = nn(k_ref[at : at + FBLK], q4)
        near_scores = nn(nk, q4)
        scales = []
        for h in range(heads):
            lanes = slice(h * FBLK, (h + 1) * FBLK)
            part = own_scores[:, lanes] + bias
            top = jnp.max(part, axis=0, keepdims=True)
            weight = jnp.exp(part - top)
            top_ref[g : g + 1, lanes] = top
            den_ref[g : g + 1, lanes] = jnp.sum(weight, axis=0, keepdims=True)
            p_ref[slot, :FBLK, lanes] = weight.astype(BF)
            part = near_scores[:, lanes]
            weight = jnp.exp(part - jnp.max(part, axis=0, keepdims=True))
            scales.append(mix_ref[1, h] / jnp.sum(weight, axis=0, keepdims=True))
            p_ref[slot, FBLK:, lanes] = weight.astype(BF)
        own_out = nn(vt_ref[:, at : at + FBLK], p_ref[slot, :FBLK])
        near_out = nn(nvt, p_ref[slot, FBLK:])
        for h in range(heads):
            rows, lanes = slice(h * width, (h + 1) * width), slice(h * FBLK, (h + 1) * FBLK)
            acc_ref[rows, at : at + FBLK] = own_out[rows, lanes]
            near_ref[rows, at : at + FBLK] = near_out[rows, lanes] * scales[h]


def rest_kernel(
    first, blocks, lists_ref, mix_ref, qt_ref, k_ref, vt_ref, comp_ref, e_ref, et_ref, bias_ref, summ_ref,
    selk_ref, selv_ref, acc_ref, near_ref, top_ref, den_ref, out_ref, kw_ref, vw_ref, kc_ref, vc_ref, q4_ref, p_ref,
):
    tok_rows, group = k_ref.shape
    heads = mix_ref.shape[1]
    width = group // heads
    others = FINE_K - 1
    fine = others * FBLK
    mid = 3 * (tok_rows // POOL2)
    far_at = fine + mid
    total = kc_ref.shape[1]
    packed = e_ref.shape[1]
    kw_ref[:tok_rows] = nn(e_ref[...], comp_ref[:packed]).astype(BF)
    kw_ref[tok_rows:] = k_ref[...]
    prev = None
    for part in range(packed // group):
        term = nn(
            comp_ref[packed + part * group : packed + (part + 1) * group],
            et_ref[part * group : (part + 1) * group],
        )
        prev = term if prev is None else prev + term
    vw_ref[:, :tok_rows] = prev.astype(BF)
    vw_ref[:, tok_rows:] = vt_ref[...]
    summ = summ_ref[...]
    coarse_k = nn(selk_ref[...], summ).astype(BF)
    coarse_v = jnp.transpose(nn(selv_ref[...], summ)).astype(BF)
    for slot in range(2):
        kc_ref[slot, fine:] = coarse_k
        vc_ref[slot, :, fine:] = coarse_v
    q4_ref[...] = jnp.zeros_like(q4_ref)
    for index in range(blocks):
        g = first + index
        at = g * FBLK
        slot = index % 2
        biases = []
        for entry in range(others):
            start = pl.multiple_of(lists_ref[g, entry + 1] * FBLK, FBLK)
            kc_ref[slot, entry * FBLK : (entry + 1) * FBLK] = kw_ref[pl.ds(start, FBLK)]
            vc_ref[slot, :, entry * FBLK : (entry + 1) * FBLK] = vw_ref[:, pl.ds(start, FBLK)]
            biases.append(bias_ref[pl.ds(start, FBLK)])
        spread_heads(q4_ref.at[slot], qt_ref, at, heads)
        scores = nn(kc_ref[slot], q4_ref[slot])
        scales, keeps = [], []
        for h in range(heads):
            lanes = slice(h * FBLK, (h + 1) * FBLK)
            parts = [scores[e * FBLK : (e + 1) * FBLK, lanes] + biases[e] for e in range(others)]
            old_top = top_ref[g : g + 1, lanes]
            top = functools.reduce(
                jnp.maximum, [jnp.max(part, axis=0, keepdims=True) for part in parts] + [old_top]
            )
            keep = jnp.exp(old_top - top)
            den = den_ref[g : g + 1, lanes] * keep
            for e, part in enumerate(parts):
                weight = jnp.exp(part - top)
                den = den + jnp.sum(weight, axis=0, keepdims=True)
                p_ref[slot, e * FBLK : (e + 1) * FBLK, lanes] = weight.astype(BF)
            scale = mix_ref[0, h] / den
            scales.append(scale)
            keeps.append(keep * scale)
            for level, (low, high) in enumerate(((fine, far_at), (far_at, total))):
                part = scores[low:high, lanes]
                weight = jnp.exp(part - jnp.max(part, axis=0, keepdims=True))
                share = mix_ref[level + 2, h] / jnp.sum(weight, axis=0, keepdims=True)
                p_ref[slot, low:high, lanes] = (weight * share).astype(BF)
        fine_out = nn(vc_ref[slot, :, :fine], p_ref[slot, :fine])
        coarse_out = nn(vc_ref[slot, :, fine:], p_ref[slot, fine:])
        rows = []
        for h in range(heads):
            pick = (slice(h * width, (h + 1) * width), slice(h * FBLK, (h + 1) * FBLK))
            mine = (pick[0], slice(at, at + FBLK))
            rows.append(
                fine_out[pick] * scales[h]
                + acc_ref[mine] * keeps[h]
                + (coarse_out[pick] + near_ref[mine])
            )
        out_ref[index * FBLK : (index + 1) * FBLK] = jnp.transpose(
            jnp.concatenate(rows, axis=0)
        ).astype(BF)


def output_kernel(place_ref, w_ref, *refs):
    out_ref = refs[-1]
    group = w_ref.shape[1]
    head = place_ref[3]
    total = None
    for distance, part in zip((0, 2, 1, 3), refs[:4]):
        start = pl.multiple_of((head ^ distance) * group, group)
        term = nn(part[...], w_ref[pl.ds(start, group)])
        total = term if total is None else total + term
    out_ref[...] = total.astype(BF)


def local(tokens, w_query, w_key, w_value, w_out, level_mix, fine_blocks, order, mask_ids):
    tok_rows, width = tokens.shape
    slabs = lax.axis_size("seq")
    slab, head = lax.axis_index("seq"), lax.axis_index("head")
    group = w_query.shape[1]
    heads = level_mix.shape[1]
    packed = tok_rows - mask_ids.shape[1]
    near, mids, fars = tok_rows // POOL1, tok_rows // POOL2, tok_rows // POOL3
    coarse = 3 * mids + fars * slabs
    step = 2 * SUMM_ROWS
    chosen = packed + SUMM_ROWS + near

    before_mask = to_next(mask_ids)
    pieces, flip, early = exchange_tokens(tokens, head)
    place = jnp.stack([slab, flip, slabs, head]).astype(I32)
    order, mask_ids, before_mask, w_q, w_v, _ = lax.optimization_barrier(
        (order, mask_ids, before_mask, w_query, w_value, early)
    )

    shape = jax.ShapeDtypeStruct
    params = pltpu.CompilerParams(vmem_limit_bytes=VMEM_LIMIT)
    permute, permute_t, select, f_col, f_row, expand, expand_t, bias, select_k, select_v, w_t = pl.pallas_call(
        prepare_kernel,
        out_shape=(
            shape((tok_rows, tok_rows), BF),
            shape((tok_rows, tok_rows), BF),
            shape((chosen, tok_rows), BF),
            shape((SUMM_ROWS + near, 128), F32),
            shape((16, SUMM_ROWS + near), F32),
            shape((tok_rows, packed), BF),
            shape((packed, tok_rows), BF),
            shape((2 * tok_rows, FBLK), F32),
            shape((coarse, step * slabs), BF),
            shape((coarse, step * slabs), BF),
            shape((2 * group, width), BF),
        ),
        in_specs=smem_specs(1) + vmem_specs(5),
        out_specs=vmem_specs(11),
        compiler_params=params,
        name="prepare",
    )(place, order, mask_ids, before_mask, w_q, w_v)

    places = tuple((row, distances) for _, row, distances in pieces)
    comp, summ, k0, qv0 = pl.pallas_call(
        functools.partial(project_kernel, places),
        out_shape=(
            shape((2 * packed, group), BF),
            shape((slabs, step, group), BF),
            shape((tok_rows, group), BF),
            shape((2 * group, tok_rows), BF),
        ),
        in_specs=smem_specs(1) + vmem_specs(len(pieces) + 5),
        out_specs=vmem_specs(4),
        scratch_shapes=[pltpu.VMEM((tok_rows, width), BF)],
        compiler_params=params,
        name="project",
    )(place, *[piece for piece, _, _ in pieces], w_t, w_key, select, f_col, f_row)
    comp_before = to_next(comp)
    summ_all = lax.all_to_all(summ, "seq", split_axis=0, concat_axis=0, tiled=True).reshape(
        slabs * step, group
    )

    q_t, v_t, keys, near_k, near_vt = pl.pallas_call(
        order_kernel,
        out_shape=(
            shape((group, tok_rows), BF),
            shape((group, tok_rows), BF),
            shape((tok_rows, group), BF),
            shape((near, group), BF),
            shape((group, near), BF),
        ),
        in_specs=vmem_specs(7),
        out_specs=vmem_specs(5),
        compiler_params=params,
        name="order",
    )(permute, permute_t, select, f_col, f_row, k0, qv0)

    blocks = tok_rows // FBLK
    acc, near_out, top, den = pl.pallas_call(
        own_kernel,
        out_shape=(
            shape((group, tok_rows), F32),
            shape((group, tok_rows), F32),
            shape((blocks, heads * FBLK), F32),
            shape((blocks, heads * FBLK), F32),
        ),
        in_specs=smem_specs(1) + vmem_specs(6),
        out_specs=vmem_specs(4),
        scratch_shapes=[
            pltpu.VMEM((2, group, heads * FBLK), BF),
            pltpu.VMEM((2, FBLK + near, heads * FBLK), BF),
        ],
        compiler_params=params,
        name="own",
    )(level_mix, q_t, keys, v_t, bias, near_k, near_vt)

    total = (FINE_K - 1) * FBLK + coarse
    halves = 2
    part_blocks = blocks // halves
    part_rows = tok_rows // halves
    out = None
    for half in range(halves):
        attended = pl.pallas_call(
            functools.partial(rest_kernel, half * part_blocks, part_blocks),
            out_shape=shape((part_rows, group), BF),
            in_specs=smem_specs(2) + vmem_specs(14),
            out_specs=pl.BlockSpec(memory_space=pltpu.VMEM),
            scratch_shapes=[
                pltpu.VMEM((2 * tok_rows, group), BF),
                pltpu.VMEM((group, 2 * tok_rows), BF),
                pltpu.VMEM((2, total, group), BF),
                pltpu.VMEM((2, group, total), BF),
                pltpu.VMEM((2, group, heads * FBLK), BF),
                pltpu.VMEM((2, total, heads * FBLK), BF),
            ],
            compiler_params=params,
            name="rest",
        )(
            fine_blocks, level_mix, q_t, keys, v_t, comp_before, expand, expand_t, bias, summ_all,
            select_k, select_v, acc, near_out, top, den,
        )
        third = over_head(attended, X_PAIRS)
        second = over_head(attended, CORE_PAIRS)
        fourth = over_head(third, CORE_PAIRS)
        steps = 2
        rows = part_rows // steps
        tile = pl.BlockSpec((rows, group), lambda i: (i, 0))
        previous = [] if out is None else [out]
        out = pl.pallas_call(
            output_kernel,
            grid=(steps,),
            out_shape=shape((tok_rows, group), BF),
            in_specs=smem_specs(1)
            + [pl.BlockSpec((width, group), lambda i: (0, 0))]
            + [tile] * 4
            + [pl.BlockSpec(memory_space=pl.ANY)] * len(previous),
            out_specs=pl.BlockSpec((rows, group), lambda i, base=half * steps: (i + base, 0)),
            input_output_aliases={6: 0} if previous else {},
            compiler_params=params,
            name="output",
        )(place, w_out, attended, third, second, fourth, *previous)
    return out


def solution(mesh):
    placed = (
        P("seq", None),
        P(None, "head"),
        P(None, "head"),
        P(None, "head"),
        P(None, "head"),
        P(None, "head"),
        P("seq", None),
        P("seq", None),
        P("seq", None),
    )
    return jax.shard_map(
        local, mesh=mesh, in_specs=placed, out_specs=P("seq", "head"), check_vma=False
    )
```

```python
import functools

import jax
import jax.numpy as jnp
from jax import lax
from jax.experimental import pallas as pl
from jax.experimental.pallas import tpu as pltpu
from jax.sharding import PartitionSpec as P

FBLK = 128
FINE_K = 4
POOL1 = 8
POOL2 = 64
POOL3 = 512
SUMM_ROWS = 32
BF = jnp.bfloat16
F32 = jnp.float32
I32 = jnp.int32
HIDE = -1e30
VMEM_LIMIT = 24 * 1024 * 1024

X_PAIRS = [(0, 2), (2, 0), (1, 3), (3, 1)]
CORE_PAIRS = [(0, 1), (1, 0), (2, 3), (3, 2)]


def nn(a, b):
    return lax.dot_general(a, b, (((1,), (0,)), ((), ())), preferred_element_type=F32)


def nt(a, b):
    return lax.dot_general(a, b, (((1,), (1,)), ((), ())), preferred_element_type=F32)


def iota(shape, axis):
    return lax.broadcasted_iota(I32, shape, axis)


def ones_where(condition):
    return jnp.where(condition, 1.0, 0.0).astype(BF)


def vmem_specs(count):
    return [pl.BlockSpec(memory_space=pltpu.VMEM)] * count


def smem_specs(count):
    return [pl.BlockSpec(memory_space=pltpu.SMEM)] * count


def over_head(block, pairs):
    return lax.ppermute(block, "head", pairs)


def to_next(block):
    return lax.ppermute(block, "seq", [(i, i + 1) for i in range(lax.axis_size("seq") - 1)])


def stack_kernel(counts, *refs):
    sources, targets = refs[: sum(counts)], refs[sum(counts) :]
    for count, target in zip(counts, targets):
        height = target.shape[0] // count
        for index in range(count):
            target[index * height : (index + 1) * height] = sources[index][...]
        sources = sources[count:]


def stacked(*lists):
    parts = [part for one in lists for part in one]
    return pl.pallas_call(
        functools.partial(stack_kernel, tuple(len(one) for one in lists)),
        out_shape=tuple(
            jax.ShapeDtypeStruct((len(one) * one[0].shape[0], one[0].shape[1]), one[0].dtype)
            for one in lists
        ),
        in_specs=vmem_specs(len(parts)),
        out_specs=vmem_specs(len(lists)),
        compiler_params=pltpu.CompilerParams(vmem_limit_bytes=VMEM_LIMIT),
        name="stack",
    )(*parts)


def by_distance(block, distance):
    return lax.ppermute(block, "seq", [(i, i ^ distance) for i in range(lax.axis_size("seq"))])


def exchange_tokens(tokens, head, prepare):
    tok_rows, width = tokens.shape
    slabs = lax.axis_size("seq")
    rows = tok_rows // slabs
    quarter = width // 4
    slab = lax.axis_index("seq")
    split = tokens.reshape(slabs, rows, width)

    def columns(other):
        return lax.dynamic_slice_in_dim(split, (head ^ other) * quarter, quarter, axis=2)

    mine = columns(0)
    if slabs != 8:
        first = lax.all_to_all(mine, "seq", split_axis=0, concat_axis=0, tiled=True).reshape(
            tok_rows, quarter
        )
        third = over_head(first, X_PAIRS)
        second = over_head(first, CORE_PAIRS)
        fourth = over_head(third, CORE_PAIRS)
        pieces = [(first, 0, (0,)), (third, 0, (2,)), (second, 0, (1,)), (fourth, 0, (3,))]
        return pieces, prepare(first)
    both = jnp.concatenate([mine, columns(2)], axis=2)

    def to_peer(source, distance):
        block = lax.dynamic_index_in_dim(source, slab ^ distance, axis=0, keepdims=False)
        return by_distance(block, distance)

    far, near = stacked(
        [to_peer(mine, d) for d in (7, 6, 5, 4)], [to_peer(both, d) for d in (3, 2, 1)]
    )
    far_x = over_head(far, X_PAIRS)
    near_core = over_head(near, CORE_PAIRS)
    far_core = over_head(far, CORE_PAIRS)
    prepared = prepare(far)
    far_x, prepared = lax.optimization_barrier((far_x, prepared))
    far_last = over_head(far_x, CORE_PAIRS)
    pieces = [(far, 0, (0,)), (far_x, 0, (2,)), (far_core, 0, (1,)), (far_last, 0, (3,))]
    pieces += [(near, 4 * rows, (0, 2)), (near_core, 4 * rows, (1, 3)), (tokens, 7 * rows, None)]
    return pieces, prepared


def column(row, lanes=128):
    return jnp.transpose(jnp.broadcast_to(row.astype(F32), (lanes, row.shape[1]))).astype(I32)


def ranks(ids, tok_rows, lanes=128):
    hidden = column(ids)
    parts = []
    for at in range(0, tok_rows, lanes):
        time = iota((1, lanes), 1) + at
        count = jnp.sum(jnp.where(hidden < time, 1.0, 0.0), axis=0, keepdims=True)
        here = jnp.sum(jnp.where(hidden == time, 1.0, 0.0), axis=0, keepdims=True)
        parts.append(jnp.where(here == 0.0, time - count.astype(I32), -1))
    return jnp.concatenate(parts, axis=1)


def prepare_kernel(
    order_ref, mask_ref, wq_ref, wv_ref, early_ref,
    p_ref, pt_ref, sel_ref, fcol_ref, frow_ref, bias_ref, wt_ref,
):
    slab, slabs = lax.axis_index("seq"), lax.axis_size("seq")
    tok_rows = order_ref.shape[1]
    packed = tok_rows - mask_ref.shape[1]
    flip = (slab ^ 7) * (tok_rows // slabs) if slabs == 8 else 0
    mids = tok_rows // POOL2
    group = wq_ref.shape[1]
    lanes = 128

    place = order_ref[...] ^ flip
    place_column = column(place)
    for at in range(0, tok_rows, lanes):
        p_ref[:, at : at + lanes] = ones_where(place_column == iota((tok_rows, lanes), 1) + at)
        pt_ref[at : at + lanes] = ones_where(iota((lanes, tok_rows), 0) + at == place)
    rank = ranks(mask_ref[...], tok_rows)
    time = jnp.where(rank >= 0, iota((1, tok_rows), 1), -1) + 1
    line = iota((16, tok_rows), 0)
    stack = jnp.where(
        line == 0,
        time >> 5,
        jnp.where(
            line == 1,
            time & 31,
            jnp.where(line == 2, (rank + 1) >> 5, jnp.where(line == 3, (rank + 1) & 31, 0)),
        ),
    )
    moved = nn(stack.astype(F32).astype(BF), p_ref[...]).astype(I32)
    time_here = (moved[0:1] << 5) + moved[1:2] - 1
    rank_here = (moved[2:3] << 5) + moved[3:4] - 1
    for at in range(0, packed, lanes):
        sel_ref[at : at + lanes] = ones_where(iota((lanes, tok_rows), 0) + at == rank_here)
    line = iota((SUMM_ROWS, tok_rows), 0)
    sel_ref[packed : packed + SUMM_ROWS] = ones_where(
        ((time_here >> 6) == line) | (((time_here >> 9) + mids == line) & (time_here >= 0))
    )
    lead = packed + SUMM_ROWS
    near = sel_ref.shape[0] - lead
    sel_ref[lead:] = ones_where((time_here >> 3) == iota((near, tok_rows), 0))
    pools = sel_ref[packed:]
    fcol_ref[...] = 1.0 / jnp.sqrt(jnp.maximum(nn(pools, jnp.ones((tok_rows, lanes), BF)), 1.0))
    frow_ref[...] = 1.0 / jnp.sqrt(jnp.maximum(nt(jnp.ones((16, tok_rows), BF), pools), 1.0))
    bias_ref[...] = jnp.where(column(rank) >= 0, 0.0, HIDE)
    wt_ref[:group] = jnp.transpose(wq_ref[...])
    wt_ref[group:] = jnp.transpose(wv_ref[...])


def project_kernel(places, *refs):
    count = len(places)
    piece_refs, refs = refs[:count], refs[count:]
    wt_ref, wk_ref, sel_ref, fcol_ref, comp_ref, summ_ref, k_ref, v_ref, x_ref, sem_ref = refs
    quarter = x_ref.shape[1] // 4
    head = lax.axis_index("head")
    loads = []
    for piece, (row, distances) in zip(piece_refs, places):
        height = piece.shape[0]
        if distances is None:
            rows = height // lax.axis_size("seq")
            start = pl.multiple_of(lax.axis_index("seq") * rows, rows)
            loads.append(
                pltpu.make_async_copy(
                    piece.at[pl.ds(start, rows)], x_ref.at[row : row + rows], sem_ref
                )
            )
            loads[-1].start()
    for piece, (row, distances) in zip(piece_refs, places):
        height = piece.shape[0]
        if distances is None:
            continue
        for part, distance in enumerate(distances):
            start = pl.multiple_of((head ^ distance) * quarter, quarter)
            x_ref[row : row + height, pl.ds(start, quarter)] = piece[
                :, part * quarter : (part + 1) * quarter
            ]
    group = wk_ref.shape[1]
    packed = comp_ref.shape[0] // 2
    lead = packed + SUMM_ROWS
    for load in loads:
        load.wait()
    x = x_ref[...]
    keys = nn(x, wk_ref[...]).astype(BF)
    k_ref[...] = keys
    vt = nt(wt_ref[group:], x).astype(BF)
    v_ref[...] = vt
    sel = sel_ref[:lead]
    kl = nn(sel, keys)
    vl = nt(vt, sel)
    comp_ref[:packed] = kl[:packed].astype(BF)
    vc = vl[:, :packed].astype(BF)
    for part in range(packed // group):
        comp_ref[packed + part * group : packed + (part + 1) * group] = vc[
            :, part * group : (part + 1) * group
        ]
    factor = fcol_ref[:SUMM_ROWS, :1]
    summ_k = (kl[packed:] * factor).astype(BF)
    tail = jnp.concatenate(
        [vl[:, packed:], jnp.zeros((group, 128 - SUMM_ROWS), F32)], axis=1
    )
    summ_v = (jnp.transpose(tail)[:SUMM_ROWS] * factor).astype(BF)
    summ_ref[:SUMM_ROWS] = summ_k
    summ_ref[SUMM_ROWS:] = summ_v


def spread_heads(q4_ref, qt_ref, at, heads):
    width = q4_ref.shape[0] // heads
    for h in range(heads):
        rows = slice(h * width, (h + 1) * width)
        q4_ref[rows, h * FBLK : (h + 1) * FBLK] = qt_ref[rows, at : at + FBLK]


def own_kernel(
    mix_ref, before_ref, p_in, pt_ref, sel_ref, fcol_ref, frow_ref, wt_ref, x_ref, k0_ref, v0_ref, seen_ref,
    qt_ref, vt_ref, k_ref, acc_ref, near_ref, top_ref, den_ref, e_ref, et_ref, bias_ref, q4_ref, p_ref,
):
    tok_rows, group = k_ref.shape
    heads = mix_ref.shape[1]
    width = group // heads
    near = tok_rows // POOL1
    q4_ref[...] = jnp.zeros_like(q4_ref)
    same = iota((FBLK, FBLK), 0) == iota((FBLK, FBLK), 1)
    k0, v0 = k0_ref[...], v0_ref[...]
    q0 = nt(wt_ref[:group], x_ref[...]).astype(BF)
    k_ref[...] = nn(p_in[...], k0).astype(BF)
    qt_ref[...] = (nn(q0, pt_ref[...]) * 0.125).astype(BF)
    vt_ref[...] = nn(v0, pt_ref[...]).astype(BF)
    pool = sel_ref[sel_ref.shape[0] - near :]
    nk = (nn(pool, k0) * fcol_ref[SUMM_ROWS:, :1]).astype(BF)
    nvt = (nt(v0, pool) * frow_ref[:1, SUMM_ROWS:]).astype(BF)
    for g in range(tok_rows // FBLK):
        at = g * FBLK
        slot = g % 2
        spread_heads(q4_ref.at[slot], qt_ref, at, heads)
        q4 = q4_ref[slot]
        bias = jnp.where(same, 0.0, seen_ref[at : at + FBLK])
        own_scores = nn(k_ref[at : at + FBLK], q4)
        near_scores = nn(nk, q4)
        scales = []
        for h in range(heads):
            lanes = slice(h * FBLK, (h + 1) * FBLK)
            part = own_scores[:, lanes] + bias
            top = jnp.max(part, axis=0, keepdims=True)
            weight = jnp.exp(part - top)
            top_ref[g : g + 1, lanes] = top
            den_ref[g : g + 1, lanes] = jnp.sum(weight, axis=0, keepdims=True)
            p_ref[slot, :FBLK, lanes] = weight.astype(BF)
            part = near_scores[:, lanes]
            weight = jnp.exp(part - jnp.max(part, axis=0, keepdims=True))
            scales.append(mix_ref[1, h] / jnp.sum(weight, axis=0, keepdims=True))
            p_ref[slot, FBLK:, lanes] = weight.astype(BF)
        own_out = nn(vt_ref[:, at : at + FBLK], p_ref[slot, :FBLK])
        near_out = nn(nvt, p_ref[slot, FBLK:])
        for h in range(heads):
            rows, lanes = slice(h * width, (h + 1) * width), slice(h * FBLK, (h + 1) * FBLK)
            acc_ref[rows, at : at + FBLK] = own_out[rows, lanes]
            near_ref[rows, at : at + FBLK] = near_out[rows, lanes] * scales[h]
    rank = jnp.where(lax.axis_index("seq") > 0, ranks(before_ref[...], tok_rows), -1)
    rank_column = column(rank)
    bias_ref[:tok_rows] = jnp.where(rank_column >= 0, 0.0, HIDE)
    bias_ref[tok_rows:] = seen_ref[...]
    for at in range(0, et_ref.shape[0], FBLK):
        e_ref[:, at : at + FBLK] = ones_where(rank_column == iota((tok_rows, FBLK), 1) + at)
        et_ref[at : at + FBLK] = ones_where(iota((FBLK, tok_rows), 0) + at == rank)


def window_kernel(k_ref, vt_ref, comp_ref, e_ref, et_ref, *refs):
    summ_refs, (kw_ref, vw_ref, ck_ref, cv_ref, all_ref) = refs[:-5], refs[-5:]
    tok_rows, group = k_ref.shape
    packed = e_ref.shape[1]
    kw_ref[:tok_rows] = nn(e_ref[...], comp_ref[:packed]).astype(BF)
    kw_ref[tok_rows:] = k_ref[...]
    prev = None
    for part in range(packed // group):
        term = nn(
            comp_ref[packed + part * group : packed + (part + 1) * group],
            et_ref[part * group : (part + 1) * group],
        )
        prev = term if prev is None else prev + term
    vw_ref[:, :tok_rows] = prev.astype(BF)
    vw_ref[:, tok_rows:] = vt_ref[...]
    at = 0
    for part in summ_refs:
        all_ref[at : at + part.shape[0]] = part[...]
        at += part.shape[0]
    slab, slabs = lax.axis_index("seq"), lax.axis_size("seq")
    mids, fars = tok_rows // POOL2, tok_rows // POOL3
    shape = (ck_ref.shape[0], all_ref.shape[0])
    line = iota(shape, 0)
    step = 2 * SUMM_ROWS
    turn = line // mids
    far = line - 3 * mids
    shard = slab - 1 + turn
    turned = slab if slabs == 8 else 0
    source = jnp.where(
        line < 3 * mids,
        (shard ^ turned) * step + line - turn * mids,
        ((far // fars) ^ turned) * step + mids + far % fars,
    )
    source = jnp.where((line >= 3 * mids) | ((shard >= 0) & (shard < slabs)), source, -step)
    gathered = all_ref[...]
    ck_ref[...] = nn(ones_where(source == iota(shape, 1)), gathered).astype(BF)
    values = nn(ones_where(source + SUMM_ROWS == iota(shape, 1)), gathered)
    cv_ref[...] = jnp.transpose(values).astype(BF)


def rest_kernel(
    first, blocks, lists_ref, mix_ref, qt_ref, kw_ref, vw_ref, ck_ref, cv_ref, bias_ref,
    acc_ref, near_ref, top_ref, den_ref, out_ref, kc_ref, vc_ref, q4_ref, p_ref,
):
    group, tok_rows = qt_ref.shape
    heads = mix_ref.shape[1]
    width = group // heads
    others = FINE_K - 1
    fine = others * FBLK
    mid = 3 * (tok_rows // POOL2)
    far_at = fine + mid
    total = kc_ref.shape[1]
    for slot in range(2):
        kc_ref[slot, fine:] = ck_ref[...]
        vc_ref[slot, :, fine:] = cv_ref[...]
    q4_ref[...] = jnp.zeros_like(q4_ref)
    for index in range(blocks):
        g = first + index
        at = g * FBLK
        slot = index % 2
        biases = []
        for entry in range(others):
            start = pl.multiple_of(lists_ref[entry + 1, g] * FBLK, FBLK)
            kc_ref[slot, entry * FBLK : (entry + 1) * FBLK] = kw_ref[pl.ds(start, FBLK)]
            vc_ref[slot, :, entry * FBLK : (entry + 1) * FBLK] = vw_ref[:, pl.ds(start, FBLK)]
            biases.append(bias_ref[pl.ds(start, FBLK)])
        spread_heads(q4_ref.at[slot], qt_ref, at, heads)
        scores = nn(kc_ref[slot], q4_ref[slot])
        scales, keeps = [], []
        for h in range(heads):
            lanes = slice(h * FBLK, (h + 1) * FBLK)
            parts = [scores[e * FBLK : (e + 1) * FBLK, lanes] + biases[e] for e in range(others)]
            old_top = top_ref[g : g + 1, lanes]
            top = functools.reduce(
                jnp.maximum, [jnp.max(part, axis=0, keepdims=True) for part in parts] + [old_top]
            )
            keep = jnp.exp(old_top - top)
            den = den_ref[g : g + 1, lanes] * keep
            for e, part in enumerate(parts):
                weight = jnp.exp(part - top)
                den = den + jnp.sum(weight, axis=0, keepdims=True)
                p_ref[slot, e * FBLK : (e + 1) * FBLK, lanes] = weight.astype(BF)
            scale = mix_ref[0, h] / den
            scales.append(scale)
            keeps.append(keep * scale)
            for level, (low, high) in enumerate(((fine, far_at), (far_at, total))):
                part = scores[low:high, lanes]
                weight = jnp.exp(part - jnp.max(part, axis=0, keepdims=True))
                share = mix_ref[level + 2, h] / jnp.sum(weight, axis=0, keepdims=True)
                p_ref[slot, low:high, lanes] = (weight * share).astype(BF)
        fine_out = nn(vc_ref[slot, :, :fine], p_ref[slot, :fine])
        coarse_out = nn(vc_ref[slot, :, fine:], p_ref[slot, fine:])
        rows = []
        for h in range(heads):
            pick = (slice(h * width, (h + 1) * width), slice(h * FBLK, (h + 1) * FBLK))
            mine = (pick[0], slice(at, at + FBLK))
            rows.append(
                fine_out[pick] * scales[h]
                + acc_ref[mine] * keeps[h]
                + (coarse_out[pick] + near_ref[mine])
            )
        out_ref[index * FBLK : (index + 1) * FBLK] = jnp.transpose(
            jnp.concatenate(rows, axis=0)
        ).astype(BF)


def output_kernel(w_ref, *refs):
    out_ref = refs[-1]
    group = w_ref.shape[1]
    head = lax.axis_index("head")
    total = None
    for distance, part in zip((0, 2, 1, 3), refs[:4]):
        start = pl.multiple_of((head ^ distance) * group, group)
        term = nn(part[...], w_ref[pl.ds(start, group)])
        total = term if total is None else total + term
    out_ref[...] = total.astype(BF)


def local(tokens, w_query, w_key, w_value, w_out, level_mix, fine_blocks, order, mask_ids):
    tok_rows, width = tokens.shape
    slabs = lax.axis_size("seq")
    slab, head = lax.axis_index("seq"), lax.axis_index("head")
    group = w_query.shape[1]
    heads = level_mix.shape[1]
    packed = tok_rows - mask_ids.shape[1]
    near, mids, fars = tok_rows // POOL1, tok_rows // POOL2, tok_rows // POOL3
    coarse = 3 * mids + fars * slabs
    step = 2 * SUMM_ROWS
    chosen = packed + SUMM_ROWS + near

    shape = jax.ShapeDtypeStruct
    params = pltpu.CompilerParams(vmem_limit_bytes=VMEM_LIMIT)
    before_mask = to_next(mask_ids)

    def prepare(early):
        return pl.pallas_call(
            prepare_kernel,
            out_shape=(
                shape((tok_rows, tok_rows), BF),
                shape((tok_rows, tok_rows), BF),
                shape((chosen, tok_rows), BF),
                shape((SUMM_ROWS + near, 128), F32),
                shape((16, SUMM_ROWS + near), F32),
                shape((tok_rows, FBLK), F32),
                shape((2 * group, width), BF),
            ),
            in_specs=vmem_specs(4) + [pl.BlockSpec(memory_space=pl.ANY)],
            out_specs=vmem_specs(7),
            compiler_params=params,
            name="prepare",
        )(order, mask_ids, w_query, w_value, early)

    pieces, prepared = exchange_tokens(tokens, head, prepare)
    permute, permute_t, select, f_col, f_row, seen, w_t = prepared
    places = tuple((row, distances) for _, row, distances in pieces)
    comp, summ, k0, v0, rows_here = pl.pallas_call(
        functools.partial(project_kernel, places),
        out_shape=(
            shape((2 * packed, group), BF),
            shape((step, group), BF),
            shape((tok_rows, group), BF),
            shape((group, tok_rows), BF),
            shape((tok_rows, width), BF),
        ),
        in_specs=[
            pl.BlockSpec(memory_space=pltpu.VMEM if distances else pl.ANY)
            for _, distances in places
        ]
        + vmem_specs(4),
        out_specs=vmem_specs(5),
        scratch_shapes=[pltpu.SemaphoreType.DMA],
        compiler_params=params,
        name="project",
    )(*[piece for piece, _, _ in pieces], w_t, w_key, select, f_col)
    comp_before = to_next(comp)
    if slabs == 8:
        summaries = [summ] + [by_distance(summ, d) for d in range(1, slabs)]
    else:
        copies = jnp.broadcast_to(summ[None], (slabs, step, group))
        copies = lax.all_to_all(copies, "seq", split_axis=0, concat_axis=0, tiled=True)
        summaries = [copies.reshape(slabs * step, group)]

    blocks = tok_rows // FBLK
    q_t, v_t, keys, acc, near_out, top, den, expand, expand_t, bias = pl.pallas_call(
        own_kernel,
        out_shape=(
            shape((group, tok_rows), BF),
            shape((group, tok_rows), BF),
            shape((tok_rows, group), BF),
            shape((group, tok_rows), F32),
            shape((group, tok_rows), F32),
            shape((blocks, heads * FBLK), F32),
            shape((blocks, heads * FBLK), F32),
            shape((tok_rows, packed), BF),
            shape((packed, tok_rows), BF),
            shape((2 * tok_rows, FBLK), F32),
        ),
        in_specs=smem_specs(1) + vmem_specs(11),
        out_specs=vmem_specs(10),
        scratch_shapes=[
            pltpu.VMEM((2, group, heads * FBLK), BF),
            pltpu.VMEM((2, FBLK + near, heads * FBLK), BF),
        ],
        compiler_params=params,
        name="own",
    )(level_mix, before_mask, permute, permute_t, select, f_col, f_row, w_t, rows_here, k0, v0, seen)

    window_k, window_v, coarse_k, coarse_v = pl.pallas_call(
        window_kernel,
        out_shape=(
            shape((2 * tok_rows, group), BF),
            shape((group, 2 * tok_rows), BF),
            shape((coarse, group), BF),
            shape((group, coarse), BF),
        ),
        in_specs=vmem_specs(5 + len(summaries)),
        out_specs=vmem_specs(4),
        scratch_shapes=[pltpu.VMEM((slabs * step, group), BF)],
        compiler_params=params,
        name="window",
    )(keys, v_t, comp_before, expand, expand_t, *summaries)

    total = (FINE_K - 1) * FBLK + coarse
    lists = fine_blocks.T
    halves = 2
    part_blocks = blocks // halves
    part_rows = tok_rows // halves
    out = None
    for half in range(halves):
        attended = pl.pallas_call(
            functools.partial(rest_kernel, half * part_blocks, part_blocks),
            out_shape=shape((part_rows, group), BF),
            in_specs=smem_specs(2) + vmem_specs(10),
            out_specs=pl.BlockSpec(memory_space=pltpu.VMEM),
            scratch_shapes=[
                pltpu.VMEM((2, total, group), BF),
                pltpu.VMEM((2, group, total), BF),
                pltpu.VMEM((2, group, heads * FBLK), BF),
                pltpu.VMEM((2, total, heads * FBLK), BF),
            ],
            compiler_params=params,
            name="rest",
        )(
            lists, level_mix, q_t, window_k, window_v, coarse_k, coarse_v, bias, acc, near_out, top, den
        )
        third = over_head(attended, X_PAIRS)
        second = over_head(attended, CORE_PAIRS)
        if out is not None:
            third, out = lax.optimization_barrier((third, out))
        fourth = over_head(third, CORE_PAIRS)
        steps = 2
        rows = part_rows // steps
        tile = pl.BlockSpec((rows, group), lambda i: (i, 0))
        previous = [] if out is None else [out]
        out = pl.pallas_call(
            output_kernel,
            grid=(steps,),
            out_shape=shape((tok_rows, group), BF),
            in_specs=[pl.BlockSpec((width, group), lambda i: (0, 0))]
            + [tile] * 4
            + [pl.BlockSpec(memory_space=pl.ANY)] * len(previous),
            out_specs=pl.BlockSpec((rows, group), lambda i, base=half * steps: (i + base, 0)),
            input_output_aliases={5: 0} if previous else {},
            compiler_params=params,
            name="output",
        )(w_out, attended, third, second, fourth, *previous)
    return out


def solution(mesh):
    placed = (
        P("seq", None),
        P(None, "head"),
        P(None, "head"),
        P(None, "head"),
        P(None, "head"),
        P(None, "head"),
        P("seq", None),
        P("seq", None),
        P("seq", None),
    )
    return jax.shard_map(
        local, mesh=mesh, in_specs=placed, out_specs=P("seq", "head"), check_vma=False
    )
```

```python
import functools

import jax
import jax.numpy as jnp
from jax import lax
from jax.experimental import pallas as pl
from jax.experimental.pallas import tpu as pltpu
from jax.sharding import PartitionSpec as P

FBLK = 128
FINE_K = 4
POOL1 = 8
POOL2 = 64
POOL3 = 512
SUMM_ROWS = 32
BF = jnp.bfloat16
F32 = jnp.float32
I32 = jnp.int32
HIDE = -1e30
VMEM_LIMIT = 24 * 1024 * 1024
PARTS = (2, 3, 3)

X_PAIRS = [(0, 2), (2, 0), (1, 3), (3, 1)]
CORE_PAIRS = [(0, 1), (1, 0), (2, 3), (3, 2)]


def nn(a, b):
    return lax.dot_general(a, b, (((1,), (0,)), ((), ())), preferred_element_type=F32)


def nt(a, b):
    return lax.dot_general(a, b, (((1,), (1,)), ((), ())), preferred_element_type=F32)


def iota(shape, axis):
    return lax.broadcasted_iota(I32, shape, axis)


def ones_where(condition):
    return jnp.where(condition, 1.0, 0.0).astype(BF)


def vmem_specs(count):
    return [pl.BlockSpec(memory_space=pltpu.VMEM)] * count


def smem_specs(count):
    return [pl.BlockSpec(memory_space=pltpu.SMEM)] * count


def over_head(block, pairs):
    return lax.ppermute(block, "head", pairs)


def to_next(block):
    return lax.ppermute(block, "seq", [(i, i + 1) for i in range(lax.axis_size("seq") - 1)])


def send_kernel(distances, tokens_ref, *refs):
    outs, own, sem_ref = refs[:-2], refs[-2], refs[-1]
    slab, head = lax.axis_index("seq"), lax.axis_index("head")
    rows = outs[0].shape[0]
    quarter = tokens_ref.shape[1] // 4
    copies = []
    for distance, out in zip(distances, outs):
        row = pl.multiple_of((slab ^ distance) * rows, rows)
        for part in range(out.shape[1] // quarter):
            start = pl.multiple_of((head ^ (2 * part)) * quarter, quarter)
            copies.append(
                pltpu.make_async_copy(
                    tokens_ref.at[pl.ds(row, rows), pl.ds(start, quarter)],
                    out.at[:, part * quarter : (part + 1) * quarter],
                    sem_ref.at[len(copies)],
                )
            )
    row = pl.multiple_of(slab * rows, rows)
    copies.append(
        pltpu.make_async_copy(tokens_ref.at[pl.ds(row, rows)], own, sem_ref.at[len(copies)])
    )
    for copy in copies:
        copy.start()
    for copy in copies:
        copy.wait()


def stack_kernel(counts, *refs):
    sources, targets = refs[: sum(counts)], refs[len(refs) - len(counts) :]
    for count, target in zip(counts, targets):
        height = target.shape[0] // count
        for index in range(count):
            target[index * height : (index + 1) * height] = sources[index][...]
        sources = sources[count:]


def stacked(lists, after):
    parts = [part for one in lists for part in one]
    return pl.pallas_call(
        functools.partial(stack_kernel, tuple(len(one) for one in lists)),
        out_shape=tuple(
            jax.ShapeDtypeStruct((len(one) * one[0].shape[0], one[0].shape[1]), one[0].dtype)
            for one in lists
        ),
        in_specs=vmem_specs(len(parts)) + [pl.BlockSpec(memory_space=pl.ANY)],
        out_specs=vmem_specs(len(lists)),
        compiler_params=pltpu.CompilerParams(vmem_limit_bytes=VMEM_LIMIT),
        name="stack",
    )(*parts, after)


def by_distance(block, distance):
    return lax.ppermute(block, "seq", [(i, i ^ distance) for i in range(lax.axis_size("seq"))])


def exchange_tokens(tokens, before_mask, prepare):
    tok_rows, width = tokens.shape
    slabs = lax.axis_size("seq")
    rows = tok_rows // slabs
    quarter = width // 4
    if slabs != 8:
        split = tokens.reshape(slabs, rows, width)
        mine = lax.dynamic_slice_in_dim(split, lax.axis_index("head") * quarter, quarter, axis=2)
        first = lax.all_to_all(mine, "seq", split_axis=0, concat_axis=0, tiled=True).reshape(
            tok_rows, quarter
        )
        third = over_head(first, X_PAIRS)
        second = over_head(first, CORE_PAIRS)
        fourth = over_head(third, CORE_PAIRS)
        pieces = [(first, 0, (0,)), (third, 0, (2,)), (second, 0, (1,)), (fourth, 0, (3,))]
        return pieces, prepare(first)
    distances = (7, 6, 5, 4, 3, 2, 1)
    *blocks, own = pl.pallas_call(
        functools.partial(send_kernel, distances),
        out_shape=tuple(
            jax.ShapeDtypeStruct((rows, columns), BF)
            for columns in [quarter if d > 3 else 2 * quarter for d in distances] + [width]
        ),
        in_specs=[pl.BlockSpec(memory_space=pl.ANY)],
        out_specs=[pl.BlockSpec(memory_space=pl.ANY)] * 8,
        scratch_shapes=[pltpu.SemaphoreType.DMA((11,))],
        compiler_params=pltpu.CompilerParams(vmem_limit_bytes=60 * 1024 * 1024),
        name="send",
    )(tokens)
    arrived = [by_distance(block, d) for block, d in zip(blocks, distances)]
    far, near = stacked((arrived[:4], arrived[4:]), before_mask)
    far_x = over_head(far, X_PAIRS)
    near_core = over_head(near, CORE_PAIRS)
    far_core = over_head(far, CORE_PAIRS)
    prepared = prepare(far)
    far_x, prepared = lax.optimization_barrier((far_x, prepared))
    far_last = over_head(far_x, CORE_PAIRS)
    pieces = [(far, 0, (0,)), (far_x, 0, (2,)), (far_core, 0, (1,)), (far_last, 0, (3,))]
    pieces += [(near, 4 * rows, (0, 2)), (near_core, 4 * rows, (1, 3)), (own, 7 * rows, None)]
    return pieces, prepared


def column(row, lanes=128):
    return jnp.transpose(jnp.broadcast_to(row.astype(F32), (lanes, row.shape[1]))).astype(I32)


def ranks(ids, tok_rows, lanes=128):
    hidden = column(ids)
    parts = []
    for at in range(0, tok_rows, lanes):
        time = iota((1, lanes), 1) + at
        count = jnp.sum(jnp.where(hidden < time, 1.0, 0.0), axis=0, keepdims=True)
        here = jnp.sum(jnp.where(hidden == time, 1.0, 0.0), axis=0, keepdims=True)
        parts.append(jnp.where(here == 0.0, time - count.astype(I32), -1))
    return jnp.concatenate(parts, axis=1)


def prepare_kernel(
    order_ref, mask_ref, before_ref, wq_ref, wv_ref, wk_in, early_ref,
    p_ref, pt_ref, sel_ref, fcol_ref, frow_ref, e_ref, et_ref, bias_ref, wt_ref, wk_ref,
):
    slab, slabs = lax.axis_index("seq"), lax.axis_size("seq")
    tok_rows = order_ref.shape[1]
    packed = tok_rows - mask_ref.shape[1]
    flip = (slab ^ 7) * (tok_rows // slabs) if slabs == 8 else 0
    mids = tok_rows // POOL2
    group = wq_ref.shape[1]
    lanes = 128

    place = order_ref[...] ^ flip
    place_column = column(place)
    for at in range(0, tok_rows, lanes):
        p_ref[:, at : at + lanes] = ones_where(place_column == iota((tok_rows, lanes), 1) + at)
        pt_ref[at : at + lanes] = ones_where(iota((lanes, tok_rows), 0) + at == place)
    rank = ranks(mask_ref[...], tok_rows)
    time = jnp.where(rank >= 0, iota((1, tok_rows), 1), -1) + 1
    line = iota((16, tok_rows), 0)
    stack = jnp.where(
        line == 0,
        time >> 5,
        jnp.where(
            line == 1,
            time & 31,
            jnp.where(line == 2, (rank + 1) >> 5, jnp.where(line == 3, (rank + 1) & 31, 0)),
        ),
    )
    moved = nn(stack.astype(F32).astype(BF), p_ref[...]).astype(I32)
    time_here = (moved[0:1] << 5) + moved[1:2] - 1
    rank_here = (moved[2:3] << 5) + moved[3:4] - 1
    for at in range(0, packed, lanes):
        sel_ref[at : at + lanes] = ones_where(iota((lanes, tok_rows), 0) + at == rank_here)
    line = iota((SUMM_ROWS, tok_rows), 0)
    sel_ref[packed : packed + SUMM_ROWS] = ones_where(
        ((time_here >> 6) == line) | (((time_here >> 9) + mids == line) & (time_here >= 0))
    )
    lead = packed + SUMM_ROWS
    near = sel_ref.shape[0] - lead
    sel_ref[lead:] = ones_where((time_here >> 3) == iota((near, tok_rows), 0))
    pools = sel_ref[packed:]
    fcol_ref[...] = 1.0 / jnp.sqrt(jnp.maximum(nn(pools, jnp.ones((tok_rows, lanes), BF)), 1.0))
    frow_ref[...] = 1.0 / jnp.sqrt(jnp.maximum(nt(jnp.ones((16, tok_rows), BF), pools), 1.0))
    rank_before = jnp.where(slab > 0, ranks(before_ref[...], tok_rows), -1)
    rank_column = column(rank_before)
    for at in range(0, packed, lanes):
        e_ref[:, at : at + lanes] = ones_where(rank_column == iota((tok_rows, lanes), 1) + at)
        et_ref[at : at + lanes] = ones_where(iota((lanes, tok_rows), 0) + at == rank_before)
    bias_ref[:tok_rows] = jnp.where(rank_column >= 0, 0.0, HIDE)
    bias_ref[tok_rows:] = jnp.where(column(rank) >= 0, 0.0, HIDE)
    wt_ref[:group] = jnp.transpose(wq_ref[...])
    wt_ref[group:] = jnp.transpose(wv_ref[...])
    wk_ref[...] = wk_in[...]


def project_kernel(places, *refs):
    count = len(places)
    piece_refs, refs = refs[:count], refs[count:]
    wt_ref, wk_ref, sel_ref, fcol_ref, comp_ref, summ_ref, k_ref, v_ref, x_ref = refs
    quarter = x_ref.shape[1] // 4
    head = lax.axis_index("head")
    for piece, (row, distances) in zip(piece_refs, places):
        height = piece.shape[0]
        if distances is None:
            x_ref[row : row + height] = piece[...]
            continue
        for part, distance in enumerate(distances):
            start = pl.multiple_of((head ^ distance) * quarter, quarter)
            x_ref[row : row + height, pl.ds(start, quarter)] = piece[
                :, part * quarter : (part + 1) * quarter
            ]
    group = wk_ref.shape[1]
    packed = comp_ref.shape[0] // 2
    lead = packed + SUMM_ROWS
    x = x_ref[...]
    keys = nn(x, wk_ref[...]).astype(BF)
    k_ref[...] = keys
    vt = nt(wt_ref[group:], x).astype(BF)
    v_ref[...] = vt
    sel = sel_ref[:lead]
    kl = nn(sel, keys)
    vl = nt(vt, sel)
    comp_ref[:packed] = kl[:packed].astype(BF)
    vc = vl[:, :packed].astype(BF)
    for part in range(packed // group):
        comp_ref[packed + part * group : packed + (part + 1) * group] = vc[
            :, part * group : (part + 1) * group
        ]
    factor = fcol_ref[:SUMM_ROWS, :1]
    summ_k = (kl[packed:] * factor).astype(BF)
    tail = jnp.concatenate(
        [vl[:, packed:], jnp.zeros((group, 128 - SUMM_ROWS), F32)], axis=1
    )
    summ_v = (jnp.transpose(tail)[:SUMM_ROWS] * factor).astype(BF)
    summ_ref[:SUMM_ROWS] = summ_k
    summ_ref[SUMM_ROWS:] = summ_v


def spread_heads(q4_ref, qt_ref, at, heads):
    width = q4_ref.shape[0] // heads
    for h in range(heads):
        rows = slice(h * width, (h + 1) * width)
        q4_ref[rows, h * FBLK : (h + 1) * FBLK] = qt_ref[rows, at : at + FBLK]


def own_kernel(
    mix_ref, p_in, pt_ref, sel_ref, fcol_ref, frow_ref, wt_ref, x_ref, k0_ref, v0_ref, bias_ref,
    qt_ref, vt_ref, k_ref, acc_ref, near_ref, top_ref, den_ref, q4_ref, p_ref,
):
    tok_rows, group = k_ref.shape
    heads = mix_ref.shape[1]
    width = group // heads
    near = tok_rows // POOL1
    q4_ref[...] = jnp.zeros_like(q4_ref)
    same = iota((FBLK, FBLK), 0) == iota((FBLK, FBLK), 1)
    k0, v0 = k0_ref[...], v0_ref[...]
    q0 = nt(wt_ref[:group], x_ref[...]).astype(BF)
    k_ref[...] = nn(p_in[...], k0).astype(BF)
    qt_ref[...] = (nn(q0, pt_ref[...]) * 0.125).astype(BF)
    vt_ref[...] = nn(v0, pt_ref[...]).astype(BF)
    pool = sel_ref[sel_ref.shape[0] - near :]
    nk = (nn(pool, k0) * fcol_ref[SUMM_ROWS:, :1]).astype(BF)
    nvt = (nt(v0, pool) * frow_ref[:1, SUMM_ROWS:]).astype(BF)
    for g in range(tok_rows // FBLK):
        at = g * FBLK
        slot = g % 2
        spread_heads(q4_ref.at[slot], qt_ref, at, heads)
        q4 = q4_ref[slot]
        bias = jnp.where(same, 0.0, bias_ref[tok_rows + at : tok_rows + at + FBLK])
        own_scores = nn(k_ref[at : at + FBLK], q4)
        near_scores = nn(nk, q4)
        scales = []
        for h in range(heads):
            lanes = slice(h * FBLK, (h + 1) * FBLK)
            part = own_scores[:, lanes] + bias
            top = jnp.max(part, axis=0, keepdims=True)
            weight = jnp.exp(part - top)
            top_ref[g : g + 1, lanes] = top
            den_ref[g : g + 1, lanes] = jnp.sum(weight, axis=0, keepdims=True)
            p_ref[slot, :FBLK, lanes] = weight.astype(BF)
            part = near_scores[:, lanes]
            weight = jnp.exp(part - jnp.max(part, axis=0, keepdims=True))
            scales.append(mix_ref[1, h] / jnp.sum(weight, axis=0, keepdims=True))
            p_ref[slot, FBLK:, lanes] = weight.astype(BF)
        own_out = nn(vt_ref[:, at : at + FBLK], p_ref[slot, :FBLK])
        near_out = nn(nvt, p_ref[slot, FBLK:])
        for h in range(heads):
            rows, lanes = slice(h * width, (h + 1) * width), slice(h * FBLK, (h + 1) * FBLK)
            acc_ref[rows, at : at + FBLK] = own_out[rows, lanes]
            near_ref[rows, at : at + FBLK] = near_out[rows, lanes] * scales[h]


def window_kernel(k_ref, vt_ref, comp_ref, e_ref, et_ref, *refs):
    summ_refs, (kw_ref, vw_ref, ck_ref, cv_ref, all_ref) = refs[:-5], refs[-5:]
    tok_rows, group = k_ref.shape
    packed = e_ref.shape[1]
    kw_ref[:tok_rows] = nn(e_ref[...], comp_ref[:packed]).astype(BF)
    kw_ref[tok_rows:] = k_ref[...]
    prev = None
    for part in range(packed // group):
        term = nn(
            comp_ref[packed + part * group : packed + (part + 1) * group],
            et_ref[part * group : (part + 1) * group],
        )
        prev = term if prev is None else prev + term
    vw_ref[:, :tok_rows] = prev.astype(BF)
    vw_ref[:, tok_rows:] = vt_ref[...]
    at = 0
    for part in summ_refs:
        all_ref[at : at + part.shape[0]] = part[...]
        at += part.shape[0]
    slab, slabs = lax.axis_index("seq"), lax.axis_size("seq")
    mids, fars = tok_rows // POOL2, tok_rows // POOL3
    shape = (ck_ref.shape[0], all_ref.shape[0])
    line = iota(shape, 0)
    step = 2 * SUMM_ROWS
    turn = line // mids
    far = line - 3 * mids
    shard = slab - 1 + turn
    turned = slab if slabs == 8 else 0
    source = jnp.where(
        line < 3 * mids,
        (shard ^ turned) * step + line - turn * mids,
        ((far // fars) ^ turned) * step + mids + far % fars,
    )
    source = jnp.where((line >= 3 * mids) | ((shard >= 0) & (shard < slabs)), source, -step)
    gathered = all_ref[...]
    ck_ref[...] = nn(ones_where(source == iota(shape, 1)), gathered).astype(BF)
    values = nn(ones_where(source + SUMM_ROWS == iota(shape, 1)), gathered)
    cv_ref[...] = jnp.transpose(values).astype(BF)


def rest_kernel(
    first, blocks, lists_ref, mix_ref, qt_ref, kw_ref, vw_ref, ck_ref, cv_ref, bias_ref,
    acc_ref, near_ref, top_ref, den_ref, out_ref, kc_ref, vc_ref, q4_ref, p_ref,
):
    group, tok_rows = qt_ref.shape
    heads = mix_ref.shape[1]
    width = group // heads
    others = FINE_K - 1
    fine = others * FBLK
    mid = 3 * (tok_rows // POOL2)
    far_at = fine + mid
    total = kc_ref.shape[1]
    for slot in range(2):
        kc_ref[slot, fine:] = ck_ref[...]
        vc_ref[slot, :, fine:] = cv_ref[...]
    q4_ref[...] = jnp.zeros_like(q4_ref)
    for index in range(blocks):
        g = first + index
        at = g * FBLK
        slot = index % 2
        biases = []
        for entry in range(others):
            start = pl.multiple_of(lists_ref[entry + 1, g] * FBLK, FBLK)
            kc_ref[slot, entry * FBLK : (entry + 1) * FBLK] = kw_ref[pl.ds(start, FBLK)]
            vc_ref[slot, :, entry * FBLK : (entry + 1) * FBLK] = vw_ref[:, pl.ds(start, FBLK)]
            biases.append(bias_ref[pl.ds(start, FBLK)])
        spread_heads(q4_ref.at[slot], qt_ref, at, heads)
        scores = nn(kc_ref[slot], q4_ref[slot])
        scales, keeps = [], []
        for h in range(heads):
            lanes = slice(h * FBLK, (h + 1) * FBLK)
            parts = [scores[e * FBLK : (e + 1) * FBLK, lanes] + biases[e] for e in range(others)]
            old_top = top_ref[g : g + 1, lanes]
            top = functools.reduce(
                jnp.maximum, [jnp.max(part, axis=0, keepdims=True) for part in parts] + [old_top]
            )
            keep = jnp.exp(old_top - top)
            den = den_ref[g : g + 1, lanes] * keep
            for e, part in enumerate(parts):
                weight = jnp.exp(part - top)
                den = den + jnp.sum(weight, axis=0, keepdims=True)
                p_ref[slot, e * FBLK : (e + 1) * FBLK, lanes] = weight.astype(BF)
            scale = mix_ref[0, h] / den
            scales.append(scale)
            keeps.append(keep * scale)
            for level, (low, high) in enumerate(((fine, far_at), (far_at, total))):
                part = scores[low:high, lanes]
                weight = jnp.exp(part - jnp.max(part, axis=0, keepdims=True))
                share = mix_ref[level + 2, h] / jnp.sum(weight, axis=0, keepdims=True)
                p_ref[slot, low:high, lanes] = (weight * share).astype(BF)
        fine_out = nn(vc_ref[slot, :, :fine], p_ref[slot, :fine])
        coarse_out = nn(vc_ref[slot, :, fine:], p_ref[slot, fine:])
        rows = []
        for h in range(heads):
            pick = (slice(h * width, (h + 1) * width), slice(h * FBLK, (h + 1) * FBLK))
            mine = (pick[0], slice(at, at + FBLK))
            rows.append(
                fine_out[pick] * scales[h]
                + acc_ref[mine] * keeps[h]
                + (coarse_out[pick] + near_ref[mine])
            )
        out_ref[index * FBLK : (index + 1) * FBLK] = jnp.transpose(
            jnp.concatenate(rows, axis=0)
        ).astype(BF)


def output_kernel(w_ref, *refs):
    out_ref = refs[-1]
    group = w_ref.shape[1]
    head = lax.axis_index("head")
    total = None
    for distance, part in zip((0, 2, 1, 3), refs[:4]):
        start = pl.multiple_of((head ^ distance) * group, group)
        term = nn(part[...], w_ref[pl.ds(start, group)])
        total = term if total is None else total + term
    out_ref[...] = total.astype(BF)


def local(tokens, w_query, w_key, w_value, w_out, level_mix, fine_blocks, order, mask_ids):
    tok_rows, width = tokens.shape
    slabs = lax.axis_size("seq")
    slab, head = lax.axis_index("seq"), lax.axis_index("head")
    group = w_query.shape[1]
    heads = level_mix.shape[1]
    packed = tok_rows - mask_ids.shape[1]
    near, mids, fars = tok_rows // POOL1, tok_rows // POOL2, tok_rows // POOL3
    coarse = 3 * mids + fars * slabs
    step = 2 * SUMM_ROWS
    chosen = packed + SUMM_ROWS + near

    shape = jax.ShapeDtypeStruct
    params = pltpu.CompilerParams(vmem_limit_bytes=VMEM_LIMIT)
    before_mask = to_next(mask_ids)

    def prepare(early):
        return pl.pallas_call(
            prepare_kernel,
            out_shape=(
                shape((tok_rows, tok_rows), BF),
                shape((tok_rows, tok_rows), BF),
                shape((chosen, tok_rows), BF),
                shape((SUMM_ROWS + near, 128), F32),
                shape((16, SUMM_ROWS + near), F32),
                shape((tok_rows, packed), BF),
                shape((packed, tok_rows), BF),
                shape((2 * tok_rows, FBLK), F32),
                shape((2 * group, width), BF),
                shape((width, group), BF),
            ),
            in_specs=vmem_specs(6) + [pl.BlockSpec(memory_space=pl.ANY)],
            out_specs=vmem_specs(10),
            compiler_params=params,
            name="prepare",
        )(order, mask_ids, before_mask, w_query, w_value, w_key, early)

    pieces, prepared = exchange_tokens(tokens, before_mask, prepare)
    permute, permute_t, select, f_col, f_row, expand, expand_t, bias, w_t, w_k = prepared
    places = tuple((row, distances) for _, row, distances in pieces)
    comp, summ, k0, v0, rows_here = pl.pallas_call(
        functools.partial(project_kernel, places),
        out_shape=(
            shape((2 * packed, group), BF),
            shape((step, group), BF),
            shape((tok_rows, group), BF),
            shape((group, tok_rows), BF),
            shape((tok_rows, width), BF),
        ),
        in_specs=vmem_specs(len(pieces) + 4),
        out_specs=vmem_specs(5),
        compiler_params=params,
        name="project",
    )(*[piece for piece, _, _ in pieces], w_t, w_k, select, f_col)
    comp_before = to_next(comp)
    if slabs == 8:
        summaries = [summ] + [by_distance(summ, d) for d in range(1, slabs)]
    else:
        copies = jnp.broadcast_to(summ[None], (slabs, step, group))
        copies = lax.all_to_all(copies, "seq", split_axis=0, concat_axis=0, tiled=True)
        summaries = [copies.reshape(slabs * step, group)]

    blocks = tok_rows // FBLK
    q_t, v_t, keys, acc, near_out, top, den = pl.pallas_call(
        own_kernel,
        out_shape=(
            shape((group, tok_rows), BF),
            shape((group, tok_rows), BF),
            shape((tok_rows, group), BF),
            shape((group, tok_rows), F32),
            shape((group, tok_rows), F32),
            shape((blocks, heads * FBLK), F32),
            shape((blocks, heads * FBLK), F32),
        ),
        in_specs=smem_specs(1) + vmem_specs(10),
        out_specs=vmem_specs(7),
        scratch_shapes=[
            pltpu.VMEM((2, group, heads * FBLK), BF),
            pltpu.VMEM((2, FBLK + near, heads * FBLK), BF),
        ],
        compiler_params=params,
        name="own",
    )(level_mix, permute, permute_t, select, f_col, f_row, w_t, rows_here, k0, v0, bias)

    window_k, window_v, coarse_k, coarse_v = pl.pallas_call(
        window_kernel,
        out_shape=(
            shape((2 * tok_rows, group), BF),
            shape((group, 2 * tok_rows), BF),
            shape((coarse, group), BF),
            shape((group, coarse), BF),
        ),
        in_specs=vmem_specs(5 + len(summaries)),
        out_specs=vmem_specs(4),
        scratch_shapes=[pltpu.VMEM((slabs * step, group), BF)],
        compiler_params=params,
        name="window",
    )(keys, v_t, comp_before, expand, expand_t, *summaries)

    total = (FINE_K - 1) * FBLK + coarse
    lists = fine_blocks.T
    parts = PARTS if sum(PARTS) == blocks else (blocks,)
    waiting, out, first = None, None, 0

    def finish(out, attended, third, second, base):
        fourth = over_head(third, CORE_PAIRS)
        rows = attended.shape[0]
        previous = [] if out is None else [out]
        tile = pl.BlockSpec((FBLK, group), lambda i: (i, 0))
        return pl.pallas_call(
            output_kernel,
            grid=(rows // FBLK,),
            out_shape=shape((tok_rows, group), BF),
            in_specs=[pl.BlockSpec((width, group), lambda i: (0, 0))]
            + [tile] * 4
            + [pl.BlockSpec(memory_space=pl.ANY)] * len(previous),
            out_specs=pl.BlockSpec((FBLK, group), lambda i, base=base: (i + base, 0)),
            input_output_aliases={5: 0} if previous else {},
            compiler_params=params,
            name="output",
        )(w_out, attended, third, second, fourth, *previous)

    for count in parts:
        attended = pl.pallas_call(
            functools.partial(rest_kernel, first, count),
            out_shape=shape((count * FBLK, group), BF),
            in_specs=smem_specs(2) + vmem_specs(10),
            out_specs=pl.BlockSpec(memory_space=pltpu.VMEM),
            scratch_shapes=[
                pltpu.VMEM((2, total, group), BF),
                pltpu.VMEM((2, group, total), BF),
                pltpu.VMEM((2, group, heads * FBLK), BF),
                pltpu.VMEM((2, total, heads * FBLK), BF),
            ],
            compiler_params=params,
            name="rest",
        )(
            lists, level_mix, q_t, window_k, window_v, coarse_k, coarse_v, bias, acc, near_out, top, den
        )
        third = over_head(attended, X_PAIRS)
        second = over_head(attended, CORE_PAIRS)
        if waiting is not None:
            old, old_third, old_second, old_base = waiting
            old_third, attended = lax.optimization_barrier((old_third, attended))
            out = finish(out, old, old_third, old_second, old_base)
            third, out = lax.optimization_barrier((third, out))
        waiting = (attended, third, second, first)
        first += count
    return finish(out, *waiting)


def solution(mesh):
    placed = (
        P("seq", None),
        P(None, "head"),
        P(None, "head"),
        P(None, "head"),
        P(None, "head"),
        P(None, "head"),
        P("seq", None),
        P("seq", None),
        P("seq", None),
    )
    return jax.shard_map(
        local, mesh=mesh, in_specs=placed, out_specs=P("seq", "head"), check_vma=False
    )
```

```python
import functools

import jax
import jax.numpy as jnp
from jax import lax
from jax.experimental import pallas as pl
from jax.experimental.pallas import tpu as pltpu
from jax.sharding import PartitionSpec as P

FBLK = 128
FINE_K = 4
POOL1 = 8
POOL2 = 64
POOL3 = 512
SUMM_ROWS = 32
BF = jnp.bfloat16
F32 = jnp.float32
I32 = jnp.int32
HIDE = -1e30
VMEM_LIMIT = 24 * 1024 * 1024
PARTS = (2, 3, 3)

X_PAIRS = [(0, 2), (2, 0), (1, 3), (3, 1)]
CORE_PAIRS = [(0, 1), (1, 0), (2, 3), (3, 2)]


def nn(a, b):
    return lax.dot_general(a, b, (((1,), (0,)), ((), ())), preferred_element_type=F32)


def nt(a, b):
    return lax.dot_general(a, b, (((1,), (1,)), ((), ())), preferred_element_type=F32)


def iota(shape, axis):
    return lax.broadcasted_iota(I32, shape, axis)


def ones_where(condition):
    return jnp.where(condition, 1.0, 0.0).astype(BF)


def vmem_specs(count):
    return [pl.BlockSpec(memory_space=pltpu.VMEM)] * count


def smem_specs(count):
    return [pl.BlockSpec(memory_space=pltpu.SMEM)] * count


def over_head(block, pairs):
    return lax.ppermute(block, "head", pairs)


def to_next(block):
    return lax.ppermute(block, "seq", [(i, i + 1) for i in range(lax.axis_size("seq") - 1)])


def send_kernel(distances, tokens_ref, *refs):
    outs, own = refs[:-1], refs[-1]
    slab, head = lax.axis_index("seq"), lax.axis_index("head")
    rows = own.shape[0]
    quarter = tokens_ref.shape[1] // 4
    for distance, out in zip(distances, outs):
        row = pl.multiple_of((slab ^ distance) * rows, rows)
        for part in range(out.shape[1] // quarter):
            start = pl.multiple_of((head ^ (2 * part)) * quarter, quarter)
            out[:, part * quarter : (part + 1) * quarter] = tokens_ref[
                pl.ds(row, rows), pl.ds(start, quarter)
            ]
    own[...] = tokens_ref[pl.ds(pl.multiple_of(slab * rows, rows), rows)]


def stack_kernel(counts, *refs):
    sources, targets = refs[: sum(counts)], refs[len(refs) - len(counts) :]
    for count, target in zip(counts, targets):
        height = target.shape[0] // count
        for index in range(count):
            target[index * height : (index + 1) * height] = sources[index][...]
        sources = sources[count:]


def stacked(lists, after):
    parts = [part for one in lists for part in one]
    return pl.pallas_call(
        functools.partial(stack_kernel, tuple(len(one) for one in lists)),
        out_shape=tuple(
            jax.ShapeDtypeStruct((len(one) * one[0].shape[0], one[0].shape[1]), one[0].dtype)
            for one in lists
        ),
        in_specs=vmem_specs(len(parts)) + [pl.BlockSpec(memory_space=pl.ANY)],
        out_specs=vmem_specs(len(lists)),
        compiler_params=pltpu.CompilerParams(vmem_limit_bytes=VMEM_LIMIT),
        name="stack",
    )(*parts, after)


def by_distance(block, distance):
    return lax.ppermute(block, "seq", [(i, i ^ distance) for i in range(lax.axis_size("seq"))])


def exchange_tokens(tokens, before_mask, prepare):
    tok_rows, width = tokens.shape
    slabs = lax.axis_size("seq")
    rows = tok_rows // slabs
    quarter = width // 4
    if slabs != 8:
        split = tokens.reshape(slabs, rows, width)
        mine = lax.dynamic_slice_in_dim(split, lax.axis_index("head") * quarter, quarter, axis=2)
        first = lax.all_to_all(mine, "seq", split_axis=0, concat_axis=0, tiled=True).reshape(
            tok_rows, quarter
        )
        third = over_head(first, X_PAIRS)
        second = over_head(first, CORE_PAIRS)
        fourth = over_head(third, CORE_PAIRS)
        pieces = [(first, 0, (0,)), (third, 0, (2,)), (second, 0, (1,)), (fourth, 0, (3,))]
        return pieces, prepare(first)
    distances = (7, 6, 5, 4, 3, 2, 1)
    *blocks, own = pl.pallas_call(
        functools.partial(send_kernel, distances),
        out_shape=tuple(
            jax.ShapeDtypeStruct((rows, columns), BF)
            for columns in [quarter if d > 3 else 2 * quarter for d in distances] + [width]
        ),
        in_specs=vmem_specs(1),
        out_specs=vmem_specs(8),
        compiler_params=pltpu.CompilerParams(vmem_limit_bytes=VMEM_LIMIT),
        name="send",
    )(tokens)
    arrived = [by_distance(block, d) for block, d in zip(blocks, distances)]
    far, near = stacked((arrived[:4], arrived[4:]), before_mask)
    far_x = over_head(far, X_PAIRS)
    near_core = over_head(near, CORE_PAIRS)
    far_core = over_head(far, CORE_PAIRS)
    prepared = prepare(far)
    far_x, prepared = lax.optimization_barrier((far_x, prepared))
    far_last = over_head(far_x, CORE_PAIRS)
    pieces = [(far, 0, (0,)), (far_x, 0, (2,)), (far_core, 0, (1,)), (far_last, 0, (3,))]
    pieces += [(near, 4 * rows, (0, 2)), (near_core, 4 * rows, (1, 3)), (own, 7 * rows, None)]
    return pieces, prepared


def column(row, lanes=128):
    return jnp.transpose(jnp.broadcast_to(row.astype(F32), (lanes, row.shape[1]))).astype(I32)


def ranks(ids, tok_rows, lanes=128):
    hidden = column(ids)
    parts = []
    for at in range(0, tok_rows, lanes):
        time = iota((1, lanes), 1) + at
        count = jnp.sum(jnp.where(hidden < time, 1.0, 0.0), axis=0, keepdims=True)
        here = jnp.sum(jnp.where(hidden == time, 1.0, 0.0), axis=0, keepdims=True)
        parts.append(jnp.where(here == 0.0, time - count.astype(I32), -1))
    return jnp.concatenate(parts, axis=1)


def prepare_kernel(
    order_ref, mask_ref, before_ref, wq_ref, wv_ref, wk_in, early_ref,
    p_ref, pt_ref, sel_ref, fcol_ref, frow_ref, e_ref, et_ref, bias_ref, wt_ref, wk_ref,
):
    slab, slabs = lax.axis_index("seq"), lax.axis_size("seq")
    tok_rows = order_ref.shape[1]
    packed = tok_rows - mask_ref.shape[1]
    flip = (slab ^ 7) * (tok_rows // slabs) if slabs == 8 else 0
    mids = tok_rows // POOL2
    group = wq_ref.shape[1]
    lanes = 128

    place = order_ref[...] ^ flip
    place_column = column(place)
    for at in range(0, tok_rows, lanes):
        p_ref[:, at : at + lanes] = ones_where(place_column == iota((tok_rows, lanes), 1) + at)
        pt_ref[at : at + lanes] = ones_where(iota((lanes, tok_rows), 0) + at == place)
    rank = ranks(mask_ref[...], tok_rows)
    time = jnp.where(rank >= 0, iota((1, tok_rows), 1), -1) + 1
    line = iota((16, tok_rows), 0)
    stack = jnp.where(
        line == 0,
        time >> 5,
        jnp.where(
            line == 1,
            time & 31,
            jnp.where(line == 2, (rank + 1) >> 5, jnp.where(line == 3, (rank + 1) & 31, 0)),
        ),
    )
    moved = nn(stack.astype(F32).astype(BF), p_ref[...]).astype(I32)
    time_here = (moved[0:1] << 5) + moved[1:2] - 1
    rank_here = (moved[2:3] << 5) + moved[3:4] - 1
    for at in range(0, packed, lanes):
        sel_ref[at : at + lanes] = ones_where(iota((lanes, tok_rows), 0) + at == rank_here)
    line = iota((SUMM_ROWS, tok_rows), 0)
    sel_ref[packed : packed + SUMM_ROWS] = ones_where(
        ((time_here >> 6) == line) | (((time_here >> 9) + mids == line) & (time_here >= 0))
    )
    lead = packed + SUMM_ROWS
    near = sel_ref.shape[0] - lead
    sel_ref[lead:] = ones_where((time_here >> 3) == iota((near, tok_rows), 0))
    pools = sel_ref[packed:]
    fcol_ref[...] = 1.0 / jnp.sqrt(jnp.maximum(nn(pools, jnp.ones((tok_rows, lanes), BF)), 1.0))
    frow_ref[...] = 1.0 / jnp.sqrt(jnp.maximum(nt(jnp.ones((16, tok_rows), BF), pools), 1.0))
    rank_before = jnp.where(slab > 0, ranks(before_ref[...], tok_rows), -1)
    rank_column = column(rank_before)
    for at in range(0, packed, lanes):
        e_ref[:, at : at + lanes] = ones_where(rank_column == iota((tok_rows, lanes), 1) + at)
        et_ref[at : at + lanes] = ones_where(iota((lanes, tok_rows), 0) + at == rank_before)
    bias_ref[:tok_rows] = jnp.where(rank_column >= 0, 0.0, HIDE)
    bias_ref[tok_rows:] = jnp.where(column(rank) >= 0, 0.0, HIDE)
    wt_ref[:group] = jnp.transpose(wq_ref[...])
    wt_ref[group:] = jnp.transpose(wv_ref[...])
    wk_ref[...] = wk_in[...]


def project_kernel(places, *refs):
    count = len(places)
    piece_refs, refs = refs[:count], refs[count:]
    wt_ref, wk_ref, sel_ref, fcol_ref, comp_ref, summ_ref, k_ref, v_ref, x_ref = refs
    quarter = x_ref.shape[1] // 4
    head = lax.axis_index("head")
    for piece, (row, distances) in zip(piece_refs, places):
        height = piece.shape[0]
        if distances is None:
            x_ref[row : row + height] = piece[...]
            continue
        for part, distance in enumerate(distances):
            start = pl.multiple_of((head ^ distance) * quarter, quarter)
            x_ref[row : row + height, pl.ds(start, quarter)] = piece[
                :, part * quarter : (part + 1) * quarter
            ]
    group = wk_ref.shape[1]
    packed = comp_ref.shape[0] // 2
    lead = packed + SUMM_ROWS
    x = x_ref[...]
    keys = nn(x, wk_ref[...]).astype(BF)
    k_ref[...] = keys
    vt = nt(wt_ref[group:], x).astype(BF)
    v_ref[...] = vt
    sel = sel_ref[:lead]
    kl = nn(sel, keys)
    vl = nt(vt, sel)
    comp_ref[:packed] = kl[:packed].astype(BF)
    vc = vl[:, :packed].astype(BF)
    for part in range(packed // group):
        comp_ref[packed + part * group : packed + (part + 1) * group] = vc[
            :, part * group : (part + 1) * group
        ]
    factor = fcol_ref[:SUMM_ROWS, :1]
    summ_k = (kl[packed:] * factor).astype(BF)
    tail = jnp.concatenate(
        [vl[:, packed:], jnp.zeros((group, 128 - SUMM_ROWS), F32)], axis=1
    )
    summ_v = (jnp.transpose(tail)[:SUMM_ROWS] * factor).astype(BF)
    summ_ref[:SUMM_ROWS] = summ_k
    summ_ref[SUMM_ROWS:] = summ_v


def spread_heads(q4_ref, qt_ref, at, heads):
    width = q4_ref.shape[0] // heads
    for h in range(heads):
        rows = slice(h * width, (h + 1) * width)
        q4_ref[rows, h * FBLK : (h + 1) * FBLK] = qt_ref[rows, at : at + FBLK]


def own_kernel(
    mix_ref, p_in, pt_ref, sel_ref, fcol_ref, frow_ref, wt_ref, x_ref, k0_ref, v0_ref, bias_ref,
    qt_ref, vt_ref, k_ref, acc_ref, near_ref, top_ref, den_ref, q4_ref, p_ref,
):
    tok_rows, group = k_ref.shape
    heads = mix_ref.shape[1]
    width = group // heads
    near = tok_rows // POOL1
    q4_ref[...] = jnp.zeros_like(q4_ref)
    same = iota((FBLK, FBLK), 0) == iota((FBLK, FBLK), 1)
    k0, v0 = k0_ref[...], v0_ref[...]
    q0 = nt(wt_ref[:group], x_ref[...]).astype(BF)
    k_ref[...] = nn(p_in[...], k0).astype(BF)
    qt_ref[...] = (nn(q0, pt_ref[...]) * 0.125).astype(BF)
    vt_ref[...] = nn(v0, pt_ref[...]).astype(BF)
    pool = sel_ref[sel_ref.shape[0] - near :]
    nk = (nn(pool, k0) * fcol_ref[SUMM_ROWS:, :1]).astype(BF)
    nvt = (nt(v0, pool) * frow_ref[:1, SUMM_ROWS:]).astype(BF)
    for g in range(tok_rows // FBLK):
        at = g * FBLK
        slot = g % 2
        spread_heads(q4_ref.at[slot], qt_ref, at, heads)
        q4 = q4_ref[slot]
        bias = jnp.where(same, 0.0, bias_ref[tok_rows + at : tok_rows + at + FBLK])
        own_scores = nn(k_ref[at : at + FBLK], q4)
        near_scores = nn(nk, q4)
        scales = []
        for h in range(heads):
            lanes = slice(h * FBLK, (h + 1) * FBLK)
            part = own_scores[:, lanes] + bias
            top = jnp.max(part, axis=0, keepdims=True)
            weight = jnp.exp(part - top)
            top_ref[g : g + 1, lanes] = top
            den_ref[g : g + 1, lanes] = jnp.sum(weight, axis=0, keepdims=True)
            p_ref[slot, :FBLK, lanes] = weight.astype(BF)
            part = near_scores[:, lanes]
            weight = jnp.exp(part - jnp.max(part, axis=0, keepdims=True))
            scales.append(mix_ref[1, h] / jnp.sum(weight, axis=0, keepdims=True))
            p_ref[slot, FBLK:, lanes] = weight.astype(BF)
        own_out = nn(vt_ref[:, at : at + FBLK], p_ref[slot, :FBLK])
        near_out = nn(nvt, p_ref[slot, FBLK:])
        for h in range(heads):
            rows, lanes = slice(h * width, (h + 1) * width), slice(h * FBLK, (h + 1) * FBLK)
            acc_ref[rows, at : at + FBLK] = own_out[rows, lanes]
            near_ref[rows, at : at + FBLK] = near_out[rows, lanes] * scales[h]


def window_kernel(k_ref, vt_ref, comp_ref, e_ref, et_ref, *refs):
    summ_refs, (kw_ref, vw_ref, ck_ref, cv_ref, all_ref) = refs[:-5], refs[-5:]
    tok_rows, group = k_ref.shape
    packed = e_ref.shape[1]
    kw_ref[:tok_rows] = nn(e_ref[...], comp_ref[:packed]).astype(BF)
    kw_ref[tok_rows:] = k_ref[...]
    prev = None
    for part in range(packed // group):
        term = nn(
            comp_ref[packed + part * group : packed + (part + 1) * group],
            et_ref[part * group : (part + 1) * group],
        )
        prev = term if prev is None else prev + term
    vw_ref[:, :tok_rows] = prev.astype(BF)
    vw_ref[:, tok_rows:] = vt_ref[...]
    at = 0
    for part in summ_refs:
        all_ref[at : at + part.shape[0]] = part[...]
        at += part.shape[0]
    slab, slabs = lax.axis_index("seq"), lax.axis_size("seq")
    mids, fars = tok_rows // POOL2, tok_rows // POOL3
    shape = (ck_ref.shape[0], all_ref.shape[0])
    line = iota(shape, 0)
    step = 2 * SUMM_ROWS
    turn = line // mids
    far = line - 3 * mids
    shard = slab - 1 + turn
    turned = slab if slabs == 8 else 0
    source = jnp.where(
        line < 3 * mids,
        (shard ^ turned) * step + line - turn * mids,
        ((far // fars) ^ turned) * step + mids + far % fars,
    )
    source = jnp.where((line >= 3 * mids) | ((shard >= 0) & (shard < slabs)), source, -step)
    gathered = all_ref[...]
    ck_ref[...] = nn(ones_where(source == iota(shape, 1)), gathered).astype(BF)
    values = nn(ones_where(source + SUMM_ROWS == iota(shape, 1)), gathered)
    cv_ref[...] = jnp.transpose(values).astype(BF)


def rest_kernel(
    first, blocks, lists_ref, mix_ref, qt_ref, kw_ref, vw_ref, ck_ref, cv_ref, bias_ref,
    acc_ref, near_ref, top_ref, den_ref, out_ref, kc_ref, vc_ref, q4_ref, p_ref,
):
    group, tok_rows = qt_ref.shape
    heads = mix_ref.shape[1]
    width = group // heads
    others = FINE_K - 1
    fine = others * FBLK
    mid = 3 * (tok_rows // POOL2)
    far_at = fine + mid
    total = kc_ref.shape[1]
    for slot in range(2):
        kc_ref[slot, fine:] = ck_ref[...]
        vc_ref[slot, :, fine:] = cv_ref[...]
    q4_ref[...] = jnp.zeros_like(q4_ref)
    for index in range(blocks):
        g = first + index
        at = g * FBLK
        slot = index % 2
        biases = []
        for entry in range(others):
            start = pl.multiple_of(lists_ref[entry + 1, g] * FBLK, FBLK)
            kc_ref[slot, entry * FBLK : (entry + 1) * FBLK] = kw_ref[pl.ds(start, FBLK)]
            vc_ref[slot, :, entry * FBLK : (entry + 1) * FBLK] = vw_ref[:, pl.ds(start, FBLK)]
            biases.append(bias_ref[pl.ds(start, FBLK)])
        spread_heads(q4_ref.at[slot], qt_ref, at, heads)
        scores = nn(kc_ref[slot], q4_ref[slot])
        scales, keeps = [], []
        for h in range(heads):
            lanes = slice(h * FBLK, (h + 1) * FBLK)
            parts = [scores[e * FBLK : (e + 1) * FBLK, lanes] + biases[e] for e in range(others)]
            old_top = top_ref[g : g + 1, lanes]
            top = functools.reduce(
                jnp.maximum, [jnp.max(part, axis=0, keepdims=True) for part in parts] + [old_top]
            )
            keep = jnp.exp(old_top - top)
            den = den_ref[g : g + 1, lanes] * keep
            for e, part in enumerate(parts):
                weight = jnp.exp(part - top)
                den = den + jnp.sum(weight, axis=0, keepdims=True)
                p_ref[slot, e * FBLK : (e + 1) * FBLK, lanes] = weight.astype(BF)
            scale = mix_ref[0, h] / den
            scales.append(scale)
            keeps.append(keep * scale)
            for level, (low, high) in enumerate(((fine, far_at), (far_at, total))):
                part = scores[low:high, lanes]
                weight = jnp.exp(part - jnp.max(part, axis=0, keepdims=True))
                share = mix_ref[level + 2, h] / jnp.sum(weight, axis=0, keepdims=True)
                p_ref[slot, low:high, lanes] = (weight * share).astype(BF)
        fine_out = nn(vc_ref[slot, :, :fine], p_ref[slot, :fine])
        coarse_out = nn(vc_ref[slot, :, fine:], p_ref[slot, fine:])
        rows = []
        for h in range(heads):
            pick = (slice(h * width, (h + 1) * width), slice(h * FBLK, (h + 1) * FBLK))
            mine = (pick[0], slice(at, at + FBLK))
            rows.append(
                fine_out[pick] * scales[h]
                + acc_ref[mine] * keeps[h]
                + (coarse_out[pick] + near_ref[mine])
            )
        out_ref[index * FBLK : (index + 1) * FBLK] = jnp.transpose(
            jnp.concatenate(rows, axis=0)
        ).astype(BF)


def output_kernel(w_ref, *refs):
    out_ref = refs[-1]
    group = w_ref.shape[1]
    head = lax.axis_index("head")
    total = None
    for distance, part in zip((0, 2, 1, 3), refs[:4]):
        start = pl.multiple_of((head ^ distance) * group, group)
        term = nn(part[...], w_ref[pl.ds(start, group)])
        total = term if total is None else total + term
    out_ref[...] = total.astype(BF)


def local(tokens, w_query, w_key, w_value, w_out, level_mix, fine_blocks, order, mask_ids):
    tok_rows, width = tokens.shape
    slabs = lax.axis_size("seq")
    slab, head = lax.axis_index("seq"), lax.axis_index("head")
    group = w_query.shape[1]
    heads = level_mix.shape[1]
    packed = tok_rows - mask_ids.shape[1]
    near, mids, fars = tok_rows // POOL1, tok_rows // POOL2, tok_rows // POOL3
    coarse = 3 * mids + fars * slabs
    step = 2 * SUMM_ROWS
    chosen = packed + SUMM_ROWS + near

    shape = jax.ShapeDtypeStruct
    params = pltpu.CompilerParams(vmem_limit_bytes=VMEM_LIMIT)
    before_mask = to_next(mask_ids)

    def prepare(early):
        return pl.pallas_call(
            prepare_kernel,
            out_shape=(
                shape((tok_rows, tok_rows), BF),
                shape((tok_rows, tok_rows), BF),
                shape((chosen, tok_rows), BF),
                shape((SUMM_ROWS + near, 128), F32),
                shape((16, SUMM_ROWS + near), F32),
                shape((tok_rows, packed), BF),
                shape((packed, tok_rows), BF),
                shape((2 * tok_rows, FBLK), F32),
                shape((2 * group, width), BF),
                shape((width, group), BF),
            ),
            in_specs=vmem_specs(6) + [pl.BlockSpec(memory_space=pl.ANY)],
            out_specs=vmem_specs(10),
            compiler_params=params,
            name="prepare",
        )(order, mask_ids, before_mask, w_query, w_value, w_key, early)

    pieces, prepared = exchange_tokens(tokens, before_mask, prepare)
    permute, permute_t, select, f_col, f_row, expand, expand_t, bias, w_t, w_k = prepared
    places = tuple((row, distances) for _, row, distances in pieces)
    comp, summ, k0, v0, rows_here = pl.pallas_call(
        functools.partial(project_kernel, places),
        out_shape=(
            shape((2 * packed, group), BF),
            shape((step, group), BF),
            shape((tok_rows, group), BF),
            shape((group, tok_rows), BF),
            shape((tok_rows, width), BF),
        ),
        in_specs=vmem_specs(len(pieces) + 4),
        out_specs=vmem_specs(5),
        compiler_params=params,
        name="project",
    )(*[piece for piece, _, _ in pieces], w_t, w_k, select, f_col)
    comp_before = to_next(comp)
    if slabs == 8:
        summaries = [summ] + [by_distance(summ, d) for d in range(1, slabs)]
    else:
        copies = jnp.broadcast_to(summ[None], (slabs, step, group))
        copies = lax.all_to_all(copies, "seq", split_axis=0, concat_axis=0, tiled=True)
        summaries = [copies.reshape(slabs * step, group)]

    blocks = tok_rows // FBLK
    q_t, v_t, keys, acc, near_out, top, den = pl.pallas_call(
        own_kernel,
        out_shape=(
            shape((group, tok_rows), BF),
            shape((group, tok_rows), BF),
            shape((tok_rows, group), BF),
            shape((group, tok_rows), F32),
            shape((group, tok_rows), F32),
            shape((blocks, heads * FBLK), F32),
            shape((blocks, heads * FBLK), F32),
        ),
        in_specs=smem_specs(1) + vmem_specs(10),
        out_specs=vmem_specs(7),
        scratch_shapes=[
            pltpu.VMEM((2, group, heads * FBLK), BF),
            pltpu.VMEM((2, FBLK + near, heads * FBLK), BF),
        ],
        compiler_params=params,
        name="own",
    )(level_mix, permute, permute_t, select, f_col, f_row, w_t, rows_here, k0, v0, bias)

    window_k, window_v, coarse_k, coarse_v = pl.pallas_call(
        window_kernel,
        out_shape=(
            shape((2 * tok_rows, group), BF),
            shape((group, 2 * tok_rows), BF),
            shape((coarse, group), BF),
            shape((group, coarse), BF),
        ),
        in_specs=vmem_specs(5 + len(summaries)),
        out_specs=vmem_specs(4),
        scratch_shapes=[pltpu.VMEM((slabs * step, group), BF)],
        compiler_params=params,
        name="window",
    )(keys, v_t, comp_before, expand, expand_t, *summaries)

    total = (FINE_K - 1) * FBLK + coarse
    lists = fine_blocks.T
    parts = PARTS if sum(PARTS) == blocks else (blocks,)
    waiting, out, first = None, None, 0

    def finish(out, attended, third, second, base):
        fourth = over_head(third, CORE_PAIRS)
        rows = attended.shape[0]
        previous = [] if out is None else [out]
        tile = pl.BlockSpec((FBLK, group), lambda i: (i, 0))
        return pl.pallas_call(
            output_kernel,
            grid=(rows // FBLK,),
            out_shape=shape((tok_rows, group), BF),
            in_specs=[pl.BlockSpec((width, group), lambda i: (0, 0))]
            + [tile] * 4
            + [pl.BlockSpec(memory_space=pl.ANY)] * len(previous),
            out_specs=pl.BlockSpec((FBLK, group), lambda i, base=base: (i + base, 0)),
            input_output_aliases={5: 0} if previous else {},
            compiler_params=params,
            name="output",
        )(w_out, attended, third, second, fourth, *previous)

    for count in parts:
        attended = pl.pallas_call(
            functools.partial(rest_kernel, first, count),
            out_shape=shape((count * FBLK, group), BF),
            in_specs=smem_specs(2) + vmem_specs(10),
            out_specs=pl.BlockSpec(memory_space=pltpu.VMEM),
            scratch_shapes=[
                pltpu.VMEM((2, total, group), BF),
                pltpu.VMEM((2, group, total), BF),
                pltpu.VMEM((2, group, heads * FBLK), BF),
                pltpu.VMEM((2, total, heads * FBLK), BF),
            ],
            compiler_params=params,
            name="rest",
        )(
            lists, level_mix, q_t, window_k, window_v, coarse_k, coarse_v, bias, acc, near_out, top, den
        )
        third = over_head(attended, X_PAIRS)
        second = over_head(attended, CORE_PAIRS)
        if waiting is not None:
            old, old_third, old_second, old_base = waiting
            old_third, attended = lax.optimization_barrier((old_third, attended))
            out = finish(out, old, old_third, old_second, old_base)
            third, out = lax.optimization_barrier((third, out))
        waiting = (attended, third, second, first)
        first += count
    return finish(out, *waiting)


def solution(mesh):
    placed = (
        P("seq", None),
        P(None, "head"),
        P(None, "head"),
        P(None, "head"),
        P(None, "head"),
        P(None, "head"),
        P("seq", None),
        P("seq", None),
        P("seq", None),
    )
    return jax.shard_map(
        local, mesh=mesh, in_specs=placed, out_specs=P("seq", "head"), check_vma=False
    )
```

```python
import functools

import jax
import jax.numpy as jnp
from jax import lax
from jax.experimental import pallas as pl
from jax.experimental.pallas import tpu as pltpu
from jax.sharding import PartitionSpec as P

FBLK = 128
FINE_K = 4
POOL1 = 8
POOL2 = 64
POOL3 = 512
SUMM_ROWS = 32
CODE_ROWS = 16
BF = jnp.bfloat16
F32 = jnp.float32
I32 = jnp.int32
HIDE = -1e30
VMEM_LIMIT = 24 * 1024 * 1024
PARTS = (2, 3, 3)

X_PAIRS = [(0, 2), (2, 0), (1, 3), (3, 1)]
CORE_PAIRS = [(0, 1), (1, 0), (2, 3), (3, 2)]


def nn(a, b):
    return lax.dot_general(a, b, (((1,), (0,)), ((), ())), preferred_element_type=F32)


def nt(a, b):
    return lax.dot_general(a, b, (((1,), (1,)), ((), ())), preferred_element_type=F32)


def iota(shape, axis):
    return lax.broadcasted_iota(I32, shape, axis)


def ones_where(condition):
    return jnp.where(condition, 1.0, 0.0).astype(BF)


def vmem_specs(count):
    return [pl.BlockSpec(memory_space=pltpu.VMEM)] * count


def smem_specs(count):
    return [pl.BlockSpec(memory_space=pltpu.SMEM)] * count


def over_head(block, pairs):
    return lax.ppermute(block, "head", pairs)


def to_next(block):
    return lax.ppermute(block, "seq", [(i, i + 1) for i in range(lax.axis_size("seq") - 1)])


def send_kernel(distances, tokens_ref, mask_ref, *refs):
    outs, own = refs[:-1], refs[-1]
    slab, head = lax.axis_index("seq"), lax.axis_index("head")
    rows = own.shape[0]
    quarter = tokens_ref.shape[1] // 4
    ids = mask_ref[...]
    line = iota((CODE_ROWS, ids.shape[1]), 0)
    code = jnp.where(line == 0, ids >> 5, jnp.where(line == 1, ids & 31, 0)).astype(F32).astype(BF)
    for distance, out in zip(distances, outs):
        row = pl.multiple_of((slab ^ distance) * rows, rows)
        parts = out.shape[1] // quarter
        for part in range(parts):
            start = pl.multiple_of((head ^ (2 * part)) * quarter, quarter)
            out[:rows, part * quarter : (part + 1) * quarter] = tokens_ref[
                pl.ds(row, rows), pl.ds(start, quarter)
            ]
        for part in range(code.shape[1] // out.shape[1]):
            at = rows + part * CODE_ROWS
            out[at : at + CODE_ROWS] = code[:, part * out.shape[1] : (part + 1) * out.shape[1]]
    own[...] = tokens_ref[pl.ds(pl.multiple_of(slab * rows, rows), rows)]


def stack_kernel(count, *refs):
    target = refs[-1]
    height = target.shape[0] // count
    for index in range(count):
        target[index * height : (index + 1) * height] = refs[index][:height]


def stacked(parts, rows, after=()):
    return pl.pallas_call(
        functools.partial(stack_kernel, len(parts)),
        out_shape=jax.ShapeDtypeStruct((len(parts) * rows, parts[0].shape[1]), parts[0].dtype),
        in_specs=vmem_specs(len(parts)) + [pl.BlockSpec(memory_space=pl.ANY)] * len(after),
        out_specs=pl.BlockSpec(memory_space=pltpu.VMEM),
        compiler_params=pltpu.CompilerParams(vmem_limit_bytes=VMEM_LIMIT),
        name="stack",
    )(*parts, *after)


def by_distance(block, distance):
    return lax.ppermute(block, "seq", [(i, i ^ distance) for i in range(lax.axis_size("seq"))])


def exchange_tokens(tokens, mask_ids, prepare):
    tok_rows, width = tokens.shape
    slabs = lax.axis_size("seq")
    rows = tok_rows // slabs
    quarter = width // 4
    if slabs != 8:
        split = tokens.reshape(slabs, rows, width)
        mine = lax.dynamic_slice_in_dim(split, lax.axis_index("head") * quarter, quarter, axis=2)
        first = lax.all_to_all(mine, "seq", split_axis=0, concat_axis=0, tiled=True).reshape(
            tok_rows, quarter
        )
        third = over_head(first, X_PAIRS)
        second = over_head(first, CORE_PAIRS)
        fourth = over_head(third, CORE_PAIRS)
        pieces = [(first, 0, (0,)), (third, 0, (2,)), (second, 0, (1,)), (fourth, 0, (3,))]
        return pieces, prepare(first), [to_next(mask_ids)]
    distances = (7, 6, 5, 4, 3, 2, 1)
    near_rows, far_rows = rows + CODE_ROWS, rows + 2 * CODE_ROWS
    *blocks, own = pl.pallas_call(
        functools.partial(send_kernel, distances),
        out_shape=tuple(
            jax.ShapeDtypeStruct((far_rows, quarter) if d > 3 else (near_rows, 2 * quarter), BF)
            for d in distances
        )
        + (jax.ShapeDtypeStruct((rows, width), BF),),
        in_specs=vmem_specs(2),
        out_specs=vmem_specs(8),
        compiler_params=pltpu.CompilerParams(vmem_limit_bytes=VMEM_LIMIT),
        name="send",
    )(tokens, mask_ids)
    arrived = [by_distance(block, d) for block, d in zip(blocks, distances)]
    far = stacked(arrived[:4], rows, (arrived[5],))
    near = stacked(arrived[4:], rows)
    far_x = over_head(far, X_PAIRS)
    near_core = over_head(near, CORE_PAIRS)
    far_core = over_head(far, CORE_PAIRS)
    prepared = prepare(far)
    far_x, prepared = lax.optimization_barrier((far_x, prepared))
    far_last = over_head(far_x, CORE_PAIRS)
    pieces = [(far, 0, (0,)), (far_x, 0, (2,)), (far_core, 0, (1,)), (far_last, 0, (3,))]
    pieces += [(near, 4 * rows, (0, 2)), (near_core, 4 * rows, (1, 3)), (own, 7 * rows, None)]
    return pieces, prepared, [arrived[6], arrived[4], arrived[0]]


def column(row, lanes=128):
    return jnp.transpose(jnp.broadcast_to(row.astype(F32), (lanes, row.shape[1]))).astype(I32)


def ranks(ids, tok_rows, lanes=128):
    hidden = column(ids)
    parts = []
    for at in range(0, tok_rows, lanes):
        time = iota((1, lanes), 1) + at
        count = jnp.sum(jnp.where(hidden < time, 1.0, 0.0), axis=0, keepdims=True)
        here = jnp.sum(jnp.where(hidden == time, 1.0, 0.0), axis=0, keepdims=True)
        parts.append(jnp.where(here == 0.0, time - count.astype(I32), -1))
    return jnp.concatenate(parts, axis=1)


def prepare_kernel(
    order_ref, mask_ref, wq_ref, wv_ref, wk_in, early_ref,
    p_ref, pt_ref, sel_ref, fcol_ref, frow_ref, bias_ref, wt_ref, wk_ref,
):
    slab, slabs = lax.axis_index("seq"), lax.axis_size("seq")
    tok_rows = order_ref.shape[1]
    packed = tok_rows - mask_ref.shape[1]
    flip = (slab ^ 7) * (tok_rows // slabs) if slabs == 8 else 0
    mids = tok_rows // POOL2
    group = wq_ref.shape[1]
    lanes = 128

    place = order_ref[...] ^ flip
    place_column = column(place)
    for at in range(0, tok_rows, lanes):
        p_ref[:, at : at + lanes] = ones_where(place_column == iota((tok_rows, lanes), 1) + at)
        pt_ref[at : at + lanes] = ones_where(iota((lanes, tok_rows), 0) + at == place)
    rank = ranks(mask_ref[...], tok_rows)
    time = jnp.where(rank >= 0, iota((1, tok_rows), 1), -1) + 1
    line = iota((16, tok_rows), 0)
    stack = jnp.where(
        line == 0,
        time >> 5,
        jnp.where(
            line == 1,
            time & 31,
            jnp.where(line == 2, (rank + 1) >> 5, jnp.where(line == 3, (rank + 1) & 31, 0)),
        ),
    )
    moved = nn(stack.astype(F32).astype(BF), p_ref[...]).astype(I32)
    time_here = (moved[0:1] << 5) + moved[1:2] - 1
    rank_here = (moved[2:3] << 5) + moved[3:4] - 1
    for at in range(0, packed, lanes):
        sel_ref[at : at + lanes] = ones_where(iota((lanes, tok_rows), 0) + at == rank_here)
    line = iota((SUMM_ROWS, tok_rows), 0)
    sel_ref[packed : packed + SUMM_ROWS] = ones_where(
        ((time_here >> 6) == line) | (((time_here >> 9) + mids == line) & (time_here >= 0))
    )
    lead = packed + SUMM_ROWS
    near = sel_ref.shape[0] - lead
    sel_ref[lead:] = ones_where((time_here >> 3) == iota((near, tok_rows), 0))
    pools = sel_ref[packed:]
    fcol_ref[...] = 1.0 / jnp.sqrt(jnp.maximum(nn(pools, jnp.ones((tok_rows, lanes), BF)), 1.0))
    frow_ref[...] = 1.0 / jnp.sqrt(jnp.maximum(nt(jnp.ones((16, tok_rows), BF), pools), 1.0))
    bias_ref[...] = jnp.where(column(rank) >= 0, 0.0, HIDE)
    wt_ref[:group] = jnp.transpose(wq_ref[...])
    wt_ref[group:] = jnp.transpose(wv_ref[...])
    wk_ref[...] = wk_in[...]


def project_kernel(places, *refs):
    count = len(places)
    piece_refs, refs = refs[:count], refs[count:]
    wt_ref, wk_ref, sel_ref, fcol_ref, comp_ref, summ_ref, k_ref, v_ref, x_ref = refs
    quarter = x_ref.shape[1] // 4
    head = lax.axis_index("head")
    for piece, (row, distances) in zip(piece_refs, places):
        height = piece.shape[0]
        if distances is None:
            x_ref[row : row + height] = piece[...]
            continue
        for part, distance in enumerate(distances):
            start = pl.multiple_of((head ^ distance) * quarter, quarter)
            x_ref[row : row + height, pl.ds(start, quarter)] = piece[
                :, part * quarter : (part + 1) * quarter
            ]
    group = wk_ref.shape[1]
    packed = comp_ref.shape[0] // 2
    lead = packed + SUMM_ROWS
    x = x_ref[...]
    keys = nn(x, wk_ref[...]).astype(BF)
    k_ref[...] = keys
    vt = nt(wt_ref[group:], x).astype(BF)
    v_ref[...] = vt
    sel = sel_ref[:lead]
    kl = nn(sel, keys)
    vl = nt(vt, sel)
    comp_ref[:packed] = kl[:packed].astype(BF)
    vc = vl[:, :packed].astype(BF)
    for part in range(packed // group):
        comp_ref[packed + part * group : packed + (part + 1) * group] = vc[
            :, part * group : (part + 1) * group
        ]
    factor = fcol_ref[:SUMM_ROWS, :1]
    summ_k = (kl[packed:] * factor).astype(BF)
    tail = jnp.concatenate(
        [vl[:, packed:], jnp.zeros((group, 128 - SUMM_ROWS), F32)], axis=1
    )
    summ_v = (jnp.transpose(tail)[:SUMM_ROWS] * factor).astype(BF)
    summ_ref[:SUMM_ROWS] = summ_k
    summ_ref[SUMM_ROWS:] = summ_v


def spread_heads(q4_ref, qt_ref, at, heads):
    width = q4_ref.shape[0] // heads
    for h in range(heads):
        rows = slice(h * width, (h + 1) * width)
        q4_ref[rows, h * FBLK : (h + 1) * FBLK] = qt_ref[rows, at : at + FBLK]


def order_kernel(
    p_ref, pt_ref, sel_ref, fcol_ref, frow_ref, wt_ref, x_ref, k0_ref, v0_ref,
    qt_ref, vt_ref, k_ref, nk_ref, nvt_ref,
):
    group = k_ref.shape[1]
    near = nk_ref.shape[0]
    k0, v0 = k0_ref[...], v0_ref[...]
    q0 = nt(wt_ref[:group], x_ref[...]).astype(BF)
    k_ref[...] = nn(p_ref[...], k0).astype(BF)
    qt_ref[...] = (nn(q0, pt_ref[...]) * 0.125).astype(BF)
    vt_ref[...] = nn(v0, pt_ref[...]).astype(BF)
    pool = sel_ref[sel_ref.shape[0] - near :]
    nk_ref[...] = (nn(pool, k0) * fcol_ref[SUMM_ROWS:, :1]).astype(BF)
    nvt_ref[...] = (nt(v0, pool) * frow_ref[:1, SUMM_ROWS:]).astype(BF)


def mask_before(refs, rows):
    if len(refs) == 1:
        return refs[0][...]
    slab = lax.axis_index("seq")
    digits = []
    for block in refs:
        width = block.shape[1]
        parts = [
            block[rows + at : rows + at + CODE_ROWS].astype(F32)
            for at in range(0, block.shape[0] - rows, CODE_ROWS)
        ]
        digits.append(jnp.concatenate(parts, axis=1) if len(parts) > 1 else parts[0])
    distance = slab ^ (slab - 1)
    code = jnp.where(distance == 1, digits[0], jnp.where(distance == 3, digits[1], digits[2]))
    code = code.astype(I32)
    return (code[0:1] << 5) + code[1:2]


def own_kernel(
    rows, codes, mix_ref, qt_ref, k_ref, vt_ref, nk_ref, nvt_ref, seen_ref, *refs,
):
    code_refs = refs[:codes]
    acc_ref, near_ref, top_ref, den_ref, e_ref, et_ref, bias_ref, q4_ref, p_ref = refs[codes:]
    tok_rows, group = k_ref.shape
    heads = mix_ref.shape[1]
    width = group // heads
    q4_ref[...] = jnp.zeros_like(q4_ref)
    same = iota((FBLK, FBLK), 0) == iota((FBLK, FBLK), 1)
    nk, nvt = nk_ref[...], nvt_ref[...]
    rank = ranks(mask_before(code_refs, rows), tok_rows)
    rank = jnp.where(lax.axis_index("seq") > 0, rank, -1)
    rank_column = column(rank)
    bias_ref[:tok_rows] = jnp.where(rank_column >= 0, 0.0, HIDE)
    bias_ref[tok_rows:] = seen_ref[...]
    for at in range(0, et_ref.shape[0], FBLK):
        e_ref[:, at : at + FBLK] = ones_where(rank_column == iota((tok_rows, FBLK), 1) + at)
        et_ref[at : at + FBLK] = ones_where(iota((FBLK, tok_rows), 0) + at == rank)
    for g in range(tok_rows // FBLK):
        at = g * FBLK
        slot = g % 2
        spread_heads(q4_ref.at[slot], qt_ref, at, heads)
        q4 = q4_ref[slot]
        bias = jnp.where(same, 0.0, seen_ref[at : at + FBLK])
        own_scores = nn(k_ref[at : at + FBLK], q4)
        near_scores = nn(nk, q4)
        scales = []
        for h in range(heads):
            lanes = slice(h * FBLK, (h + 1) * FBLK)
            part = own_scores[:, lanes] + bias
            top = jnp.max(part, axis=0, keepdims=True)
            weight = jnp.exp(part - top)
            top_ref[g : g + 1, lanes] = top
            den_ref[g : g + 1, lanes] = jnp.sum(weight, axis=0, keepdims=True)
            p_ref[slot, :FBLK, lanes] = weight.astype(BF)
            part = near_scores[:, lanes]
            weight = jnp.exp(part - jnp.max(part, axis=0, keepdims=True))
            scales.append(mix_ref[1, h] / jnp.sum(weight, axis=0, keepdims=True))
            p_ref[slot, FBLK:, lanes] = weight.astype(BF)
        own_out = nn(vt_ref[:, at : at + FBLK], p_ref[slot, :FBLK])
        near_out = nn(nvt, p_ref[slot, FBLK:])
        for h in range(heads):
            rows, lanes = slice(h * width, (h + 1) * width), slice(h * FBLK, (h + 1) * FBLK)
            acc_ref[rows, at : at + FBLK] = own_out[rows, lanes]
            near_ref[rows, at : at + FBLK] = near_out[rows, lanes] * scales[h]


def window_kernel(k_ref, vt_ref, comp_ref, e_ref, et_ref, *refs):
    summ_refs, (kw_ref, vw_ref, ck_ref, cv_ref, all_ref) = refs[:-5], refs[-5:]
    tok_rows, group = k_ref.shape
    packed = e_ref.shape[1]
    kw_ref[:tok_rows] = nn(e_ref[...], comp_ref[:packed]).astype(BF)
    kw_ref[tok_rows:] = k_ref[...]
    prev = None
    for part in range(packed // group):
        term = nn(
            comp_ref[packed + part * group : packed + (part + 1) * group],
            et_ref[part * group : (part + 1) * group],
        )
        prev = term if prev is None else prev + term
    vw_ref[:, :tok_rows] = prev.astype(BF)
    vw_ref[:, tok_rows:] = vt_ref[...]
    at = 0
    for part in summ_refs:
        all_ref[at : at + part.shape[0]] = part[...]
        at += part.shape[0]
    slab, slabs = lax.axis_index("seq"), lax.axis_size("seq")
    mids, fars = tok_rows // POOL2, tok_rows // POOL3
    shape = (ck_ref.shape[0], all_ref.shape[0])
    line = iota(shape, 0)
    step = 2 * SUMM_ROWS
    turn = line // mids
    far = line - 3 * mids
    shard = slab - 1 + turn
    turned = slab if slabs == 8 else 0
    source = jnp.where(
        line < 3 * mids,
        (shard ^ turned) * step + line - turn * mids,
        ((far // fars) ^ turned) * step + mids + far % fars,
    )
    source = jnp.where((line >= 3 * mids) | ((shard >= 0) & (shard < slabs)), source, -step)
    gathered = all_ref[...]
    ck_ref[...] = nn(ones_where(source == iota(shape, 1)), gathered).astype(BF)
    values = nn(ones_where(source + SUMM_ROWS == iota(shape, 1)), gathered)
    cv_ref[...] = jnp.transpose(values).astype(BF)


def rest_kernel(
    first, blocks, lists_ref, mix_ref, qt_ref, kw_ref, vw_ref, ck_ref, cv_ref, bias_ref,
    acc_ref, near_ref, top_ref, den_ref, out_ref, kc_ref, vc_ref, q4_ref, p_ref,
):
    group, tok_rows = qt_ref.shape
    heads = mix_ref.shape[1]
    width = group // heads
    others = FINE_K - 1
    fine = others * FBLK
    mid = 3 * (tok_rows // POOL2)
    far_at = fine + mid
    total = kc_ref.shape[1]
    for slot in range(2):
        kc_ref[slot, fine:] = ck_ref[...]
        vc_ref[slot, :, fine:] = cv_ref[...]
    q4_ref[...] = jnp.zeros_like(q4_ref)
    for index in range(blocks):
        g = first + index
        at = g * FBLK
        slot = index % 2
        biases = []
        for entry in range(others):
            start = pl.multiple_of(lists_ref[entry + 1, g] * FBLK, FBLK)
            kc_ref[slot, entry * FBLK : (entry + 1) * FBLK] = kw_ref[pl.ds(start, FBLK)]
            vc_ref[slot, :, entry * FBLK : (entry + 1) * FBLK] = vw_ref[:, pl.ds(start, FBLK)]
            biases.append(bias_ref[pl.ds(start, FBLK)])
        spread_heads(q4_ref.at[slot], qt_ref, at, heads)
        scores = nn(kc_ref[slot], q4_ref[slot])
        scales, keeps = [], []
        for h in range(heads):
            lanes = slice(h * FBLK, (h + 1) * FBLK)
            parts = [scores[e * FBLK : (e + 1) * FBLK, lanes] + biases[e] for e in range(others)]
            old_top = top_ref[g : g + 1, lanes]
            top = functools.reduce(
                jnp.maximum, [jnp.max(part, axis=0, keepdims=True) for part in parts] + [old_top]
            )
            keep = jnp.exp(old_top - top)
            den = den_ref[g : g + 1, lanes] * keep
            for e, part in enumerate(parts):
                weight = jnp.exp(part - top)
                den = den + jnp.sum(weight, axis=0, keepdims=True)
                p_ref[slot, e * FBLK : (e + 1) * FBLK, lanes] = weight.astype(BF)
            scale = mix_ref[0, h] / den
            scales.append(scale)
            keeps.append(keep * scale)
            for level, (low, high) in enumerate(((fine, far_at), (far_at, total))):
                part = scores[low:high, lanes]
                weight = jnp.exp(part - jnp.max(part, axis=0, keepdims=True))
                share = mix_ref[level + 2, h] / jnp.sum(weight, axis=0, keepdims=True)
                p_ref[slot, low:high, lanes] = (weight * share).astype(BF)
        fine_out = nn(vc_ref[slot, :, :fine], p_ref[slot, :fine])
        coarse_out = nn(vc_ref[slot, :, fine:], p_ref[slot, fine:])
        rows = []
        for h in range(heads):
            pick = (slice(h * width, (h + 1) * width), slice(h * FBLK, (h + 1) * FBLK))
            mine = (pick[0], slice(at, at + FBLK))
            rows.append(
                fine_out[pick] * scales[h]
                + acc_ref[mine] * keeps[h]
                + (coarse_out[pick] + near_ref[mine])
            )
        out_ref[index * FBLK : (index + 1) * FBLK] = jnp.transpose(
            jnp.concatenate(rows, axis=0)
        ).astype(BF)


def output_kernel(w_ref, *refs):
    out_ref = refs[-1]
    group = w_ref.shape[1]
    head = lax.axis_index("head")
    total = None
    for distance, part in zip((0, 2, 1, 3), refs[:4]):
        start = pl.multiple_of((head ^ distance) * group, group)
        term = nn(part[...], w_ref[pl.ds(start, group)])
        total = term if total is None else total + term
    out_ref[...] = total.astype(BF)


def local(tokens, w_query, w_key, w_value, w_out, level_mix, fine_blocks, order, mask_ids):
    tok_rows, width = tokens.shape
    slabs = lax.axis_size("seq")
    slab, head = lax.axis_index("seq"), lax.axis_index("head")
    group = w_query.shape[1]
    heads = level_mix.shape[1]
    packed = tok_rows - mask_ids.shape[1]
    near, mids, fars = tok_rows // POOL1, tok_rows // POOL2, tok_rows // POOL3
    coarse = 3 * mids + fars * slabs
    step = 2 * SUMM_ROWS
    chosen = packed + SUMM_ROWS + near

    shape = jax.ShapeDtypeStruct
    params = pltpu.CompilerParams(vmem_limit_bytes=VMEM_LIMIT)

    def prepare(early):
        return pl.pallas_call(
            prepare_kernel,
            out_shape=(
                shape((tok_rows, tok_rows), BF),
                shape((tok_rows, tok_rows), BF),
                shape((chosen, tok_rows), BF),
                shape((SUMM_ROWS + near, 128), F32),
                shape((16, SUMM_ROWS + near), F32),
                shape((tok_rows, FBLK), F32),
                shape((2 * group, width), BF),
                shape((width, group), BF),
            ),
            in_specs=vmem_specs(5) + [pl.BlockSpec(memory_space=pl.ANY)],
            out_specs=vmem_specs(8),
            compiler_params=params,
            name="prepare",
        )(order, mask_ids, w_query, w_value, w_key, early)

    pieces, prepared, before = exchange_tokens(tokens, mask_ids, prepare)
    permute, permute_t, select, f_col, f_row, seen, w_t, w_k = prepared
    places = tuple((row, distances) for _, row, distances in pieces)
    comp, summ, k0, v0, rows_here = pl.pallas_call(
        functools.partial(project_kernel, places),
        out_shape=(
            shape((2 * packed, group), BF),
            shape((step, group), BF),
            shape((tok_rows, group), BF),
            shape((group, tok_rows), BF),
            shape((tok_rows, width), BF),
        ),
        in_specs=vmem_specs(len(pieces) + 4),
        out_specs=vmem_specs(5),
        compiler_params=params,
        name="project",
    )(*[piece for piece, _, _ in pieces], w_t, w_k, select, f_col)
    if slabs == 8:
        other = by_distance(summ, 1)
    comp_before = to_next(comp)

    q_t, v_t, keys, near_k, near_vt = pl.pallas_call(
        order_kernel,
        out_shape=(
            shape((group, tok_rows), BF),
            shape((group, tok_rows), BF),
            shape((tok_rows, group), BF),
            shape((near, group), BF),
            shape((group, near), BF),
        ),
        in_specs=vmem_specs(9),
        out_specs=vmem_specs(5),
        compiler_params=params,
        name="order",
    )(permute, permute_t, select, f_col, f_row, w_t, rows_here, k0, v0)
    if slabs == 8:
        pair = stacked((summ, other), step, (near_k,))
        summaries = [pair] + [by_distance(pair, d) for d in (2, 4, 6)]
    else:
        copies = jnp.broadcast_to(summ[None], (slabs, step, group))
        copies = lax.all_to_all(copies, "seq", split_axis=0, concat_axis=0, tiled=True)
        summaries = [copies.reshape(slabs * step, group)]

    blocks = tok_rows // FBLK
    acc, near_out, top, den, expand, expand_t, bias = pl.pallas_call(
        functools.partial(own_kernel, tok_rows // slabs, len(before)),
        out_shape=(
            shape((group, tok_rows), F32),
            shape((group, tok_rows), F32),
            shape((blocks, heads * FBLK), F32),
            shape((blocks, heads * FBLK), F32),
            shape((tok_rows, packed), BF),
            shape((packed, tok_rows), BF),
            shape((2 * tok_rows, FBLK), F32),
        ),
        in_specs=smem_specs(1) + vmem_specs(6 + len(before)),
        out_specs=vmem_specs(7),
        scratch_shapes=[
            pltpu.VMEM((2, group, heads * FBLK), BF),
            pltpu.VMEM((2, FBLK + near, heads * FBLK), BF),
        ],
        compiler_params=params,
        name="own",
    )(level_mix, q_t, keys, v_t, near_k, near_vt, seen, *before)

    window_k, window_v, coarse_k, coarse_v = pl.pallas_call(
        window_kernel,
        out_shape=(
            shape((2 * tok_rows, group), BF),
            shape((group, 2 * tok_rows), BF),
            shape((coarse, group), BF),
            shape((group, coarse), BF),
        ),
        in_specs=vmem_specs(5 + len(summaries)),
        out_specs=vmem_specs(4),
        scratch_shapes=[pltpu.VMEM((slabs * step, group), BF)],
        compiler_params=params,
        name="window",
    )(keys, v_t, comp_before, expand, expand_t, *summaries)

    total = (FINE_K - 1) * FBLK + coarse
    lists = fine_blocks.T
    parts = PARTS if sum(PARTS) == blocks else (blocks,)
    waiting, out, first = None, None, 0

    def finish(out, attended, third, second, base):
        fourth = over_head(third, CORE_PAIRS)
        rows = attended.shape[0]
        previous = [] if out is None else [out]
        tile = pl.BlockSpec((FBLK, group), lambda i: (i, 0))
        return pl.pallas_call(
            output_kernel,
            grid=(rows // FBLK,),
            out_shape=shape((tok_rows, group), BF),
            in_specs=[pl.BlockSpec((width, group), lambda i: (0, 0))]
            + [tile] * 4
            + [pl.BlockSpec(memory_space=pl.ANY)] * len(previous),
            out_specs=pl.BlockSpec((FBLK, group), lambda i, base=base: (i + base, 0)),
            input_output_aliases={5: 0} if previous else {},
            compiler_params=params,
            name="output",
        )(w_out, attended, third, second, fourth, *previous)

    for count in parts:
        attended = pl.pallas_call(
            functools.partial(rest_kernel, first, count),
            out_shape=shape((count * FBLK, group), BF),
            in_specs=smem_specs(2) + vmem_specs(10),
            out_specs=pl.BlockSpec(memory_space=pltpu.VMEM),
            scratch_shapes=[
                pltpu.VMEM((2, total, group), BF),
                pltpu.VMEM((2, group, total), BF),
                pltpu.VMEM((2, group, heads * FBLK), BF),
                pltpu.VMEM((2, total, heads * FBLK), BF),
            ],
            compiler_params=params,
            name="rest",
        )(
            lists, level_mix, q_t, window_k, window_v, coarse_k, coarse_v, bias, acc, near_out, top, den
        )
        third = over_head(attended, X_PAIRS)
        second = over_head(attended, CORE_PAIRS)
        if waiting is not None:
            old, old_third, old_second, old_base = waiting
            old_third, attended = lax.optimization_barrier((old_third, attended))
            out = finish(out, old, old_third, old_second, old_base)
        waiting = (attended, third, second, first)
        first += count
    return finish(out, *waiting)


def solution(mesh):
    placed = (
        P("seq", None),
        P(None, "head"),
        P(None, "head"),
        P(None, "head"),
        P(None, "head"),
        P(None, "head"),
        P("seq", None),
        P("seq", None),
        P("seq", None),
    )
    return jax.shard_map(
        local, mesh=mesh, in_specs=placed, out_specs=P("seq", "head"), check_vma=False
    )
```

```python
import functools

import jax
import jax.numpy as jnp
from jax import lax
from jax.experimental import pallas as pl
from jax.experimental.pallas import tpu as pltpu
from jax.sharding import PartitionSpec as P

FBLK = 128
FINE_K = 4
POOL1 = 8
POOL2 = 64
POOL3 = 512
SUMM_ROWS = 32
CODE_ROWS = 16
BF = jnp.bfloat16
F32 = jnp.float32
I32 = jnp.int32
HIDE = -1e30
VMEM_LIMIT = 24 * 1024 * 1024
COST = pl.CostEstimate(flops=1, bytes_accessed=1, transcendentals=0)
PARTS = (4, 4)

X_PAIRS = [(0, 2), (2, 0), (1, 3), (3, 1)]
CORE_PAIRS = [(0, 1), (1, 0), (2, 3), (3, 2)]


def nn(a, b):
    return lax.dot_general(a, b, (((1,), (0,)), ((), ())), preferred_element_type=F32)


def nt(a, b):
    return lax.dot_general(a, b, (((1,), (1,)), ((), ())), preferred_element_type=F32)


def iota(shape, axis):
    return lax.broadcasted_iota(I32, shape, axis)


def ones_where(condition):
    return jnp.where(condition, 1.0, 0.0).astype(BF)


def vmem_specs(count):
    return [pl.BlockSpec(memory_space=pltpu.VMEM)] * count


def smem_specs(count):
    return [pl.BlockSpec(memory_space=pltpu.SMEM)] * count


def over_head(block, pairs):
    return lax.ppermute(block, "head", pairs)


def to_next(block):
    return lax.ppermute(block, "seq", [(i, i + 1) for i in range(lax.axis_size("seq") - 1)])


def send_kernel(distances, tokens_ref, mask_ref, *refs):
    outs, own = refs[:-1], refs[-1]
    slab, head = lax.axis_index("seq"), lax.axis_index("head")
    rows = own.shape[0]
    quarter = tokens_ref.shape[1] // 4
    ids = mask_ref[...]
    line = iota((CODE_ROWS, ids.shape[1]), 0)
    code = jnp.where(line == 0, ids >> 5, jnp.where(line == 1, ids & 31, 0)).astype(F32).astype(BF)
    for distance, out in zip(distances, outs):
        row = pl.multiple_of((slab ^ distance) * rows, rows)
        parts = out.shape[1] // quarter
        for part in range(parts):
            start = pl.multiple_of((head ^ (2 * part)) * quarter, quarter)
            out[:rows, part * quarter : (part + 1) * quarter] = tokens_ref[
                pl.ds(row, rows), pl.ds(start, quarter)
            ]
        for part in range(code.shape[1] // out.shape[1]):
            at = rows + part * CODE_ROWS
            out[at : at + CODE_ROWS] = code[:, part * out.shape[1] : (part + 1) * out.shape[1]]
    own[...] = tokens_ref[pl.ds(pl.multiple_of(slab * rows, rows), rows)]


def stack_kernel(count, *refs):
    target = refs[-1]
    height = target.shape[0] // count
    for index in range(count):
        target[index * height : (index + 1) * height] = refs[index][:height]


def stacked(parts, rows, after=()):
    return pl.pallas_call(
        functools.partial(stack_kernel, len(parts)),
        out_shape=jax.ShapeDtypeStruct((len(parts) * rows, parts[0].shape[1]), parts[0].dtype),
        in_specs=vmem_specs(len(parts)) + [pl.BlockSpec(memory_space=pl.ANY)] * len(after),
        out_specs=pl.BlockSpec(memory_space=pltpu.VMEM),
        compiler_params=pltpu.CompilerParams(vmem_limit_bytes=VMEM_LIMIT),
        cost_estimate=COST,
        name="stack",
    )(*parts, *after)


def packed_rows(select, packed, parts):
    quarter = min(part.shape[1] for part in parts)
    return pl.pallas_call(
        pack_kernel,
        out_shape=jax.ShapeDtypeStruct((packed, quarter), BF),
        in_specs=vmem_specs(1 + len(parts)),
        out_specs=pl.BlockSpec(memory_space=pltpu.VMEM),
        scratch_shapes=[pltpu.VMEM((sum(part.shape[0] for part in parts), quarter), BF)],
        compiler_params=pltpu.CompilerParams(vmem_limit_bytes=VMEM_LIMIT),
        cost_estimate=COST,
        name="pack",
    )(select, *parts)


def by_distance(block, distance):
    return lax.ppermute(block, "seq", [(i, i ^ distance) for i in range(lax.axis_size("seq"))])


def exchange_tokens(tokens, mask_ids, prepare):
    tok_rows, width = tokens.shape
    slabs = lax.axis_size("seq")
    rows = tok_rows // slabs
    quarter = width // 4
    packed = tok_rows - mask_ids.shape[1]
    if slabs != 8:
        split = tokens.reshape(slabs, rows, width)
        mine = lax.dynamic_slice_in_dim(split, lax.axis_index("head") * quarter, quarter, axis=2)
        first = lax.all_to_all(mine, "seq", split_axis=0, concat_axis=0, tiled=True).reshape(
            tok_rows, quarter
        )
        third = over_head(first, X_PAIRS)
        second = over_head(first, CORE_PAIRS)
        fourth = over_head(third, CORE_PAIRS)
        pieces = [(first, 0, (0,)), (third, 0, (2,)), (second, 0, (1,)), (fourth, 0, (3,))]
        prepared = prepare(first)
        halo = to_next(packed_rows(prepared[2], packed, (first,)))
        return pieces, prepared, [to_next(mask_ids)], halo
    distances = (7, 6, 5, 4, 3, 2, 1)
    near_rows, far_rows = rows + CODE_ROWS, rows + 2 * CODE_ROWS
    *blocks, own = pl.pallas_call(
        functools.partial(send_kernel, distances),
        out_shape=tuple(
            jax.ShapeDtypeStruct((far_rows, quarter) if d > 3 else (near_rows, 2 * quarter), BF)
            for d in distances
        )
        + (jax.ShapeDtypeStruct((rows, width), BF),),
        in_specs=vmem_specs(2),
        out_specs=vmem_specs(8),
        compiler_params=pltpu.CompilerParams(vmem_limit_bytes=VMEM_LIMIT),
        cost_estimate=COST,
        name="send",
    )(tokens, mask_ids)
    arrived = [by_distance(block, d) for block, d in zip(blocks, distances)]
    prepared = prepare(arrived[0])
    far = stacked(arrived[:4], rows, (arrived[6], prepared[2]))
    near = stacked(arrived[4:], rows)
    far_x = over_head(far, X_PAIRS)
    halo = packed_rows(prepared[2], packed, (far, near, own))
    near_core = over_head(near, CORE_PAIRS)
    far_core = over_head(far, CORE_PAIRS)
    far_x, _ = lax.optimization_barrier((far_x, halo))
    halo = to_next(halo)
    far_last = over_head(far_x, CORE_PAIRS)
    pieces = [(far, 0, (0,)), (far_x, 0, (2,)), (far_core, 0, (1,)), (far_last, 0, (3,))]
    pieces += [(near, 4 * rows, (0, 2)), (near_core, 4 * rows, (1, 3)), (own, 7 * rows, None)]
    return pieces, prepared, [arrived[6], arrived[4], arrived[0]], halo


def column(row, lanes=128):
    return jnp.transpose(jnp.broadcast_to(row.astype(F32), (lanes, row.shape[1]))).astype(I32)


def ranks(ids, tok_rows, lanes=128):
    hidden = column(ids)
    parts = []
    for at in range(0, tok_rows, lanes):
        time = iota((1, lanes), 1) + at
        count = jnp.sum(jnp.where(hidden < time, 1.0, 0.0), axis=0, keepdims=True)
        here = jnp.sum(jnp.where(hidden == time, 1.0, 0.0), axis=0, keepdims=True)
        parts.append(jnp.where(here == 0.0, time - count.astype(I32), -1))
    return jnp.concatenate(parts, axis=1)


def prepare_kernel(
    order_ref, mask_ref, wq_ref, wv_ref, wk_in, early_ref,
    p_ref, pt_ref, sel_ref, fcol_ref, frow_ref, bias_ref, wt_ref, wk_ref,
):
    slab, slabs = lax.axis_index("seq"), lax.axis_size("seq")
    tok_rows = order_ref.shape[1]
    packed = tok_rows - mask_ref.shape[1]
    flip = (slab ^ 7) * (tok_rows // slabs) if slabs == 8 else 0
    mids = tok_rows // POOL2
    group = wq_ref.shape[1]
    lanes = 128

    place = order_ref[...] ^ flip
    place_column = column(place)
    for at in range(0, tok_rows, lanes):
        p_ref[:, at : at + lanes] = ones_where(place_column == iota((tok_rows, lanes), 1) + at)
        pt_ref[at : at + lanes] = ones_where(iota((lanes, tok_rows), 0) + at == place)
    rank = ranks(mask_ref[...], tok_rows)
    time = jnp.where(rank >= 0, iota((1, tok_rows), 1), -1) + 1
    line = iota((16, tok_rows), 0)
    stack = jnp.where(
        line == 0,
        time >> 5,
        jnp.where(
            line == 1,
            time & 31,
            jnp.where(line == 2, (rank + 1) >> 5, jnp.where(line == 3, (rank + 1) & 31, 0)),
        ),
    )
    moved = nn(stack.astype(F32).astype(BF), p_ref[...]).astype(I32)
    time_here = (moved[0:1] << 5) + moved[1:2] - 1
    rank_here = (moved[2:3] << 5) + moved[3:4] - 1
    for at in range(0, packed, lanes):
        sel_ref[at : at + lanes] = ones_where(iota((lanes, tok_rows), 0) + at == rank_here)
    line = iota((SUMM_ROWS, tok_rows), 0)
    sel_ref[packed : packed + SUMM_ROWS] = ones_where(
        ((time_here >> 6) == line) | (((time_here >> 9) + mids == line) & (time_here >= 0))
    )
    lead = packed + SUMM_ROWS
    near = sel_ref.shape[0] - lead
    sel_ref[lead:] = ones_where((time_here >> 3) == iota((near, tok_rows), 0))
    pools = sel_ref[packed:]
    fcol_ref[...] = 1.0 / jnp.sqrt(jnp.maximum(nn(pools, jnp.ones((tok_rows, lanes), BF)), 1.0))
    frow_ref[...] = 1.0 / jnp.sqrt(jnp.maximum(nt(jnp.ones((16, tok_rows), BF), pools), 1.0))
    bias_ref[...] = jnp.where(column(rank) >= 0, 0.0, HIDE)
    wt_ref[:group] = jnp.transpose(wq_ref[...])
    wt_ref[group:] = jnp.transpose(wv_ref[...])
    wk_ref[...] = wk_in[...]


def pack_kernel(sel_ref, *refs):
    parts, (out_ref, rows_ref) = refs[:-2], refs[-2:]
    quarter = out_ref.shape[1]
    at = 0
    for part in parts:
        height, width = part.shape
        if width == 4 * quarter:
            start = pl.multiple_of(lax.axis_index("head") * quarter, quarter)
            rows_ref[at : at + height] = part[:, pl.ds(start, quarter)]
        else:
            rows_ref[at : at + height] = part[:, :quarter]
        at += height
    out_ref[...] = nn(sel_ref[: out_ref.shape[0]], rows_ref[...]).astype(BF)


def project_kernel(places, *refs):
    count = len(places)
    piece_refs, refs = refs[:count], refs[count:]
    wt_ref, wk_ref, sel_ref, fcol_ref, summ_ref, k_ref, v_ref, x_ref = refs
    quarter = x_ref.shape[1] // 4
    head = lax.axis_index("head")
    for piece, (row, distances) in zip(piece_refs, places):
        height = piece.shape[0]
        if distances is None:
            x_ref[row : row + height] = piece[...]
            continue
        for part, distance in enumerate(distances):
            start = pl.multiple_of((head ^ distance) * quarter, quarter)
            x_ref[row : row + height, pl.ds(start, quarter)] = piece[
                :, part * quarter : (part + 1) * quarter
            ]
    group = wk_ref.shape[1]
    near = x_ref.shape[0] // POOL1
    lead = sel_ref.shape[0] - near
    x = x_ref[...]
    keys = nn(x, wk_ref[...]).astype(BF)
    k_ref[...] = keys
    vt = nt(wt_ref[group:], x).astype(BF)
    v_ref[...] = vt
    sel = sel_ref[lead - SUMM_ROWS : lead]
    kl = nn(sel, keys)
    vl = nt(vt, sel)
    factor = fcol_ref[:SUMM_ROWS, :1]
    summ_k = (kl * factor).astype(BF)
    tail = jnp.concatenate(
        [vl, jnp.zeros((group, 128 - SUMM_ROWS), F32)], axis=1
    )
    summ_v = (jnp.transpose(tail)[:SUMM_ROWS] * factor).astype(BF)
    summ_ref[:SUMM_ROWS] = summ_k
    summ_ref[SUMM_ROWS:] = summ_v


def spread_heads(q4_ref, qt_ref, at, heads):
    width = q4_ref.shape[0] // heads
    for h in range(heads):
        rows = slice(h * width, (h + 1) * width)
        q4_ref[rows, h * FBLK : (h + 1) * FBLK] = qt_ref[rows, at : at + FBLK]


def order_kernel(
    p_ref, pt_ref, sel_ref, fcol_ref, frow_ref, wt_ref, x_ref, k0_ref, v0_ref,
    qt_ref, vt_ref, k_ref, nk_ref, nvt_ref,
):
    group = k_ref.shape[1]
    near = nk_ref.shape[0]
    k0, v0 = k0_ref[...], v0_ref[...]
    q0 = nt(wt_ref[:group], x_ref[...]).astype(BF)
    k_ref[...] = nn(p_ref[...], k0).astype(BF)
    qt_ref[...] = (nn(q0, pt_ref[...]) * 0.125).astype(BF)
    vt_ref[...] = nn(v0, pt_ref[...]).astype(BF)
    pool = sel_ref[sel_ref.shape[0] - near :]
    nk_ref[...] = (nn(pool, k0) * fcol_ref[SUMM_ROWS:, :1]).astype(BF)
    nvt_ref[...] = (nt(v0, pool) * frow_ref[:1, SUMM_ROWS:]).astype(BF)


def mask_before(refs, rows):
    if len(refs) == 1:
        return refs[0][...]
    slab = lax.axis_index("seq")
    digits = []
    for block in refs:
        width = block.shape[1]
        parts = [
            block[rows + at : rows + at + CODE_ROWS].astype(F32)
            for at in range(0, block.shape[0] - rows, CODE_ROWS)
        ]
        digits.append(jnp.concatenate(parts, axis=1) if len(parts) > 1 else parts[0])
    distance = slab ^ (slab - 1)
    code = jnp.where(distance == 1, digits[0], jnp.where(distance == 3, digits[1], digits[2]))
    code = code.astype(I32)
    return (code[0:1] << 5) + code[1:2]


def own_kernel(
    rows, codes, mix_ref, qt_ref, k_ref, vt_ref, nk_ref, nvt_ref, seen_ref, *refs,
):
    code_refs = refs[:codes]
    acc_ref, near_ref, top_ref, den_ref, e_ref, et_ref, bias_ref, q4_ref, p_ref = refs[codes:]
    tok_rows, group = k_ref.shape
    heads = mix_ref.shape[1]
    width = group // heads
    q4_ref[...] = jnp.zeros_like(q4_ref)
    same = iota((FBLK, FBLK), 0) == iota((FBLK, FBLK), 1)
    nk, nvt = nk_ref[...], nvt_ref[...]
    rank = ranks(mask_before(code_refs, rows), tok_rows)
    rank = jnp.where(lax.axis_index("seq") > 0, rank, -1)
    rank_column = column(rank)
    bias_ref[:tok_rows] = jnp.where(rank_column >= 0, 0.0, HIDE)
    bias_ref[tok_rows:] = seen_ref[...]
    for at in range(0, et_ref.shape[0], FBLK):
        e_ref[:, at : at + FBLK] = ones_where(rank_column == iota((tok_rows, FBLK), 1) + at)
        et_ref[at : at + FBLK] = ones_where(iota((FBLK, tok_rows), 0) + at == rank)
    for g in range(tok_rows // FBLK):
        at = g * FBLK
        slot = g % 2
        spread_heads(q4_ref.at[slot], qt_ref, at, heads)
        q4 = q4_ref[slot]
        bias = jnp.where(same, 0.0, seen_ref[at : at + FBLK])
        own_scores = nn(k_ref[at : at + FBLK], q4)
        near_scores = nn(nk, q4)
        scales = []
        for h in range(heads):
            lanes = slice(h * FBLK, (h + 1) * FBLK)
            part = own_scores[:, lanes] + bias
            top = jnp.max(part, axis=0, keepdims=True)
            weight = jnp.exp(part - top)
            top_ref[g : g + 1, lanes] = top
            den_ref[g : g + 1, lanes] = jnp.sum(weight, axis=0, keepdims=True)
            p_ref[slot, :FBLK, lanes] = weight.astype(BF)
            part = near_scores[:, lanes]
            weight = jnp.exp(part - jnp.max(part, axis=0, keepdims=True))
            scales.append(mix_ref[1, h] / jnp.sum(weight, axis=0, keepdims=True))
            p_ref[slot, FBLK:, lanes] = weight.astype(BF)
        own_out = nn(vt_ref[:, at : at + FBLK], p_ref[slot, :FBLK])
        near_out = nn(nvt, p_ref[slot, FBLK:])
        for h in range(heads):
            rows, lanes = slice(h * width, (h + 1) * width), slice(h * FBLK, (h + 1) * FBLK)
            acc_ref[rows, at : at + FBLK] = own_out[rows, lanes]
            near_ref[rows, at : at + FBLK] = near_out[rows, lanes] * scales[h]


def window_kernel(k_ref, vt_ref, wt_ref, wk_ref, e_ref, et_ref, *refs):
    halo_refs, refs = refs[:4], refs[4:]
    summ_refs, (kw_ref, vw_ref, ck_ref, cv_ref, all_ref, x_ref) = refs[:-6], refs[-6:]
    tok_rows, group = k_ref.shape
    quarter = x_ref.shape[1] // 4
    head = lax.axis_index("head")
    for distance, part in zip((0, 2, 1, 3), halo_refs):
        start = pl.multiple_of((head ^ distance) * quarter, quarter)
        x_ref[:, pl.ds(start, quarter)] = part[...]
    x = x_ref[...]
    kw_ref[:tok_rows] = nn(e_ref[...], nn(x, wk_ref[...]).astype(BF)).astype(BF)
    kw_ref[tok_rows:] = k_ref[...]
    vw_ref[:, :tok_rows] = nn(nt(wt_ref[group:], x).astype(BF), et_ref[...]).astype(BF)
    vw_ref[:, tok_rows:] = vt_ref[...]
    at = 0
    for part in summ_refs:
        all_ref[at : at + part.shape[0]] = part[...]
        at += part.shape[0]
    slab, slabs = lax.axis_index("seq"), lax.axis_size("seq")
    mids, fars = tok_rows // POOL2, tok_rows // POOL3
    shape = (ck_ref.shape[0], all_ref.shape[0])
    line = iota(shape, 0)
    step = 2 * SUMM_ROWS
    turn = line // mids
    far = line - 3 * mids
    shard = slab - 1 + turn
    turned = slab if slabs == 8 else 0
    source = jnp.where(
        line < 3 * mids,
        (shard ^ turned) * step + line - turn * mids,
        ((far // fars) ^ turned) * step + mids + far % fars,
    )
    source = jnp.where((line >= 3 * mids) | ((shard >= 0) & (shard < slabs)), source, -step)
    gathered = all_ref[...]
    ck_ref[...] = nn(ones_where(source == iota(shape, 1)), gathered).astype(BF)
    values = nn(ones_where(source + SUMM_ROWS == iota(shape, 1)), gathered)
    cv_ref[...] = jnp.transpose(values).astype(BF)


def rest_kernel(
    first, blocks, lists_ref, mix_ref, qt_ref, kw_ref, vw_ref, ck_ref, cv_ref, bias_ref,
    acc_ref, near_ref, top_ref, den_ref, out_ref, kc_ref, vc_ref, q4_ref, p_ref,
):
    group, tok_rows = qt_ref.shape
    heads = mix_ref.shape[1]
    width = group // heads
    others = FINE_K - 1
    fine = others * FBLK
    mid = 3 * (tok_rows // POOL2)
    far_at = fine + mid
    total = kc_ref.shape[1]
    for slot in range(2):
        kc_ref[slot, fine:] = ck_ref[...]
        vc_ref[slot, :, fine:] = cv_ref[...]
    q4_ref[...] = jnp.zeros_like(q4_ref)
    for index in range(blocks):
        g = first + index
        at = g * FBLK
        slot = index % 2
        biases = []
        for entry in range(others):
            start = pl.multiple_of(lists_ref[entry + 1, g] * FBLK, FBLK)
            kc_ref[slot, entry * FBLK : (entry + 1) * FBLK] = kw_ref[pl.ds(start, FBLK)]
            vc_ref[slot, :, entry * FBLK : (entry + 1) * FBLK] = vw_ref[:, pl.ds(start, FBLK)]
            biases.append(bias_ref[pl.ds(start, FBLK)])
        spread_heads(q4_ref.at[slot], qt_ref, at, heads)
        scores = nn(kc_ref[slot], q4_ref[slot])
        scales, keeps = [], []
        for h in range(heads):
            lanes = slice(h * FBLK, (h + 1) * FBLK)
            parts = [scores[e * FBLK : (e + 1) * FBLK, lanes] + biases[e] for e in range(others)]
            old_top = top_ref[g : g + 1, lanes]
            top = functools.reduce(
                jnp.maximum, [jnp.max(part, axis=0, keepdims=True) for part in parts] + [old_top]
            )
            keep = jnp.exp(old_top - top)
            den = den_ref[g : g + 1, lanes] * keep
            for e, part in enumerate(parts):
                weight = jnp.exp(part - top)
                den = den + jnp.sum(weight, axis=0, keepdims=True)
                p_ref[slot, e * FBLK : (e + 1) * FBLK, lanes] = weight.astype(BF)
            scale = mix_ref[0, h] / den
            scales.append(scale)
            keeps.append(keep * scale)
            for level, (low, high) in enumerate(((fine, far_at), (far_at, total))):
                part = scores[low:high, lanes]
                weight = jnp.exp(part - jnp.max(part, axis=0, keepdims=True))
                share = mix_ref[level + 2, h] / jnp.sum(weight, axis=0, keepdims=True)
                p_ref[slot, low:high, lanes] = (weight * share).astype(BF)
        fine_out = nn(vc_ref[slot, :, :fine], p_ref[slot, :fine])
        coarse_out = nn(vc_ref[slot, :, fine:], p_ref[slot, fine:])
        rows = []
        for h in range(heads):
            pick = (slice(h * width, (h + 1) * width), slice(h * FBLK, (h + 1) * FBLK))
            mine = (pick[0], slice(at, at + FBLK))
            rows.append(
                fine_out[pick] * scales[h]
                + acc_ref[mine] * keeps[h]
                + (coarse_out[pick] + near_ref[mine])
            )
        out_ref[index * FBLK : (index + 1) * FBLK] = jnp.transpose(
            jnp.concatenate(rows, axis=0)
        ).astype(BF)


def output_kernel(w_ref, *refs):
    out_ref = refs[-1]
    group = w_ref.shape[1]
    head = lax.axis_index("head")
    total = None
    for distance, part in zip((0, 2, 1, 3), refs[:4]):
        start = pl.multiple_of((head ^ distance) * group, group)
        term = nn(part[...], w_ref[pl.ds(start, group)])
        total = term if total is None else total + term
    out_ref[...] = total.astype(BF)


def local(tokens, w_query, w_key, w_value, w_out, level_mix, fine_blocks, order, mask_ids):
    tok_rows, width = tokens.shape
    slabs = lax.axis_size("seq")
    slab, head = lax.axis_index("seq"), lax.axis_index("head")
    group = w_query.shape[1]
    heads = level_mix.shape[1]
    packed = tok_rows - mask_ids.shape[1]
    near, mids, fars = tok_rows // POOL1, tok_rows // POOL2, tok_rows // POOL3
    coarse = 3 * mids + fars * slabs
    step = 2 * SUMM_ROWS
    chosen = packed + SUMM_ROWS + near

    shape = jax.ShapeDtypeStruct
    params = pltpu.CompilerParams(vmem_limit_bytes=VMEM_LIMIT)

    def prepare(early):
        return pl.pallas_call(
            prepare_kernel,
            out_shape=(
                shape((tok_rows, tok_rows), BF),
                shape((tok_rows, tok_rows), BF),
                shape((chosen, tok_rows), BF),
                shape((SUMM_ROWS + near, 128), F32),
                shape((16, SUMM_ROWS + near), F32),
                shape((tok_rows, FBLK), F32),
                shape((2 * group, width), BF),
                shape((width, group), BF),
            ),
            in_specs=vmem_specs(5) + [pl.BlockSpec(memory_space=pl.ANY)],
            out_specs=vmem_specs(8),
            compiler_params=params,
            cost_estimate=COST,
            name="prepare",
        )(order, mask_ids, w_query, w_value, w_key, early)

    pieces, prepared, before, halo = exchange_tokens(tokens, mask_ids, prepare)
    permute, permute_t, select, f_col, f_row, seen, w_t, w_k = prepared
    places = tuple((row, distances) for _, row, distances in pieces)
    summ, k0, v0, rows_here = pl.pallas_call(
        functools.partial(project_kernel, places),
        out_shape=(
            shape((step, group), BF),
            shape((tok_rows, group), BF),
            shape((group, tok_rows), BF),
            shape((tok_rows, width), BF),
        ),
        in_specs=vmem_specs(len(pieces) + 4),
        out_specs=vmem_specs(4),
        compiler_params=params,
        cost_estimate=COST,
        name="project",
    )(*[piece for piece, _, _ in pieces], w_t, w_k, select, f_col)
    if slabs == 8:
        other = by_distance(summ, 1)
    halo, summ = lax.optimization_barrier((halo, summ))
    halo_x = over_head(halo, X_PAIRS)
    halo_core = over_head(halo, CORE_PAIRS)

    q_t, v_t, keys, near_k, near_vt = pl.pallas_call(
        order_kernel,
        out_shape=(
            shape((group, tok_rows), BF),
            shape((group, tok_rows), BF),
            shape((tok_rows, group), BF),
            shape((near, group), BF),
            shape((group, near), BF),
        ),
        in_specs=vmem_specs(9),
        out_specs=vmem_specs(5),
        compiler_params=params,
        cost_estimate=COST,
        name="order",
    )(permute, permute_t, select, f_col, f_row, w_t, rows_here, k0, v0)
    if slabs == 8:
        pair = stacked((summ, other), step, (near_k,))
        summaries = [pair] + [by_distance(pair, d) for d in (2, 4, 6)]
    else:
        copies = jnp.broadcast_to(summ[None], (slabs, step, group))
        copies = lax.all_to_all(copies, "seq", split_axis=0, concat_axis=0, tiled=True)
        summaries = [copies.reshape(slabs * step, group)]

    blocks = tok_rows // FBLK
    acc, near_out, top, den, expand, expand_t, bias = pl.pallas_call(
        functools.partial(own_kernel, tok_rows // slabs, len(before)),
        out_shape=(
            shape((group, tok_rows), F32),
            shape((group, tok_rows), F32),
            shape((blocks, heads * FBLK), F32),
            shape((blocks, heads * FBLK), F32),
            shape((tok_rows, packed), BF),
            shape((packed, tok_rows), BF),
            shape((2 * tok_rows, FBLK), F32),
        ),
        in_specs=smem_specs(1) + vmem_specs(6 + len(before)),
        out_specs=vmem_specs(7),
        scratch_shapes=[
            pltpu.VMEM((2, group, heads * FBLK), BF),
            pltpu.VMEM((2, FBLK + near, heads * FBLK), BF),
        ],
        compiler_params=params,
        cost_estimate=COST,
        name="own",
    )(level_mix, q_t, keys, v_t, near_k, near_vt, seen, *before)

    halo_x, _ = lax.optimization_barrier((halo_x, top))
    halo_last = over_head(halo_x, CORE_PAIRS)
    window_k, window_v, coarse_k, coarse_v = pl.pallas_call(
        window_kernel,
        out_shape=(
            shape((2 * tok_rows, group), BF),
            shape((group, 2 * tok_rows), BF),
            shape((coarse, group), BF),
            shape((group, coarse), BF),
        ),
        in_specs=vmem_specs(10 + len(summaries)),
        out_specs=vmem_specs(4),
        scratch_shapes=[pltpu.VMEM((slabs * step, group), BF), pltpu.VMEM((packed, width), BF)],
        compiler_params=params,
        cost_estimate=COST,
        name="window",
    )(keys, v_t, w_t, w_k, expand, expand_t, halo, halo_x, halo_core, halo_last, *summaries)

    total = (FINE_K - 1) * FBLK + coarse
    lists = fine_blocks.T
    parts = PARTS if sum(PARTS) == blocks else (blocks,)
    waiting, out, first = None, None, 0

    def finish(out, attended, third, second, base):
        fourth = over_head(third, CORE_PAIRS)
        rows = attended.shape[0]
        previous = [] if out is None else [out]
        tile = pl.BlockSpec((FBLK, group), lambda i: (i, 0))
        return pl.pallas_call(
            output_kernel,
            grid=(rows // FBLK,),
            out_shape=shape((tok_rows, group), BF),
            in_specs=[pl.BlockSpec((width, group), lambda i: (0, 0))]
            + [tile] * 4
            + [pl.BlockSpec(memory_space=pl.ANY)] * len(previous),
            out_specs=pl.BlockSpec((FBLK, group), lambda i, base=base: (i + base, 0)),
            input_output_aliases={5: 0} if previous else {},
            compiler_params=params,
            cost_estimate=COST,
            name="output",
        )(w_out, attended, third, second, fourth, *previous)

    for count in parts:
        attended = pl.pallas_call(
            functools.partial(rest_kernel, first, count),
            out_shape=shape((count * FBLK, group), BF),
            in_specs=smem_specs(2) + vmem_specs(10),
            out_specs=pl.BlockSpec(memory_space=pltpu.VMEM),
            scratch_shapes=[
                pltpu.VMEM((2, total, group), BF),
                pltpu.VMEM((2, group, total), BF),
                pltpu.VMEM((2, group, heads * FBLK), BF),
                pltpu.VMEM((2, total, heads * FBLK), BF),
            ],
            compiler_params=params,
            cost_estimate=COST,
            name="rest",
        )(
            lists, level_mix, q_t, window_k, window_v, coarse_k, coarse_v, bias, acc, near_out, top, den
        )
        third = over_head(attended, X_PAIRS)
        second = over_head(attended, CORE_PAIRS)
        if waiting is not None:
            old, old_third, old_second, old_base = waiting
            old_third, attended = lax.optimization_barrier((old_third, attended))
            out = finish(out, old, old_third, old_second, old_base)
            third, out = lax.optimization_barrier((third, out))
        waiting = (attended, third, second, first)
        first += count
    return finish(out, *waiting)


def solution(mesh):
    placed = (
        P("seq", None),
        P(None, "head"),
        P(None, "head"),
        P(None, "head"),
        P(None, "head"),
        P(None, "head"),
        P("seq", None),
        P("seq", None),
        P("seq", None),
    )
    return jax.shard_map(
        local, mesh=mesh, in_specs=placed, out_specs=P("seq", "head"), check_vma=False
    )
```

```python
import functools

import jax
import jax.numpy as jnp
from jax import lax
from jax.experimental import pallas as pl
from jax.experimental.pallas import tpu as pltpu
from jax.sharding import PartitionSpec as P

FBLK = 128
FINE_K = 4
POOL1 = 8
POOL2 = 64
POOL3 = 512
SUMM_ROWS = 32
CODE_ROWS = 16
BF = jnp.bfloat16
F32 = jnp.float32
I32 = jnp.int32
HIDE = -1e30
VMEM_LIMIT = 24 * 1024 * 1024
COST = pl.CostEstimate(flops=1, bytes_accessed=1, transcendentals=0)
PARTS = (4, 4)

X_PAIRS = [(0, 2), (2, 0), (1, 3), (3, 1)]
CORE_PAIRS = [(0, 1), (1, 0), (2, 3), (3, 2)]


def nn(a, b):
    return lax.dot_general(a, b, (((1,), (0,)), ((), ())), preferred_element_type=F32)


def nt(a, b):
    return lax.dot_general(a, b, (((1,), (1,)), ((), ())), preferred_element_type=F32)


def iota(shape, axis):
    return lax.broadcasted_iota(I32, shape, axis)


def ones_where(condition):
    return jnp.where(condition, 1.0, 0.0).astype(BF)


def vmem_specs(count):
    return [pl.BlockSpec(memory_space=pltpu.VMEM)] * count


def smem_specs(count):
    return [pl.BlockSpec(memory_space=pltpu.SMEM)] * count


def over_head(block, pairs):
    return lax.ppermute(block, "head", pairs)


def to_next(block):
    return lax.ppermute(block, "seq", [(i, i + 1) for i in range(lax.axis_size("seq") - 1)])


def send_kernel(tokens_ref, mask_ref, *refs):
    outs, own = refs[:-1], refs[-1]
    slab, head = lax.axis_index("seq"), lax.axis_index("head")
    core = head & 1
    rows, width = own.shape
    half = width // 2
    ids = mask_ref[...]
    line = iota((CODE_ROWS, ids.shape[1]), 0)
    code = jnp.where(line == 0, ids >> 5, jnp.where(line == 1, ids & 31, 0)).astype(F32).astype(BF)
    sides = (head >> 1, head >> 1, None, core)
    for distance, side, out in zip((7 - core, 5 - core, 3 - core, 1), sides, outs):
        row = pl.multiple_of((slab ^ distance) * rows, rows)
        start = 0 if side is None else pl.multiple_of(side * half, half)
        out[:rows] = tokens_ref[pl.ds(row, rows), pl.ds(start, out.shape[1])]
        out[rows:, : code.shape[1]] = code
    own[...] = tokens_ref[pl.ds(pl.multiple_of(slab * rows, rows), rows)]


def stack_kernel(places, *refs):
    target = refs[-1]
    at = 0
    for source, row, height, column in places:
        target[at : at + height] = refs[source][row : row + height, column : column + target.shape[1]]
        at += height


def stacked(parts, places, width, after=()):
    return pl.pallas_call(
        functools.partial(stack_kernel, places),
        out_shape=jax.ShapeDtypeStruct((sum(place[2] for place in places), width), BF),
        in_specs=vmem_specs(len(parts)) + [pl.BlockSpec(memory_space=pl.ANY)] * len(after),
        out_specs=pl.BlockSpec(memory_space=pltpu.VMEM),
        compiler_params=pltpu.CompilerParams(vmem_limit_bytes=VMEM_LIMIT),
        cost_estimate=COST,
        name="stack",
    )(*parts, *after)


def by_distance(block, distance):
    return lax.ppermute(block, "seq", [(i, i ^ distance) for i in range(lax.axis_size("seq"))])


def by_core(block, distances):
    heads = lax.axis_size("head")
    pairs = [
        (slab * heads + head, (slab ^ distances[head & 1]) * heads + head)
        for slab in range(lax.axis_size("seq"))
        for head in range(heads)
    ]
    return lax.ppermute(block, ("seq", "head"), pairs)


def exchange_tokens(tokens, mask_ids, prepare, expand):
    tok_rows, width = tokens.shape
    slabs = lax.axis_size("seq")
    rows = tok_rows // slabs
    if slabs != 8:
        quarter = width // 4
        split = tokens.reshape(slabs, rows, width)
        mine = lax.dynamic_slice_in_dim(split, lax.axis_index("head") * quarter, quarter, axis=2)
        first = lax.all_to_all(mine, "seq", split_axis=0, concat_axis=0, tiled=True).reshape(
            tok_rows, quarter
        )
        third = over_head(first, X_PAIRS)
        second = over_head(first, CORE_PAIRS)
        fourth = over_head(third, CORE_PAIRS)
        prepared = prepare(first)
        return [first, third, second, fourth], prepared, expand(prepared, [to_next(mask_ids)])
    half = width // 2
    tall = rows + CODE_ROWS
    *blocks, own = pl.pallas_call(
        send_kernel,
        out_shape=(
            jax.ShapeDtypeStruct((tall, half), BF),
            jax.ShapeDtypeStruct((tall, half), BF),
            jax.ShapeDtypeStruct((tall, width), BF),
            jax.ShapeDtypeStruct((tall, half), BF),
            jax.ShapeDtypeStruct((rows, width), BF),
        ),
        in_specs=vmem_specs(2),
        out_specs=vmem_specs(5),
        compiler_params=pltpu.CompilerParams(vmem_limit_bytes=60 * 1024 * 1024),
        cost_estimate=COST,
        name="send",
    )(tokens, mask_ids)
    routes = ((7, 6), (5, 4), (3, 2), (1, 1))
    one, two, three, four = [by_core(block, route) for block, route in zip(blocks, routes)]
    far = stacked((one, two), ((0, 0, rows, 0), (1, 0, rows, 0), (0, rows, CODE_ROWS, 0)), half, (four,))
    near = stacked(
        (three, four),
        (
            (0, 0, rows, 0),
            (0, 0, rows, half),
            (1, 0, rows, 0),
            (0, rows, CODE_ROWS, 0),
            (1, rows, CODE_ROWS, 0),
        ),
        half,
    )
    far_x = over_head(far, X_PAIRS)
    near_core = over_head(near, CORE_PAIRS)
    far_core = over_head(far, CORE_PAIRS)
    prepared = prepare(far)
    expanded = expand(prepared, [far, far_core, near, near_core])
    far_x, _, _ = lax.optimization_barrier((far_x, prepared, expanded))
    far_last = over_head(far_x, CORE_PAIRS)
    return [far, far_x, far_core, far_last, near, near_core, own], prepared, expanded


def column(row, lanes=128):
    return jnp.transpose(jnp.broadcast_to(row.astype(F32), (lanes, row.shape[1]))).astype(I32)


def ranks(ids, tok_rows, lanes=128):
    hidden = column(ids)
    parts = []
    for at in range(0, tok_rows, lanes):
        time = iota((1, lanes), 1) + at
        count = jnp.sum(jnp.where(hidden < time, 1.0, 0.0), axis=0, keepdims=True)
        here = jnp.sum(jnp.where(hidden == time, 1.0, 0.0), axis=0, keepdims=True)
        parts.append(jnp.where(here == 0.0, time - count.astype(I32), -1))
    return jnp.concatenate(parts, axis=1)


def prepare_kernel(
    order_ref, mask_ref, wq_ref, wv_ref, wk_in, early_ref,
    p_ref, pt_ref, sel_ref, fcol_ref, frow_ref, bias_ref, wt_ref, wk_ref,
):
    slab, slabs = lax.axis_index("seq"), lax.axis_size("seq")
    tok_rows = order_ref.shape[1]
    packed = tok_rows - mask_ref.shape[1]
    flip = (slab ^ 7) * (tok_rows // slabs) if slabs == 8 else 0
    mids = tok_rows // POOL2
    group = wq_ref.shape[1]
    lanes = 128

    place = order_ref[...] ^ flip
    place_column = column(place)
    for at in range(0, tok_rows, lanes):
        p_ref[:, at : at + lanes] = ones_where(place_column == iota((tok_rows, lanes), 1) + at)
        pt_ref[at : at + lanes] = ones_where(iota((lanes, tok_rows), 0) + at == place)
    rank = ranks(mask_ref[...], tok_rows)
    time = jnp.where(rank >= 0, iota((1, tok_rows), 1), -1) + 1
    line = iota((16, tok_rows), 0)
    stack = jnp.where(
        line == 0,
        time >> 5,
        jnp.where(
            line == 1,
            time & 31,
            jnp.where(line == 2, (rank + 1) >> 5, jnp.where(line == 3, (rank + 1) & 31, 0)),
        ),
    )
    moved = nn(stack.astype(F32).astype(BF), p_ref[...]).astype(I32)
    time_here = (moved[0:1] << 5) + moved[1:2] - 1
    rank_here = (moved[2:3] << 5) + moved[3:4] - 1
    for at in range(0, packed, lanes):
        sel_ref[at : at + lanes] = ones_where(iota((lanes, tok_rows), 0) + at == rank_here)
    line = iota((SUMM_ROWS, tok_rows), 0)
    sel_ref[packed : packed + SUMM_ROWS] = ones_where(
        ((time_here >> 6) == line) | (((time_here >> 9) + mids == line) & (time_here >= 0))
    )
    lead = packed + SUMM_ROWS
    near = sel_ref.shape[0] - lead
    sel_ref[lead:] = ones_where((time_here >> 3) == iota((near, tok_rows), 0))
    pools = sel_ref[packed:]
    fcol_ref[...] = 1.0 / jnp.sqrt(jnp.maximum(nn(pools, jnp.ones((tok_rows, lanes), BF)), 1.0))
    frow_ref[...] = 1.0 / jnp.sqrt(jnp.maximum(nt(jnp.ones((16, tok_rows), BF), pools), 1.0))
    bias_ref[...] = jnp.where(column(rank) >= 0, 0.0, HIDE)
    wt_ref[:group] = jnp.transpose(wq_ref[...])
    wt_ref[group:] = jnp.transpose(wv_ref[...])
    wk_ref[...] = wk_in[...]


def mask_before(refs, rows):
    if len(refs) == 1:
        return refs[0][...]
    far, far_core, near, near_core = refs
    core = lax.axis_index("head") & 1

    def digits(ref, row):
        return ref[row : row + CODE_ROWS].astype(F32)

    by_one = digits(near, 3 * rows + CODE_ROWS)
    by_three = jnp.where(core == 0, digits(near, 3 * rows), digits(near_core, 3 * rows))
    by_seven = jnp.where(core == 0, digits(far, 2 * rows), digits(far_core, 2 * rows))
    slab = lax.axis_index("seq")
    distance = slab ^ (slab - 1)
    code = jnp.where(distance == 1, by_one, jnp.where(distance == 3, by_three, by_seven)).astype(I32)
    return (code[0:1] << 5) + code[1:2]


def expand_kernel(rows, seen_ref, *refs):
    code_refs, (e_ref, et_ref, bias_ref) = refs[:-3], refs[-3:]
    tok_rows = seen_ref.shape[0]
    rank = ranks(mask_before(code_refs, rows), tok_rows)
    rank = jnp.where(lax.axis_index("seq") > 0, rank, -1)
    rank_column = column(rank)
    bias_ref[:tok_rows] = jnp.where(rank_column >= 0, 0.0, HIDE)
    bias_ref[tok_rows:] = seen_ref[...]
    for at in range(0, et_ref.shape[0], FBLK):
        e_ref[:, at : at + FBLK] = ones_where(rank_column == iota((tok_rows, FBLK), 1) + at)
        et_ref[at : at + FBLK] = ones_where(iota((FBLK, tok_rows), 0) + at == rank)


def assemble(piece_refs, x_ref):
    head = lax.axis_index("head")
    tok_rows, width = x_ref.shape
    if len(piece_refs) == 4:
        quarter = width // 4
        for distance, piece in zip((0, 2, 1, 3), piece_refs):
            start = pl.multiple_of((head ^ distance) * quarter, quarter)
            x_ref[:, pl.ds(start, quarter)] = piece[...]
        return
    far, far_x, far_core, far_last, near, near_core, own = piece_refs
    rows, half = own.shape[0], width // 2
    core, side = head & 1, head >> 1
    for holder, pieces in ((core, (far, far_x)), (1 - core, (far_core, far_last))):
        for part in range(2):
            row = pl.multiple_of((2 * part + holder) * rows, rows)
            for turn, piece in enumerate(pieces):
                start = pl.multiple_of((side ^ turn) * half, half)
                x_ref[pl.ds(row, rows), pl.ds(start, half)] = piece[part * rows : (part + 1) * rows]
    for holder, piece in ((core, near), (1 - core, near_core)):
        row = pl.multiple_of((4 + holder) * rows, rows)
        x_ref[pl.ds(row, rows), :half] = piece[:rows]
        x_ref[pl.ds(row, rows), half:] = piece[rows : 2 * rows]
        start = pl.multiple_of(holder * half, half)
        x_ref[6 * rows : 7 * rows, pl.ds(start, half)] = piece[2 * rows : 3 * rows]
    x_ref[7 * rows :] = own[...]


def project_kernel(count, *refs):
    piece_refs, refs = refs[:count], refs[count:]
    wt_ref, wk_ref, sel_ref, fcol_ref, comp_ref, summ_ref, k_ref, v_ref, x_ref = refs
    assemble(piece_refs, x_ref)
    group = wk_ref.shape[1]
    packed = comp_ref.shape[0] // 2
    lead = packed + SUMM_ROWS
    x = x_ref[...]
    keys = nn(x, wk_ref[...]).astype(BF)
    k_ref[...] = keys
    vt = nt(wt_ref[group:], x).astype(BF)
    v_ref[...] = vt
    sel = sel_ref[:lead]
    kl = nn(sel, keys)
    vl = nt(vt, sel)
    comp_ref[:packed] = kl[:packed].astype(BF)
    vc = vl[:, :packed].astype(BF)
    for part in range(packed // group):
        comp_ref[packed + part * group : packed + (part + 1) * group] = vc[
            :, part * group : (part + 1) * group
        ]
    factor = fcol_ref[:SUMM_ROWS, :1]
    summ_k = (kl[packed:] * factor).astype(BF)
    tail = jnp.concatenate(
        [vl[:, packed:], jnp.zeros((group, 128 - SUMM_ROWS), F32)], axis=1
    )
    summ_v = (jnp.transpose(tail)[:SUMM_ROWS] * factor).astype(BF)
    summ_ref[:SUMM_ROWS] = summ_k
    summ_ref[SUMM_ROWS:] = summ_v


def spread_heads(q4_ref, qt_ref, at, heads):
    width = q4_ref.shape[0] // heads
    for h in range(heads):
        rows = slice(h * width, (h + 1) * width)
        q4_ref[rows, h * FBLK : (h + 1) * FBLK] = qt_ref[rows, at : at + FBLK]


def order_kernel(
    p_ref, pt_ref, sel_ref, fcol_ref, frow_ref, wt_ref, x_ref, k0_ref, v0_ref,
    qt_ref, vt_ref, k_ref, nk_ref, nvt_ref,
):
    group = k_ref.shape[1]
    near = nk_ref.shape[0]
    k0, v0 = k0_ref[...], v0_ref[...]
    q0 = nt(wt_ref[:group], x_ref[...]).astype(BF)
    k_ref[...] = nn(p_ref[...], k0).astype(BF)
    qt_ref[...] = (nn(q0, pt_ref[...]) * 0.125).astype(BF)
    vt_ref[...] = nn(v0, pt_ref[...]).astype(BF)
    pool = sel_ref[sel_ref.shape[0] - near :]
    nk_ref[...] = (nn(pool, k0) * fcol_ref[SUMM_ROWS:, :1]).astype(BF)
    nvt_ref[...] = (nt(v0, pool) * frow_ref[:1, SUMM_ROWS:]).astype(BF)


def own_kernel(
    mix_ref, qt_ref, k_ref, vt_ref, nk_ref, nvt_ref, seen_ref, column_ref,
    acc_ref, near_ref, top_ref, den_ref, q4_ref, p_ref,
):
    tok_rows, group = k_ref.shape
    heads = mix_ref.shape[1]
    width = group // heads
    q4_ref[...] = jnp.zeros_like(q4_ref)
    same = iota((FBLK, FBLK), 0) == iota((FBLK, FBLK), 1)
    nk, nvt = nk_ref[...], nvt_ref[...]
    for g in range(tok_rows // FBLK):
        at = g * FBLK
        slot = g % 2
        spread_heads(q4_ref.at[slot], qt_ref, at, heads)
        q4 = q4_ref[slot]
        bias = jnp.where(same, 0.0, seen_ref[at : at + FBLK])
        own_scores = nn(k_ref[at : at + FBLK], q4)
        near_scores = nn(nk, q4)
        scales = []
        for h in range(heads):
            lanes = slice(h * FBLK, (h + 1) * FBLK)
            part = own_scores[:, lanes] + bias
            top = jnp.max(part, axis=0, keepdims=True)
            weight = jnp.exp(part - top)
            top_ref[g : g + 1, lanes] = top
            den_ref[g : g + 1, lanes] = jnp.sum(weight, axis=0, keepdims=True)
            p_ref[slot, :FBLK, lanes] = weight.astype(BF)
            part = near_scores[:, lanes]
            weight = jnp.exp(part - jnp.max(part, axis=0, keepdims=True))
            scales.append(mix_ref[1, h] / jnp.sum(weight, axis=0, keepdims=True))
            p_ref[slot, FBLK:, lanes] = weight.astype(BF)
        own_out = nn(vt_ref[:, at : at + FBLK], p_ref[slot, :FBLK])
        near_out = nn(nvt, p_ref[slot, FBLK:])
        for h in range(heads):
            rows, lanes = slice(h * width, (h + 1) * width), slice(h * FBLK, (h + 1) * FBLK)
            acc_ref[rows, at : at + FBLK] = own_out[rows, lanes]
            near_ref[rows, at : at + FBLK] = near_out[rows, lanes] * scales[h]


def window_kernel(k_ref, vt_ref, comp_ref, e_ref, et_ref, *refs):
    summ_refs, (kw_ref, vw_ref, ck_ref, cv_ref, all_ref) = refs[:-5], refs[-5:]
    tok_rows, group = k_ref.shape
    packed = e_ref.shape[1]
    kw_ref[:tok_rows] = nn(e_ref[...], comp_ref[:packed]).astype(BF)
    kw_ref[tok_rows:] = k_ref[...]
    prev = None
    for part in range(packed // group):
        term = nn(
            comp_ref[packed + part * group : packed + (part + 1) * group],
            et_ref[part * group : (part + 1) * group],
        )
        prev = term if prev is None else prev + term
    vw_ref[:, :tok_rows] = prev.astype(BF)
    vw_ref[:, tok_rows:] = vt_ref[...]
    at = 0
    for part in summ_refs:
        all_ref[at : at + part.shape[0]] = part[...]
        at += part.shape[0]
    slab, slabs = lax.axis_index("seq"), lax.axis_size("seq")
    mids, fars = tok_rows // POOL2, tok_rows // POOL3
    shape = (ck_ref.shape[0], all_ref.shape[0])
    line = iota(shape, 0)
    step = 2 * SUMM_ROWS
    turn = line // mids
    far = line - 3 * mids
    shard = slab - 1 + turn
    turned = slab if slabs == 8 else 0
    distance = jnp.where(line < 3 * mids, shard, far // fars) ^ turned
    slot = (distance >> 1) + (distance & 1) * (slabs // 2) if slabs == 8 else distance
    source = slot * step + jnp.where(line < 3 * mids, line - turn * mids, mids + far % fars)
    source = jnp.where((line >= 3 * mids) | ((shard >= 0) & (shard < slabs)), source, -step)
    gathered = all_ref[...]
    ck_ref[...] = nn(ones_where(source == iota(shape, 1)), gathered).astype(BF)
    values = nn(ones_where(source + SUMM_ROWS == iota(shape, 1)), gathered)
    cv_ref[...] = jnp.transpose(values).astype(BF)


def rest_kernel(
    first, blocks, lists_ref, mix_ref, qt_ref, kw_ref, vw_ref, ck_ref, cv_ref, bias_ref,
    acc_ref, near_ref, top_ref, den_ref, out_ref, kc_ref, vc_ref, q4_ref, p_ref,
):
    group, tok_rows = qt_ref.shape
    heads = mix_ref.shape[1]
    width = group // heads
    others = FINE_K - 1
    fine = others * FBLK
    mid = 3 * (tok_rows // POOL2)
    far_at = fine + mid
    total = kc_ref.shape[1]
    for slot in range(2):
        kc_ref[slot, fine:] = ck_ref[...]
        vc_ref[slot, :, fine:] = cv_ref[...]
    q4_ref[...] = jnp.zeros_like(q4_ref)
    for index in range(blocks):
        g = first + index
        at = g * FBLK
        slot = index % 2
        biases = []
        for entry in range(others):
            start = pl.multiple_of(lists_ref[entry + 1, g] * FBLK, FBLK)
            kc_ref[slot, entry * FBLK : (entry + 1) * FBLK] = kw_ref[pl.ds(start, FBLK)]
            vc_ref[slot, :, entry * FBLK : (entry + 1) * FBLK] = vw_ref[:, pl.ds(start, FBLK)]
            biases.append(bias_ref[pl.ds(start, FBLK)])
        spread_heads(q4_ref.at[slot], qt_ref, at, heads)
        scores = nn(kc_ref[slot], q4_ref[slot])
        scales, keeps = [], []
        for h in range(heads):
            lanes = slice(h * FBLK, (h + 1) * FBLK)
            parts = [scores[e * FBLK : (e + 1) * FBLK, lanes] + biases[e] for e in range(others)]
            old_top = top_ref[g : g + 1, lanes]
            top = functools.reduce(
                jnp.maximum, [jnp.max(part, axis=0, keepdims=True) for part in parts] + [old_top]
            )
            keep = jnp.exp(old_top - top)
            den = den_ref[g : g + 1, lanes] * keep
            for e, part in enumerate(parts):
                weight = jnp.exp(part - top)
                den = den + jnp.sum(weight, axis=0, keepdims=True)
                p_ref[slot, e * FBLK : (e + 1) * FBLK, lanes] = weight.astype(BF)
            scale = mix_ref[0, h] / den
            scales.append(scale)
            keeps.append(keep * scale)
            for level, (low, high) in enumerate(((fine, far_at), (far_at, total))):
                part = scores[low:high, lanes]
                weight = jnp.exp(part - jnp.max(part, axis=0, keepdims=True))
                share = mix_ref[level + 2, h] / jnp.sum(weight, axis=0, keepdims=True)
                p_ref[slot, low:high, lanes] = (weight * share).astype(BF)
        fine_out = nn(vc_ref[slot, :, :fine], p_ref[slot, :fine])
        coarse_out = nn(vc_ref[slot, :, fine:], p_ref[slot, fine:])
        rows = []
        for h in range(heads):
            pick = (slice(h * width, (h + 1) * width), slice(h * FBLK, (h + 1) * FBLK))
            mine = (pick[0], slice(at, at + FBLK))
            rows.append(
                fine_out[pick] * scales[h]
                + acc_ref[mine] * keeps[h]
                + (coarse_out[pick] + near_ref[mine])
            )
        out_ref[index * FBLK : (index + 1) * FBLK] = jnp.transpose(
            jnp.concatenate(rows, axis=0)
        ).astype(BF)


def output_kernel(w_ref, *refs):
    out_ref = refs[-1]
    group = w_ref.shape[1]
    head = lax.axis_index("head")
    total = None
    for distance, part in zip((0, 2, 1, 3), refs[:4]):
        start = pl.multiple_of((head ^ distance) * group, group)
        term = nn(part[...], w_ref[pl.ds(start, group)])
        total = term if total is None else total + term
    out_ref[...] = total.astype(BF)


def local(tokens, w_query, w_key, w_value, w_out, level_mix, fine_blocks, order, mask_ids):
    tok_rows, width = tokens.shape
    slabs = lax.axis_size("seq")
    slab, head = lax.axis_index("seq"), lax.axis_index("head")
    group = w_query.shape[1]
    heads = level_mix.shape[1]
    packed = tok_rows - mask_ids.shape[1]
    near, mids, fars = tok_rows // POOL1, tok_rows // POOL2, tok_rows // POOL3
    coarse = 3 * mids + fars * slabs
    step = 2 * SUMM_ROWS
    chosen = packed + SUMM_ROWS + near

    shape = jax.ShapeDtypeStruct
    params = pltpu.CompilerParams(vmem_limit_bytes=VMEM_LIMIT)

    def prepare(early):
        return pl.pallas_call(
            prepare_kernel,
            out_shape=(
                shape((tok_rows, tok_rows), BF),
                shape((tok_rows, tok_rows), BF),
                shape((chosen, tok_rows), BF),
                shape((SUMM_ROWS + near, 128), F32),
                shape((16, SUMM_ROWS + near), F32),
                shape((tok_rows, FBLK), F32),
                shape((2 * group, width), BF),
                shape((width, group), BF),
            ),
            in_specs=vmem_specs(5) + [pl.BlockSpec(memory_space=pl.ANY)],
            out_specs=vmem_specs(8),
            compiler_params=params,
            cost_estimate=COST,
            name="prepare",
        )(order, mask_ids, w_query, w_value, w_key, early)

    def expand(prepared, sources):
        return pl.pallas_call(
            functools.partial(expand_kernel, tok_rows // slabs),
            out_shape=(
                shape((tok_rows, packed), BF),
                shape((packed, tok_rows), BF),
                shape((2 * tok_rows, FBLK), F32),
            ),
            in_specs=vmem_specs(1 + len(sources)),
            out_specs=vmem_specs(3),
            compiler_params=params,
            cost_estimate=COST,
            name="expand",
        )(prepared[5], *sources)

    pieces, prepared, expanded = exchange_tokens(tokens, mask_ids, prepare, expand)
    permute, permute_t, select, f_col, f_row, seen, w_t, w_k = prepared
    spread, spread_t, bias = expanded
    comp, summ, k0, v0, rows_here = pl.pallas_call(
        functools.partial(project_kernel, len(pieces)),
        out_shape=(
            shape((2 * packed, group), BF),
            shape((step, group), BF),
            shape((tok_rows, group), BF),
            shape((group, tok_rows), BF),
            shape((tok_rows, width), BF),
        ),
        in_specs=vmem_specs(len(pieces) + 4),
        out_specs=vmem_specs(5),
        compiler_params=params,
        cost_estimate=COST,
        name="project",
    )(*pieces, w_t, w_k, select, f_col)
    if slabs == 8:
        lined = [summ] + [by_distance(summ, d) for d in (2, 4, 6)]
    comp_before = to_next(comp)

    q_t, v_t, keys, near_k, near_vt = pl.pallas_call(
        order_kernel,
        out_shape=(
            shape((group, tok_rows), BF),
            shape((group, tok_rows), BF),
            shape((tok_rows, group), BF),
            shape((near, group), BF),
            shape((group, near), BF),
        ),
        in_specs=vmem_specs(9),
        out_specs=vmem_specs(5),
        compiler_params=params,
        cost_estimate=COST,
        name="order",
    )(permute, permute_t, select, f_col, f_row, w_t, rows_here, k0, v0)
    if slabs == 8:
        places = tuple((index, 0, step, 0) for index in range(4))
        column = stacked(lined, places, group, (near_k,))
        summaries = [column, by_distance(column, 1)]
    else:
        copies = jnp.broadcast_to(summ[None], (slabs, step, group))
        copies = lax.all_to_all(copies, "seq", split_axis=0, concat_axis=0, tiled=True)
        summaries = [copies.reshape(slabs * step, group)]

    blocks = tok_rows // FBLK
    acc, near_out, top, den = pl.pallas_call(
        own_kernel,
        out_shape=(
            shape((group, tok_rows), F32),
            shape((group, tok_rows), F32),
            shape((blocks, heads * FBLK), F32),
            shape((blocks, heads * FBLK), F32),
        ),
        in_specs=smem_specs(1) + vmem_specs(6) + [pl.BlockSpec(memory_space=pl.ANY)],
        out_specs=vmem_specs(4),
        scratch_shapes=[
            pltpu.VMEM((2, group, heads * FBLK), BF),
            pltpu.VMEM((2, FBLK + near, heads * FBLK), BF),
        ],
        compiler_params=params,
        cost_estimate=COST,
        name="own",
    )(level_mix, q_t, keys, v_t, near_k, near_vt, seen, summaries[0])

    window_k, window_v, coarse_k, coarse_v = pl.pallas_call(
        window_kernel,
        out_shape=(
            shape((2 * tok_rows, group), BF),
            shape((group, 2 * tok_rows), BF),
            shape((coarse, group), BF),
            shape((group, coarse), BF),
        ),
        in_specs=vmem_specs(5 + len(summaries)),
        out_specs=vmem_specs(4),
        scratch_shapes=[pltpu.VMEM((slabs * step, group), BF)],
        compiler_params=params,
        cost_estimate=COST,
        name="window",
    )(keys, v_t, comp_before, spread, spread_t, *summaries)

    total = (FINE_K - 1) * FBLK + coarse
    lists = fine_blocks.T
    parts = PARTS if sum(PARTS) == blocks else (blocks,)
    waiting, out, first = None, None, 0

    def finish(out, attended, third, second, base):
        fourth = over_head(third, CORE_PAIRS)
        rows = attended.shape[0]
        previous = [] if out is None else [out]
        tile = pl.BlockSpec((FBLK, group), lambda i: (i, 0))
        return pl.pallas_call(
            output_kernel,
            grid=(rows // FBLK,),
            out_shape=shape((tok_rows, group), BF),
            in_specs=[pl.BlockSpec((width, group), lambda i: (0, 0))]
            + [tile] * 4
            + [pl.BlockSpec(memory_space=pl.ANY)] * len(previous),
            out_specs=pl.BlockSpec((FBLK, group), lambda i, base=base: (i + base, 0)),
            input_output_aliases={5: 0} if previous else {},
            compiler_params=params,
            cost_estimate=COST,
            name="output",
        )(w_out, attended, third, second, fourth, *previous)

    for count in parts:
        attended = pl.pallas_call(
            functools.partial(rest_kernel, first, count),
            out_shape=shape((count * FBLK, group), BF),
            in_specs=smem_specs(2) + vmem_specs(10),
            out_specs=pl.BlockSpec(memory_space=pltpu.VMEM),
            scratch_shapes=[
                pltpu.VMEM((2, total, group), BF),
                pltpu.VMEM((2, group, total), BF),
                pltpu.VMEM((2, group, heads * FBLK), BF),
                pltpu.VMEM((2, total, heads * FBLK), BF),
            ],
            compiler_params=params,
            cost_estimate=COST,
            name="rest",
        )(
            lists, level_mix, q_t, window_k, window_v, coarse_k, coarse_v, bias, acc, near_out, top, den
        )
        third = over_head(attended, X_PAIRS)
        second = over_head(attended, CORE_PAIRS)
        if waiting is not None:
            old, old_third, old_second, old_base = waiting
            old_third, attended = lax.optimization_barrier((old_third, attended))
            out = finish(out, old, old_third, old_second, old_base)
            third, out = lax.optimization_barrier((third, out))
        waiting = (attended, third, second, first)
        first += count
    return finish(out, *waiting)


def solution(mesh):
    placed = (
        P("seq", None),
        P(None, "head"),
        P(None, "head"),
        P(None, "head"),
        P(None, "head"),
        P(None, "head"),
        P("seq", None),
        P("seq", None),
        P("seq", None),
    )
    return jax.shard_map(
        local, mesh=mesh, in_specs=placed, out_specs=P("seq", "head"), check_vma=False
    )
```

```python
import functools

import jax
import jax.numpy as jnp
from jax import lax
from jax.experimental import pallas as pl
from jax.experimental.pallas import tpu as pltpu
from jax.sharding import PartitionSpec as P

FBLK = 128
FINE_K = 4
POOL1 = 8
POOL2 = 64
POOL3 = 512
SUMM_ROWS = 32
CODE_ROWS = 16
BF = jnp.bfloat16
F32 = jnp.float32
I32 = jnp.int32
HIDE = -1e30
VMEM_LIMIT = 24 * 1024 * 1024
COST = pl.CostEstimate(flops=1, bytes_accessed=1, transcendentals=0)
PARTS = (4, 4)

X_PAIRS = [(0, 2), (2, 0), (1, 3), (3, 1)]
CORE_PAIRS = [(0, 1), (1, 0), (2, 3), (3, 2)]


def nn(a, b):
    return lax.dot_general(a, b, (((1,), (0,)), ((), ())), preferred_element_type=F32)


def nt(a, b):
    return lax.dot_general(a, b, (((1,), (1,)), ((), ())), preferred_element_type=F32)


def iota(shape, axis):
    return lax.broadcasted_iota(I32, shape, axis)


def ones_where(condition):
    return jnp.where(condition, 1.0, 0.0).astype(BF)


def vmem_specs(count):
    return [pl.BlockSpec(memory_space=pltpu.VMEM)] * count


def smem_specs(count):
    return [pl.BlockSpec(memory_space=pltpu.SMEM)] * count


def over_head(block, pairs):
    return lax.ppermute(block, "head", pairs)


def to_next(block):
    return lax.ppermute(block, "seq", [(i, i + 1) for i in range(lax.axis_size("seq") - 1)])


def send_kernel(tokens_ref, mask_ref, *refs):
    outs, own = refs[:-1], refs[-1]
    slab, head = lax.axis_index("seq"), lax.axis_index("head")
    core = head & 1
    rows, width = own.shape
    half = width // 2
    ids = mask_ref[...]
    line = iota((CODE_ROWS, ids.shape[1]), 0)
    code = jnp.where(line == 0, ids >> 5, jnp.where(line == 1, ids & 31, 0)).astype(F32).astype(BF)
    sides = (head >> 1, head >> 1, core, core, core)
    for distance, side, out in zip((7 - core, 5 - core, 3, 2, 1), sides, outs):
        row = pl.multiple_of((slab ^ distance) * rows, rows)
        start = pl.multiple_of(side * half, half)
        out[:rows] = tokens_ref[pl.ds(row, rows), pl.ds(start, half)]
        if out.shape[0] > rows:
            out[rows:] = code
    own[...] = tokens_ref[pl.ds(pl.multiple_of(slab * rows, rows), rows)]


def stack_kernel(places, *refs):
    target = refs[-1]
    at = 0
    for source, row, height, column in places:
        target[at : at + height] = refs[source][row : row + height, column : column + target.shape[1]]
        at += height


def stacked(parts, places, width, after=()):
    return pl.pallas_call(
        functools.partial(stack_kernel, places),
        out_shape=jax.ShapeDtypeStruct((sum(place[2] for place in places), width), BF),
        in_specs=vmem_specs(len(parts)) + [pl.BlockSpec(memory_space=pl.ANY)] * len(after),
        out_specs=pl.BlockSpec(memory_space=pltpu.VMEM),
        compiler_params=pltpu.CompilerParams(vmem_limit_bytes=VMEM_LIMIT),
        cost_estimate=COST,
        name="stack",
    )(*parts, *after)


def by_distance(block, distance):
    return lax.ppermute(block, "seq", [(i, i ^ distance) for i in range(lax.axis_size("seq"))])


def by_core(block, distances):
    heads = lax.axis_size("head")
    pairs = [
        (slab * heads + head, (slab ^ distances[head & 1]) * heads + head)
        for slab in range(lax.axis_size("seq"))
        for head in range(heads)
    ]
    return lax.ppermute(block, ("seq", "head"), pairs)


def exchange_tokens(tokens, mask_ids, prepare, expand):
    tok_rows, width = tokens.shape
    slabs = lax.axis_size("seq")
    rows = tok_rows // slabs
    if slabs != 8:
        quarter = width // 4
        split = tokens.reshape(slabs, rows, width)
        mine = lax.dynamic_slice_in_dim(split, lax.axis_index("head") * quarter, quarter, axis=2)
        first = lax.all_to_all(mine, "seq", split_axis=0, concat_axis=0, tiled=True).reshape(
            tok_rows, quarter
        )
        third = over_head(first, X_PAIRS)
        second = over_head(first, CORE_PAIRS)
        fourth = over_head(third, CORE_PAIRS)
        prepared = prepare(first)
        return [first, third, second, fourth], prepared, expand(prepared, [to_next(mask_ids)])
    half = width // 2
    tall = rows + CODE_ROWS
    *blocks, own = pl.pallas_call(
        send_kernel,
        out_shape=(
            jax.ShapeDtypeStruct((tall, half), BF),
            jax.ShapeDtypeStruct((rows, half), BF),
            jax.ShapeDtypeStruct((tall, half), BF),
            jax.ShapeDtypeStruct((rows, half), BF),
            jax.ShapeDtypeStruct((tall, half), BF),
            jax.ShapeDtypeStruct((rows, width), BF),
        ),
        in_specs=vmem_specs(2),
        out_specs=vmem_specs(6),
        compiler_params=pltpu.CompilerParams(vmem_limit_bytes=60 * 1024 * 1024),
        cost_estimate=COST,
        name="send",
    )(tokens, mask_ids)
    routes = ((7, 6), (5, 4), (3, 3), (2, 2), (1, 1))
    one, two, three, four, five = [by_core(block, route) for block, route in zip(blocks, routes)]
    prepared = prepare(own)
    one, _ = lax.optimization_barrier((one, prepared))
    far = [one, two]
    far_core = [over_head(part, CORE_PAIRS) for part in far]
    far_x = [over_head(part, X_PAIRS) for part in far]
    near = stacked(
        (three, four, five),
        (
            (0, 0, rows, 0),
            (1, 0, rows, 0),
            (2, 0, rows, 0),
            (0, rows, CODE_ROWS, 0),
            (2, rows, CODE_ROWS, 0),
        ),
        half,
        (one, two),
    )
    near_core = over_head(near, CORE_PAIRS)
    expanded = expand(prepared, [one, far_core[0], near])
    far_x[1], _ = lax.optimization_barrier((far_x[1], expanded))
    far_last = [over_head(part, CORE_PAIRS) for part in far_x]
    return far + far_x + far_core + far_last + [near, near_core, own], prepared, expanded


def column(row, lanes=128):
    return jnp.transpose(jnp.broadcast_to(row.astype(F32), (lanes, row.shape[1]))).astype(I32)


def ranks(ids, tok_rows, lanes=128):
    hidden = column(ids)
    parts = []
    for at in range(0, tok_rows, lanes):
        time = iota((1, lanes), 1) + at
        count = jnp.sum(jnp.where(hidden < time, 1.0, 0.0), axis=0, keepdims=True)
        here = jnp.sum(jnp.where(hidden == time, 1.0, 0.0), axis=0, keepdims=True)
        parts.append(jnp.where(here == 0.0, time - count.astype(I32), -1))
    return jnp.concatenate(parts, axis=1)


def prepare_kernel(
    order_ref, mask_ref, wq_ref, wv_ref, wk_in, early_ref,
    p_ref, pt_ref, sel_ref, fcol_ref, frow_ref, bias_ref, wt_ref, wk_ref,
):
    slab, slabs = lax.axis_index("seq"), lax.axis_size("seq")
    tok_rows = order_ref.shape[1]
    packed = tok_rows - mask_ref.shape[1]
    flip = (slab ^ 7) * (tok_rows // slabs) if slabs == 8 else 0
    mids = tok_rows // POOL2
    group = wq_ref.shape[1]
    lanes = 128

    place = order_ref[...] ^ flip
    place_column = column(place)
    for at in range(0, tok_rows, lanes):
        p_ref[:, at : at + lanes] = ones_where(place_column == iota((tok_rows, lanes), 1) + at)
        pt_ref[at : at + lanes] = ones_where(iota((lanes, tok_rows), 0) + at == place)
    rank = ranks(mask_ref[...], tok_rows)
    time = jnp.where(rank >= 0, iota((1, tok_rows), 1), -1) + 1
    line = iota((16, tok_rows), 0)
    stack = jnp.where(
        line == 0,
        time >> 5,
        jnp.where(
            line == 1,
            time & 31,
            jnp.where(line == 2, (rank + 1) >> 5, jnp.where(line == 3, (rank + 1) & 31, 0)),
        ),
    )
    moved = nn(stack.astype(F32).astype(BF), p_ref[...]).astype(I32)
    time_here = (moved[0:1] << 5) + moved[1:2] - 1
    rank_here = (moved[2:3] << 5) + moved[3:4] - 1
    for at in range(0, packed, lanes):
        sel_ref[at : at + lanes] = ones_where(iota((lanes, tok_rows), 0) + at == rank_here)
    line = iota((SUMM_ROWS, tok_rows), 0)
    sel_ref[packed : packed + SUMM_ROWS] = ones_where(
        ((time_here >> 6) == line) | (((time_here >> 9) + mids == line) & (time_here >= 0))
    )
    lead = packed + SUMM_ROWS
    near = sel_ref.shape[0] - lead
    sel_ref[lead:] = ones_where((time_here >> 3) == iota((near, tok_rows), 0))
    pools = sel_ref[packed:]
    fcol_ref[...] = 1.0 / jnp.sqrt(jnp.maximum(nn(pools, jnp.ones((tok_rows, lanes), BF)), 1.0))
    frow_ref[...] = 1.0 / jnp.sqrt(jnp.maximum(nt(jnp.ones((16, tok_rows), BF), pools), 1.0))
    bias_ref[...] = jnp.where(column(rank) >= 0, 0.0, HIDE)
    wt_ref[:group] = jnp.transpose(wq_ref[...])
    wt_ref[group:] = jnp.transpose(wv_ref[...])
    wk_ref[...] = wk_in[...]


def mask_before(refs, rows):
    if len(refs) == 1:
        return refs[0][...]
    far, far_core, near = refs
    core = lax.axis_index("head") & 1

    def digits(ref, row):
        return ref[row : row + CODE_ROWS].astype(F32)

    by_one = digits(near, 3 * rows + CODE_ROWS)
    by_three = digits(near, 3 * rows)
    by_seven = jnp.where(core == 0, digits(far, rows), digits(far_core, rows))
    slab = lax.axis_index("seq")
    distance = slab ^ (slab - 1)
    code = jnp.where(distance == 1, by_one, jnp.where(distance == 3, by_three, by_seven)).astype(I32)
    return (code[0:1] << 5) + code[1:2]


def expand_kernel(rows, seen_ref, *refs):
    code_refs, (e_ref, et_ref, bias_ref) = refs[:-3], refs[-3:]
    tok_rows = seen_ref.shape[0]
    rank = ranks(mask_before(code_refs, rows), tok_rows)
    rank = jnp.where(lax.axis_index("seq") > 0, rank, -1)
    rank_column = column(rank)
    bias_ref[:tok_rows] = jnp.where(rank_column >= 0, 0.0, HIDE)
    bias_ref[tok_rows:] = seen_ref[...]
    for at in range(0, et_ref.shape[0], FBLK):
        e_ref[:, at : at + FBLK] = ones_where(rank_column == iota((tok_rows, FBLK), 1) + at)
        et_ref[at : at + FBLK] = ones_where(iota((FBLK, tok_rows), 0) + at == rank)


def assemble(piece_refs, x_ref):
    head = lax.axis_index("head")
    tok_rows, width = x_ref.shape
    if len(piece_refs) == 4:
        quarter = width // 4
        for distance, piece in zip((0, 2, 1, 3), piece_refs):
            start = pl.multiple_of((head ^ distance) * quarter, quarter)
            x_ref[:, pl.ds(start, quarter)] = piece[...]
        return
    far_refs, (near, near_core, own) = piece_refs[:8], piece_refs[8:]
    rows, half = own.shape[0], width // 2
    core, side = head & 1, head >> 1
    for index, piece in enumerate(far_refs):
        turn, crossed = (index // 2) % 2, index // 4
        row = pl.multiple_of((2 * (index % 2) + (core ^ crossed)) * rows, rows)
        start = pl.multiple_of((side ^ turn) * half, half)
        x_ref[pl.ds(row, rows), pl.ds(start, half)] = piece[:rows]
    for crossed, piece in enumerate((near, near_core)):
        start = pl.multiple_of((core ^ crossed) * half, half)
        x_ref[4 * rows : 7 * rows, pl.ds(start, half)] = piece[: 3 * rows]
    x_ref[7 * rows :] = own[...]


def project_kernel(count, *refs):
    piece_refs, refs = refs[:count], refs[count:]
    wt_ref, wk_ref, sel_ref, fcol_ref, comp_ref, summ_ref, k_ref, v_ref, x_ref = refs
    assemble(piece_refs, x_ref)
    group = wk_ref.shape[1]
    packed = comp_ref.shape[0] // 2
    lead = packed + SUMM_ROWS
    x = x_ref[...]
    keys = nn(x, wk_ref[...]).astype(BF)
    k_ref[...] = keys
    vt = nt(wt_ref[group:], x).astype(BF)
    v_ref[...] = vt
    sel = sel_ref[:lead]
    kl = nn(sel, keys)
    vl = nt(vt, sel)
    comp_ref[:packed] = kl[:packed].astype(BF)
    vc = vl[:, :packed].astype(BF)
    for part in range(packed // group):
        comp_ref[packed + part * group : packed + (part + 1) * group] = vc[
            :, part * group : (part + 1) * group
        ]
    factor = fcol_ref[:SUMM_ROWS, :1]
    summ_k = (kl[packed:] * factor).astype(BF)
    tail = jnp.concatenate(
        [vl[:, packed:], jnp.zeros((group, 128 - SUMM_ROWS), F32)], axis=1
    )
    summ_v = (jnp.transpose(tail)[:SUMM_ROWS] * factor).astype(BF)
    summ_ref[:SUMM_ROWS] = summ_k
    summ_ref[SUMM_ROWS:] = summ_v


def spread_heads(q4_ref, qt_ref, at, heads):
    width = q4_ref.shape[0] // heads
    for h in range(heads):
        rows = slice(h * width, (h + 1) * width)
        q4_ref[rows, h * FBLK : (h + 1) * FBLK] = qt_ref[rows, at : at + FBLK]


def order_kernel(
    p_ref, pt_ref, sel_ref, fcol_ref, frow_ref, wt_ref, x_ref, k0_ref, v0_ref,
    qt_ref, vt_ref, k_ref, nk_ref, nvt_ref,
):
    group = k_ref.shape[1]
    near = nk_ref.shape[0]
    k0, v0 = k0_ref[...], v0_ref[...]
    q0 = nt(wt_ref[:group], x_ref[...]).astype(BF)
    k_ref[...] = nn(p_ref[...], k0).astype(BF)
    qt_ref[...] = (nn(q0, pt_ref[...]) * 0.125).astype(BF)
    vt_ref[...] = nn(v0, pt_ref[...]).astype(BF)
    pool = sel_ref[sel_ref.shape[0] - near :]
    nk_ref[...] = (nn(pool, k0) * fcol_ref[SUMM_ROWS:, :1]).astype(BF)
    nvt_ref[...] = (nt(v0, pool) * frow_ref[:1, SUMM_ROWS:]).astype(BF)


def own_kernel(
    mix_ref, qt_ref, k_ref, vt_ref, nk_ref, nvt_ref, seen_ref,
    acc_ref, near_ref, top_ref, den_ref, q4_ref, p_ref,
):
    tok_rows, group = k_ref.shape
    heads = mix_ref.shape[1]
    width = group // heads
    q4_ref[...] = jnp.zeros_like(q4_ref)
    same = iota((FBLK, FBLK), 0) == iota((FBLK, FBLK), 1)
    nk, nvt = nk_ref[...], nvt_ref[...]
    for g in range(tok_rows // FBLK):
        at = g * FBLK
        slot = g % 2
        spread_heads(q4_ref.at[slot], qt_ref, at, heads)
        q4 = q4_ref[slot]
        bias = jnp.where(same, 0.0, seen_ref[at : at + FBLK])
        own_scores = nn(k_ref[at : at + FBLK], q4)
        near_scores = nn(nk, q4)
        scales = []
        for h in range(heads):
            lanes = slice(h * FBLK, (h + 1) * FBLK)
            part = own_scores[:, lanes] + bias
            top = jnp.max(part, axis=0, keepdims=True)
            weight = jnp.exp(part - top)
            top_ref[g : g + 1, lanes] = top
            den_ref[g : g + 1, lanes] = jnp.sum(weight, axis=0, keepdims=True)
            p_ref[slot, :FBLK, lanes] = weight.astype(BF)
            part = near_scores[:, lanes]
            weight = jnp.exp(part - jnp.max(part, axis=0, keepdims=True))
            scales.append(mix_ref[1, h] / jnp.sum(weight, axis=0, keepdims=True))
            p_ref[slot, FBLK:, lanes] = weight.astype(BF)
        own_out = nn(vt_ref[:, at : at + FBLK], p_ref[slot, :FBLK])
        near_out = nn(nvt, p_ref[slot, FBLK:])
        for h in range(heads):
            rows, lanes = slice(h * width, (h + 1) * width), slice(h * FBLK, (h + 1) * FBLK)
            acc_ref[rows, at : at + FBLK] = own_out[rows, lanes]
            near_ref[rows, at : at + FBLK] = near_out[rows, lanes] * scales[h]


def window_kernel(k_ref, vt_ref, comp_ref, e_ref, et_ref, *refs):
    summ_refs, (kw_ref, vw_ref, ck_ref, cv_ref, all_ref) = refs[:-5], refs[-5:]
    tok_rows, group = k_ref.shape
    packed = e_ref.shape[1]
    kw_ref[:tok_rows] = nn(e_ref[...], comp_ref[:packed]).astype(BF)
    kw_ref[tok_rows:] = k_ref[...]
    prev = None
    for part in range(packed // group):
        term = nn(
            comp_ref[packed + part * group : packed + (part + 1) * group],
            et_ref[part * group : (part + 1) * group],
        )
        prev = term if prev is None else prev + term
    vw_ref[:, :tok_rows] = prev.astype(BF)
    vw_ref[:, tok_rows:] = vt_ref[...]
    at = 0
    for part in summ_refs:
        all_ref[at : at + part.shape[0]] = part[...]
        at += part.shape[0]
    slab, slabs = lax.axis_index("seq"), lax.axis_size("seq")
    mids, fars = tok_rows // POOL2, tok_rows // POOL3
    shape = (ck_ref.shape[0], all_ref.shape[0])
    line = iota(shape, 0)
    step = 2 * SUMM_ROWS
    turn = line // mids
    far = line - 3 * mids
    shard = slab - 1 + turn
    turned = slab if slabs == 8 else 0
    distance = jnp.where(line < 3 * mids, shard, far // fars) ^ turned
    slot = (distance >> 1) + (distance & 1) * (slabs // 2) if slabs == 8 else distance
    source = slot * step + jnp.where(line < 3 * mids, line - turn * mids, mids + far % fars)
    source = jnp.where((line >= 3 * mids) | ((shard >= 0) & (shard < slabs)), source, -step)
    gathered = all_ref[...]
    ck_ref[...] = nn(ones_where(source == iota(shape, 1)), gathered).astype(BF)
    values = nn(ones_where(source + SUMM_ROWS == iota(shape, 1)), gathered)
    cv_ref[...] = jnp.transpose(values).astype(BF)


def rest_kernel(
    first, blocks, lists_ref, mix_ref, qt_ref, kw_ref, vw_ref, ck_ref, cv_ref, bias_ref,
    acc_ref, near_ref, top_ref, den_ref, out_ref, kc_ref, vc_ref, q4_ref, p_ref,
):
    group, tok_rows = qt_ref.shape
    heads = mix_ref.shape[1]
    width = group // heads
    others = FINE_K - 1
    fine = others * FBLK
    mid = 3 * (tok_rows // POOL2)
    far_at = fine + mid
    total = kc_ref.shape[1]
    for slot in range(2):
        kc_ref[slot, fine:] = ck_ref[...]
        vc_ref[slot, :, fine:] = cv_ref[...]
    q4_ref[...] = jnp.zeros_like(q4_ref)
    for index in range(blocks):
        g = first + index
        at = g * FBLK
        slot = index % 2
        biases = []
        for entry in range(others):
            start = pl.multiple_of(lists_ref[entry + 1, g] * FBLK, FBLK)
            kc_ref[slot, entry * FBLK : (entry + 1) * FBLK] = kw_ref[pl.ds(start, FBLK)]
            vc_ref[slot, :, entry * FBLK : (entry + 1) * FBLK] = vw_ref[:, pl.ds(start, FBLK)]
            biases.append(bias_ref[pl.ds(start, FBLK)])
        spread_heads(q4_ref.at[slot], qt_ref, at, heads)
        scores = nn(kc_ref[slot], q4_ref[slot])
        scales, keeps = [], []
        for h in range(heads):
            lanes = slice(h * FBLK, (h + 1) * FBLK)
            parts = [scores[e * FBLK : (e + 1) * FBLK, lanes] + biases[e] for e in range(others)]
            old_top = top_ref[g : g + 1, lanes]
            top = functools.reduce(
                jnp.maximum, [jnp.max(part, axis=0, keepdims=True) for part in parts] + [old_top]
            )
            keep = jnp.exp(old_top - top)
            den = den_ref[g : g + 1, lanes] * keep
            for e, part in enumerate(parts):
                weight = jnp.exp(part - top)
                den = den + jnp.sum(weight, axis=0, keepdims=True)
                p_ref[slot, e * FBLK : (e + 1) * FBLK, lanes] = weight.astype(BF)
            scale = mix_ref[0, h] / den
            scales.append(scale)
            keeps.append(keep * scale)
            for level, (low, high) in enumerate(((fine, far_at), (far_at, total))):
                part = scores[low:high, lanes]
                weight = jnp.exp(part - jnp.max(part, axis=0, keepdims=True))
                share = mix_ref[level + 2, h] / jnp.sum(weight, axis=0, keepdims=True)
                p_ref[slot, low:high, lanes] = (weight * share).astype(BF)
        fine_out = nn(vc_ref[slot, :, :fine], p_ref[slot, :fine])
        coarse_out = nn(vc_ref[slot, :, fine:], p_ref[slot, fine:])
        rows = []
        for h in range(heads):
            pick = (slice(h * width, (h + 1) * width), slice(h * FBLK, (h + 1) * FBLK))
            mine = (pick[0], slice(at, at + FBLK))
            rows.append(
                fine_out[pick] * scales[h]
                + acc_ref[mine] * keeps[h]
                + (coarse_out[pick] + near_ref[mine])
            )
        out_ref[index * FBLK : (index + 1) * FBLK] = jnp.transpose(
            jnp.concatenate(rows, axis=0)
        ).astype(BF)


def output_kernel(w_ref, *refs):
    out_ref = refs[-1]
    group = w_ref.shape[1]
    head = lax.axis_index("head")
    total = None
    for distance, part in zip((0, 2, 1, 3), refs[:4]):
        start = pl.multiple_of((head ^ distance) * group, group)
        term = nn(part[...], w_ref[pl.ds(start, group)])
        total = term if total is None else total + term
    out_ref[...] = total.astype(BF)


def local(tokens, w_query, w_key, w_value, w_out, level_mix, fine_blocks, order, mask_ids):
    tok_rows, width = tokens.shape
    slabs = lax.axis_size("seq")
    slab, head = lax.axis_index("seq"), lax.axis_index("head")
    group = w_query.shape[1]
    heads = level_mix.shape[1]
    packed = tok_rows - mask_ids.shape[1]
    near, mids, fars = tok_rows // POOL1, tok_rows // POOL2, tok_rows // POOL3
    coarse = 3 * mids + fars * slabs
    step = 2 * SUMM_ROWS
    chosen = packed + SUMM_ROWS + near

    shape = jax.ShapeDtypeStruct
    params = pltpu.CompilerParams(vmem_limit_bytes=VMEM_LIMIT)

    def prepare(early):
        return pl.pallas_call(
            prepare_kernel,
            out_shape=(
                shape((tok_rows, tok_rows), BF),
                shape((tok_rows, tok_rows), BF),
                shape((chosen, tok_rows), BF),
                shape((SUMM_ROWS + near, 128), F32),
                shape((16, SUMM_ROWS + near), F32),
                shape((tok_rows, FBLK), F32),
                shape((2 * group, width), BF),
                shape((width, group), BF),
            ),
            in_specs=vmem_specs(5) + [pl.BlockSpec(memory_space=pl.ANY)],
            out_specs=vmem_specs(8),
            compiler_params=params,
            cost_estimate=COST,
            name="prepare",
        )(order, mask_ids, w_query, w_value, w_key, early)

    def expand(prepared, sources):
        return pl.pallas_call(
            functools.partial(expand_kernel, tok_rows // slabs),
            out_shape=(
                shape((tok_rows, packed), BF),
                shape((packed, tok_rows), BF),
                shape((2 * tok_rows, FBLK), F32),
            ),
            in_specs=vmem_specs(1 + len(sources)),
            out_specs=vmem_specs(3),
            compiler_params=params,
            cost_estimate=COST,
            name="expand",
        )(prepared[5], *sources)

    pieces, prepared, expanded = exchange_tokens(tokens, mask_ids, prepare, expand)
    permute, permute_t, select, f_col, f_row, seen, w_t, w_k = prepared
    spread, spread_t, bias = expanded
    comp, summ, k0, v0, rows_here = pl.pallas_call(
        functools.partial(project_kernel, len(pieces)),
        out_shape=(
            shape((2 * packed, group), BF),
            shape((step, group), BF),
            shape((tok_rows, group), BF),
            shape((group, tok_rows), BF),
            shape((tok_rows, width), BF),
        ),
        in_specs=vmem_specs(len(pieces) + 4),
        out_specs=vmem_specs(5),
        compiler_params=params,
        cost_estimate=COST,
        name="project",
    )(*pieces, w_t, w_k, select, f_col)
    if slabs == 8:
        lined = [summ] + [by_distance(summ, d) for d in (2, 4, 6)]
    comp_before = to_next(comp)

    q_t, v_t, keys, near_k, near_vt = pl.pallas_call(
        order_kernel,
        out_shape=(
            shape((group, tok_rows), BF),
            shape((group, tok_rows), BF),
            shape((tok_rows, group), BF),
            shape((near, group), BF),
            shape((group, near), BF),
        ),
        in_specs=vmem_specs(9),
        out_specs=vmem_specs(5),
        compiler_params=params,
        cost_estimate=COST,
        name="order",
    )(permute, permute_t, select, f_col, f_row, w_t, rows_here, k0, v0)
    blocks = tok_rows // FBLK
    acc, near_out, top, den = pl.pallas_call(
        own_kernel,
        out_shape=(
            shape((group, tok_rows), F32),
            shape((group, tok_rows), F32),
            shape((blocks, heads * FBLK), F32),
            shape((blocks, heads * FBLK), F32),
        ),
        in_specs=smem_specs(1) + vmem_specs(6),
        out_specs=vmem_specs(4),
        scratch_shapes=[
            pltpu.VMEM((2, group, heads * FBLK), BF),
            pltpu.VMEM((2, FBLK + near, heads * FBLK), BF),
        ],
        compiler_params=params,
        cost_estimate=COST,
        name="own",
    )(level_mix, q_t, keys, v_t, near_k, near_vt, seen)

    if slabs == 8:
        places = tuple((index, 0, step, 0) for index in range(4))
        column = stacked(lined, places, group, (top,))
        summaries = [column, by_distance(column, 1)]
    else:
        copies = jnp.broadcast_to(summ[None], (slabs, step, group))
        copies = lax.all_to_all(copies, "seq", split_axis=0, concat_axis=0, tiled=True)
        summaries = [copies.reshape(slabs * step, group)]

    window_k, window_v, coarse_k, coarse_v = pl.pallas_call(
        window_kernel,
        out_shape=(
            shape((2 * tok_rows, group), BF),
            shape((group, 2 * tok_rows), BF),
            shape((coarse, group), BF),
            shape((group, coarse), BF),
        ),
        in_specs=vmem_specs(5 + len(summaries)),
        out_specs=vmem_specs(4),
        scratch_shapes=[pltpu.VMEM((slabs * step, group), BF)],
        compiler_params=params,
        cost_estimate=COST,
        name="window",
    )(keys, v_t, comp_before, spread, spread_t, *summaries)

    total = (FINE_K - 1) * FBLK + coarse
    lists = fine_blocks.T
    parts = PARTS if sum(PARTS) == blocks else (blocks,)
    waiting, out, first = None, None, 0

    def finish(out, attended, third, second, base):
        fourth = over_head(third, CORE_PAIRS)
        rows = attended.shape[0]
        previous = [] if out is None else [out]
        tile = pl.BlockSpec((FBLK, group), lambda i: (i, 0))
        return pl.pallas_call(
            output_kernel,
            grid=(rows // FBLK,),
            out_shape=shape((tok_rows, group), BF),
            in_specs=[pl.BlockSpec((width, group), lambda i: (0, 0))]
            + [tile] * 4
            + [pl.BlockSpec(memory_space=pl.ANY)] * len(previous),
            out_specs=pl.BlockSpec((FBLK, group), lambda i, base=base: (i + base, 0)),
            input_output_aliases={5: 0} if previous else {},
            compiler_params=params,
            cost_estimate=COST,
            name="output",
        )(w_out, attended, third, second, fourth, *previous)

    for count in parts:
        attended = pl.pallas_call(
            functools.partial(rest_kernel, first, count),
            out_shape=shape((count * FBLK, group), BF),
            in_specs=smem_specs(2) + vmem_specs(10),
            out_specs=pl.BlockSpec(memory_space=pltpu.VMEM),
            scratch_shapes=[
                pltpu.VMEM((2, total, group), BF),
                pltpu.VMEM((2, group, total), BF),
                pltpu.VMEM((2, group, heads * FBLK), BF),
                pltpu.VMEM((2, total, heads * FBLK), BF),
            ],
            compiler_params=params,
            cost_estimate=COST,
            name="rest",
        )(
            lists, level_mix, q_t, window_k, window_v, coarse_k, coarse_v, bias, acc, near_out, top, den
        )
        third = over_head(attended, X_PAIRS)
        second = over_head(attended, CORE_PAIRS)
        if waiting is not None:
            old, old_third, old_second, old_base = waiting
            old_third, attended = lax.optimization_barrier((old_third, attended))
            out = finish(out, old, old_third, old_second, old_base)
            third, out = lax.optimization_barrier((third, out))
        waiting = (attended, third, second, first)
        first += count
    return finish(out, *waiting)


def solution(mesh):
    placed = (
        P("seq", None),
        P(None, "head"),
        P(None, "head"),
        P(None, "head"),
        P(None, "head"),
        P(None, "head"),
        P("seq", None),
        P("seq", None),
        P("seq", None),
    )
    return jax.shard_map(
        local, mesh=mesh, in_specs=placed, out_specs=P("seq", "head"), check_vma=False
    )
```

```python
import functools

import jax
import jax.numpy as jnp
from jax import lax
from jax.experimental import pallas as pl
from jax.experimental.pallas import tpu as pltpu
from jax.sharding import PartitionSpec as P

FBLK = 128
FINE_K = 4
POOL1 = 8
POOL2 = 64
POOL3 = 512
SUMM_ROWS = 32
CODE_ROWS = 16
BF = jnp.bfloat16
F32 = jnp.float32
I32 = jnp.int32
HIDE = -1e30
VMEM_LIMIT = 24 * 1024 * 1024
LONG_BYTES = 20_000_000
COST = pl.CostEstimate(flops=1, bytes_accessed=1, transcendentals=0)
LONG = pl.CostEstimate(flops=1, bytes_accessed=LONG_BYTES, transcendentals=0)
PARTS = (4, 4)

X_PAIRS = [(0, 2), (2, 0), (1, 3), (3, 1)]
CORE_PAIRS = [(0, 1), (1, 0), (2, 3), (3, 2)]


def nn(a, b):
    return lax.dot_general(a, b, (((1,), (0,)), ((), ())), preferred_element_type=F32)


def nt(a, b):
    return lax.dot_general(a, b, (((1,), (1,)), ((), ())), preferred_element_type=F32)


def iota(shape, axis):
    return lax.broadcasted_iota(I32, shape, axis)


def ones_where(condition):
    return jnp.where(condition, 1.0, 0.0).astype(BF)


def vmem_specs(count):
    return [pl.BlockSpec(memory_space=pltpu.VMEM)] * count


def smem_specs(count):
    return [pl.BlockSpec(memory_space=pltpu.SMEM)] * count


def over_head(block, pairs):
    return lax.ppermute(block, "head", pairs)


def to_next(block):
    return lax.ppermute(block, "seq", [(i, i + 1) for i in range(lax.axis_size("seq") - 1)])


def send_kernel(tokens_ref, mask_ref, *refs):
    outs, own = refs[:-1], refs[-1]
    slab, head = lax.axis_index("seq"), lax.axis_index("head")
    core = head & 1
    rows, width = own.shape
    half = width // 2
    ids = mask_ref[...]
    line = iota((CODE_ROWS, ids.shape[1]), 0)
    code = jnp.where(line == 0, ids >> 5, jnp.where(line == 1, ids & 31, 0)).astype(F32).astype(BF)
    sides = (head >> 1, head >> 1, core, core, core)
    for distance, side, out in zip((7 - core, 5 - core, 3, 2, 1), sides, outs):
        row = pl.multiple_of((slab ^ distance) * rows, rows)
        start = pl.multiple_of(side * half, half)
        out[:rows] = tokens_ref[pl.ds(row, rows), pl.ds(start, half)]
        if out.shape[0] > rows:
            out[rows:] = code[: out.shape[0] - rows]
    own[...] = tokens_ref[pl.ds(pl.multiple_of(slab * rows, rows), rows)]


def stack_kernel(places, *refs):
    target = refs[-1]
    at = 0
    for source, row, height, column in places:
        target[at : at + height] = refs[source][row : row + height, column : column + target.shape[1]]
        at += height


def stacked(parts, places, width, after=(), cost=COST):
    return pl.pallas_call(
        functools.partial(stack_kernel, places),
        out_shape=jax.ShapeDtypeStruct((sum(place[2] for place in places), width), BF),
        in_specs=vmem_specs(len(parts)) + [pl.BlockSpec(memory_space=pl.ANY)] * len(after),
        out_specs=pl.BlockSpec(memory_space=pltpu.VMEM),
        compiler_params=pltpu.CompilerParams(vmem_limit_bytes=VMEM_LIMIT),
        cost_estimate=cost,
        name="stack",
    )(*parts, *after)


def by_distance(block, distance):
    return lax.ppermute(block, "seq", [(i, i ^ distance) for i in range(lax.axis_size("seq"))])


def by_core(block, distances):
    heads = lax.axis_size("head")
    pairs = [
        (slab * heads + head, (slab ^ distances[head & 1]) * heads + head)
        for slab in range(lax.axis_size("seq"))
        for head in range(heads)
    ]
    return lax.ppermute(block, ("seq", "head"), pairs)


def exchange_tokens(tokens, mask_ids, prepare, expand):
    tok_rows, width = tokens.shape
    slabs = lax.axis_size("seq")
    rows = tok_rows // slabs
    if slabs != 8:
        quarter = width // 4
        split = tokens.reshape(slabs, rows, width)
        mine = lax.dynamic_slice_in_dim(split, lax.axis_index("head") * quarter, quarter, axis=2)
        first = lax.all_to_all(mine, "seq", split_axis=0, concat_axis=0, tiled=True).reshape(
            tok_rows, quarter
        )
        third = over_head(first, X_PAIRS)
        second = over_head(first, CORE_PAIRS)
        fourth = over_head(third, CORE_PAIRS)
        prepared = prepare(first)
        return [first, third, second, fourth], prepared, expand(prepared, [to_next(mask_ids)])
    half = width // 2
    tall = rows + CODE_ROWS
    *blocks, own = pl.pallas_call(
        send_kernel,
        out_shape=(
            jax.ShapeDtypeStruct((tall, half), BF),
            jax.ShapeDtypeStruct((tall, half), BF),
            jax.ShapeDtypeStruct((tall, half), BF),
            jax.ShapeDtypeStruct((rows, half), BF),
            jax.ShapeDtypeStruct((tall, half), BF),
            jax.ShapeDtypeStruct((rows, width), BF),
        ),
        in_specs=vmem_specs(2),
        out_specs=vmem_specs(6),
        compiler_params=pltpu.CompilerParams(vmem_limit_bytes=60 * 1024 * 1024),
        cost_estimate=COST,
        name="send",
    )(tokens, mask_ids)
    routes = ((7, 6), (5, 4), (3, 3), (2, 2), (1, 1))
    one, two, three, four, five = [by_core(block, route) for block, route in zip(blocks, routes)]
    prepared = prepare(own)
    one, _ = lax.optimization_barrier((one, prepared))
    first_x = over_head(one, X_PAIRS)
    two, first_x = lax.optimization_barrier((two, first_x))
    far = [one, two]
    far_core = [over_head(part, CORE_PAIRS) for part in far]
    far_x = [first_x, over_head(two, X_PAIRS)]
    near = [three, four, five]
    near_core = [over_head(part, CORE_PAIRS) for part in near]
    expanded = expand(prepared, [one, far_core[0], three, five])
    far_x[1], _ = lax.optimization_barrier((far_x[1], expanded))
    far_last = [over_head(part, CORE_PAIRS) for part in far_x]
    return far + far_x + far_core + far_last + near + near_core + [own], prepared, expanded


def column(row, lanes=128):
    return jnp.transpose(jnp.broadcast_to(row.astype(F32), (lanes, row.shape[1]))).astype(I32)


def ranks(ids, tok_rows, lanes=128):
    hidden = column(ids)
    parts = []
    for at in range(0, tok_rows, lanes):
        time = iota((1, lanes), 1) + at
        count = jnp.sum(jnp.where(hidden < time, 1.0, 0.0), axis=0, keepdims=True)
        here = jnp.sum(jnp.where(hidden == time, 1.0, 0.0), axis=0, keepdims=True)
        parts.append(jnp.where(here == 0.0, time - count.astype(I32), -1))
    return jnp.concatenate(parts, axis=1)


def prepare_kernel(
    order_ref, mask_ref, wq_ref, wv_ref, wk_in, early_ref,
    p_ref, pt_ref, sel_ref, fcol_ref, frow_ref, bias_ref, wt_ref, wk_ref,
):
    slab, slabs = lax.axis_index("seq"), lax.axis_size("seq")
    tok_rows = order_ref.shape[1]
    packed = tok_rows - mask_ref.shape[1]
    flip = (slab ^ 7) * (tok_rows // slabs) if slabs == 8 else 0
    mids = tok_rows // POOL2
    group = wq_ref.shape[1]
    lanes = 128

    place = order_ref[...] ^ flip
    place_column = column(place)
    for at in range(0, tok_rows, lanes):
        p_ref[:, at : at + lanes] = ones_where(place_column == iota((tok_rows, lanes), 1) + at)
        pt_ref[at : at + lanes] = ones_where(iota((lanes, tok_rows), 0) + at == place)
    rank = ranks(mask_ref[...], tok_rows)
    time = jnp.where(rank >= 0, iota((1, tok_rows), 1), -1) + 1
    line = iota((16, tok_rows), 0)
    stack = jnp.where(
        line == 0,
        time >> 5,
        jnp.where(
            line == 1,
            time & 31,
            jnp.where(line == 2, (rank + 1) >> 5, jnp.where(line == 3, (rank + 1) & 31, 0)),
        ),
    )
    moved = nn(stack.astype(F32).astype(BF), p_ref[...]).astype(I32)
    time_here = (moved[0:1] << 5) + moved[1:2] - 1
    rank_here = (moved[2:3] << 5) + moved[3:4] - 1
    for at in range(0, packed, lanes):
        sel_ref[at : at + lanes] = ones_where(iota((lanes, tok_rows), 0) + at == rank_here)
    line = iota((SUMM_ROWS, tok_rows), 0)
    sel_ref[packed : packed + SUMM_ROWS] = ones_where(
        ((time_here >> 6) == line) | (((time_here >> 9) + mids == line) & (time_here >= 0))
    )
    lead = packed + SUMM_ROWS
    near = sel_ref.shape[0] - lead
    sel_ref[lead:] = ones_where((time_here >> 3) == iota((near, tok_rows), 0))
    pools = sel_ref[packed:]
    fcol_ref[...] = 1.0 / jnp.sqrt(jnp.maximum(nn(pools, jnp.ones((tok_rows, lanes), BF)), 1.0))
    frow_ref[...] = 1.0 / jnp.sqrt(jnp.maximum(nt(jnp.ones((16, tok_rows), BF), pools), 1.0))
    bias_ref[...] = jnp.where(column(rank) >= 0, 0.0, HIDE)
    wt_ref[:group] = jnp.transpose(wq_ref[...])
    wt_ref[group:] = jnp.transpose(wv_ref[...])
    wk_ref[...] = wk_in[...]


def mask_before(refs, rows):
    if len(refs) == 1:
        return refs[0][...]
    far, far_core, near_three, near_one = refs
    core = lax.axis_index("head") & 1

    def digits(ref):
        return ref[rows : rows + CODE_ROWS // 2].astype(F32)

    three, one = digits(near_three), digits(near_one)
    seven = jnp.where(core == 0, digits(far), digits(far_core))
    slab = lax.axis_index("seq")
    distance = slab ^ (slab - 1)

    code = jnp.where(distance == 1, one, jnp.where(distance == 3, three, seven)).astype(I32)
    return (code[0:1] << 5) + code[1:2]


def expand_kernel(rows, seen_ref, *refs):
    code_refs, (e_ref, et_ref, bias_ref) = refs[:-3], refs[-3:]
    tok_rows = seen_ref.shape[0]
    rank = ranks(mask_before(code_refs, rows), tok_rows)
    rank = jnp.where(lax.axis_index("seq") > 0, rank, -1)
    rank_column = column(rank)
    bias_ref[:tok_rows] = jnp.where(rank_column >= 0, 0.0, HIDE)
    bias_ref[tok_rows:] = seen_ref[...]
    for at in range(0, et_ref.shape[0], FBLK):
        e_ref[:, at : at + FBLK] = ones_where(rank_column == iota((tok_rows, FBLK), 1) + at)
        et_ref[at : at + FBLK] = ones_where(iota((FBLK, tok_rows), 0) + at == rank)


def assemble(piece_refs, x_ref):
    head = lax.axis_index("head")
    tok_rows, width = x_ref.shape
    if len(piece_refs) == 4:
        quarter = width // 4
        for distance, piece in zip((0, 2, 1, 3), piece_refs):
            start = pl.multiple_of((head ^ distance) * quarter, quarter)
            x_ref[:, pl.ds(start, quarter)] = piece[...]
        return
    far_refs, near_refs, own = piece_refs[:8], piece_refs[8:14], piece_refs[14]
    rows, half = own.shape[0], width // 2
    core, side = head & 1, head >> 1
    for index, piece in enumerate(far_refs):
        turn, crossed = (index // 2) % 2, index // 4
        row = pl.multiple_of((2 * (index % 2) + (core ^ crossed)) * rows, rows)
        start = pl.multiple_of((side ^ turn) * half, half)
        x_ref[pl.ds(row, rows), pl.ds(start, half)] = piece[:rows]
    for index, piece in enumerate(near_refs):
        row = (4 + index % 3) * rows
        start = pl.multiple_of((core ^ (index // 3)) * half, half)
        x_ref[row : row + rows, pl.ds(start, half)] = piece[:rows]
    x_ref[7 * rows :] = own[...]


def project_kernel(count, *refs):
    piece_refs, refs = refs[:count], refs[count:]
    wt_ref, wk_ref, sel_ref, fcol_ref, comp_ref, summ_ref, k_ref, v_ref, x_ref = refs
    assemble(piece_refs, x_ref)
    group = wk_ref.shape[1]
    packed = comp_ref.shape[0] // 2
    lead = packed + SUMM_ROWS
    x = x_ref[...]
    keys = nn(x, wk_ref[...]).astype(BF)
    k_ref[...] = keys
    vt = nt(wt_ref[group:], x).astype(BF)
    v_ref[...] = vt
    sel = sel_ref[:lead]
    kl = nn(sel, keys)
    vl = nt(vt, sel)
    comp_ref[:packed] = kl[:packed].astype(BF)
    vc = vl[:, :packed].astype(BF)
    for part in range(packed // group):
        comp_ref[packed + part * group : packed + (part + 1) * group] = vc[
            :, part * group : (part + 1) * group
        ]
    factor = fcol_ref[:SUMM_ROWS, :1]
    summ_k = kl[packed:] * factor
    tail = jnp.concatenate(
        [vl[:, packed:], jnp.zeros((group, 128 - SUMM_ROWS), F32)], axis=1
    )
    summ_v = jnp.transpose(tail)[:SUMM_ROWS] * factor
    mids = x_ref.shape[0] // POOL2
    fars = x_ref.shape[0] // POOL3
    summ_ref[:mids] = summ_k[:mids].astype(BF)
    summ_ref[mids : 2 * mids] = summ_v[:mids].astype(BF)
    summ_ref[2 * mids :] = (summ_k[mids:] + pltpu.roll(summ_v[mids:], fars, 0)).astype(BF)


def spread_heads(q4_ref, qt_ref, at, heads):
    width = q4_ref.shape[0] // heads
    for h in range(heads):
        rows = slice(h * width, (h + 1) * width)
        q4_ref[rows, h * FBLK : (h + 1) * FBLK] = qt_ref[rows, at : at + FBLK]


def order_kernel(
    p_ref, pt_ref, sel_ref, fcol_ref, frow_ref, wt_ref, x_ref, k0_ref, v0_ref,
    qt_ref, vt_ref, k_ref, nk_ref, nvt_ref,
):
    group = k_ref.shape[1]
    near = nk_ref.shape[0]
    k0, v0 = k0_ref[...], v0_ref[...]
    q0 = nt(wt_ref[:group], x_ref[...]).astype(BF)
    k_ref[...] = nn(p_ref[...], k0).astype(BF)
    qt_ref[...] = (nn(q0, pt_ref[...]) * 0.125).astype(BF)
    vt_ref[...] = nn(v0, pt_ref[...]).astype(BF)
    pool = sel_ref[sel_ref.shape[0] - near :]
    nk_ref[...] = (nn(pool, k0) * fcol_ref[SUMM_ROWS:, :1]).astype(BF)
    nvt_ref[...] = (nt(v0, pool) * frow_ref[:1, SUMM_ROWS:]).astype(BF)


def own_kernel(
    mix_ref, qt_ref, k_ref, vt_ref, nk_ref, nvt_ref, seen_ref,
    acc_ref, near_ref, top_ref, den_ref, q4_ref, p_ref,
):
    tok_rows, group = k_ref.shape
    heads = mix_ref.shape[1]
    width = group // heads
    q4_ref[...] = jnp.zeros_like(q4_ref)
    same = iota((FBLK, FBLK), 0) == iota((FBLK, FBLK), 1)
    nk, nvt = nk_ref[...], nvt_ref[...]
    for g in range(tok_rows // FBLK):
        at = g * FBLK
        slot = g % 2
        spread_heads(q4_ref.at[slot], qt_ref, at, heads)
        q4 = q4_ref[slot]
        bias = jnp.where(same, 0.0, seen_ref[at : at + FBLK])
        own_scores = nn(k_ref[at : at + FBLK], q4)
        near_scores = nn(nk, q4)
        scales = []
        for h in range(heads):
            lanes = slice(h * FBLK, (h + 1) * FBLK)
            part = own_scores[:, lanes] + bias
            top = jnp.max(part, axis=0, keepdims=True)
            weight = jnp.exp(part - top)
            top_ref[g : g + 1, lanes] = top
            den_ref[g : g + 1, lanes] = jnp.sum(weight, axis=0, keepdims=True)
            p_ref[slot, :FBLK, lanes] = weight.astype(BF)
            part = near_scores[:, lanes]
            weight = jnp.exp(part - jnp.max(part, axis=0, keepdims=True))
            scales.append(mix_ref[1, h] / jnp.sum(weight, axis=0, keepdims=True))
            p_ref[slot, FBLK:, lanes] = weight.astype(BF)
        own_out = nn(vt_ref[:, at : at + FBLK], p_ref[slot, :FBLK])
        near_out = nn(nvt, p_ref[slot, FBLK:])
        for h in range(heads):
            rows, lanes = slice(h * width, (h + 1) * width), slice(h * FBLK, (h + 1) * FBLK)
            acc_ref[rows, at : at + FBLK] = own_out[rows, lanes]
            near_ref[rows, at : at + FBLK] = near_out[rows, lanes] * scales[h]


def window_kernel(k_ref, vt_ref, comp_ref, e_ref, et_ref, *refs):
    summ_refs, (kw_ref, vw_ref, ck_ref, cv_ref, all_ref) = refs[:-5], refs[-5:]
    tok_rows, group = k_ref.shape
    packed = e_ref.shape[1]
    kw_ref[:tok_rows] = nn(e_ref[...], comp_ref[:packed]).astype(BF)
    kw_ref[tok_rows:] = k_ref[...]
    prev = None
    for part in range(packed // group):
        term = nn(
            comp_ref[packed + part * group : packed + (part + 1) * group],
            et_ref[part * group : (part + 1) * group],
        )
        prev = term if prev is None else prev + term
    vw_ref[:, :tok_rows] = prev.astype(BF)
    vw_ref[:, tok_rows:] = vt_ref[...]
    at = 0
    for part in summ_refs:
        all_ref[at : at + part.shape[0]] = part[...]
        at += part.shape[0]
    slab, slabs = lax.axis_index("seq"), lax.axis_size("seq")
    mids, fars = tok_rows // POOL2, tok_rows // POOL3
    shape = (ck_ref.shape[0], all_ref.shape[0])
    line = iota(shape, 0)
    step = 3 * mids
    turn = line // mids
    far = line - 3 * mids
    shard = slab - 1 + turn
    turned = slab if slabs == 8 else 0
    distance = jnp.where(line < 3 * mids, shard, far // fars) ^ turned
    slot = (distance >> 1) + (distance & 1) * (slabs // 2) if slabs == 8 else distance
    source = slot * step + jnp.where(line < 3 * mids, line - turn * mids, 2 * mids + far % fars)
    source = jnp.where((line >= 3 * mids) | ((shard >= 0) & (shard < slabs)), source, -2 * step)
    gathered = all_ref[...]
    ck_ref[...] = nn(ones_where(source == iota(shape, 1)), gathered).astype(BF)
    values = nn(ones_where(source + jnp.where(line < 3 * mids, mids, fars) == iota(shape, 1)), gathered)
    cv_ref[...] = jnp.transpose(values).astype(BF)


def rest_kernel(
    first, blocks, lists_ref, mix_ref, qt_ref, kw_ref, vw_ref, ck_ref, cv_ref, bias_ref,
    acc_ref, near_ref, top_ref, den_ref, out_ref, kc_ref, vc_ref, q4_ref, p_ref,
):
    group, tok_rows = qt_ref.shape
    heads = mix_ref.shape[1]
    width = group // heads
    others = FINE_K - 1
    fine = others * FBLK
    mid = 3 * (tok_rows // POOL2)
    far_at = fine + mid
    total = kc_ref.shape[1]
    for slot in range(2):
        kc_ref[slot, fine:] = ck_ref[...]
        vc_ref[slot, :, fine:] = cv_ref[...]
    q4_ref[...] = jnp.zeros_like(q4_ref)
    for index in range(blocks):
        g = first + index
        at = g * FBLK
        slot = index % 2
        biases = []
        for entry in range(others):
            start = pl.multiple_of(lists_ref[entry + 1, g] * FBLK, FBLK)
            kc_ref[slot, entry * FBLK : (entry + 1) * FBLK] = kw_ref[pl.ds(start, FBLK)]
            vc_ref[slot, :, entry * FBLK : (entry + 1) * FBLK] = vw_ref[:, pl.ds(start, FBLK)]
            biases.append(bias_ref[pl.ds(start, FBLK)])
        spread_heads(q4_ref.at[slot], qt_ref, at, heads)
        scores = nn(kc_ref[slot], q4_ref[slot])
        scales, keeps = [], []
        for h in range(heads):
            lanes = slice(h * FBLK, (h + 1) * FBLK)
            parts = [scores[e * FBLK : (e + 1) * FBLK, lanes] + biases[e] for e in range(others)]
            old_top = top_ref[g : g + 1, lanes]
            top = functools.reduce(
                jnp.maximum, [jnp.max(part, axis=0, keepdims=True) for part in parts] + [old_top]
            )
            keep = jnp.exp(old_top - top)
            den = den_ref[g : g + 1, lanes] * keep
            for e, part in enumerate(parts):
                weight = jnp.exp(part - top)
                den = den + jnp.sum(weight, axis=0, keepdims=True)
                p_ref[slot, e * FBLK : (e + 1) * FBLK, lanes] = weight.astype(BF)
            scale = mix_ref[0, h] / den
            scales.append(scale)
            keeps.append(keep * scale)
            relative = den / mix_ref[0, h]
            for level, (low, high) in enumerate(((fine, far_at), (far_at, total))):
                part = scores[low:high, lanes]
                weight = jnp.exp(part - jnp.max(part, axis=0, keepdims=True))
                share = mix_ref[level + 2, h] / jnp.sum(weight, axis=0, keepdims=True) * relative
                p_ref[slot, low:high, lanes] = (weight * share).astype(BF)
        total_out = nn(vc_ref[slot], p_ref[slot])
        rows = []
        for h in range(heads):
            pick = (slice(h * width, (h + 1) * width), slice(h * FBLK, (h + 1) * FBLK))
            mine = (pick[0], slice(at, at + FBLK))
            rows.append(total_out[pick] * scales[h] + acc_ref[mine] * keeps[h] + near_ref[mine])
        out_ref[index * FBLK : (index + 1) * FBLK] = jnp.transpose(
            jnp.concatenate(rows, axis=0)
        ).astype(BF)


def output_kernel(w_ref, *refs):
    out_ref = refs[-1]
    group = w_ref.shape[1]
    head = lax.axis_index("head")
    total = None
    for distance, part in zip((0, 2, 1, 3), refs[:4]):
        start = pl.multiple_of((head ^ distance) * group, group)
        term = nn(part[...], w_ref[pl.ds(start, group)])
        total = term if total is None else total + term
    out_ref[...] = total.astype(BF)


def local(tokens, w_query, w_key, w_value, w_out, level_mix, fine_blocks, order, mask_ids):
    tok_rows, width = tokens.shape
    slabs = lax.axis_size("seq")
    slab, head = lax.axis_index("seq"), lax.axis_index("head")
    group = w_query.shape[1]
    heads = level_mix.shape[1]
    packed = tok_rows - mask_ids.shape[1]
    near, mids, fars = tok_rows // POOL1, tok_rows // POOL2, tok_rows // POOL3
    coarse = 3 * mids + fars * slabs
    step = 3 * mids
    chosen = packed + SUMM_ROWS + near

    shape = jax.ShapeDtypeStruct
    params = pltpu.CompilerParams(vmem_limit_bytes=VMEM_LIMIT)

    def prepare(early):
        return pl.pallas_call(
            prepare_kernel,
            out_shape=(
                shape((tok_rows, tok_rows), BF),
                shape((tok_rows, tok_rows), BF),
                shape((chosen, tok_rows), BF),
                shape((SUMM_ROWS + near, 128), F32),
                shape((16, SUMM_ROWS + near), F32),
                shape((tok_rows, FBLK), F32),
                shape((2 * group, width), BF),
                shape((width, group), BF),
            ),
            in_specs=vmem_specs(5) + [pl.BlockSpec(memory_space=pl.ANY)],
            out_specs=vmem_specs(8),
            compiler_params=params,
            cost_estimate=COST,
            name="prepare",
        )(order, mask_ids, w_query, w_value, w_key, early)

    def expand(prepared, sources):
        return pl.pallas_call(
            functools.partial(expand_kernel, tok_rows // slabs),
            out_shape=(
                shape((tok_rows, packed), BF),
                shape((packed, tok_rows), BF),
                shape((2 * tok_rows, FBLK), F32),
            ),
            in_specs=vmem_specs(1 + len(sources)),
            out_specs=vmem_specs(3),
            compiler_params=params,
            cost_estimate=COST,
            name="expand",
        )(prepared[5], *sources)

    pieces, prepared, expanded = exchange_tokens(tokens, mask_ids, prepare, expand)
    permute, permute_t, select, f_col, f_row, seen, w_t, w_k = prepared
    spread, spread_t, bias = expanded
    comp, summ, k0, v0, rows_here = pl.pallas_call(
        functools.partial(project_kernel, len(pieces)),
        out_shape=(
            shape((2 * packed, group), BF),
            shape((step, group), BF),
            shape((tok_rows, group), BF),
            shape((group, tok_rows), BF),
            shape((tok_rows, width), BF),
        ),
        in_specs=vmem_specs(len(pieces) + 4),
        out_specs=vmem_specs(5),
        compiler_params=params,
        cost_estimate=COST,
        name="project",
    )(*pieces, w_t, w_k, select, f_col)
    if slabs == 8:
        lined = [summ] + [by_distance(summ, d) for d in (2, 4, 6)]
    comp_before = to_next(comp)

    q_t, v_t, keys, near_k, near_vt = pl.pallas_call(
        order_kernel,
        out_shape=(
            shape((group, tok_rows), BF),
            shape((group, tok_rows), BF),
            shape((tok_rows, group), BF),
            shape((near, group), BF),
            shape((group, near), BF),
        ),
        in_specs=vmem_specs(9),
        out_specs=vmem_specs(5),
        compiler_params=params,
        cost_estimate=COST,
        name="order",
    )(permute, permute_t, select, f_col, f_row, w_t, rows_here, k0, v0)
    blocks = tok_rows // FBLK
    acc, near_out, top, den = pl.pallas_call(
        own_kernel,
        out_shape=(
            shape((group, tok_rows), F32),
            shape((group, tok_rows), F32),
            shape((blocks, heads * FBLK), F32),
            shape((blocks, heads * FBLK), F32),
        ),
        in_specs=smem_specs(1) + vmem_specs(6),
        out_specs=vmem_specs(4),
        scratch_shapes=[
            pltpu.VMEM((2, group, heads * FBLK), BF),
            pltpu.VMEM((2, FBLK + near, heads * FBLK), BF),
        ],
        compiler_params=params,
        cost_estimate=COST,
        name="own",
    )(level_mix, q_t, keys, v_t, near_k, near_vt, seen)

    if slabs == 8:
        places = tuple((index, 0, step, 0) for index in range(4))
        column = stacked(lined, places, group, (top,))
        summaries = [column, by_distance(column, 1)]
    else:
        copies = jnp.broadcast_to(summ[None], (slabs, step, group))
        copies = lax.all_to_all(copies, "seq", split_axis=0, concat_axis=0, tiled=True)
        summaries = [copies.reshape(slabs * step, group)]

    window_k, window_v, coarse_k, coarse_v = pl.pallas_call(
        window_kernel,
        out_shape=(
            shape((2 * tok_rows, group), BF),
            shape((group, 2 * tok_rows), BF),
            shape((coarse, group), BF),
            shape((group, coarse), BF),
        ),
        in_specs=vmem_specs(5 + len(summaries)),
        out_specs=vmem_specs(4),
        scratch_shapes=[pltpu.VMEM((slabs * step, group), BF)],
        compiler_params=params,
        cost_estimate=COST,
        name="window",
    )(keys, v_t, comp_before, spread, spread_t, *summaries)

    total = (FINE_K - 1) * FBLK + coarse
    lists = fine_blocks.T
    parts = PARTS if sum(PARTS) == blocks else (blocks,)
    waiting, out, first = None, None, 0

    def finish(out, attended, third, second, base, after=()):
        fourth = over_head(third, CORE_PAIRS)
        rows = attended.shape[0]
        previous = [] if out is None else [out]
        height = min(2 * FBLK, rows)
        tile = pl.BlockSpec((height, group), lambda i: (i, 0))
        return pl.pallas_call(
            output_kernel,
            grid=(rows // height,),
            out_shape=shape((tok_rows, group), BF),
            in_specs=[pl.BlockSpec((width, group), lambda i: (0, 0))]
            + [tile] * 4
            + [pl.BlockSpec(memory_space=pl.ANY)] * (len(previous) + len(after)),
            out_specs=pl.BlockSpec((height, group), lambda i, base=base * FBLK // height: (i + base, 0)),
            input_output_aliases={5: 0} if previous else {},
            compiler_params=params,
            cost_estimate=COST,
            name="output",
        )(w_out, attended, third, second, fourth, *previous, *after)

    for count in parts:
        attended = pl.pallas_call(
            functools.partial(rest_kernel, first, count),
            out_shape=shape((count * FBLK, group), BF),
            in_specs=smem_specs(2) + vmem_specs(10),
            out_specs=pl.BlockSpec(memory_space=pltpu.VMEM),
            scratch_shapes=[
                pltpu.VMEM((2, total, group), BF),
                pltpu.VMEM((2, group, total), BF),
                pltpu.VMEM((2, group, heads * FBLK), BF),
                pltpu.VMEM((2, total, heads * FBLK), BF),
            ],
            compiler_params=params,
            cost_estimate=COST,
            name="rest",
        )(
            lists, level_mix, q_t, window_k, window_v, coarse_k, coarse_v, bias, acc, near_out, top, den
        )
        third = over_head(attended, X_PAIRS)
        second = over_head(attended, CORE_PAIRS)
        if waiting is not None:
            old, old_third, old_second, old_base = waiting
            old_third, attended = lax.optimization_barrier((old_third, attended))
            out = finish(out, old, old_third, old_second, old_base, [third])
        waiting = (attended, third, second, first)
        first += count
    return finish(out, *waiting)


def solution(mesh):
    placed = (
        P("seq", None),
        P(None, "head"),
        P(None, "head"),
        P(None, "head"),
        P(None, "head"),
        P(None, "head"),
        P("seq", None),
        P("seq", None),
        P("seq", None),
    )
    return jax.shard_map(
        local, mesh=mesh, in_specs=placed, out_specs=P("seq", "head"), check_vma=False
    )
```

```python
import functools

import jax
import jax.numpy as jnp
from jax import lax
from jax.experimental import pallas as pl
from jax.experimental.pallas import tpu as pltpu
from jax.sharding import PartitionSpec as P

FBLK = 128
FINE_K = 4
POOL1 = 8
POOL2 = 64
POOL3 = 512
SUMM_ROWS = 32
CODE_ROWS = 16
BF = jnp.bfloat16
F32 = jnp.float32
I32 = jnp.int32
HIDE = -1e30
VMEM_LIMIT = 24 * 1024 * 1024
LONG_BYTES = 20_000_000
COST = pl.CostEstimate(flops=1, bytes_accessed=1, transcendentals=0)
LONG = pl.CostEstimate(flops=1, bytes_accessed=LONG_BYTES, transcendentals=0)
PARTS = (4, 4)

X_PAIRS = [(0, 2), (2, 0), (1, 3), (3, 1)]
CORE_PAIRS = [(0, 1), (1, 0), (2, 3), (3, 2)]


def nn(a, b):
    return lax.dot_general(a, b, (((1,), (0,)), ((), ())), preferred_element_type=F32)


def nt(a, b):
    return lax.dot_general(a, b, (((1,), (1,)), ((), ())), preferred_element_type=F32)


def iota(shape, axis):
    return lax.broadcasted_iota(I32, shape, axis)


def ones_where(condition):
    return jnp.where(condition, 1.0, 0.0).astype(BF)


def vmem_specs(count):
    return [pl.BlockSpec(memory_space=pltpu.VMEM)] * count


def smem_specs(count):
    return [pl.BlockSpec(memory_space=pltpu.SMEM)] * count


def over_head(block, pairs):
    return lax.ppermute(block, "head", pairs)


def to_next(block):
    return lax.ppermute(block, "seq", [(i, i + 1) for i in range(lax.axis_size("seq") - 1)])


def send_kernel(tokens_ref, mask_ref, *refs):
    outs, own = refs[:-1], refs[-1]
    slab, head = lax.axis_index("seq"), lax.axis_index("head")
    core = head & 1
    rows, width = own.shape
    half = width // 2
    ids = mask_ref[...]
    line = iota((CODE_ROWS, ids.shape[1]), 0)
    code = jnp.where(line == 0, ids >> 5, jnp.where(line == 1, ids & 31, 0)).astype(F32).astype(BF)
    sides = (head >> 1, head >> 1, core, core, core)
    for distance, side, out in zip((7 - core, 5 - core, 3, 2, 1), sides, outs):
        row = pl.multiple_of((slab ^ distance) * rows, rows)
        start = pl.multiple_of(side * half, half)
        out[:rows] = tokens_ref[pl.ds(row, rows), pl.ds(start, half)]
        if out.shape[0] > rows:
            out[rows:] = code[: out.shape[0] - rows]
    own[...] = tokens_ref[pl.ds(pl.multiple_of(slab * rows, rows), rows)]


def stack_kernel(places, *refs):
    target = refs[-1]
    at = 0
    for source, row, height, column in places:
        target[at : at + height] = refs[source][row : row + height, column : column + target.shape[1]]
        at += height


def stacked(parts, places, width, after=(), cost=COST):
    return pl.pallas_call(
        functools.partial(stack_kernel, places),
        out_shape=jax.ShapeDtypeStruct((sum(place[2] for place in places), width), BF),
        in_specs=vmem_specs(len(parts)) + [pl.BlockSpec(memory_space=pl.ANY)] * len(after),
        out_specs=pl.BlockSpec(memory_space=pltpu.VMEM),
        compiler_params=pltpu.CompilerParams(vmem_limit_bytes=VMEM_LIMIT),
        cost_estimate=cost,
        name="stack",
    )(*parts, *after)


def by_distance(block, distance):
    return lax.ppermute(block, "seq", [(i, i ^ distance) for i in range(lax.axis_size("seq"))])


def by_core(block, distances):
    heads = lax.axis_size("head")
    pairs = [
        (slab * heads + head, (slab ^ distances[head & 1]) * heads + head)
        for slab in range(lax.axis_size("seq"))
        for head in range(heads)
    ]
    return lax.ppermute(block, ("seq", "head"), pairs)


def exchange_tokens(tokens, mask_ids, prepare, expand):
    tok_rows, width = tokens.shape
    slabs = lax.axis_size("seq")
    rows = tok_rows // slabs
    if slabs != 8:
        quarter = width // 4
        split = tokens.reshape(slabs, rows, width)
        mine = lax.dynamic_slice_in_dim(split, lax.axis_index("head") * quarter, quarter, axis=2)
        first = lax.all_to_all(mine, "seq", split_axis=0, concat_axis=0, tiled=True).reshape(
            tok_rows, quarter
        )
        third = over_head(first, X_PAIRS)
        second = over_head(first, CORE_PAIRS)
        fourth = over_head(third, CORE_PAIRS)
        prepared = prepare(first)
        return [first, third, second, fourth], prepared, expand(prepared, [to_next(mask_ids)])
    half = width // 2
    tall = rows + CODE_ROWS
    *blocks, own = pl.pallas_call(
        send_kernel,
        out_shape=(
            jax.ShapeDtypeStruct((tall, half), BF),
            jax.ShapeDtypeStruct((tall, half), BF),
            jax.ShapeDtypeStruct((tall, half), BF),
            jax.ShapeDtypeStruct((tall, half), BF),
            jax.ShapeDtypeStruct((tall, half), BF),
            jax.ShapeDtypeStruct((rows, width), BF),
        ),
        in_specs=vmem_specs(2),
        out_specs=vmem_specs(6),
        compiler_params=pltpu.CompilerParams(vmem_limit_bytes=60 * 1024 * 1024),
        cost_estimate=COST,
        name="send",
    )(tokens, mask_ids)
    routes = ((7, 6), (5, 4), (3, 3), (2, 2), (1, 1))
    one, two, three, four, five = [by_core(block, route) for block, route in zip(blocks, routes)]
    prepared = prepare(own)
    one, _ = lax.optimization_barrier((one, prepared))
    first_x = over_head(stacked((one,), ((0, 0, rows, 0),), half, (three, four, five)), X_PAIRS)
    two, first_x = lax.optimization_barrier((two, first_x))
    two = stacked((two,), ((0, 0, rows, 0),), half)
    far = [one, two]
    far_core = [over_head(part, CORE_PAIRS) for part in far]
    far_x = [first_x, over_head(two, X_PAIRS)]
    near = [three, four, five]
    near_core = [over_head(part, CORE_PAIRS) for part in near]
    expanded = expand(prepared, [one, far_core[0], three, five])
    far_x[1], _ = lax.optimization_barrier((far_x[1], expanded))
    far_last = [over_head(part, CORE_PAIRS) for part in far_x]
    return far + far_x + far_core + far_last + near + near_core + [own], prepared, expanded


def column(row, lanes=128):
    return jnp.transpose(jnp.broadcast_to(row.astype(F32), (lanes, row.shape[1]))).astype(I32)


def ranks(ids, tok_rows, lanes=128):
    hidden = column(ids)
    parts = []
    for at in range(0, tok_rows, lanes):
        time = iota((1, lanes), 1) + at
        count = jnp.sum(jnp.where(hidden < time, 1.0, 0.0), axis=0, keepdims=True)
        here = jnp.sum(jnp.where(hidden == time, 1.0, 0.0), axis=0, keepdims=True)
        parts.append(jnp.where(here == 0.0, time - count.astype(I32), -1))
    return jnp.concatenate(parts, axis=1)


def prepare_kernel(
    order_ref, mask_ref, wq_ref, wv_ref, wk_in, early_ref,
    p_ref, pt_ref, sel_ref, fcol_ref, frow_ref, bias_ref, wt_ref, wk_ref,
):
    slab, slabs = lax.axis_index("seq"), lax.axis_size("seq")
    tok_rows = order_ref.shape[1]
    packed = tok_rows - mask_ref.shape[1]
    flip = (slab ^ 7) * (tok_rows // slabs) if slabs == 8 else 0
    mids = tok_rows // POOL2
    group = wq_ref.shape[1]
    lanes = 128

    place = order_ref[...] ^ flip
    place_column = column(place)
    for at in range(0, tok_rows, lanes):
        p_ref[:, at : at + lanes] = ones_where(place_column == iota((tok_rows, lanes), 1) + at)
        pt_ref[at : at + lanes] = ones_where(iota((lanes, tok_rows), 0) + at == place)
    rank = ranks(mask_ref[...], tok_rows)
    time = jnp.where(rank >= 0, iota((1, tok_rows), 1), -1) + 1
    line = iota((16, tok_rows), 0)
    stack = jnp.where(
        line == 0,
        time >> 5,
        jnp.where(
            line == 1,
            time & 31,
            jnp.where(line == 2, (rank + 1) >> 5, jnp.where(line == 3, (rank + 1) & 31, 0)),
        ),
    )
    moved = nn(stack.astype(F32).astype(BF), p_ref[...]).astype(I32)
    time_here = (moved[0:1] << 5) + moved[1:2] - 1
    rank_here = (moved[2:3] << 5) + moved[3:4] - 1
    for at in range(0, packed, lanes):
        sel_ref[at : at + lanes] = ones_where(iota((lanes, tok_rows), 0) + at == rank_here)
    line = iota((SUMM_ROWS, tok_rows), 0)
    sel_ref[packed : packed + SUMM_ROWS] = ones_where(
        ((time_here >> 6) == line) | (((time_here >> 9) + mids == line) & (time_here >= 0))
    )
    lead = packed + SUMM_ROWS
    near = sel_ref.shape[0] - lead
    sel_ref[lead:] = ones_where((time_here >> 3) == iota((near, tok_rows), 0))
    pools = sel_ref[packed:]
    fcol_ref[...] = 1.0 / jnp.sqrt(jnp.maximum(nn(pools, jnp.ones((tok_rows, lanes), BF)), 1.0))
    frow_ref[...] = 1.0 / jnp.sqrt(jnp.maximum(nt(jnp.ones((16, tok_rows), BF), pools), 1.0))
    bias_ref[...] = jnp.where(column(rank) >= 0, 0.0, HIDE)
    wt_ref[:group] = jnp.transpose(wq_ref[...])
    wt_ref[group:] = jnp.transpose(wv_ref[...])
    wk_ref[...] = wk_in[...]


def mask_before(refs, rows):
    if len(refs) == 1:
        return refs[0][...]
    far, far_core, near_three, near_one = refs
    core = lax.axis_index("head") & 1

    def digits(ref):
        return ref[rows : rows + CODE_ROWS // 2].astype(F32)

    three, one = digits(near_three), digits(near_one)
    seven = jnp.where(core == 0, digits(far), digits(far_core))
    slab = lax.axis_index("seq")
    distance = slab ^ (slab - 1)

    code = jnp.where(distance == 1, one, jnp.where(distance == 3, three, seven)).astype(I32)
    return (code[0:1] << 5) + code[1:2]


def expand_kernel(rows, seen_ref, *refs):
    code_refs, (e_ref, et_ref, bias_ref) = refs[:-3], refs[-3:]
    tok_rows = seen_ref.shape[0]
    rank = ranks(mask_before(code_refs, rows), tok_rows)
    rank = jnp.where(lax.axis_index("seq") > 0, rank, -1)
    rank_column = column(rank)
    bias_ref[:tok_rows] = jnp.where(rank_column >= 0, 0.0, HIDE)
    bias_ref[tok_rows:] = seen_ref[...]
    for at in range(0, et_ref.shape[0], FBLK):
        e_ref[:, at : at + FBLK] = ones_where(rank_column == iota((tok_rows, FBLK), 1) + at)
        et_ref[at : at + FBLK] = ones_where(iota((FBLK, tok_rows), 0) + at == rank)


def assemble(piece_refs, x_ref):
    head = lax.axis_index("head")
    tok_rows, width = x_ref.shape
    if len(piece_refs) == 4:
        quarter = width // 4
        for distance, piece in zip((0, 2, 1, 3), piece_refs):
            start = pl.multiple_of((head ^ distance) * quarter, quarter)
            x_ref[:, pl.ds(start, quarter)] = piece[...]
        return
    far_refs, near_refs, own = piece_refs[:8], piece_refs[8:14], piece_refs[14]
    rows, half = own.shape[0], width // 2
    core, side = head & 1, head >> 1
    for index, piece in enumerate(far_refs):
        turn, crossed = (index // 2) % 2, index // 4
        row = pl.multiple_of((2 * (index % 2) + (core ^ crossed)) * rows, rows)
        start = pl.multiple_of((side ^ turn) * half, half)
        x_ref[pl.ds(row, rows), pl.ds(start, half)] = piece[:rows]
    for index, piece in enumerate(near_refs):
        row = (4 + index % 3) * rows
        start = pl.multiple_of((core ^ (index // 3)) * half, half)
        x_ref[row : row + rows, pl.ds(start, half)] = piece[:rows]
    x_ref[7 * rows :] = own[...]


def project_kernel(count, *refs):
    piece_refs, refs = refs[:count], refs[count:]
    wt_ref, wk_ref, sel_ref, fcol_ref, comp_ref, summ_ref, k_ref, v_ref, x_ref = refs
    assemble(piece_refs, x_ref)
    group = wk_ref.shape[1]
    packed = comp_ref.shape[0] // 2
    lead = packed + SUMM_ROWS
    x = x_ref[...]
    keys = nn(x, wk_ref[...]).astype(BF)
    k_ref[...] = keys
    vt = nt(wt_ref[group:], x).astype(BF)
    v_ref[...] = vt
    sel = sel_ref[:lead]
    kl = nn(sel, keys)
    vl = nt(vt, sel)
    comp_ref[:packed] = kl[:packed].astype(BF)
    vc = vl[:, :packed].astype(BF)
    for part in range(packed // group):
        comp_ref[packed + part * group : packed + (part + 1) * group] = vc[
            :, part * group : (part + 1) * group
        ]
    factor = fcol_ref[:SUMM_ROWS, :1]
    summ_k = kl[packed:] * factor
    tail = jnp.concatenate(
        [vl[:, packed:], jnp.zeros((group, 128 - SUMM_ROWS), F32)], axis=1
    )
    summ_v = jnp.transpose(tail)[:SUMM_ROWS] * factor
    mids = x_ref.shape[0] // POOL2
    fars = x_ref.shape[0] // POOL3
    summ_ref[:mids] = summ_k[:mids].astype(BF)
    summ_ref[mids : 2 * mids] = summ_v[:mids].astype(BF)
    summ_ref[2 * mids :] = (summ_k[mids:] + pltpu.roll(summ_v[mids:], fars, 0)).astype(BF)


def spread_heads(q4_ref, qt_ref, at, heads):
    width = q4_ref.shape[0] // heads
    for h in range(heads):
        rows = slice(h * width, (h + 1) * width)
        q4_ref[rows, h * FBLK : (h + 1) * FBLK] = qt_ref[rows, at : at + FBLK]


def order_kernel(
    p_ref, pt_ref, sel_ref, fcol_ref, frow_ref, wt_ref, x_ref, k0_ref, v0_ref,
    qt_ref, vt_ref, k_ref, nk_ref, nvt_ref,
):
    group = k_ref.shape[1]
    near = nk_ref.shape[0]
    k0, v0 = k0_ref[...], v0_ref[...]
    q0 = nt(wt_ref[:group], x_ref[...]).astype(BF)
    k_ref[...] = nn(p_ref[...], k0).astype(BF)
    qt_ref[...] = (nn(q0, pt_ref[...]) * 0.125).astype(BF)
    vt_ref[...] = nn(v0, pt_ref[...]).astype(BF)
    pool = sel_ref[sel_ref.shape[0] - near :]
    nk_ref[...] = (nn(pool, k0) * fcol_ref[SUMM_ROWS:, :1]).astype(BF)
    nvt_ref[...] = (nt(v0, pool) * frow_ref[:1, SUMM_ROWS:]).astype(BF)


def own_kernel(
    mix_ref, qt_ref, k_ref, vt_ref, nk_ref, nvt_ref, seen_ref,
    acc_ref, near_ref, top_ref, den_ref, q4_ref, p_ref,
):
    tok_rows, group = k_ref.shape
    heads = mix_ref.shape[1]
    width = group // heads
    q4_ref[...] = jnp.zeros_like(q4_ref)
    same = iota((FBLK, FBLK), 0) == iota((FBLK, FBLK), 1)
    nk, nvt = nk_ref[...], nvt_ref[...]
    for g in range(tok_rows // FBLK):
        at = g * FBLK
        slot = g % 2
        spread_heads(q4_ref.at[slot], qt_ref, at, heads)
        q4 = q4_ref[slot]
        bias = jnp.where(same, 0.0, seen_ref[at : at + FBLK])
        own_scores = nn(k_ref[at : at + FBLK], q4)
        near_scores = nn(nk, q4)
        scales = []
        for h in range(heads):
            lanes = slice(h * FBLK, (h + 1) * FBLK)
            part = own_scores[:, lanes] + bias
            top = jnp.max(part, axis=0, keepdims=True)
            weight = jnp.exp(part - top)
            top_ref[g : g + 1, lanes] = top
            den_ref[g : g + 1, lanes] = jnp.sum(weight, axis=0, keepdims=True)
            p_ref[slot, :FBLK, lanes] = weight.astype(BF)
            part = near_scores[:, lanes]
            weight = jnp.exp(part - jnp.max(part, axis=0, keepdims=True))
            scales.append(mix_ref[1, h] / jnp.sum(weight, axis=0, keepdims=True))
            p_ref[slot, FBLK:, lanes] = weight.astype(BF)
        own_out = nn(vt_ref[:, at : at + FBLK], p_ref[slot, :FBLK])
        near_out = nn(nvt, p_ref[slot, FBLK:])
        for h in range(heads):
            rows, lanes = slice(h * width, (h + 1) * width), slice(h * FBLK, (h + 1) * FBLK)
            acc_ref[rows, at : at + FBLK] = own_out[rows, lanes]
            near_ref[rows, at : at + FBLK] = near_out[rows, lanes] * scales[h]


def window_kernel(k_ref, vt_ref, comp_ref, e_ref, et_ref, *refs):
    summ_refs, (kw_ref, vw_ref, ck_ref, cv_ref, all_ref) = refs[:-5], refs[-5:]
    tok_rows, group = k_ref.shape
    packed = e_ref.shape[1]
    kw_ref[:tok_rows] = nn(e_ref[...], comp_ref[:packed]).astype(BF)
    kw_ref[tok_rows:] = k_ref[...]
    prev = None
    for part in range(packed // group):
        term = nn(
            comp_ref[packed + part * group : packed + (part + 1) * group],
            et_ref[part * group : (part + 1) * group],
        )
        prev = term if prev is None else prev + term
    vw_ref[:, :tok_rows] = prev.astype(BF)
    vw_ref[:, tok_rows:] = vt_ref[...]
    at = 0
    for part in summ_refs:
        all_ref[at : at + part.shape[0]] = part[...]
        at += part.shape[0]
    slab, slabs = lax.axis_index("seq"), lax.axis_size("seq")
    mids, fars = tok_rows // POOL2, tok_rows // POOL3
    shape = (ck_ref.shape[0], all_ref.shape[0])
    line = iota(shape, 0)
    step = 3 * mids
    turn = line // mids
    far = line - 3 * mids
    shard = slab - 1 + turn
    turned = slab if slabs == 8 else 0
    distance = jnp.where(line < 3 * mids, shard, far // fars) ^ turned
    slot = (distance >> 1) + (distance & 1) * (slabs // 2) if slabs == 8 else distance
    source = slot * step + jnp.where(line < 3 * mids, line - turn * mids, 2 * mids + far % fars)
    source = jnp.where((line >= 3 * mids) | ((shard >= 0) & (shard < slabs)), source, -2 * step)
    gathered = all_ref[...]
    ck_ref[...] = nn(ones_where(source == iota(shape, 1)), gathered).astype(BF)
    values = nn(ones_where(source + jnp.where(line < 3 * mids, mids, fars) == iota(shape, 1)), gathered)
    cv_ref[...] = jnp.transpose(values).astype(BF)


def rest_kernel(
    first, blocks, lists_ref, mix_ref, qt_ref, kw_ref, vw_ref, ck_ref, cv_ref, bias_ref,
    acc_ref, near_ref, top_ref, den_ref, out_ref, kc_ref, vc_ref, q4_ref, p_ref,
):
    group, tok_rows = qt_ref.shape
    heads = mix_ref.shape[1]
    width = group // heads
    others = FINE_K - 1
    fine = others * FBLK
    mid = 3 * (tok_rows // POOL2)
    far_at = fine + mid
    total = kc_ref.shape[1]
    for slot in range(2):
        kc_ref[slot, fine:] = ck_ref[...]
        vc_ref[slot, :, fine:] = cv_ref[...]
    q4_ref[...] = jnp.zeros_like(q4_ref)
    for index in range(blocks):
        g = first + index
        at = g * FBLK
        slot = index % 2
        biases = []
        for entry in range(others):
            start = pl.multiple_of(lists_ref[entry + 1, g] * FBLK, FBLK)
            kc_ref[slot, entry * FBLK : (entry + 1) * FBLK] = kw_ref[pl.ds(start, FBLK)]
            vc_ref[slot, :, entry * FBLK : (entry + 1) * FBLK] = vw_ref[:, pl.ds(start, FBLK)]
            biases.append(bias_ref[pl.ds(start, FBLK)])
        spread_heads(q4_ref.at[slot], qt_ref, at, heads)
        scores = nn(kc_ref[slot], q4_ref[slot])
        scales, keeps = [], []
        for h in range(heads):
            lanes = slice(h * FBLK, (h + 1) * FBLK)
            parts = [scores[e * FBLK : (e + 1) * FBLK, lanes] + biases[e] for e in range(others)]
            old_top = top_ref[g : g + 1, lanes]
            top = functools.reduce(
                jnp.maximum, [jnp.max(part, axis=0, keepdims=True) for part in parts] + [old_top]
            )
            keep = jnp.exp(old_top - top)
            den = den_ref[g : g + 1, lanes] * keep
            for e, part in enumerate(parts):
                weight = jnp.exp(part - top)
                den = den + jnp.sum(weight, axis=0, keepdims=True)
                p_ref[slot, e * FBLK : (e + 1) * FBLK, lanes] = weight.astype(BF)
            scale = mix_ref[0, h] / den
            scales.append(scale)
            keeps.append(keep * scale)
            relative = den / mix_ref[0, h]
            for level, (low, high) in enumerate(((fine, far_at), (far_at, total))):
                part = scores[low:high, lanes]
                weight = jnp.exp(part - jnp.max(part, axis=0, keepdims=True))
                share = mix_ref[level + 2, h] / jnp.sum(weight, axis=0, keepdims=True) * relative
                p_ref[slot, low:high, lanes] = (weight * share).astype(BF)
        total_out = nn(vc_ref[slot], p_ref[slot])
        rows = []
        for h in range(heads):
            pick = (slice(h * width, (h + 1) * width), slice(h * FBLK, (h + 1) * FBLK))
            mine = (pick[0], slice(at, at + FBLK))
            rows.append(total_out[pick] * scales[h] + acc_ref[mine] * keeps[h] + near_ref[mine])
        out_ref[index * FBLK : (index + 1) * FBLK] = jnp.transpose(
            jnp.concatenate(rows, axis=0)
        ).astype(BF)


def output_kernel(w_ref, *refs):
    out_ref = refs[-1]
    group = w_ref.shape[1]
    head = lax.axis_index("head")
    total = None
    for distance, part in zip((0, 2, 1, 3), refs[:4]):
        start = pl.multiple_of((head ^ distance) * group, group)
        term = nn(part[...], w_ref[pl.ds(start, group)])
        total = term if total is None else total + term
    out_ref[...] = total.astype(BF)


def local(tokens, w_query, w_key, w_value, w_out, level_mix, fine_blocks, order, mask_ids):
    tok_rows, width = tokens.shape
    slabs = lax.axis_size("seq")
    slab, head = lax.axis_index("seq"), lax.axis_index("head")
    group = w_query.shape[1]
    heads = level_mix.shape[1]
    packed = tok_rows - mask_ids.shape[1]
    near, mids, fars = tok_rows // POOL1, tok_rows // POOL2, tok_rows // POOL3
    coarse = 3 * mids + fars * slabs
    step = 3 * mids
    chosen = packed + SUMM_ROWS + near

    shape = jax.ShapeDtypeStruct
    params = pltpu.CompilerParams(vmem_limit_bytes=VMEM_LIMIT)

    def prepare(early):
        return pl.pallas_call(
            prepare_kernel,
            out_shape=(
                shape((tok_rows, tok_rows), BF),
                shape((tok_rows, tok_rows), BF),
                shape((chosen, tok_rows), BF),
                shape((SUMM_ROWS + near, 128), F32),
                shape((16, SUMM_ROWS + near), F32),
                shape((tok_rows, FBLK), F32),
                shape((2 * group, width), BF),
                shape((width, group), BF),
            ),
            in_specs=vmem_specs(5) + [pl.BlockSpec(memory_space=pl.ANY)],
            out_specs=vmem_specs(8),
            compiler_params=params,
            cost_estimate=COST,
            name="prepare",
        )(order, mask_ids, w_query, w_value, w_key, early)

    def expand(prepared, sources):
        return pl.pallas_call(
            functools.partial(expand_kernel, tok_rows // slabs),
            out_shape=(
                shape((tok_rows, packed), BF),
                shape((packed, tok_rows), BF),
                shape((2 * tok_rows, FBLK), F32),
            ),
            in_specs=vmem_specs(1 + len(sources)),
            out_specs=vmem_specs(3),
            compiler_params=params,
            cost_estimate=COST,
            name="expand",
        )(prepared[5], *sources)

    pieces, prepared, expanded = exchange_tokens(tokens, mask_ids, prepare, expand)
    permute, permute_t, select, f_col, f_row, seen, w_t, w_k = prepared
    spread, spread_t, bias = expanded
    comp, summ, k0, v0, rows_here = pl.pallas_call(
        functools.partial(project_kernel, len(pieces)),
        out_shape=(
            shape((2 * packed, group), BF),
            shape((step, group), BF),
            shape((tok_rows, group), BF),
            shape((group, tok_rows), BF),
            shape((tok_rows, width), BF),
        ),
        in_specs=vmem_specs(len(pieces) + 4),
        out_specs=vmem_specs(5),
        compiler_params=params,
        cost_estimate=COST,
        name="project",
    )(*pieces, w_t, w_k, select, f_col)
    if slabs == 8:
        lined = [summ] + [by_distance(summ, d) for d in (2, 4, 6)]
    comp_before = to_next(comp)

    q_t, v_t, keys, near_k, near_vt = pl.pallas_call(
        order_kernel,
        out_shape=(
            shape((group, tok_rows), BF),
            shape((group, tok_rows), BF),
            shape((tok_rows, group), BF),
            shape((near, group), BF),
            shape((group, near), BF),
        ),
        in_specs=vmem_specs(9),
        out_specs=vmem_specs(5),
        compiler_params=params,
        cost_estimate=COST,
        name="order",
    )(permute, permute_t, select, f_col, f_row, w_t, rows_here, k0, v0)
    blocks = tok_rows // FBLK
    acc, near_out, top, den = pl.pallas_call(
        own_kernel,
        out_shape=(
            shape((group, tok_rows), F32),
            shape((group, tok_rows), F32),
            shape((blocks, heads * FBLK), F32),
            shape((blocks, heads * FBLK), F32),
        ),
        in_specs=smem_specs(1) + vmem_specs(6),
        out_specs=vmem_specs(4),
        scratch_shapes=[
            pltpu.VMEM((2, group, heads * FBLK), BF),
            pltpu.VMEM((2, FBLK + near, heads * FBLK), BF),
        ],
        compiler_params=params,
        cost_estimate=COST,
        name="own",
    )(level_mix, q_t, keys, v_t, near_k, near_vt, seen)

    if slabs == 8:
        places = tuple((index, 0, step, 0) for index in range(4))
        column = stacked(lined, places, group, (top,))
        summaries = [column, by_distance(column, 1)]
    else:
        copies = jnp.broadcast_to(summ[None], (slabs, step, group))
        copies = lax.all_to_all(copies, "seq", split_axis=0, concat_axis=0, tiled=True)
        summaries = [copies.reshape(slabs * step, group)]

    window_k, window_v, coarse_k, coarse_v = pl.pallas_call(
        window_kernel,
        out_shape=(
            shape((2 * tok_rows, group), BF),
            shape((group, 2 * tok_rows), BF),
            shape((coarse, group), BF),
            shape((group, coarse), BF),
        ),
        in_specs=vmem_specs(5 + len(summaries)),
        out_specs=vmem_specs(4),
        scratch_shapes=[pltpu.VMEM((slabs * step, group), BF)],
        compiler_params=params,
        cost_estimate=COST,
        name="window",
    )(keys, v_t, comp_before, spread, spread_t, *summaries)

    total = (FINE_K - 1) * FBLK + coarse
    lists = fine_blocks.T
    parts = PARTS if sum(PARTS) == blocks else (blocks,)
    waiting, out, first = None, None, 0

    def finish(out, attended, third, second, base, after=()):
        fourth = over_head(third, CORE_PAIRS)
        rows = attended.shape[0]
        previous = [] if out is None else [out]
        height = min(2 * FBLK, rows)
        tile = pl.BlockSpec((height, group), lambda i: (i, 0))
        return pl.pallas_call(
            output_kernel,
            grid=(rows // height,),
            out_shape=shape((tok_rows, group), BF),
            in_specs=[pl.BlockSpec((width, group), lambda i: (0, 0))]
            + [tile] * 4
            + [pl.BlockSpec(memory_space=pl.ANY)] * (len(previous) + len(after)),
            out_specs=pl.BlockSpec((height, group), lambda i, base=base * FBLK // height: (i + base, 0)),
            input_output_aliases={5: 0} if previous else {},
            compiler_params=params,
            cost_estimate=COST,
            name="output",
        )(w_out, attended, third, second, fourth, *previous, *after)

    for count in parts:
        attended = pl.pallas_call(
            functools.partial(rest_kernel, first, count),
            out_shape=shape((count * FBLK, group), BF),
            in_specs=smem_specs(2) + vmem_specs(10),
            out_specs=pl.BlockSpec(memory_space=pltpu.VMEM),
            scratch_shapes=[
                pltpu.VMEM((2, total, group), BF),
                pltpu.VMEM((2, group, total), BF),
                pltpu.VMEM((2, group, heads * FBLK), BF),
                pltpu.VMEM((2, total, heads * FBLK), BF),
            ],
            compiler_params=params,
            cost_estimate=COST,
            name="rest",
        )(
            lists, level_mix, q_t, window_k, window_v, coarse_k, coarse_v, bias, acc, near_out, top, den
        )
        third = over_head(attended, X_PAIRS)
        second = over_head(attended, CORE_PAIRS)
        if waiting is not None:
            old, old_third, old_second, old_base = waiting
            old_third, attended = lax.optimization_barrier((old_third, attended))
            out = finish(out, old, old_third, old_second, old_base, [third])
        waiting = (attended, third, second, first)
        first += count
    return finish(out, *waiting)


def solution(mesh):
    placed = (
        P("seq", None),
        P(None, "head"),
        P(None, "head"),
        P(None, "head"),
        P(None, "head"),
        P(None, "head"),
        P("seq", None),
        P("seq", None),
        P("seq", None),
    )
    return jax.shard_map(
        local, mesh=mesh, in_specs=placed, out_specs=P("seq", "head"), check_vma=False
    )
```

```python
import functools

import jax
import jax.numpy as jnp
from jax import lax
from jax.experimental import pallas as pl
from jax.experimental.pallas import tpu as pltpu
from jax.sharding import PartitionSpec as P

FBLK = 128
FINE_K = 4
POOL1 = 8
POOL2 = 64
POOL3 = 512
SUMM_ROWS = 32
CODE_ROWS = 16
BF = jnp.bfloat16
F32 = jnp.float32
I32 = jnp.int32
HIDE = -1e30
VMEM_LIMIT = 24 * 1024 * 1024
LONG_BYTES = 20_000_000
COST = pl.CostEstimate(flops=1, bytes_accessed=1, transcendentals=0)
LONG = pl.CostEstimate(flops=1, bytes_accessed=LONG_BYTES, transcendentals=0)
PARTS = (4, 4)

X_PAIRS = [(0, 2), (2, 0), (1, 3), (3, 1)]
CORE_PAIRS = [(0, 1), (1, 0), (2, 3), (3, 2)]


def nn(a, b):
    return lax.dot_general(a, b, (((1,), (0,)), ((), ())), preferred_element_type=F32)


def nt(a, b):
    return lax.dot_general(a, b, (((1,), (1,)), ((), ())), preferred_element_type=F32)


def iota(shape, axis):
    return lax.broadcasted_iota(I32, shape, axis)


def ones_where(condition):
    return jnp.where(condition, 1.0, 0.0).astype(BF)


def vmem_specs(count):
    return [pl.BlockSpec(memory_space=pltpu.VMEM)] * count


def smem_specs(count):
    return [pl.BlockSpec(memory_space=pltpu.SMEM)] * count


def over_head(block, pairs):
    return lax.ppermute(block, "head", pairs)


def to_next(block):
    return lax.ppermute(block, "seq", [(i, i + 1) for i in range(lax.axis_size("seq") - 1)])


def send_kernel(tokens_ref, mask_ref, *refs):
    outs, own = refs[:-1], refs[-1]
    slab, head = lax.axis_index("seq"), lax.axis_index("head")
    core = head & 1
    rows, width = own.shape
    half = width // 2
    ids = mask_ref[...]
    line = iota((CODE_ROWS, ids.shape[1]), 0)
    code = jnp.where(line == 0, ids >> 5, jnp.where(line == 1, ids & 31, 0)).astype(F32).astype(BF)
    sides = (head >> 1, head >> 1, core, core, core)
    for distance, side, out in zip((7 - core, 5 - core, 3, 2, 1), sides, outs):
        row = pl.multiple_of((slab ^ distance) * rows, rows)
        start = pl.multiple_of(side * half, half)
        out[:rows] = tokens_ref[pl.ds(row, rows), pl.ds(start, half)]
        if out.shape[0] > rows:
            out[rows : rows + CODE_ROWS] = code
    own[...] = tokens_ref[pl.ds(pl.multiple_of(slab * rows, rows), rows)]


def stack_kernel(places, *refs):
    target = refs[-1]
    at = 0
    for source, row, height, column in places:
        target[at : at + height] = refs[source][row : row + height, column : column + target.shape[1]]
        at += height


def stacked(parts, places, width, after=(), cost=COST):
    return pl.pallas_call(
        functools.partial(stack_kernel, places),
        out_shape=jax.ShapeDtypeStruct((sum(place[2] for place in places), width), BF),
        in_specs=vmem_specs(len(parts)) + [pl.BlockSpec(memory_space=pl.ANY)] * len(after),
        out_specs=pl.BlockSpec(memory_space=pltpu.VMEM),
        compiler_params=pltpu.CompilerParams(vmem_limit_bytes=VMEM_LIMIT),
        cost_estimate=cost,
        name="stack",
    )(*parts, *after)


def by_distance(block, distance):
    return lax.ppermute(block, "seq", [(i, i ^ distance) for i in range(lax.axis_size("seq"))])


def by_core(block, distances):
    heads = lax.axis_size("head")
    pairs = [
        (slab * heads + head, (slab ^ distances[head & 1]) * heads + head)
        for slab in range(lax.axis_size("seq"))
        for head in range(heads)
    ]
    return lax.ppermute(block, ("seq", "head"), pairs)


def exchange_tokens(tokens, mask_ids, prepare, expand):
    tok_rows, width = tokens.shape
    slabs = lax.axis_size("seq")
    rows = tok_rows // slabs
    if slabs != 8:
        quarter = width // 4
        split = tokens.reshape(slabs, rows, width)
        mine = lax.dynamic_slice_in_dim(split, lax.axis_index("head") * quarter, quarter, axis=2)
        first = lax.all_to_all(mine, "seq", split_axis=0, concat_axis=0, tiled=True).reshape(
            tok_rows, quarter
        )
        third = over_head(first, X_PAIRS)
        second = over_head(first, CORE_PAIRS)
        fourth = over_head(third, CORE_PAIRS)
        prepared = prepare()
        return [first, third, second, fourth], prepared, expand(prepared, [to_next(mask_ids)])
    half = width // 2
    tall = rows + CODE_ROWS
    *blocks, own = pl.pallas_call(
        send_kernel,
        out_shape=(
            jax.ShapeDtypeStruct((tall, half), BF),
            jax.ShapeDtypeStruct((tall, half), BF),
            jax.ShapeDtypeStruct((tall, half), BF),
            jax.ShapeDtypeStruct((tall, half), BF),
            jax.ShapeDtypeStruct((tall, half), BF),
            jax.ShapeDtypeStruct((rows, width), BF),
        ),
        in_specs=vmem_specs(2),
        out_specs=vmem_specs(6),
        compiler_params=pltpu.CompilerParams(vmem_limit_bytes=60 * 1024 * 1024),
        cost_estimate=COST,
        name="send",
    )(tokens, mask_ids)
    routes = ((7, 6), (5, 4), (3, 3), (2, 2), (1, 1))
    one, two, three, four, five = [by_core(block, route) for block, route in zip(blocks, routes)]
    prepared = prepare()
    one, _ = lax.optimization_barrier((one, prepared))
    first_x = over_head(stacked((one,), ((0, 0, rows, 0),), half, (three, four, five)), X_PAIRS)
    two, first_x = lax.optimization_barrier((two, first_x))
    two = stacked((two,), ((0, 0, rows, 0),), half)
    far = [one, two]
    far_core = [over_head(part, CORE_PAIRS) for part in far]
    far_x = [first_x, over_head(two, X_PAIRS)]
    near = [three, four, five]
    near_core = [over_head(part, CORE_PAIRS) for part in near]
    expanded = expand(prepared, [one, far_core[0], three, five])
    far_x[1], _ = lax.optimization_barrier((far_x[1], expanded))
    far_last = [over_head(part, CORE_PAIRS) for part in far_x]
    return far + far_x + far_core + far_last + near + near_core + [own], prepared, expanded


def column(row, lanes=128):
    return jnp.transpose(jnp.broadcast_to(row.astype(F32), (lanes, row.shape[1]))).astype(I32)


def ranks(ids, tok_rows, lanes=128):
    hidden = column(ids)
    parts = []
    for at in range(0, tok_rows, lanes):
        time = iota((1, lanes), 1) + at
        count = jnp.sum(jnp.where(hidden < time, 1.0, 0.0), axis=0, keepdims=True)
        here = jnp.sum(jnp.where(hidden == time, 1.0, 0.0), axis=0, keepdims=True)
        parts.append(jnp.where(here == 0.0, time - count.astype(I32), -1))
    return jnp.concatenate(parts, axis=1)


def prepare_kernel(
    order_ref, mask_ref, wq_ref, wv_ref, wk_in,
    p_ref, pt_ref, sel_ref, fcol_ref, frow_ref, bias_ref, wt_ref, wk_ref,
):
    slab, slabs = lax.axis_index("seq"), lax.axis_size("seq")
    tok_rows = order_ref.shape[1]
    packed = tok_rows - mask_ref.shape[1]
    flip = (slab ^ 7) * (tok_rows // slabs) if slabs == 8 else 0
    mids = tok_rows // POOL2
    group = wq_ref.shape[1]
    lanes = 128

    place = order_ref[...] ^ flip
    place_column = column(place)
    for at in range(0, tok_rows, lanes):
        p_ref[:, at : at + lanes] = ones_where(place_column == iota((tok_rows, lanes), 1) + at)
        pt_ref[at : at + lanes] = ones_where(iota((lanes, tok_rows), 0) + at == place)
    rank = ranks(mask_ref[...], tok_rows)
    time = jnp.where(rank >= 0, iota((1, tok_rows), 1), -1) + 1
    line = iota((16, tok_rows), 0)
    stack = jnp.where(
        line == 0,
        time >> 5,
        jnp.where(
            line == 1,
            time & 31,
            jnp.where(line == 2, (rank + 1) >> 5, jnp.where(line == 3, (rank + 1) & 31, 0)),
        ),
    )
    moved = nn(stack.astype(F32).astype(BF), p_ref[...]).astype(I32)
    time_here = (moved[0:1] << 5) + moved[1:2] - 1
    rank_here = (moved[2:3] << 5) + moved[3:4] - 1
    for at in range(0, packed, lanes):
        sel_ref[at : at + lanes] = ones_where(iota((lanes, tok_rows), 0) + at == rank_here)
    line = iota((SUMM_ROWS, tok_rows), 0)
    sel_ref[packed : packed + SUMM_ROWS] = ones_where(
        ((time_here >> 6) == line) | (((time_here >> 9) + mids == line) & (time_here >= 0))
    )
    lead = packed + SUMM_ROWS
    near = sel_ref.shape[0] - lead
    sel_ref[lead:] = ones_where((time_here >> 3) == iota((near, tok_rows), 0))
    pools = sel_ref[packed:]
    fcol_ref[...] = 1.0 / jnp.sqrt(jnp.maximum(nn(pools, jnp.ones((tok_rows, lanes), BF)), 1.0))
    frow_ref[...] = 1.0 / jnp.sqrt(jnp.maximum(nt(jnp.ones((16, tok_rows), BF), pools), 1.0))
    bias_ref[...] = jnp.where(column(rank) >= 0, 0.0, HIDE)
    wt_ref[:group] = jnp.transpose(wq_ref[...])
    wt_ref[group:] = jnp.transpose(wv_ref[...])
    wk_ref[...] = wk_in[...]


def mask_before(refs, rows):
    if len(refs) == 1:
        return refs[0][...]
    far, far_core, near_three, near_one = refs
    core = lax.axis_index("head") & 1

    def digits(ref):
        return ref[rows : rows + CODE_ROWS // 2].astype(F32)

    three, one = digits(near_three), digits(near_one)
    seven = jnp.where(core == 0, digits(far), digits(far_core))
    slab = lax.axis_index("seq")
    distance = slab ^ (slab - 1)

    code = jnp.where(distance == 1, one, jnp.where(distance == 3, three, seven)).astype(I32)
    return (code[0:1] << 5) + code[1:2]


def expand_kernel(rows, seen_ref, *refs):
    code_refs, (e_ref, et_ref, bias_ref) = refs[:-3], refs[-3:]
    tok_rows = seen_ref.shape[0]
    rank = ranks(mask_before(code_refs, rows), tok_rows)
    rank = jnp.where(lax.axis_index("seq") > 0, rank, -1)
    rank_column = column(rank)
    bias_ref[:tok_rows] = jnp.where(rank_column >= 0, 0.0, HIDE)
    bias_ref[tok_rows:] = seen_ref[...]
    for at in range(0, et_ref.shape[0], FBLK):
        e_ref[:, at : at + FBLK] = ones_where(rank_column == iota((tok_rows, FBLK), 1) + at)
        et_ref[at : at + FBLK] = ones_where(iota((FBLK, tok_rows), 0) + at == rank)


def assemble(piece_refs, x_ref):
    head = lax.axis_index("head")
    tok_rows, width = x_ref.shape
    if len(piece_refs) == 4:
        quarter = width // 4
        for distance, piece in zip((0, 2, 1, 3), piece_refs):
            start = pl.multiple_of((head ^ distance) * quarter, quarter)
            x_ref[:, pl.ds(start, quarter)] = piece[...]
        return
    far_refs, near_refs, own = piece_refs[:8], piece_refs[8:14], piece_refs[14]
    rows, half = own.shape[0], width // 2
    core, side = head & 1, head >> 1
    for index, piece in enumerate(far_refs):
        turn, crossed = (index // 2) % 2, index // 4
        row = pl.multiple_of((2 * (index % 2) + (core ^ crossed)) * rows, rows)
        start = pl.multiple_of((side ^ turn) * half, half)
        x_ref[pl.ds(row, rows), pl.ds(start, half)] = piece[:rows]
    for index, piece in enumerate(near_refs):
        row = (4 + index % 3) * rows
        start = pl.multiple_of((core ^ (index // 3)) * half, half)
        x_ref[row : row + rows, pl.ds(start, half)] = piece[:rows]
    x_ref[7 * rows :] = own[...]


def project_kernel(count, *refs):
    piece_refs, refs = refs[:count], refs[count:]
    wt_ref, wk_ref, sel_ref, fcol_ref, comp_ref, summ_ref, k_ref, v_ref, x_ref = refs
    assemble(piece_refs, x_ref)
    group = wk_ref.shape[1]
    packed = comp_ref.shape[0] // 2
    lead = packed + SUMM_ROWS
    x = x_ref[...]
    keys = nn(x, wk_ref[...]).astype(BF)
    k_ref[...] = keys
    vt = nt(wt_ref[group:], x).astype(BF)
    v_ref[...] = vt
    sel = sel_ref[:lead]
    kl = nn(sel, keys)
    vl = nt(vt, sel)
    comp_ref[:packed] = kl[:packed].astype(BF)
    vc = vl[:, :packed].astype(BF)
    for part in range(packed // group):
        comp_ref[packed + part * group : packed + (part + 1) * group] = vc[
            :, part * group : (part + 1) * group
        ]
    factor = fcol_ref[:SUMM_ROWS, :1]
    summ_k = kl[packed:] * factor
    tail = jnp.concatenate(
        [vl[:, packed:], jnp.zeros((group, 128 - SUMM_ROWS), F32)], axis=1
    )
    summ_v = jnp.transpose(tail)[:SUMM_ROWS] * factor
    mids = x_ref.shape[0] // POOL2
    fars = x_ref.shape[0] // POOL3
    summ_ref[:mids] = summ_k[:mids].astype(BF)
    summ_ref[mids : 2 * mids] = summ_v[:mids].astype(BF)
    summ_ref[2 * mids :] = (summ_k[mids:] + pltpu.roll(summ_v[mids:], fars, 0)).astype(BF)


def spread_heads(q4_ref, qt_ref, at, heads):
    width = q4_ref.shape[0] // heads
    for h in range(heads):
        rows = slice(h * width, (h + 1) * width)
        q4_ref[rows, h * FBLK : (h + 1) * FBLK] = qt_ref[rows, at : at + FBLK]


def order_kernel(
    p_ref, pt_ref, sel_ref, fcol_ref, frow_ref, wt_ref, x_ref, k0_ref, v0_ref,
    qt_ref, vt_ref, k_ref, nk_ref, nvt_ref,
):
    group = k_ref.shape[1]
    near = nk_ref.shape[0]
    k0, v0 = k0_ref[...], v0_ref[...]
    q0 = nt(wt_ref[:group], x_ref[...]).astype(BF)
    k_ref[...] = nn(p_ref[...], k0).astype(BF)
    qt_ref[...] = (nn(q0, pt_ref[...]) * 0.125).astype(BF)
    vt_ref[...] = nn(v0, pt_ref[...]).astype(BF)
    pool = sel_ref[sel_ref.shape[0] - near :]
    nk_ref[...] = (nn(pool, k0) * fcol_ref[SUMM_ROWS:, :1]).astype(BF)
    nvt_ref[...] = (nt(v0, pool) * frow_ref[:1, SUMM_ROWS:]).astype(BF)


def own_kernel(
    mix_ref, qt_ref, k_ref, vt_ref, nk_ref, nvt_ref, seen_ref,
    acc_ref, near_ref, top_ref, den_ref, q4_ref, p_ref,
):
    tok_rows, group = k_ref.shape
    heads = mix_ref.shape[1]
    width = group // heads
    q4_ref[...] = jnp.zeros_like(q4_ref)
    same = iota((FBLK, FBLK), 0) == iota((FBLK, FBLK), 1)
    nk, nvt = nk_ref[...], nvt_ref[...]
    for g in range(tok_rows // FBLK):
        at = g * FBLK
        slot = g % 2
        spread_heads(q4_ref.at[slot], qt_ref, at, heads)
        q4 = q4_ref[slot]
        bias = jnp.where(same, 0.0, seen_ref[at : at + FBLK])
        own_scores = nn(k_ref[at : at + FBLK], q4)
        near_scores = nn(nk, q4)
        scales = []
        for h in range(heads):
            lanes = slice(h * FBLK, (h + 1) * FBLK)
            part = own_scores[:, lanes] + bias
            top = jnp.max(part, axis=0, keepdims=True)
            weight = jnp.exp(part - top)
            top_ref[g : g + 1, lanes] = top
            den_ref[g : g + 1, lanes] = jnp.sum(weight, axis=0, keepdims=True)
            p_ref[slot, :FBLK, lanes] = weight.astype(BF)
            part = near_scores[:, lanes]
            weight = jnp.exp(part - jnp.max(part, axis=0, keepdims=True))
            scales.append(mix_ref[1, h] / jnp.sum(weight, axis=0, keepdims=True))
            p_ref[slot, FBLK:, lanes] = weight.astype(BF)
        own_out = nn(vt_ref[:, at : at + FBLK], p_ref[slot, :FBLK])
        near_out = nn(nvt, p_ref[slot, FBLK:])
        for h in range(heads):
            rows, lanes = slice(h * width, (h + 1) * width), slice(h * FBLK, (h + 1) * FBLK)
            acc_ref[rows, at : at + FBLK] = own_out[rows, lanes]
            near_ref[rows, at : at + FBLK] = near_out[rows, lanes] * scales[h]


def window_kernel(k_ref, vt_ref, comp_ref, e_ref, et_ref, *refs):
    summ_refs, (kw_ref, vw_ref, ck_ref, cv_ref, all_ref) = refs[:-5], refs[-5:]
    tok_rows, group = k_ref.shape
    packed = e_ref.shape[1]
    kw_ref[:tok_rows] = nn(e_ref[...], comp_ref[:packed]).astype(BF)
    kw_ref[tok_rows:] = k_ref[...]
    prev = None
    for part in range(packed // group):
        term = nn(
            comp_ref[packed + part * group : packed + (part + 1) * group],
            et_ref[part * group : (part + 1) * group],
        )
        prev = term if prev is None else prev + term
    vw_ref[:, :tok_rows] = prev.astype(BF)
    vw_ref[:, tok_rows:] = vt_ref[...]
    at = 0
    for part in summ_refs:
        all_ref[at : at + part.shape[0]] = part[...]
        at += part.shape[0]
    slab, slabs = lax.axis_index("seq"), lax.axis_size("seq")
    mids, fars = tok_rows // POOL2, tok_rows // POOL3
    shape = (ck_ref.shape[0], all_ref.shape[0])
    line = iota(shape, 0)
    step = 3 * mids
    turn = line // mids
    far = line - 3 * mids
    shard = slab - 1 + turn
    turned = slab if slabs == 8 else 0
    distance = jnp.where(line < 3 * mids, shard, far // fars) ^ turned
    slot = (distance >> 1) + (distance & 1) * (slabs // 2) if slabs == 8 else distance
    source = slot * step + jnp.where(line < 3 * mids, line - turn * mids, 2 * mids + far % fars)
    source = jnp.where((line >= 3 * mids) | ((shard >= 0) & (shard < slabs)), source, -2 * step)
    gathered = all_ref[...]
    ck_ref[...] = nn(ones_where(source == iota(shape, 1)), gathered).astype(BF)
    values = nn(ones_where(source + jnp.where(line < 3 * mids, mids, fars) == iota(shape, 1)), gathered)
    cv_ref[...] = jnp.transpose(values).astype(BF)


def rest_kernel(
    first, blocks, lists_ref, mix_ref, qt_ref, kw_ref, vw_ref, ck_ref, cv_ref, bias_ref,
    acc_ref, near_ref, top_ref, den_ref, out_ref, kc_ref, vc_ref, q4_ref, p_ref,
):
    group, tok_rows = qt_ref.shape
    heads = mix_ref.shape[1]
    width = group // heads
    others = FINE_K - 1
    fine = others * FBLK
    mid = 3 * (tok_rows // POOL2)
    far_at = fine + mid
    total = kc_ref.shape[1]
    for slot in range(2):
        kc_ref[slot, fine:] = ck_ref[...]
        vc_ref[slot, :, fine:] = cv_ref[...]
    q4_ref[...] = jnp.zeros_like(q4_ref)
    for index in range(blocks):
        g = first + index
        at = g * FBLK
        slot = index % 2
        biases = []
        for entry in range(others):
            start = pl.multiple_of(lists_ref[entry + 1, g] * FBLK, FBLK)
            kc_ref[slot, entry * FBLK : (entry + 1) * FBLK] = kw_ref[pl.ds(start, FBLK)]
            vc_ref[slot, :, entry * FBLK : (entry + 1) * FBLK] = vw_ref[:, pl.ds(start, FBLK)]
            biases.append(bias_ref[pl.ds(start, FBLK)])
        spread_heads(q4_ref.at[slot], qt_ref, at, heads)
        scores = nn(kc_ref[slot], q4_ref[slot])
        scales, keeps = [], []
        for h in range(heads):
            lanes = slice(h * FBLK, (h + 1) * FBLK)
            parts = [scores[e * FBLK : (e + 1) * FBLK, lanes] + biases[e] for e in range(others)]
            old_top = top_ref[g : g + 1, lanes]
            top = functools.reduce(
                jnp.maximum, [jnp.max(part, axis=0, keepdims=True) for part in parts] + [old_top]
            )
            keep = jnp.exp(old_top - top)
            den = den_ref[g : g + 1, lanes] * keep
            for e, part in enumerate(parts):
                weight = jnp.exp(part - top)
                den = den + jnp.sum(weight, axis=0, keepdims=True)
                p_ref[slot, e * FBLK : (e + 1) * FBLK, lanes] = weight.astype(BF)
            scale = mix_ref[0, h] / den
            scales.append(scale)
            keeps.append(keep * scale)
            relative = den / mix_ref[0, h]
            for level, (low, high) in enumerate(((fine, far_at), (far_at, total))):
                part = scores[low:high, lanes]
                weight = jnp.exp(part - jnp.max(part, axis=0, keepdims=True))
                share = mix_ref[level + 2, h] / jnp.sum(weight, axis=0, keepdims=True) * relative
                p_ref[slot, low:high, lanes] = (weight * share).astype(BF)
        total_out = nn(vc_ref[slot], p_ref[slot])
        rows = []
        for h in range(heads):
            pick = (slice(h * width, (h + 1) * width), slice(h * FBLK, (h + 1) * FBLK))
            mine = (pick[0], slice(at, at + FBLK))
            rows.append(total_out[pick] * scales[h] + acc_ref[mine] * keeps[h] + near_ref[mine])
        out_ref[index * FBLK : (index + 1) * FBLK] = jnp.transpose(
            jnp.concatenate(rows, axis=0)
        ).astype(BF)


def output_kernel(w_ref, *refs):
    out_ref = refs[-1]
    group = w_ref.shape[1]
    head = lax.axis_index("head")
    total = None
    for distance, part in zip((0, 2, 1, 3), refs[:4]):
        start = pl.multiple_of((head ^ distance) * group, group)
        term = nn(part[...], w_ref[pl.ds(start, group)])
        total = term if total is None else total + term
    out_ref[...] = total.astype(BF)


def local(tokens, w_query, w_key, w_value, w_out, level_mix, fine_blocks, order, mask_ids):
    tok_rows, width = tokens.shape
    slabs = lax.axis_size("seq")
    slab, head = lax.axis_index("seq"), lax.axis_index("head")
    group = w_query.shape[1]
    heads = level_mix.shape[1]
    packed = tok_rows - mask_ids.shape[1]
    near, mids, fars = tok_rows // POOL1, tok_rows // POOL2, tok_rows // POOL3
    coarse = 3 * mids + fars * slabs
    step = 3 * mids
    chosen = packed + SUMM_ROWS + near

    shape = jax.ShapeDtypeStruct
    params = pltpu.CompilerParams(vmem_limit_bytes=VMEM_LIMIT)

    def prepare():
        return pl.pallas_call(
            prepare_kernel,
            out_shape=(
                shape((tok_rows, tok_rows), BF),
                shape((tok_rows, tok_rows), BF),
                shape((chosen, tok_rows), BF),
                shape((SUMM_ROWS + near, 128), F32),
                shape((16, SUMM_ROWS + near), F32),
                shape((tok_rows, FBLK), F32),
                shape((2 * group, width), BF),
                shape((width, group), BF),
            ),
            in_specs=vmem_specs(5),
            out_specs=vmem_specs(8),
            compiler_params=params,
            cost_estimate=COST,
            name="prepare",
        )(order, mask_ids, w_query, w_value, w_key)

    def expand(prepared, sources):
        return pl.pallas_call(
            functools.partial(expand_kernel, tok_rows // slabs),
            out_shape=(
                shape((tok_rows, packed), BF),
                shape((packed, tok_rows), BF),
                shape((2 * tok_rows, FBLK), F32),
            ),
            in_specs=vmem_specs(1 + len(sources)),
            out_specs=vmem_specs(3),
            compiler_params=params,
            cost_estimate=COST,
            name="expand",
        )(prepared[5], *sources)

    pieces, prepared, expanded = exchange_tokens(tokens, mask_ids, prepare, expand)
    permute, permute_t, select, f_col, f_row, seen, w_t, w_k = prepared
    spread, spread_t, bias = expanded
    comp, summ, k0, v0, rows_here = pl.pallas_call(
        functools.partial(project_kernel, len(pieces)),
        out_shape=(
            shape((2 * packed, group), BF),
            shape((step, group), BF),
            shape((tok_rows, group), BF),
            shape((group, tok_rows), BF),
            shape((tok_rows, width), BF),
        ),
        in_specs=vmem_specs(len(pieces) + 4),
        out_specs=vmem_specs(5),
        compiler_params=params,
        cost_estimate=COST,
        name="project",
    )(*pieces, w_t, w_k, select, f_col)
    if slabs == 8:
        lined = [summ] + [by_distance(summ, d) for d in (2, 4, 6)]
        comp, *lined = lax.optimization_barrier((comp, *lined))
    comp_before = to_next(comp)

    q_t, v_t, keys, near_k, near_vt = pl.pallas_call(
        order_kernel,
        out_shape=(
            shape((group, tok_rows), BF),
            shape((group, tok_rows), BF),
            shape((tok_rows, group), BF),
            shape((near, group), BF),
            shape((group, near), BF),
        ),
        in_specs=vmem_specs(9),
        out_specs=vmem_specs(5),
        compiler_params=params,
        cost_estimate=COST,
        name="order",
    )(permute, permute_t, select, f_col, f_row, w_t, rows_here, k0, v0)
    blocks = tok_rows // FBLK
    acc, near_out, top, den = pl.pallas_call(
        own_kernel,
        out_shape=(
            shape((group, tok_rows), F32),
            shape((group, tok_rows), F32),
            shape((blocks, heads * FBLK), F32),
            shape((blocks, heads * FBLK), F32),
        ),
        in_specs=smem_specs(1) + vmem_specs(6),
        out_specs=vmem_specs(4),
        scratch_shapes=[
            pltpu.VMEM((2, group, heads * FBLK), BF),
            pltpu.VMEM((2, FBLK + near, heads * FBLK), BF),
        ],
        compiler_params=params,
        cost_estimate=COST,
        name="own",
    )(level_mix, q_t, keys, v_t, near_k, near_vt, seen)

    if slabs == 8:
        places = tuple((index, 0, step, 0) for index in range(4))
        column = stacked(lined, places, group, (top,))
        summaries = [column, by_distance(column, 1)]
    else:
        copies = jnp.broadcast_to(summ[None], (slabs, step, group))
        copies = lax.all_to_all(copies, "seq", split_axis=0, concat_axis=0, tiled=True)
        summaries = [copies.reshape(slabs * step, group)]

    window_k, window_v, coarse_k, coarse_v = pl.pallas_call(
        window_kernel,
        out_shape=(
            shape((2 * tok_rows, group), BF),
            shape((group, 2 * tok_rows), BF),
            shape((coarse, group), BF),
            shape((group, coarse), BF),
        ),
        in_specs=vmem_specs(5 + len(summaries)),
        out_specs=vmem_specs(4),
        scratch_shapes=[pltpu.VMEM((slabs * step, group), BF)],
        compiler_params=params,
        cost_estimate=COST,
        name="window",
    )(keys, v_t, comp_before, spread, spread_t, *summaries)

    total = (FINE_K - 1) * FBLK + coarse
    lists = fine_blocks.T
    parts = PARTS if sum(PARTS) == blocks else (blocks,)
    waiting, out, first = None, None, 0

    def finish(out, attended, third, second, base, after=()):
        fourth = over_head(third, CORE_PAIRS)
        rows = attended.shape[0]
        previous = [] if out is None else [out]
        height = min(2 * FBLK, rows)
        tile = pl.BlockSpec((height, group), lambda i: (i, 0))
        return pl.pallas_call(
            output_kernel,
            grid=(rows // height,),
            out_shape=shape((tok_rows, group), BF),
            in_specs=[pl.BlockSpec((width, group), lambda i: (0, 0))]
            + [tile] * 4
            + [pl.BlockSpec(memory_space=pl.ANY)] * (len(previous) + len(after)),
            out_specs=pl.BlockSpec((height, group), lambda i, base=base * FBLK // height: (i + base, 0)),
            input_output_aliases={5: 0} if previous else {},
            compiler_params=params,
            cost_estimate=COST,
            name="output",
        )(w_out, attended, third, second, fourth, *previous, *after)

    for count in parts:
        attended = pl.pallas_call(
            functools.partial(rest_kernel, first, count),
            out_shape=shape((count * FBLK, group), BF),
            in_specs=smem_specs(2) + vmem_specs(10),
            out_specs=pl.BlockSpec(memory_space=pltpu.VMEM),
            scratch_shapes=[
                pltpu.VMEM((2, total, group), BF),
                pltpu.VMEM((2, group, total), BF),
                pltpu.VMEM((2, group, heads * FBLK), BF),
                pltpu.VMEM((2, total, heads * FBLK), BF),
            ],
            compiler_params=params,
            cost_estimate=COST,
            name="rest",
        )(
            lists, level_mix, q_t, window_k, window_v, coarse_k, coarse_v, bias, acc, near_out, top, den
        )
        third = over_head(attended, X_PAIRS)
        second = over_head(attended, CORE_PAIRS)
        if waiting is not None:
            old, old_third, old_second, old_base = waiting
            old_third, attended = lax.optimization_barrier((old_third, attended))
            out = finish(out, old, old_third, old_second, old_base, [third])
        waiting = (attended, third, second, first)
        first += count
    return finish(out, *waiting)


def solution(mesh):
    placed = (
        P("seq", None),
        P(None, "head"),
        P(None, "head"),
        P(None, "head"),
        P(None, "head"),
        P(None, "head"),
        P("seq", None),
        P("seq", None),
        P("seq", None),
    )
    return jax.shard_map(
        local, mesh=mesh, in_specs=placed, out_specs=P("seq", "head"), check_vma=False
    )
```

```python
import functools

import jax
import jax.numpy as jnp
from jax import lax
from jax.experimental import pallas as pl
from jax.experimental.pallas import tpu as pltpu
from jax.sharding import PartitionSpec as P

FBLK = 128
FINE_K = 4
POOL1 = 8
POOL2 = 64
POOL3 = 512
SUMM_ROWS = 32
CODE_ROWS = 16
BF = jnp.bfloat16
F32 = jnp.float32
I32 = jnp.int32
HIDE = -1e30
VMEM_LIMIT = 24 * 1024 * 1024
LONG_BYTES = 20_000_000
COST = pl.CostEstimate(flops=1, bytes_accessed=1, transcendentals=0)
LONG = pl.CostEstimate(flops=1, bytes_accessed=LONG_BYTES, transcendentals=0)
PARTS = (4, 4)

X_PAIRS = [(0, 2), (2, 0), (1, 3), (3, 1)]
CORE_PAIRS = [(0, 1), (1, 0), (2, 3), (3, 2)]


def nn(a, b):
    return lax.dot_general(a, b, (((1,), (0,)), ((), ())), preferred_element_type=F32)


def nt(a, b):
    return lax.dot_general(a, b, (((1,), (1,)), ((), ())), preferred_element_type=F32)


def iota(shape, axis):
    return lax.broadcasted_iota(I32, shape, axis)


def ones_where(condition):
    return jnp.where(condition, 1.0, 0.0).astype(BF)


def vmem_specs(count):
    return [pl.BlockSpec(memory_space=pltpu.VMEM)] * count


def smem_specs(count):
    return [pl.BlockSpec(memory_space=pltpu.SMEM)] * count


def over_head(block, pairs):
    return lax.ppermute(block, "head", pairs)


def to_next(block):
    return lax.ppermute(block, "seq", [(i, i + 1) for i in range(lax.axis_size("seq") - 1)])


def send_kernel(tokens_ref, mask_ref, *refs):
    outs, own = refs[:-1], refs[-1]
    slab, head = lax.axis_index("seq"), lax.axis_index("head")
    core = head & 1
    rows, width = own.shape
    half = width // 2
    ids = mask_ref[...]
    line = iota((CODE_ROWS, ids.shape[1]), 0)
    code = jnp.where(line == 0, ids >> 5, jnp.where(line == 1, ids & 31, 0)).astype(F32).astype(BF)
    sides = (head >> 1, head >> 1, core, core, core)
    for distance, side, out in zip((7 - core, 5 - core, 3, 2, 1), sides, outs):
        row = pl.multiple_of((slab ^ distance) * rows, rows)
        start = pl.multiple_of(side * half, half)
        out[:rows] = tokens_ref[pl.ds(row, rows), pl.ds(start, half)]
        if out.shape[0] > rows:
            out[rows : rows + CODE_ROWS] = code
    own[...] = tokens_ref[pl.ds(pl.multiple_of(slab * rows, rows), rows)]


def stack_kernel(places, *refs):
    target = refs[-1]
    at = 0
    for source, row, height, column in places:
        target[at : at + height] = refs[source][row : row + height, column : column + target.shape[1]]
        at += height


def stacked(parts, places, width, after=(), cost=COST):
    return pl.pallas_call(
        functools.partial(stack_kernel, places),
        out_shape=jax.ShapeDtypeStruct((sum(place[2] for place in places), width), BF),
        in_specs=vmem_specs(len(parts)) + [pl.BlockSpec(memory_space=pl.ANY)] * len(after),
        out_specs=pl.BlockSpec(memory_space=pltpu.VMEM),
        compiler_params=pltpu.CompilerParams(vmem_limit_bytes=VMEM_LIMIT),
        cost_estimate=cost,
        name="stack",
    )(*parts, *after)


def packed_rows(select, packed, quarter, parts):
    return pl.pallas_call(
        pack_kernel,
        out_shape=jax.ShapeDtypeStruct((packed, quarter), BF),
        in_specs=vmem_specs(1 + len(parts)),
        out_specs=pl.BlockSpec(memory_space=pltpu.VMEM),
        scratch_shapes=[pltpu.VMEM((select.shape[1], quarter), BF)],
        compiler_params=pltpu.CompilerParams(vmem_limit_bytes=VMEM_LIMIT),
        cost_estimate=COST,
        name="pack",
    )(select, *parts)


def by_distance(block, distance):
    return lax.ppermute(block, "seq", [(i, i ^ distance) for i in range(lax.axis_size("seq"))])


def by_core(block, distances):
    heads = lax.axis_size("head")
    pairs = [
        (slab * heads + head, (slab ^ distances[head & 1]) * heads + head)
        for slab in range(lax.axis_size("seq"))
        for head in range(heads)
    ]
    return lax.ppermute(block, ("seq", "head"), pairs)


def exchange_tokens(tokens, mask_ids, prepare, expand):
    tok_rows, width = tokens.shape
    slabs = lax.axis_size("seq")
    rows = tok_rows // slabs
    if slabs != 8:
        quarter = width // 4
        split = tokens.reshape(slabs, rows, width)
        mine = lax.dynamic_slice_in_dim(split, lax.axis_index("head") * quarter, quarter, axis=2)
        first = lax.all_to_all(mine, "seq", split_axis=0, concat_axis=0, tiled=True).reshape(
            tok_rows, quarter
        )
        third = over_head(first, X_PAIRS)
        second = over_head(first, CORE_PAIRS)
        fourth = over_head(third, CORE_PAIRS)
        prepared = prepare()
        halo = to_next(packed_rows(prepared[2], tok_rows - mask_ids.shape[1], quarter, [first]))
        expanded = expand(prepared, [to_next(mask_ids)])
        return [first, third, second, fourth], prepared, expanded, halo
    half = width // 2
    tall = rows + CODE_ROWS
    *blocks, own = pl.pallas_call(
        send_kernel,
        out_shape=(
            jax.ShapeDtypeStruct((tall, half), BF),
            jax.ShapeDtypeStruct((tall, half), BF),
            jax.ShapeDtypeStruct((tall, half), BF),
            jax.ShapeDtypeStruct((tall, half), BF),
            jax.ShapeDtypeStruct((tall, half), BF),
            jax.ShapeDtypeStruct((rows, width), BF),
        ),
        in_specs=vmem_specs(2),
        out_specs=vmem_specs(6),
        compiler_params=pltpu.CompilerParams(vmem_limit_bytes=60 * 1024 * 1024),
        cost_estimate=COST,
        name="send",
    )(tokens, mask_ids)
    routes = ((7, 6), (5, 4), (3, 3), (2, 2), (1, 1))
    one, two, three, four, five = [by_core(block, route) for block, route in zip(blocks, routes)]
    prepared = prepare()
    one, _ = lax.optimization_barrier((one, prepared))
    first_x = over_head(stacked((one,), ((0, 0, rows, 0),), half, (three, four, five)), X_PAIRS)
    two, first_x = lax.optimization_barrier((two, first_x))
    two = stacked((two,), ((0, 0, rows, 0),), half)
    far = [one, two]
    far_core = [over_head(part, CORE_PAIRS) for part in far]
    far_x = [first_x, over_head(two, X_PAIRS)]
    near = [three, four, five]
    near_core = [over_head(part, CORE_PAIRS) for part in near]
    expanded = expand(prepared, [one, far_core[0], three, five])
    halo = packed_rows(
        prepared[2], tok_rows - mask_ids.shape[1], half // 2, far + far_core + near + near_core + [own]
    )
    far_x[1], _, _ = lax.optimization_barrier((far_x[1], expanded, halo))
    halo = to_next(halo)
    far_last = [over_head(part, CORE_PAIRS) for part in far_x]
    return far + far_x + far_core + far_last + near + near_core + [own], prepared, expanded, halo


def column(row, lanes=128):
    return jnp.transpose(jnp.broadcast_to(row.astype(F32), (lanes, row.shape[1]))).astype(I32)


def ranks(ids, tok_rows, lanes=128):
    hidden = column(ids)
    parts = []
    for at in range(0, tok_rows, lanes):
        time = iota((1, lanes), 1) + at
        count = jnp.sum(jnp.where(hidden < time, 1.0, 0.0), axis=0, keepdims=True)
        here = jnp.sum(jnp.where(hidden == time, 1.0, 0.0), axis=0, keepdims=True)
        parts.append(jnp.where(here == 0.0, time - count.astype(I32), -1))
    return jnp.concatenate(parts, axis=1)


def prepare_kernel(
    order_ref, mask_ref, wq_ref, wv_ref, wk_in,
    p_ref, pt_ref, sel_ref, fcol_ref, frow_ref, bias_ref, wt_ref, wk_ref,
):
    slab, slabs = lax.axis_index("seq"), lax.axis_size("seq")
    tok_rows = order_ref.shape[1]
    packed = tok_rows - mask_ref.shape[1]
    flip = (slab ^ 7) * (tok_rows // slabs) if slabs == 8 else 0
    mids = tok_rows // POOL2
    group = wq_ref.shape[1]
    lanes = 128

    place = order_ref[...] ^ flip
    place_column = column(place)
    for at in range(0, tok_rows, lanes):
        p_ref[:, at : at + lanes] = ones_where(place_column == iota((tok_rows, lanes), 1) + at)
        pt_ref[at : at + lanes] = ones_where(iota((lanes, tok_rows), 0) + at == place)
    rank = ranks(mask_ref[...], tok_rows)
    time = jnp.where(rank >= 0, iota((1, tok_rows), 1), -1) + 1
    line = iota((16, tok_rows), 0)
    stack = jnp.where(
        line == 0,
        time >> 5,
        jnp.where(
            line == 1,
            time & 31,
            jnp.where(line == 2, (rank + 1) >> 5, jnp.where(line == 3, (rank + 1) & 31, 0)),
        ),
    )
    moved = nn(stack.astype(F32).astype(BF), p_ref[...]).astype(I32)
    time_here = (moved[0:1] << 5) + moved[1:2] - 1
    rank_here = (moved[2:3] << 5) + moved[3:4] - 1
    for at in range(0, packed, lanes):
        sel_ref[at : at + lanes] = ones_where(iota((lanes, tok_rows), 0) + at == rank_here)
    line = iota((SUMM_ROWS, tok_rows), 0)
    sel_ref[packed : packed + SUMM_ROWS] = ones_where(
        ((time_here >> 6) == line) | (((time_here >> 9) + mids == line) & (time_here >= 0))
    )
    lead = packed + SUMM_ROWS
    near = sel_ref.shape[0] - lead
    sel_ref[lead:] = ones_where((time_here >> 3) == iota((near, tok_rows), 0))
    pools = sel_ref[packed:]
    fcol_ref[...] = 1.0 / jnp.sqrt(jnp.maximum(nn(pools, jnp.ones((tok_rows, lanes), BF)), 1.0))
    frow_ref[...] = 1.0 / jnp.sqrt(jnp.maximum(nt(jnp.ones((16, tok_rows), BF), pools), 1.0))
    bias_ref[...] = jnp.where(column(rank) >= 0, 0.0, HIDE)
    wt_ref[:group] = jnp.transpose(wq_ref[...])
    wt_ref[group:] = jnp.transpose(wv_ref[...])
    wk_ref[...] = wk_in[...]


def mask_before(refs, rows):
    if len(refs) == 1:
        return refs[0][...]
    far, far_core, near_three, near_one = refs
    core = lax.axis_index("head") & 1

    def digits(ref):
        return ref[rows : rows + CODE_ROWS // 2].astype(F32)

    three, one = digits(near_three), digits(near_one)
    seven = jnp.where(core == 0, digits(far), digits(far_core))
    slab = lax.axis_index("seq")
    distance = slab ^ (slab - 1)

    code = jnp.where(distance == 1, one, jnp.where(distance == 3, three, seven)).astype(I32)
    return (code[0:1] << 5) + code[1:2]


def expand_kernel(rows, seen_ref, *refs):
    code_refs, (e_ref, et_ref, bias_ref) = refs[:-3], refs[-3:]
    tok_rows = seen_ref.shape[0]
    rank = ranks(mask_before(code_refs, rows), tok_rows)
    rank = jnp.where(lax.axis_index("seq") > 0, rank, -1)
    rank_column = column(rank)
    bias_ref[:tok_rows] = jnp.where(rank_column >= 0, 0.0, HIDE)
    bias_ref[tok_rows:] = seen_ref[...]
    for at in range(0, et_ref.shape[0], FBLK):
        e_ref[:, at : at + FBLK] = ones_where(rank_column == iota((tok_rows, FBLK), 1) + at)
        et_ref[at : at + FBLK] = ones_where(iota((FBLK, tok_rows), 0) + at == rank)


def assemble(piece_refs, x_ref):
    head = lax.axis_index("head")
    tok_rows, width = x_ref.shape
    if len(piece_refs) == 4:
        quarter = width // 4
        for distance, piece in zip((0, 2, 1, 3), piece_refs):
            start = pl.multiple_of((head ^ distance) * quarter, quarter)
            x_ref[:, pl.ds(start, quarter)] = piece[...]
        return
    far_refs, near_refs, own = piece_refs[:8], piece_refs[8:14], piece_refs[14]
    rows, half = own.shape[0], width // 2
    core, side = head & 1, head >> 1
    for index, piece in enumerate(far_refs):
        turn, crossed = (index // 2) % 2, index // 4
        row = pl.multiple_of((2 * (index % 2) + (core ^ crossed)) * rows, rows)
        start = pl.multiple_of((side ^ turn) * half, half)
        x_ref[pl.ds(row, rows), pl.ds(start, half)] = piece[:rows]
    for index, piece in enumerate(near_refs):
        row = (4 + index % 3) * rows
        start = pl.multiple_of((core ^ (index // 3)) * half, half)
        x_ref[row : row + rows, pl.ds(start, half)] = piece[:rows]
    x_ref[7 * rows :] = own[...]


def pack_kernel(sel_ref, *refs):
    parts, (out_ref, rows_ref) = refs[:-2], refs[-2:]
    packed, quarter = out_ref.shape
    head = lax.axis_index("head")
    if len(parts) == 1:
        rows_ref[...] = parts[0][...]
    else:
        core, side = head & 1, head >> 1
        far_refs, near_refs, own = parts[:4], parts[4:10], parts[10]
        rows = own.shape[0]
        here = pl.ds(pl.multiple_of(core * quarter, quarter), quarter)
        for index, piece in enumerate(far_refs):
            row = pl.multiple_of((2 * (index % 2) + (core ^ (index // 2))) * rows, rows)
            rows_ref[pl.ds(row, rows)] = piece[:rows, here]
        for index in range(3):
            rows_ref[(4 + index) * rows : (5 + index) * rows] = jnp.where(
                core == side, near_refs[index][:rows, here], near_refs[3 + index][:rows, here]
            )
        rows_ref[7 * rows :] = own[:, pl.ds(pl.multiple_of(head * quarter, quarter), quarter)]
    out_ref[...] = nn(sel_ref[:packed], rows_ref[...]).astype(BF)


def project_kernel(count, *refs):
    piece_refs, refs = refs[:count], refs[count:]
    wt_ref, wk_ref, sel_ref, fcol_ref, summ_ref, k_ref, v_ref, x_ref = refs
    assemble(piece_refs, x_ref)
    group = wk_ref.shape[1]
    near = x_ref.shape[0] // POOL1
    lead = sel_ref.shape[0] - near
    x = x_ref[...]
    keys = nn(x, wk_ref[...]).astype(BF)
    k_ref[...] = keys
    vt = nt(wt_ref[group:], x).astype(BF)
    v_ref[...] = vt
    sel = sel_ref[lead - SUMM_ROWS : lead]
    kl = nn(sel, keys)
    vl = nt(vt, sel)
    factor = fcol_ref[:SUMM_ROWS, :1]
    summ_k = kl * factor
    tail = jnp.concatenate(
        [vl, jnp.zeros((group, 128 - SUMM_ROWS), F32)], axis=1
    )
    summ_v = jnp.transpose(tail)[:SUMM_ROWS] * factor
    mids = x_ref.shape[0] // POOL2
    fars = x_ref.shape[0] // POOL3
    summ_ref[:mids] = summ_k[:mids].astype(BF)
    summ_ref[mids : 2 * mids] = summ_v[:mids].astype(BF)
    summ_ref[2 * mids :] = (summ_k[mids:] + pltpu.roll(summ_v[mids:], fars, 0)).astype(BF)


def spread_heads(q4_ref, qt_ref, at, heads):
    width = q4_ref.shape[0] // heads
    for h in range(heads):
        rows = slice(h * width, (h + 1) * width)
        q4_ref[rows, h * FBLK : (h + 1) * FBLK] = qt_ref[rows, at : at + FBLK]


def order_kernel(
    p_ref, pt_ref, sel_ref, fcol_ref, frow_ref, wt_ref, x_ref, k0_ref, v0_ref,
    qt_ref, vt_ref, k_ref, nk_ref, nvt_ref,
):
    group = k_ref.shape[1]
    near = nk_ref.shape[0]
    k0, v0 = k0_ref[...], v0_ref[...]
    q0 = nt(wt_ref[:group], x_ref[...]).astype(BF)
    k_ref[...] = nn(p_ref[...], k0).astype(BF)
    qt_ref[...] = (nn(q0, pt_ref[...]) * 0.125).astype(BF)
    vt_ref[...] = nn(v0, pt_ref[...]).astype(BF)
    pool = sel_ref[sel_ref.shape[0] - near :]
    nk_ref[...] = (nn(pool, k0) * fcol_ref[SUMM_ROWS:, :1]).astype(BF)
    nvt_ref[...] = (nt(v0, pool) * frow_ref[:1, SUMM_ROWS:]).astype(BF)


def own_kernel(
    mix_ref, qt_ref, k_ref, vt_ref, nk_ref, nvt_ref, seen_ref,
    acc_ref, near_ref, top_ref, den_ref, q4_ref, p_ref,
):
    tok_rows, group = k_ref.shape
    heads = mix_ref.shape[1]
    width = group // heads
    q4_ref[...] = jnp.zeros_like(q4_ref)
    same = iota((FBLK, FBLK), 0) == iota((FBLK, FBLK), 1)
    nk, nvt = nk_ref[...], nvt_ref[...]
    for g in range(tok_rows // FBLK):
        at = g * FBLK
        slot = g % 2
        spread_heads(q4_ref.at[slot], qt_ref, at, heads)
        q4 = q4_ref[slot]
        bias = jnp.where(same, 0.0, seen_ref[at : at + FBLK])
        own_scores = nn(k_ref[at : at + FBLK], q4)
        near_scores = nn(nk, q4)
        scales = []
        for h in range(heads):
            lanes = slice(h * FBLK, (h + 1) * FBLK)
            part = own_scores[:, lanes] + bias
            top = jnp.max(part, axis=0, keepdims=True)
            weight = jnp.exp(part - top)
            top_ref[g : g + 1, lanes] = top
            den_ref[g : g + 1, lanes] = jnp.sum(weight, axis=0, keepdims=True)
            p_ref[slot, :FBLK, lanes] = weight.astype(BF)
            part = near_scores[:, lanes]
            weight = jnp.exp(part - jnp.max(part, axis=0, keepdims=True))
            scales.append(mix_ref[1, h] / jnp.sum(weight, axis=0, keepdims=True))
            p_ref[slot, FBLK:, lanes] = weight.astype(BF)
        own_out = nn(vt_ref[:, at : at + FBLK], p_ref[slot, :FBLK])
        near_out = nn(nvt, p_ref[slot, FBLK:])
        for h in range(heads):
            rows, lanes = slice(h * width, (h + 1) * width), slice(h * FBLK, (h + 1) * FBLK)
            acc_ref[rows, at : at + FBLK] = own_out[rows, lanes]
            near_ref[rows, at : at + FBLK] = near_out[rows, lanes] * scales[h]


def window_kernel(k_ref, vt_ref, wt_ref, wk_ref, e_ref, et_ref, *refs):
    halo_refs, refs = refs[:4], refs[4:]
    summ_refs, (kw_ref, vw_ref, ck_ref, cv_ref, all_ref, x_ref) = refs[:-6], refs[-6:]
    tok_rows, group = k_ref.shape
    quarter = x_ref.shape[1] // 4
    head = lax.axis_index("head")
    for distance, part in zip((0, 2, 1, 3), halo_refs):
        start = pl.multiple_of((head ^ distance) * quarter, quarter)
        x_ref[:, pl.ds(start, quarter)] = part[...]
    x = x_ref[...]
    kw_ref[:tok_rows] = nn(e_ref[...], nn(x, wk_ref[...]).astype(BF)).astype(BF)
    kw_ref[tok_rows:] = k_ref[...]
    vw_ref[:, :tok_rows] = nn(nt(wt_ref[group:], x).astype(BF), et_ref[...]).astype(BF)
    vw_ref[:, tok_rows:] = vt_ref[...]
    at = 0
    for part in summ_refs:
        all_ref[at : at + part.shape[0]] = part[...]
        at += part.shape[0]
    slab, slabs = lax.axis_index("seq"), lax.axis_size("seq")
    mids, fars = tok_rows // POOL2, tok_rows // POOL3
    shape = (ck_ref.shape[0], all_ref.shape[0])
    line = iota(shape, 0)
    step = 3 * mids
    turn = line // mids
    far = line - 3 * mids
    shard = slab - 1 + turn
    turned = slab if slabs == 8 else 0
    distance = jnp.where(line < 3 * mids, shard, far // fars) ^ turned
    slot = (distance >> 1) + (distance & 1) * (slabs // 2) if slabs == 8 else distance
    source = slot * step + jnp.where(line < 3 * mids, line - turn * mids, 2 * mids + far % fars)
    source = jnp.where((line >= 3 * mids) | ((shard >= 0) & (shard < slabs)), source, -2 * step)
    gathered = all_ref[...]
    ck_ref[...] = nn(ones_where(source == iota(shape, 1)), gathered).astype(BF)
    values = nn(ones_where(source + jnp.where(line < 3 * mids, mids, fars) == iota(shape, 1)), gathered)
    cv_ref[...] = jnp.transpose(values).astype(BF)


def rest_kernel(
    first, blocks, lists_ref, mix_ref, qt_ref, kw_ref, vw_ref, ck_ref, cv_ref, bias_ref,
    acc_ref, near_ref, top_ref, den_ref, out_ref, kc_ref, vc_ref, q4_ref, p_ref,
):
    group, tok_rows = qt_ref.shape
    heads = mix_ref.shape[1]
    width = group // heads
    others = FINE_K - 1
    fine = others * FBLK
    mid = 3 * (tok_rows // POOL2)
    far_at = fine + mid
    total = kc_ref.shape[1]
    for slot in range(2):
        kc_ref[slot, fine:] = ck_ref[...]
        vc_ref[slot, :, fine:] = cv_ref[...]
    q4_ref[...] = jnp.zeros_like(q4_ref)
    for index in range(blocks):
        g = first + index
        at = g * FBLK
        slot = index % 2
        biases = []
        for entry in range(others):
            start = pl.multiple_of(lists_ref[entry + 1, g] * FBLK, FBLK)
            kc_ref[slot, entry * FBLK : (entry + 1) * FBLK] = kw_ref[pl.ds(start, FBLK)]
            vc_ref[slot, :, entry * FBLK : (entry + 1) * FBLK] = vw_ref[:, pl.ds(start, FBLK)]
            biases.append(bias_ref[pl.ds(start, FBLK)])
        spread_heads(q4_ref.at[slot], qt_ref, at, heads)
        scores = nn(kc_ref[slot], q4_ref[slot])
        scales, keeps = [], []
        for h in range(heads):
            lanes = slice(h * FBLK, (h + 1) * FBLK)
            parts = [scores[e * FBLK : (e + 1) * FBLK, lanes] + biases[e] for e in range(others)]
            old_top = top_ref[g : g + 1, lanes]
            top = functools.reduce(
                jnp.maximum, [jnp.max(part, axis=0, keepdims=True) for part in parts] + [old_top]
            )
            keep = jnp.exp(old_top - top)
            den = den_ref[g : g + 1, lanes] * keep
            for e, part in enumerate(parts):
                weight = jnp.exp(part - top)
                den = den + jnp.sum(weight, axis=0, keepdims=True)
                p_ref[slot, e * FBLK : (e + 1) * FBLK, lanes] = weight.astype(BF)
            scale = mix_ref[0, h] / den
            scales.append(scale)
            keeps.append(keep * scale)
            relative = den / mix_ref[0, h]
            for level, (low, high) in enumerate(((fine, far_at), (far_at, total))):
                part = scores[low:high, lanes]
                weight = jnp.exp(part - jnp.max(part, axis=0, keepdims=True))
                share = mix_ref[level + 2, h] / jnp.sum(weight, axis=0, keepdims=True) * relative
                p_ref[slot, low:high, lanes] = (weight * share).astype(BF)
        total_out = nn(vc_ref[slot], p_ref[slot])
        rows = []
        for h in range(heads):
            pick = (slice(h * width, (h + 1) * width), slice(h * FBLK, (h + 1) * FBLK))
            mine = (pick[0], slice(at, at + FBLK))
            rows.append(total_out[pick] * scales[h] + acc_ref[mine] * keeps[h] + near_ref[mine])
        out_ref[index * FBLK : (index + 1) * FBLK] = jnp.transpose(
            jnp.concatenate(rows, axis=0)
        ).astype(BF)


def output_kernel(w_ref, *refs):
    out_ref = refs[-1]
    group = w_ref.shape[1]
    head = lax.axis_index("head")
    total = None
    for distance, part in zip((0, 2, 1, 3), refs[:4]):
        start = pl.multiple_of((head ^ distance) * group, group)
        term = nn(part[...], w_ref[pl.ds(start, group)])
        total = term if total is None else total + term
    out_ref[...] = total.astype(BF)


def local(tokens, w_query, w_key, w_value, w_out, level_mix, fine_blocks, order, mask_ids):
    tok_rows, width = tokens.shape
    slabs = lax.axis_size("seq")
    slab, head = lax.axis_index("seq"), lax.axis_index("head")
    group = w_query.shape[1]
    heads = level_mix.shape[1]
    packed = tok_rows - mask_ids.shape[1]
    near, mids, fars = tok_rows // POOL1, tok_rows // POOL2, tok_rows // POOL3
    coarse = 3 * mids + fars * slabs
    step = 3 * mids
    chosen = packed + SUMM_ROWS + near

    shape = jax.ShapeDtypeStruct
    params = pltpu.CompilerParams(vmem_limit_bytes=VMEM_LIMIT)

    def prepare():
        return pl.pallas_call(
            prepare_kernel,
            out_shape=(
                shape((tok_rows, tok_rows), BF),
                shape((tok_rows, tok_rows), BF),
                shape((chosen, tok_rows), BF),
                shape((SUMM_ROWS + near, 128), F32),
                shape((16, SUMM_ROWS + near), F32),
                shape((tok_rows, FBLK), F32),
                shape((2 * group, width), BF),
                shape((width, group), BF),
            ),
            in_specs=vmem_specs(5),
            out_specs=vmem_specs(8),
            compiler_params=params,
            cost_estimate=COST,
            name="prepare",
        )(order, mask_ids, w_query, w_value, w_key)

    def expand(prepared, sources):
        return pl.pallas_call(
            functools.partial(expand_kernel, tok_rows // slabs),
            out_shape=(
                shape((tok_rows, packed), BF),
                shape((packed, tok_rows), BF),
                shape((2 * tok_rows, FBLK), F32),
            ),
            in_specs=vmem_specs(1 + len(sources)),
            out_specs=vmem_specs(3),
            compiler_params=params,
            cost_estimate=COST,
            name="expand",
        )(prepared[5], *sources)

    pieces, prepared, expanded, halo = exchange_tokens(tokens, mask_ids, prepare, expand)
    permute, permute_t, select, f_col, f_row, seen, w_t, w_k = prepared
    spread, spread_t, bias = expanded
    summ, k0, v0, rows_here = pl.pallas_call(
        functools.partial(project_kernel, len(pieces)),
        out_shape=(
            shape((step, group), BF),
            shape((tok_rows, group), BF),
            shape((group, tok_rows), BF),
            shape((tok_rows, width), BF),
        ),
        in_specs=vmem_specs(len(pieces) + 4),
        out_specs=vmem_specs(4),
        compiler_params=params,
        cost_estimate=COST,
        name="project",
    )(*pieces, w_t, w_k, select, f_col)
    if slabs == 8:
        lined = [summ] + [by_distance(summ, d) for d in (2, 4, 6)]
    else:
        lined = [summ]

    q_t, v_t, keys, near_k, near_vt = pl.pallas_call(
        order_kernel,
        out_shape=(
            shape((group, tok_rows), BF),
            shape((group, tok_rows), BF),
            shape((tok_rows, group), BF),
            shape((near, group), BF),
            shape((group, near), BF),
        ),
        in_specs=vmem_specs(9),
        out_specs=vmem_specs(5),
        compiler_params=params,
        cost_estimate=COST,
        name="order",
    )(permute, permute_t, select, f_col, f_row, w_t, rows_here, k0, v0)
    halo, near_k, *lined = lax.optimization_barrier((halo, near_k, *lined))
    halo_x = over_head(halo, X_PAIRS)
    halo_core = over_head(halo, CORE_PAIRS)
    if slabs == 8:
        places = tuple((index, 0, step, 0) for index in range(4))
        column = stacked(lined, places, group)
        column, q_t = lax.optimization_barrier((column, q_t))
        summaries = [column, by_distance(column, 1)]
    else:
        copies = jnp.broadcast_to(summ[None], (slabs, step, group))
        copies = lax.all_to_all(copies, "seq", split_axis=0, concat_axis=0, tiled=True)
        summaries = [copies.reshape(slabs * step, group)]

    blocks = tok_rows // FBLK
    acc, near_out, top, den = pl.pallas_call(
        own_kernel,
        out_shape=(
            shape((group, tok_rows), F32),
            shape((group, tok_rows), F32),
            shape((blocks, heads * FBLK), F32),
            shape((blocks, heads * FBLK), F32),
        ),
        in_specs=smem_specs(1) + vmem_specs(6),
        out_specs=vmem_specs(4),
        scratch_shapes=[
            pltpu.VMEM((2, group, heads * FBLK), BF),
            pltpu.VMEM((2, FBLK + near, heads * FBLK), BF),
        ],
        compiler_params=params,
        cost_estimate=COST,
        name="own",
    )(level_mix, q_t, keys, v_t, near_k, near_vt, seen)

    halo_x, _, *summaries = lax.optimization_barrier((halo_x, top, *summaries))
    halo_last = over_head(halo_x, CORE_PAIRS)
    window_k, window_v, coarse_k, coarse_v = pl.pallas_call(
        window_kernel,
        out_shape=(
            shape((2 * tok_rows, group), BF),
            shape((group, 2 * tok_rows), BF),
            shape((coarse, group), BF),
            shape((group, coarse), BF),
        ),
        in_specs=vmem_specs(10 + len(summaries)),
        out_specs=vmem_specs(4),
        scratch_shapes=[pltpu.VMEM((slabs * step, group), BF), pltpu.VMEM((packed, width), BF)],
        compiler_params=params,
        cost_estimate=COST,
        name="window",
    )(keys, v_t, w_t, w_k, spread, spread_t, halo, halo_x, halo_core, halo_last, *summaries)

    total = (FINE_K - 1) * FBLK + coarse
    lists = fine_blocks.T
    parts = PARTS if sum(PARTS) == blocks else (blocks,)
    waiting, out, first = None, None, 0

    def finish(out, attended, third, second, base, after=()):
        fourth = over_head(third, CORE_PAIRS)
        rows = attended.shape[0]
        previous = [] if out is None else [out]
        height = min(2 * FBLK, rows)
        tile = pl.BlockSpec((height, group), lambda i: (i, 0))
        return pl.pallas_call(
            output_kernel,
            grid=(rows // height,),
            out_shape=shape((tok_rows, group), BF),
            in_specs=[pl.BlockSpec((width, group), lambda i: (0, 0))]
            + [tile] * 4
            + [pl.BlockSpec(memory_space=pl.ANY)] * (len(previous) + len(after)),
            out_specs=pl.BlockSpec((height, group), lambda i, base=base * FBLK // height: (i + base, 0)),
            input_output_aliases={5: 0} if previous else {},
            compiler_params=params,
            cost_estimate=COST,
            name="output",
        )(w_out, attended, third, second, fourth, *previous, *after)

    for count in parts:
        attended = pl.pallas_call(
            functools.partial(rest_kernel, first, count),
            out_shape=shape((count * FBLK, group), BF),
            in_specs=smem_specs(2) + vmem_specs(10),
            out_specs=pl.BlockSpec(memory_space=pltpu.VMEM),
            scratch_shapes=[
                pltpu.VMEM((2, total, group), BF),
                pltpu.VMEM((2, group, total), BF),
                pltpu.VMEM((2, group, heads * FBLK), BF),
                pltpu.VMEM((2, total, heads * FBLK), BF),
            ],
            compiler_params=params,
            cost_estimate=COST,
            name="rest",
        )(
            lists, level_mix, q_t, window_k, window_v, coarse_k, coarse_v, bias, acc, near_out, top, den
        )
        third = over_head(attended, X_PAIRS)
        second = over_head(attended, CORE_PAIRS)
        if waiting is not None:
            old, old_third, old_second, old_base = waiting
            old_third, attended = lax.optimization_barrier((old_third, attended))
            out = finish(out, old, old_third, old_second, old_base, [third])
        waiting = (attended, third, second, first)
        first += count
    return finish(out, *waiting)


def solution(mesh):
    placed = (
        P("seq", None),
        P(None, "head"),
        P(None, "head"),
        P(None, "head"),
        P(None, "head"),
        P(None, "head"),
        P("seq", None),
        P("seq", None),
        P("seq", None),
    )
    return jax.shard_map(
        local, mesh=mesh, in_specs=placed, out_specs=P("seq", "head"), check_vma=False
    )
```

```python
import functools

import jax
import jax.numpy as jnp
from jax import lax
from jax.experimental import pallas as pl
from jax.experimental.pallas import tpu as pltpu
from jax.sharding import PartitionSpec as P

FBLK = 128
FINE_K = 4
POOL1 = 8
POOL2 = 64
POOL3 = 512
SUMM_ROWS = 32
CODE_ROWS = 16
BF = jnp.bfloat16
F32 = jnp.float32
I32 = jnp.int32
HIDE = -1e30
VMEM_LIMIT = 24 * 1024 * 1024
LONG_BYTES = 20_000_000
COST = pl.CostEstimate(flops=1, bytes_accessed=1, transcendentals=0)
LONG = pl.CostEstimate(flops=1, bytes_accessed=LONG_BYTES, transcendentals=0)
PARTS = (4, 4)

X_PAIRS = [(0, 2), (2, 0), (1, 3), (3, 1)]
CORE_PAIRS = [(0, 1), (1, 0), (2, 3), (3, 2)]


def nn(a, b):
    return lax.dot_general(a, b, (((1,), (0,)), ((), ())), preferred_element_type=F32)


def nt(a, b):
    return lax.dot_general(a, b, (((1,), (1,)), ((), ())), preferred_element_type=F32)


def iota(shape, axis):
    return lax.broadcasted_iota(I32, shape, axis)


def ones_where(condition):
    return jnp.where(condition, 1.0, 0.0).astype(BF)


def vmem_specs(count):
    return [pl.BlockSpec(memory_space=pltpu.VMEM)] * count


def smem_specs(count):
    return [pl.BlockSpec(memory_space=pltpu.SMEM)] * count


def over_head(block, pairs):
    return lax.ppermute(block, "head", pairs)


def to_next(block):
    return lax.ppermute(block, "seq", [(i, i + 1) for i in range(lax.axis_size("seq") - 1)])


def send_kernel(tokens_ref, mask_ref, *refs):
    outs, own, sem_ref = refs[:-2], refs[-2], refs[-1]
    slab, head = lax.axis_index("seq"), lax.axis_index("head")
    core = head & 1
    rows, width = own.shape
    half = width // 2
    sides = (head >> 1, head >> 1, core, core, core)
    loads = []
    for distance, side, out in zip((7 - core, 5 - core, 3, 2, 1), sides, outs):
        row = pl.multiple_of((slab ^ distance) * rows, rows)
        start = pl.multiple_of(side * half, half)
        loads.append((tokens_ref.at[pl.ds(row, rows), pl.ds(start, half)], out.at[:rows]))
    loads.append((tokens_ref.at[pl.ds(pl.multiple_of(slab * rows, rows), rows)], own))
    copies = [
        pltpu.make_async_copy(source, target, sem_ref.at[index])
        for index, (source, target) in enumerate(loads)
    ]
    for copy in copies:
        copy.start()
    ids = mask_ref[...]
    line = iota((CODE_ROWS, ids.shape[1]), 0)
    code = jnp.where(line == 0, ids >> 5, jnp.where(line == 1, ids & 31, 0)).astype(F32).astype(BF)
    for out in outs:
        out[rows:] = code
    for copy in copies:
        copy.wait()


def stack_kernel(places, *refs):
    target = refs[-1]
    at = 0
    for source, row, height, column in places:
        target[at : at + height] = refs[source][row : row + height, column : column + target.shape[1]]
        at += height


def stacked(parts, places, width, after=(), cost=COST):
    return pl.pallas_call(
        functools.partial(stack_kernel, places),
        out_shape=jax.ShapeDtypeStruct((sum(place[2] for place in places), width), BF),
        in_specs=vmem_specs(len(parts)) + [pl.BlockSpec(memory_space=pl.ANY)] * len(after),
        out_specs=pl.BlockSpec(memory_space=pltpu.VMEM),
        compiler_params=pltpu.CompilerParams(vmem_limit_bytes=VMEM_LIMIT),
        cost_estimate=cost,
        name="stack",
    )(*parts, *after)


def packed_rows(select, packed, quarter, parts):
    return pl.pallas_call(
        pack_kernel,
        out_shape=jax.ShapeDtypeStruct((packed, quarter), BF),
        in_specs=vmem_specs(1 + len(parts)),
        out_specs=pl.BlockSpec(memory_space=pltpu.VMEM),
        scratch_shapes=[pltpu.VMEM((select.shape[1], quarter), BF)],
        compiler_params=pltpu.CompilerParams(vmem_limit_bytes=VMEM_LIMIT),
        cost_estimate=COST,
        name="pack",
    )(select, *parts)


def by_distance(block, distance):
    return lax.ppermute(block, "seq", [(i, i ^ distance) for i in range(lax.axis_size("seq"))])


def by_core(block, distances):
    heads = lax.axis_size("head")
    pairs = [
        (slab * heads + head, (slab ^ distances[head & 1]) * heads + head)
        for slab in range(lax.axis_size("seq"))
        for head in range(heads)
    ]
    return lax.ppermute(block, ("seq", "head"), pairs)


def exchange_tokens(tokens, mask_ids, prepare):
    tok_rows, width = tokens.shape
    slabs = lax.axis_size("seq")
    rows = tok_rows // slabs
    if slabs != 8:
        quarter = width // 4
        split = tokens.reshape(slabs, rows, width)
        mine = lax.dynamic_slice_in_dim(split, lax.axis_index("head") * quarter, quarter, axis=2)
        first = lax.all_to_all(mine, "seq", split_axis=0, concat_axis=0, tiled=True).reshape(
            tok_rows, quarter
        )
        third = over_head(first, X_PAIRS)
        second = over_head(first, CORE_PAIRS)
        fourth = over_head(third, CORE_PAIRS)
        prepared = prepare()
        halo = to_next(packed_rows(prepared[2], tok_rows - mask_ids.shape[1], quarter, [first]))
        return [first, third, second, fourth], prepared, [to_next(mask_ids)], halo
    half = width // 2
    tall = rows + CODE_ROWS
    *blocks, own = pl.pallas_call(
        send_kernel,
        out_shape=(
            jax.ShapeDtypeStruct((tall, half), BF),
            jax.ShapeDtypeStruct((tall, half), BF),
            jax.ShapeDtypeStruct((tall, half), BF),
            jax.ShapeDtypeStruct((tall, half), BF),
            jax.ShapeDtypeStruct((tall, half), BF),
            jax.ShapeDtypeStruct((rows, width), BF),
        ),
        in_specs=[pl.BlockSpec(memory_space=pl.ANY)] + vmem_specs(1),
        out_specs=vmem_specs(6),
        scratch_shapes=[pltpu.SemaphoreType.DMA((6,))],
        compiler_params=pltpu.CompilerParams(vmem_limit_bytes=60 * 1024 * 1024),
        cost_estimate=COST,
        name="send",
    )(tokens, mask_ids)
    routes = ((7, 6), (5, 4), (3, 3), (2, 2), (1, 1))
    one, two, three, four, five = [by_core(block, route) for block, route in zip(blocks, routes)]
    prepared = prepare()
    one, _ = lax.optimization_barrier((one, prepared))
    first_x = over_head(stacked((one,), ((0, 0, rows, 0),), half, (three, four, five)), X_PAIRS)
    two, first_x = lax.optimization_barrier((two, first_x))
    two = stacked((two,), ((0, 0, rows, 0),), half)
    far = [one, two]
    far_core = [over_head(part, CORE_PAIRS) for part in far]
    far_x = [first_x, over_head(two, X_PAIRS)]
    near = [three, four, five]
    near_core = [over_head(part, CORE_PAIRS) for part in near]
    halo = packed_rows(
        prepared[2], tok_rows - mask_ids.shape[1], half // 2, far + far_core + near + near_core + [own]
    )
    far_x[1], _ = lax.optimization_barrier((far_x[1], halo))
    halo = to_next(halo)
    far_last = [over_head(part, CORE_PAIRS) for part in far_x]
    return far + far_x + far_core + far_last + near + near_core + [own], prepared, [one, far_core[0], three, five], halo


def column(row, lanes=128):
    return jnp.transpose(jnp.broadcast_to(row.astype(F32), (lanes, row.shape[1]))).astype(I32)


def ranks(ids, tok_rows, lanes=128):
    hidden = column(ids)
    parts = []
    for at in range(0, tok_rows, lanes):
        time = iota((1, lanes), 1) + at
        count = jnp.sum(jnp.where(hidden < time, 1.0, 0.0), axis=0, keepdims=True)
        here = jnp.sum(jnp.where(hidden == time, 1.0, 0.0), axis=0, keepdims=True)
        parts.append(jnp.where(here == 0.0, time - count.astype(I32), -1))
    return jnp.concatenate(parts, axis=1)


def prepare_kernel(
    order_ref, mask_ref, wq_ref, wv_ref, wk_in,
    p_ref, pt_ref, sel_ref, fcol_ref, frow_ref, bias_ref, wt_ref, wk_ref,
):
    slab, slabs = lax.axis_index("seq"), lax.axis_size("seq")
    tok_rows = order_ref.shape[1]
    packed = tok_rows - mask_ref.shape[1]
    flip = (slab ^ 7) * (tok_rows // slabs) if slabs == 8 else 0
    mids = tok_rows // POOL2
    group = wq_ref.shape[1]
    lanes = 128

    place = order_ref[...] ^ flip
    place_column = column(place)
    for at in range(0, tok_rows, lanes):
        p_ref[:, at : at + lanes] = ones_where(place_column == iota((tok_rows, lanes), 1) + at)
        pt_ref[at : at + lanes] = ones_where(iota((lanes, tok_rows), 0) + at == place)
    rank = ranks(mask_ref[...], tok_rows)
    time = jnp.where(rank >= 0, iota((1, tok_rows), 1), -1) + 1
    line = iota((16, tok_rows), 0)
    stack = jnp.where(
        line == 0,
        time >> 5,
        jnp.where(
            line == 1,
            time & 31,
            jnp.where(line == 2, (rank + 1) >> 5, jnp.where(line == 3, (rank + 1) & 31, 0)),
        ),
    )
    moved = nn(stack.astype(F32).astype(BF), p_ref[...]).astype(I32)
    time_here = (moved[0:1] << 5) + moved[1:2] - 1
    rank_here = (moved[2:3] << 5) + moved[3:4] - 1
    for at in range(0, packed, lanes):
        sel_ref[at : at + lanes] = ones_where(iota((lanes, tok_rows), 0) + at == rank_here)
    line = iota((SUMM_ROWS, tok_rows), 0)
    sel_ref[packed : packed + SUMM_ROWS] = ones_where(
        ((time_here >> 6) == line) | (((time_here >> 9) + mids == line) & (time_here >= 0))
    )
    lead = packed + SUMM_ROWS
    near = sel_ref.shape[0] - lead
    sel_ref[lead:] = ones_where((time_here >> 3) == iota((near, tok_rows), 0))
    pools = sel_ref[packed:]
    fcol_ref[...] = 1.0 / jnp.sqrt(jnp.maximum(nn(pools, jnp.ones((tok_rows, lanes), BF)), 1.0))
    frow_ref[...] = 1.0 / jnp.sqrt(jnp.maximum(nt(jnp.ones((16, tok_rows), BF), pools), 1.0))
    bias_ref[...] = jnp.where(column(rank) >= 0, 0.0, HIDE)
    wt_ref[:group] = jnp.transpose(wq_ref[...])
    wt_ref[group:] = jnp.transpose(wv_ref[...])
    wk_ref[...] = wk_in[...]


def mask_before(refs, rows):
    if len(refs) == 1:
        return refs[0][...]
    far, far_core, near_three, near_one = refs
    core = lax.axis_index("head") & 1

    def digits(ref):
        return ref[rows : rows + CODE_ROWS // 2].astype(F32)

    three, one = digits(near_three), digits(near_one)
    seven = jnp.where(core == 0, digits(far), digits(far_core))
    slab = lax.axis_index("seq")
    distance = slab ^ (slab - 1)

    code = jnp.where(distance == 1, one, jnp.where(distance == 3, three, seven)).astype(I32)
    return (code[0:1] << 5) + code[1:2]


def expand_kernel(rows, seen_ref, *refs):
    code_refs, (e_ref, et_ref, bias_ref) = refs[:-3], refs[-3:]
    tok_rows = seen_ref.shape[0]
    rank = ranks(mask_before(code_refs, rows), tok_rows)
    rank = jnp.where(lax.axis_index("seq") > 0, rank, -1)
    rank_column = column(rank)
    bias_ref[:tok_rows] = jnp.where(rank_column >= 0, 0.0, HIDE)
    bias_ref[tok_rows:] = seen_ref[...]
    for at in range(0, et_ref.shape[0], FBLK):
        e_ref[:, at : at + FBLK] = ones_where(rank_column == iota((tok_rows, FBLK), 1) + at)
        et_ref[at : at + FBLK] = ones_where(iota((FBLK, tok_rows), 0) + at == rank)


def assemble(piece_refs, x_ref):
    head = lax.axis_index("head")
    tok_rows, width = x_ref.shape
    if len(piece_refs) == 4:
        quarter = width // 4
        for distance, piece in zip((0, 2, 1, 3), piece_refs):
            start = pl.multiple_of((head ^ distance) * quarter, quarter)
            x_ref[:, pl.ds(start, quarter)] = piece[...]
        return
    far_refs, near_refs, own = piece_refs[:8], piece_refs[8:14], piece_refs[14]
    rows, half = own.shape[0], width // 2
    core, side = head & 1, head >> 1
    for index, piece in enumerate(far_refs):
        turn, crossed = (index // 2) % 2, index // 4
        row = pl.multiple_of((2 * (index % 2) + (core ^ crossed)) * rows, rows)
        start = pl.multiple_of((side ^ turn) * half, half)
        x_ref[pl.ds(row, rows), pl.ds(start, half)] = piece[:rows]
    for index, piece in enumerate(near_refs):
        row = (4 + index % 3) * rows
        start = pl.multiple_of((core ^ (index // 3)) * half, half)
        x_ref[row : row + rows, pl.ds(start, half)] = piece[:rows]
    x_ref[7 * rows :] = own[...]


def pack_kernel(sel_ref, *refs):
    parts, (out_ref, rows_ref) = refs[:-2], refs[-2:]
    packed, quarter = out_ref.shape
    head = lax.axis_index("head")
    if len(parts) == 1:
        rows_ref[...] = parts[0][...]
    else:
        core, side = head & 1, head >> 1
        far_refs, near_refs, own = parts[:4], parts[4:10], parts[10]
        rows = own.shape[0]
        here = pl.ds(pl.multiple_of(core * quarter, quarter), quarter)
        for index, piece in enumerate(far_refs):
            row = pl.multiple_of((2 * (index % 2) + (core ^ (index // 2))) * rows, rows)
            rows_ref[pl.ds(row, rows)] = piece[:rows, here]
        for index in range(3):
            rows_ref[(4 + index) * rows : (5 + index) * rows] = jnp.where(
                core == side, near_refs[index][:rows, here], near_refs[3 + index][:rows, here]
            )
        rows_ref[7 * rows :] = own[:, pl.ds(pl.multiple_of(head * quarter, quarter), quarter)]
    out_ref[...] = nn(sel_ref[:packed], rows_ref[...]).astype(BF)


def project_kernel(count, *refs):
    piece_refs, refs = refs[:count], refs[count:]
    wt_ref, wk_ref, sel_ref, fcol_ref, summ_ref, k_ref, v_ref, x_ref = refs
    assemble(piece_refs, x_ref)
    group = wk_ref.shape[1]
    near = x_ref.shape[0] // POOL1
    lead = sel_ref.shape[0] - near
    x = x_ref[...]
    keys = nn(x, wk_ref[...]).astype(BF)
    k_ref[...] = keys
    vt = nt(wt_ref[group:], x).astype(BF)
    v_ref[...] = vt
    sel = sel_ref[lead - SUMM_ROWS : lead]
    kl = nn(sel, keys)
    vl = nt(vt, sel)
    factor = fcol_ref[:SUMM_ROWS, :1]
    summ_k = kl * factor
    tail = jnp.concatenate(
        [vl, jnp.zeros((group, 128 - SUMM_ROWS), F32)], axis=1
    )
    summ_v = jnp.transpose(tail)[:SUMM_ROWS] * factor
    mids = x_ref.shape[0] // POOL2
    fars = x_ref.shape[0] // POOL3
    summ_ref[:mids] = summ_k[:mids].astype(BF)
    summ_ref[mids : 2 * mids] = summ_v[:mids].astype(BF)
    summ_ref[2 * mids :] = (summ_k[mids:] + pltpu.roll(summ_v[mids:], fars, 0)).astype(BF)


def spread_heads(q4_ref, qt_ref, at, heads):
    width = q4_ref.shape[0] // heads
    for h in range(heads):
        rows = slice(h * width, (h + 1) * width)
        q4_ref[rows, h * FBLK : (h + 1) * FBLK] = qt_ref[rows, at : at + FBLK]


def order_kernel(
    p_ref, pt_ref, sel_ref, fcol_ref, frow_ref, wt_ref, x_ref, k0_ref, v0_ref,
    qt_ref, vt_ref, k_ref, nk_ref, nvt_ref,
):
    group = k_ref.shape[1]
    near = nk_ref.shape[0]
    k0, v0 = k0_ref[...], v0_ref[...]
    q0 = nt(wt_ref[:group], x_ref[...]).astype(BF)
    k_ref[...] = nn(p_ref[...], k0).astype(BF)
    qt_ref[...] = (nn(q0, pt_ref[...]) * 0.125).astype(BF)
    vt_ref[...] = nn(v0, pt_ref[...]).astype(BF)
    pool = sel_ref[sel_ref.shape[0] - near :]
    nk_ref[...] = (nn(pool, k0) * fcol_ref[SUMM_ROWS:, :1]).astype(BF)
    nvt_ref[...] = (nt(v0, pool) * frow_ref[:1, SUMM_ROWS:]).astype(BF)


def own_kernel(
    mix_ref, qt_ref, k_ref, vt_ref, nk_ref, nvt_ref, seen_ref,
    acc_ref, near_ref, top_ref, den_ref, q4_ref, p_ref,
):
    tok_rows, group = k_ref.shape
    heads = mix_ref.shape[1]
    width = group // heads
    q4_ref[...] = jnp.zeros_like(q4_ref)
    same = iota((FBLK, FBLK), 0) == iota((FBLK, FBLK), 1)
    nk, nvt = nk_ref[...], nvt_ref[...]
    for g in range(tok_rows // FBLK):
        at = g * FBLK
        slot = g % 2
        spread_heads(q4_ref.at[slot], qt_ref, at, heads)
        q4 = q4_ref[slot]
        bias = jnp.where(same, 0.0, seen_ref[at : at + FBLK])
        own_scores = nn(k_ref[at : at + FBLK], q4)
        near_scores = nn(nk, q4)
        scales = []
        for h in range(heads):
            lanes = slice(h * FBLK, (h + 1) * FBLK)
            part = own_scores[:, lanes] + bias
            top = jnp.max(part, axis=0, keepdims=True)
            weight = jnp.exp(part - top)
            top_ref[g : g + 1, lanes] = top
            den_ref[g : g + 1, lanes] = jnp.sum(weight, axis=0, keepdims=True)
            p_ref[slot, :FBLK, lanes] = weight.astype(BF)
            part = near_scores[:, lanes]
            weight = jnp.exp(part - jnp.max(part, axis=0, keepdims=True))
            scales.append(mix_ref[1, h] / jnp.sum(weight, axis=0, keepdims=True))
            p_ref[slot, FBLK:, lanes] = weight.astype(BF)
        own_out = nn(vt_ref[:, at : at + FBLK], p_ref[slot, :FBLK])
        near_out = nn(nvt, p_ref[slot, FBLK:])
        for h in range(heads):
            rows, lanes = slice(h * width, (h + 1) * width), slice(h * FBLK, (h + 1) * FBLK)
            acc_ref[rows, at : at + FBLK] = own_out[rows, lanes]
            near_ref[rows, at : at + FBLK] = near_out[rows, lanes] * scales[h]


def window_kernel(k_ref, vt_ref, wt_ref, wk_ref, e_ref, et_ref, *refs):
    halo_refs, refs = refs[:4], refs[4:]
    summ_refs, (kw_ref, vw_ref, ck_ref, cv_ref, all_ref, x_ref) = refs[:-6], refs[-6:]
    tok_rows, group = k_ref.shape
    quarter = x_ref.shape[1] // 4
    head = lax.axis_index("head")
    for distance, part in zip((0, 2, 1, 3), halo_refs):
        start = pl.multiple_of((head ^ distance) * quarter, quarter)
        x_ref[:, pl.ds(start, quarter)] = part[...]
    x = x_ref[...]
    kw_ref[:tok_rows] = nn(e_ref[...], nn(x, wk_ref[...]).astype(BF)).astype(BF)
    kw_ref[tok_rows:] = k_ref[...]
    vw_ref[:, :tok_rows] = nn(nt(wt_ref[group:], x).astype(BF), et_ref[...]).astype(BF)
    vw_ref[:, tok_rows:] = vt_ref[...]
    at = 0
    for part in summ_refs:
        all_ref[at : at + part.shape[0]] = part[...]
        at += part.shape[0]
    slab, slabs = lax.axis_index("seq"), lax.axis_size("seq")
    mids, fars = tok_rows // POOL2, tok_rows // POOL3
    shape = (ck_ref.shape[0], all_ref.shape[0])
    line = iota(shape, 0)
    step = 3 * mids
    turn = line // mids
    far = line - 3 * mids
    shard = slab - 1 + turn
    turned = slab if slabs == 8 else 0
    distance = jnp.where(line < 3 * mids, shard, far // fars) ^ turned
    slot = (distance >> 1) + (distance & 1) * (slabs // 2) if slabs == 8 else distance
    source = slot * step + jnp.where(line < 3 * mids, line - turn * mids, 2 * mids + far % fars)
    source = jnp.where((line >= 3 * mids) | ((shard >= 0) & (shard < slabs)), source, -2 * step)
    gathered = all_ref[...]
    ck_ref[...] = nn(ones_where(source == iota(shape, 1)), gathered).astype(BF)
    values = nn(ones_where(source + jnp.where(line < 3 * mids, mids, fars) == iota(shape, 1)), gathered)
    cv_ref[...] = jnp.transpose(values).astype(BF)


def rest_kernel(
    first, blocks, lists_ref, mix_ref, qt_ref, kw_ref, vw_ref, ck_ref, cv_ref, bias_ref,
    acc_ref, near_ref, top_ref, den_ref, out_ref, kc_ref, vc_ref, q4_ref, p_ref,
):
    group, tok_rows = qt_ref.shape
    heads = mix_ref.shape[1]
    width = group // heads
    others = FINE_K - 1
    fine = others * FBLK
    mid = 3 * (tok_rows // POOL2)
    far_at = fine + mid
    total = kc_ref.shape[1]
    for slot in range(2):
        kc_ref[slot, fine:] = ck_ref[...]
        vc_ref[slot, :, fine:] = cv_ref[...]
    q4_ref[...] = jnp.zeros_like(q4_ref)
    for index in range(blocks):
        g = first + index
        at = g * FBLK
        slot = index % 2
        biases = []
        for entry in range(others):
            start = pl.multiple_of(lists_ref[entry + 1, g] * FBLK, FBLK)
            kc_ref[slot, entry * FBLK : (entry + 1) * FBLK] = kw_ref[pl.ds(start, FBLK)]
            vc_ref[slot, :, entry * FBLK : (entry + 1) * FBLK] = vw_ref[:, pl.ds(start, FBLK)]
            biases.append(bias_ref[pl.ds(start, FBLK)])
        spread_heads(q4_ref.at[slot], qt_ref, at, heads)
        scores = nn(kc_ref[slot], q4_ref[slot])
        scales, keeps = [], []
        for h in range(heads):
            lanes = slice(h * FBLK, (h + 1) * FBLK)
            parts = [scores[e * FBLK : (e + 1) * FBLK, lanes] + biases[e] for e in range(others)]
            old_top = top_ref[g : g + 1, lanes]
            top = functools.reduce(
                jnp.maximum, [jnp.max(part, axis=0, keepdims=True) for part in parts] + [old_top]
            )
            keep = jnp.exp(old_top - top)
            den = den_ref[g : g + 1, lanes] * keep
            for e, part in enumerate(parts):
                weight = jnp.exp(part - top)
                den = den + jnp.sum(weight, axis=0, keepdims=True)
                p_ref[slot, e * FBLK : (e + 1) * FBLK, lanes] = weight.astype(BF)
            scale = mix_ref[0, h] / den
            scales.append(scale)
            keeps.append(keep * scale)
            relative = den / mix_ref[0, h]
            for level, (low, high) in enumerate(((fine, far_at), (far_at, total))):
                part = scores[low:high, lanes]
                weight = jnp.exp(part - jnp.max(part, axis=0, keepdims=True))
                share = mix_ref[level + 2, h] / jnp.sum(weight, axis=0, keepdims=True) * relative
                p_ref[slot, low:high, lanes] = (weight * share).astype(BF)
        total_out = nn(vc_ref[slot], p_ref[slot])
        rows = []
        for h in range(heads):
            pick = (slice(h * width, (h + 1) * width), slice(h * FBLK, (h + 1) * FBLK))
            mine = (pick[0], slice(at, at + FBLK))
            rows.append(total_out[pick] * scales[h] + acc_ref[mine] * keeps[h] + near_ref[mine])
        out_ref[index * FBLK : (index + 1) * FBLK] = jnp.transpose(
            jnp.concatenate(rows, axis=0)
        ).astype(BF)


def output_kernel(w_ref, *refs):
    out_ref = refs[-1]
    group = w_ref.shape[1]
    head = lax.axis_index("head")
    total = None
    for distance, part in zip((0, 2, 1, 3), refs[:4]):
        start = pl.multiple_of((head ^ distance) * group, group)
        term = nn(part[...], w_ref[pl.ds(start, group)])
        total = term if total is None else total + term
    out_ref[...] = total.astype(BF)


def local(tokens, w_query, w_key, w_value, w_out, level_mix, fine_blocks, order, mask_ids):
    tok_rows, width = tokens.shape
    slabs = lax.axis_size("seq")
    slab, head = lax.axis_index("seq"), lax.axis_index("head")
    group = w_query.shape[1]
    heads = level_mix.shape[1]
    packed = tok_rows - mask_ids.shape[1]
    near, mids, fars = tok_rows // POOL1, tok_rows // POOL2, tok_rows // POOL3
    coarse = 3 * mids + fars * slabs
    step = 3 * mids
    chosen = packed + SUMM_ROWS + near

    shape = jax.ShapeDtypeStruct
    params = pltpu.CompilerParams(vmem_limit_bytes=VMEM_LIMIT)

    def prepare():
        return pl.pallas_call(
            prepare_kernel,
            out_shape=(
                shape((tok_rows, tok_rows), BF),
                shape((tok_rows, tok_rows), BF),
                shape((chosen, tok_rows), BF),
                shape((SUMM_ROWS + near, 128), F32),
                shape((16, SUMM_ROWS + near), F32),
                shape((tok_rows, FBLK), F32),
                shape((2 * group, width), BF),
                shape((width, group), BF),
            ),
            in_specs=vmem_specs(5),
            out_specs=vmem_specs(8),
            compiler_params=params,
            cost_estimate=COST,
            name="prepare",
        )(order, mask_ids, w_query, w_value, w_key)

    def expand(seen, sources):
        return pl.pallas_call(
            functools.partial(expand_kernel, tok_rows // slabs),
            out_shape=(
                shape((tok_rows, packed), BF),
                shape((packed, tok_rows), BF),
                shape((2 * tok_rows, FBLK), F32),
            ),
            in_specs=vmem_specs(1 + len(sources)),
            out_specs=vmem_specs(3),
            compiler_params=params,
            cost_estimate=COST,
            name="expand",
        )(seen, *sources)

    pieces, prepared, before, halo = exchange_tokens(tokens, mask_ids, prepare)
    permute, permute_t, select, f_col, f_row, seen, w_t, w_k = prepared
    summ, k0, v0, rows_here = pl.pallas_call(
        functools.partial(project_kernel, len(pieces)),
        out_shape=(
            shape((step, group), BF),
            shape((tok_rows, group), BF),
            shape((group, tok_rows), BF),
            shape((tok_rows, width), BF),
        ),
        in_specs=vmem_specs(len(pieces) + 4),
        out_specs=vmem_specs(4),
        compiler_params=params,
        cost_estimate=COST,
        name="project",
    )(*pieces, w_t, w_k, select, f_col)
    if slabs == 8:
        lined = [summ] + [by_distance(summ, d) for d in (2, 4, 6)]
    else:
        lined = [summ]

    q_t, v_t, keys, near_k, near_vt = pl.pallas_call(
        order_kernel,
        out_shape=(
            shape((group, tok_rows), BF),
            shape((group, tok_rows), BF),
            shape((tok_rows, group), BF),
            shape((near, group), BF),
            shape((group, near), BF),
        ),
        in_specs=vmem_specs(9),
        out_specs=vmem_specs(5),
        compiler_params=params,
        cost_estimate=COST,
        name="order",
    )(permute, permute_t, select, f_col, f_row, w_t, rows_here, k0, v0)
    halo, near_k, *lined = lax.optimization_barrier((halo, near_k, *lined))
    halo_x = over_head(halo, X_PAIRS)
    halo_core = over_head(halo, CORE_PAIRS)
    if slabs == 8:
        places = tuple((index, 0, step, 0) for index in range(4))
        column = stacked(lined, places, group)
        column, q_t = lax.optimization_barrier((column, q_t))
        summaries = [column, by_distance(column, 1)]
    else:
        copies = jnp.broadcast_to(summ[None], (slabs, step, group))
        copies = lax.all_to_all(copies, "seq", split_axis=0, concat_axis=0, tiled=True)
        summaries = [copies.reshape(slabs * step, group)]

    blocks = tok_rows // FBLK
    acc, near_out, top, den = pl.pallas_call(
        own_kernel,
        out_shape=(
            shape((group, tok_rows), F32),
            shape((group, tok_rows), F32),
            shape((blocks, heads * FBLK), F32),
            shape((blocks, heads * FBLK), F32),
        ),
        in_specs=smem_specs(1) + vmem_specs(6),
        out_specs=vmem_specs(4),
        scratch_shapes=[
            pltpu.VMEM((2, group, heads * FBLK), BF),
            pltpu.VMEM((2, FBLK + near, heads * FBLK), BF),
        ],
        compiler_params=params,
        cost_estimate=COST,
        name="own",
    )(level_mix, q_t, keys, v_t, near_k, near_vt, seen)

    halo_x, _, *summaries = lax.optimization_barrier((halo_x, top, *summaries))
    halo_last = over_head(halo_x, CORE_PAIRS)
    seen, _ = lax.optimization_barrier((seen, top))
    spread, spread_t, bias = expand(seen, before)
    window_k, window_v, coarse_k, coarse_v = pl.pallas_call(
        window_kernel,
        out_shape=(
            shape((2 * tok_rows, group), BF),
            shape((group, 2 * tok_rows), BF),
            shape((coarse, group), BF),
            shape((group, coarse), BF),
        ),
        in_specs=vmem_specs(10 + len(summaries)),
        out_specs=vmem_specs(4),
        scratch_shapes=[pltpu.VMEM((slabs * step, group), BF), pltpu.VMEM((packed, width), BF)],
        compiler_params=params,
        cost_estimate=COST,
        name="window",
    )(keys, v_t, w_t, w_k, spread, spread_t, halo, halo_x, halo_core, halo_last, *summaries)

    total = (FINE_K - 1) * FBLK + coarse
    lists = fine_blocks.T
    parts = PARTS if sum(PARTS) == blocks else (blocks,)
    waiting, out, first = None, None, 0

    def finish(out, attended, third, second, base, after=()):
        fourth = over_head(third, CORE_PAIRS)
        rows = attended.shape[0]
        previous = [] if out is None else [out]
        height = min(2 * FBLK, rows)
        tile = pl.BlockSpec((height, group), lambda i: (i, 0))
        return pl.pallas_call(
            output_kernel,
            grid=(rows // height,),
            out_shape=shape((tok_rows, group), BF),
            in_specs=[pl.BlockSpec((width, group), lambda i: (0, 0))]
            + [tile] * 4
            + [pl.BlockSpec(memory_space=pl.ANY)] * (len(previous) + len(after)),
            out_specs=pl.BlockSpec((height, group), lambda i, base=base * FBLK // height: (i + base, 0)),
            input_output_aliases={5: 0} if previous else {},
            compiler_params=params,
            cost_estimate=COST,
            name="output",
        )(w_out, attended, third, second, fourth, *previous, *after)

    for count in parts:
        attended = pl.pallas_call(
            functools.partial(rest_kernel, first, count),
            out_shape=shape((count * FBLK, group), BF),
            in_specs=smem_specs(2) + vmem_specs(10),
            out_specs=pl.BlockSpec(memory_space=pltpu.VMEM),
            scratch_shapes=[
                pltpu.VMEM((2, total, group), BF),
                pltpu.VMEM((2, group, total), BF),
                pltpu.VMEM((2, group, heads * FBLK), BF),
                pltpu.VMEM((2, total, heads * FBLK), BF),
            ],
            compiler_params=params,
            cost_estimate=COST,
            name="rest",
        )(
            lists, level_mix, q_t, window_k, window_v, coarse_k, coarse_v, bias, acc, near_out, top, den
        )
        third = over_head(attended, X_PAIRS)
        second = over_head(attended, CORE_PAIRS)
        if waiting is not None:
            old, old_third, old_second, old_base = waiting
            old_third, attended = lax.optimization_barrier((old_third, attended))
            out = finish(out, old, old_third, old_second, old_base, [third])
        waiting = (attended, third, second, first)
        first += count
    return finish(out, *waiting)


def solution(mesh):
    placed = (
        P("seq", None),
        P(None, "head"),
        P(None, "head"),
        P(None, "head"),
        P(None, "head"),
        P(None, "head"),
        P("seq", None),
        P("seq", None),
        P("seq", None),
    )
    return jax.shard_map(
        local, mesh=mesh, in_specs=placed, out_specs=P("seq", "head"), check_vma=False
    )
```

```python
import functools

import jax
import jax.numpy as jnp
from jax import lax
from jax.experimental import pallas as pl
from jax.experimental.pallas import tpu as pltpu
from jax.sharding import PartitionSpec as P

FBLK = 128
FINE_K = 4
POOL1 = 8
POOL2 = 64
POOL3 = 512
SUMM_ROWS = 32
CODE_ROWS = 16
BF = jnp.bfloat16
F32 = jnp.float32
I32 = jnp.int32
HIDE = -1e30
VMEM_LIMIT = 24 * 1024 * 1024
LONG_BYTES = 20_000_000
COST = pl.CostEstimate(flops=1, bytes_accessed=1, transcendentals=0)
LONG = pl.CostEstimate(flops=1, bytes_accessed=LONG_BYTES, transcendentals=0)
PARTS = (2, 2, 4)

X_PAIRS = [(0, 2), (2, 0), (1, 3), (3, 1)]
CORE_PAIRS = [(0, 1), (1, 0), (2, 3), (3, 2)]


def nn(a, b):
    return lax.dot_general(a, b, (((1,), (0,)), ((), ())), preferred_element_type=F32)


def nt(a, b):
    return lax.dot_general(a, b, (((1,), (1,)), ((), ())), preferred_element_type=F32)


def iota(shape, axis):
    return lax.broadcasted_iota(I32, shape, axis)


def ones_where(condition):
    return jnp.where(condition, 1.0, 0.0).astype(BF)


def vmem_specs(count):
    return [pl.BlockSpec(memory_space=pltpu.VMEM)] * count


def smem_specs(count):
    return [pl.BlockSpec(memory_space=pltpu.SMEM)] * count


def over_head(block, pairs):
    return lax.ppermute(block, "head", pairs)


def to_next(block):
    return lax.ppermute(block, "seq", [(i, i + 1) for i in range(lax.axis_size("seq") - 1)])


def send_kernel(tokens_ref, mask_ref, *refs):
    outs, own = refs[:-1], refs[-1]
    slab, head = lax.axis_index("seq"), lax.axis_index("head")
    core = head & 1
    rows, width = own.shape
    half = width // 2
    ids = mask_ref[...]
    line = iota((CODE_ROWS, ids.shape[1]), 0)
    code = jnp.where(line == 0, ids >> 5, jnp.where(line == 1, ids & 31, 0)).astype(F32).astype(BF)
    sides = (head >> 1, head >> 1, core, core, core)
    for distance, side, out in zip((7 - core, 5 - core, 3, 2, 1), sides, outs):
        row = pl.multiple_of((slab ^ distance) * rows, rows)
        start = pl.multiple_of(side * half, half)
        out[:rows] = tokens_ref[pl.ds(row, rows), pl.ds(start, half)]
        if out.shape[0] > rows:
            out[rows : rows + CODE_ROWS] = code
    own[...] = tokens_ref[pl.ds(pl.multiple_of(slab * rows, rows), rows)]


def stack_kernel(places, *refs):
    target = refs[-1]
    at = 0
    for source, row, height, column in places:
        target[at : at + height] = refs[source][row : row + height, column : column + target.shape[1]]
        at += height


def stacked(parts, places, width, after=(), cost=COST):
    return pl.pallas_call(
        functools.partial(stack_kernel, places),
        out_shape=jax.ShapeDtypeStruct((sum(place[2] for place in places), width), BF),
        in_specs=vmem_specs(len(parts)) + [pl.BlockSpec(memory_space=pl.ANY)] * len(after),
        out_specs=pl.BlockSpec(memory_space=pltpu.VMEM),
        compiler_params=pltpu.CompilerParams(vmem_limit_bytes=VMEM_LIMIT),
        cost_estimate=cost,
        name="stack",
    )(*parts, *after)


def by_distance(block, distance):
    return lax.ppermute(block, "seq", [(i, i ^ distance) for i in range(lax.axis_size("seq"))])


def by_core(block, distances):
    heads = lax.axis_size("head")
    pairs = [
        (slab * heads + head, (slab ^ distances[head & 1]) * heads + head)
        for slab in range(lax.axis_size("seq"))
        for head in range(heads)
    ]
    return lax.ppermute(block, ("seq", "head"), pairs)


def exchange_tokens(tokens, mask_ids, prepare, expand):
    tok_rows, width = tokens.shape
    slabs = lax.axis_size("seq")
    rows = tok_rows // slabs
    if slabs != 8:
        quarter = width // 4
        split = tokens.reshape(slabs, rows, width)
        mine = lax.dynamic_slice_in_dim(split, lax.axis_index("head") * quarter, quarter, axis=2)
        first = lax.all_to_all(mine, "seq", split_axis=0, concat_axis=0, tiled=True).reshape(
            tok_rows, quarter
        )
        third = over_head(first, X_PAIRS)
        second = over_head(first, CORE_PAIRS)
        fourth = over_head(third, CORE_PAIRS)
        prepared = prepare()
        return [first, third, second, fourth], prepared, expand(prepared, [to_next(mask_ids)])
    half = width // 2
    tall = rows + CODE_ROWS
    *blocks, own = pl.pallas_call(
        send_kernel,
        out_shape=(
            jax.ShapeDtypeStruct((tall, half), BF),
            jax.ShapeDtypeStruct((tall, half), BF),
            jax.ShapeDtypeStruct((tall, half), BF),
            jax.ShapeDtypeStruct((tall, half), BF),
            jax.ShapeDtypeStruct((tall, half), BF),
            jax.ShapeDtypeStruct((rows, width), BF),
        ),
        in_specs=vmem_specs(2),
        out_specs=vmem_specs(6),
        compiler_params=pltpu.CompilerParams(vmem_limit_bytes=60 * 1024 * 1024),
        cost_estimate=COST,
        name="send",
    )(tokens, mask_ids)
    routes = ((7, 6), (5, 4), (3, 3), (2, 2), (1, 1))
    one, two, three, four, five = [by_core(block, route) for block, route in zip(blocks, routes)]
    prepared = prepare()
    one, _ = lax.optimization_barrier((one, prepared))
    first_x = over_head(stacked((one,), ((0, 0, rows, 0),), half, (three, four, five)), X_PAIRS)
    two, first_x = lax.optimization_barrier((two, first_x))
    two = stacked((two,), ((0, 0, rows, 0),), half)
    far = [one, two]
    far_core = [over_head(part, CORE_PAIRS) for part in far]
    far_x = [first_x, over_head(two, X_PAIRS)]
    near = [three, four, five]
    near_core = [over_head(part, CORE_PAIRS) for part in near]
    expanded = expand(prepared, [one, far_core[0], three, five])
    far_x[1], _ = lax.optimization_barrier((far_x[1], expanded))
    far_last = [over_head(part, CORE_PAIRS) for part in far_x]
    return far + far_x + far_core + far_last + near + near_core + [own], prepared, expanded


def column(row, lanes=128):
    return jnp.transpose(jnp.broadcast_to(row.astype(F32), (lanes, row.shape[1]))).astype(I32)


def ranks(ids, tok_rows, lanes=128):
    hidden = column(ids)
    parts = []
    for at in range(0, tok_rows, lanes):
        time = iota((1, lanes), 1) + at
        count = jnp.sum(jnp.where(hidden < time, 1.0, 0.0), axis=0, keepdims=True)
        here = jnp.sum(jnp.where(hidden == time, 1.0, 0.0), axis=0, keepdims=True)
        parts.append(jnp.where(here == 0.0, time - count.astype(I32), -1))
    return jnp.concatenate(parts, axis=1)


def prepare_kernel(
    order_ref, mask_ref, wq_ref, wv_ref, wk_in,
    p_ref, pt_ref, sel_ref, fcol_ref, frow_ref, bias_ref, wt_ref, wk_ref,
):
    slab, slabs = lax.axis_index("seq"), lax.axis_size("seq")
    tok_rows = order_ref.shape[1]
    packed = tok_rows - mask_ref.shape[1]
    flip = (slab ^ 7) * (tok_rows // slabs) if slabs == 8 else 0
    mids = tok_rows // POOL2
    group = wq_ref.shape[1]
    lanes = 128

    place = order_ref[...] ^ flip
    place_column = column(place)
    for at in range(0, tok_rows, lanes):
        p_ref[:, at : at + lanes] = ones_where(place_column == iota((tok_rows, lanes), 1) + at)
        pt_ref[at : at + lanes] = ones_where(iota((lanes, tok_rows), 0) + at == place)
    rank = ranks(mask_ref[...], tok_rows)
    time = jnp.where(rank >= 0, iota((1, tok_rows), 1), -1) + 1
    line = iota((16, tok_rows), 0)
    stack = jnp.where(
        line == 0,
        time >> 5,
        jnp.where(
            line == 1,
            time & 31,
            jnp.where(line == 2, (rank + 1) >> 5, jnp.where(line == 3, (rank + 1) & 31, 0)),
        ),
    )
    moved = nn(stack.astype(F32).astype(BF), p_ref[...]).astype(I32)
    time_here = (moved[0:1] << 5) + moved[1:2] - 1
    rank_here = (moved[2:3] << 5) + moved[3:4] - 1
    for at in range(0, packed, lanes):
        sel_ref[at : at + lanes] = ones_where(iota((lanes, tok_rows), 0) + at == rank_here)
    line = iota((SUMM_ROWS, tok_rows), 0)
    sel_ref[packed : packed + SUMM_ROWS] = ones_where(
        ((time_here >> 6) == line) | (((time_here >> 9) + mids == line) & (time_here >= 0))
    )
    lead = packed + SUMM_ROWS
    near = sel_ref.shape[0] - lead
    sel_ref[lead:] = ones_where((time_here >> 3) == iota((near, tok_rows), 0))
    pools = sel_ref[packed:]
    fcol_ref[...] = 1.0 / jnp.sqrt(jnp.maximum(nn(pools, jnp.ones((tok_rows, lanes), BF)), 1.0))
    frow_ref[...] = 1.0 / jnp.sqrt(jnp.maximum(nt(jnp.ones((16, tok_rows), BF), pools), 1.0))
    bias_ref[...] = jnp.where(column(rank) >= 0, 0.0, HIDE)
    wt_ref[:group] = jnp.transpose(wq_ref[...])
    wt_ref[group:] = jnp.transpose(wv_ref[...])
    wk_ref[...] = wk_in[...]


def mask_before(refs, rows):
    if len(refs) == 1:
        return refs[0][...]
    far, far_core, near_three, near_one = refs
    core = lax.axis_index("head") & 1

    def digits(ref):
        return ref[rows : rows + CODE_ROWS // 2].astype(F32)

    three, one = digits(near_three), digits(near_one)
    seven = jnp.where(core == 0, digits(far), digits(far_core))
    slab = lax.axis_index("seq")
    distance = slab ^ (slab - 1)

    code = jnp.where(distance == 1, one, jnp.where(distance == 3, three, seven)).astype(I32)
    return (code[0:1] << 5) + code[1:2]


def expand_kernel(rows, seen_ref, *refs):
    code_refs, (e_ref, et_ref, bias_ref) = refs[:-3], refs[-3:]
    tok_rows = seen_ref.shape[0]
    rank = ranks(mask_before(code_refs, rows), tok_rows)
    rank = jnp.where(lax.axis_index("seq") > 0, rank, -1)
    rank_column = column(rank)
    bias_ref[:tok_rows] = jnp.where(rank_column >= 0, 0.0, HIDE)
    bias_ref[tok_rows:] = seen_ref[...]
    for at in range(0, et_ref.shape[0], FBLK):
        e_ref[:, at : at + FBLK] = ones_where(rank_column == iota((tok_rows, FBLK), 1) + at)
        et_ref[at : at + FBLK] = ones_where(iota((FBLK, tok_rows), 0) + at == rank)


def assemble(piece_refs, x_ref):
    head = lax.axis_index("head")
    tok_rows, width = x_ref.shape
    if len(piece_refs) == 4:
        quarter = width // 4
        for distance, piece in zip((0, 2, 1, 3), piece_refs):
            start = pl.multiple_of((head ^ distance) * quarter, quarter)
            x_ref[:, pl.ds(start, quarter)] = piece[...]
        return
    far_refs, near_refs, own = piece_refs[:8], piece_refs[8:14], piece_refs[14]
    rows, half = own.shape[0], width // 2
    core, side = head & 1, head >> 1
    for index, piece in enumerate(far_refs):
        turn, crossed = (index // 2) % 2, index // 4
        row = pl.multiple_of((2 * (index % 2) + (core ^ crossed)) * rows, rows)
        start = pl.multiple_of((side ^ turn) * half, half)
        x_ref[pl.ds(row, rows), pl.ds(start, half)] = piece[:rows]
    for index, piece in enumerate(near_refs):
        row = (4 + index % 3) * rows
        start = pl.multiple_of((core ^ (index // 3)) * half, half)
        x_ref[row : row + rows, pl.ds(start, half)] = piece[:rows]
    x_ref[7 * rows :] = own[...]


def project_kernel(count, *refs):
    piece_refs, refs = refs[:count], refs[count:]
    wt_ref, wk_ref, sel_ref, fcol_ref, comp_ref, summ_ref, k_ref, v_ref, x_ref = refs
    assemble(piece_refs, x_ref)
    group = wk_ref.shape[1]
    packed = comp_ref.shape[0] // 2
    lead = packed + SUMM_ROWS
    x = x_ref[...]
    keys = nn(x, wk_ref[...]).astype(BF)
    k_ref[...] = keys
    vt = nt(wt_ref[group:], x).astype(BF)
    v_ref[...] = vt
    sel = sel_ref[:lead]
    kl = nn(sel, keys)
    vl = nt(vt, sel)
    comp_ref[:packed] = kl[:packed].astype(BF)
    vc = vl[:, :packed].astype(BF)
    for part in range(packed // group):
        comp_ref[packed + part * group : packed + (part + 1) * group] = vc[
            :, part * group : (part + 1) * group
        ]
    factor = fcol_ref[:SUMM_ROWS, :1]
    summ_k = kl[packed:] * factor
    tail = jnp.concatenate(
        [vl[:, packed:], jnp.zeros((group, 128 - SUMM_ROWS), F32)], axis=1
    )
    summ_v = jnp.transpose(tail)[:SUMM_ROWS] * factor
    mids = x_ref.shape[0] // POOL2
    fars = x_ref.shape[0] // POOL3
    summ_ref[:mids] = summ_k[:mids].astype(BF)
    summ_ref[mids : 2 * mids] = summ_v[:mids].astype(BF)
    summ_ref[2 * mids :] = (summ_k[mids:] + pltpu.roll(summ_v[mids:], fars, 0)).astype(BF)


def spread_heads(q4_ref, qt_ref, at, heads):
    width = q4_ref.shape[0] // heads
    for h in range(heads):
        rows = slice(h * width, (h + 1) * width)
        q4_ref[rows, h * FBLK : (h + 1) * FBLK] = qt_ref[rows, at : at + FBLK]


def order_kernel(
    p_ref, pt_ref, sel_ref, fcol_ref, frow_ref, wt_ref, x_ref, k0_ref, v0_ref,
    qt_ref, vt_ref, k_ref, nk_ref, nvt_ref,
):
    group = k_ref.shape[1]
    near = nk_ref.shape[0]
    k0, v0 = k0_ref[...], v0_ref[...]
    q0 = nt(wt_ref[:group], x_ref[...]).astype(BF)
    k_ref[...] = nn(p_ref[...], k0).astype(BF)
    qt_ref[...] = (nn(q0, pt_ref[...]) * 0.125).astype(BF)
    vt_ref[...] = nn(v0, pt_ref[...]).astype(BF)
    pool = sel_ref[sel_ref.shape[0] - near :]
    nk_ref[...] = (nn(pool, k0) * fcol_ref[SUMM_ROWS:, :1]).astype(BF)
    nvt_ref[...] = (nt(v0, pool) * frow_ref[:1, SUMM_ROWS:]).astype(BF)


def own_kernel(
    mix_ref, qt_ref, k_ref, vt_ref, nk_ref, nvt_ref, seen_ref,
    acc_ref, near_ref, top_ref, den_ref, q4_ref, p_ref,
):
    tok_rows, group = k_ref.shape
    heads = mix_ref.shape[1]
    width = group // heads
    q4_ref[...] = jnp.zeros_like(q4_ref)
    same = iota((FBLK, FBLK), 0) == iota((FBLK, FBLK), 1)
    nk, nvt = nk_ref[...], nvt_ref[...]
    for g in range(tok_rows // FBLK):
        at = g * FBLK
        slot = g % 2
        spread_heads(q4_ref.at[slot], qt_ref, at, heads)
        q4 = q4_ref[slot]
        bias = jnp.where(same, 0.0, seen_ref[at : at + FBLK])
        own_scores = nn(k_ref[at : at + FBLK], q4)
        near_scores = nn(nk, q4)
        scales = []
        for h in range(heads):
            lanes = slice(h * FBLK, (h + 1) * FBLK)
            part = own_scores[:, lanes] + bias
            top = jnp.max(part, axis=0, keepdims=True)
            weight = jnp.exp(part - top)
            top_ref[g : g + 1, lanes] = top
            den_ref[g : g + 1, lanes] = jnp.sum(weight, axis=0, keepdims=True)
            p_ref[slot, :FBLK, lanes] = weight.astype(BF)
            part = near_scores[:, lanes]
            weight = jnp.exp(part - jnp.max(part, axis=0, keepdims=True))
            scales.append(mix_ref[1, h] / jnp.sum(weight, axis=0, keepdims=True))
            p_ref[slot, FBLK:, lanes] = weight.astype(BF)
        own_out = nn(vt_ref[:, at : at + FBLK], p_ref[slot, :FBLK])
        near_out = nn(nvt, p_ref[slot, FBLK:])
        for h in range(heads):
            rows, lanes = slice(h * width, (h + 1) * width), slice(h * FBLK, (h + 1) * FBLK)
            acc_ref[rows, at : at + FBLK] = own_out[rows, lanes]
            near_ref[rows, at : at + FBLK] = near_out[rows, lanes] * scales[h]


def window_kernel(k_ref, vt_ref, comp_ref, e_ref, et_ref, *refs):
    summ_refs, (kw_ref, vw_ref, ck_ref, cv_ref, all_ref) = refs[:-5], refs[-5:]
    tok_rows, group = k_ref.shape
    packed = e_ref.shape[1]
    kw_ref[:tok_rows] = nn(e_ref[...], comp_ref[:packed]).astype(BF)
    kw_ref[tok_rows:] = k_ref[...]
    prev = None
    for part in range(packed // group):
        term = nn(
            comp_ref[packed + part * group : packed + (part + 1) * group],
            et_ref[part * group : (part + 1) * group],
        )
        prev = term if prev is None else prev + term
    vw_ref[:, :tok_rows] = prev.astype(BF)
    vw_ref[:, tok_rows:] = vt_ref[...]
    at = 0
    for part in summ_refs:
        all_ref[at : at + part.shape[0]] = part[...]
        at += part.shape[0]
    slab, slabs = lax.axis_index("seq"), lax.axis_size("seq")
    mids, fars = tok_rows // POOL2, tok_rows // POOL3
    shape = (ck_ref.shape[0], all_ref.shape[0])
    line = iota(shape, 0)
    step = 3 * mids
    turn = line // mids
    far = line - 3 * mids
    shard = slab - 1 + turn
    turned = slab if slabs == 8 else 0
    distance = jnp.where(line < 3 * mids, shard, far // fars) ^ turned
    slot = (distance >> 1) + (distance & 1) * (slabs // 2) if slabs == 8 else distance
    source = slot * step + jnp.where(line < 3 * mids, line - turn * mids, 2 * mids + far % fars)
    source = jnp.where((line >= 3 * mids) | ((shard >= 0) & (shard < slabs)), source, -2 * step)
    gathered = all_ref[...]
    ck_ref[...] = nn(ones_where(source == iota(shape, 1)), gathered).astype(BF)
    values = nn(ones_where(source + jnp.where(line < 3 * mids, mids, fars) == iota(shape, 1)), gathered)
    cv_ref[...] = jnp.transpose(values).astype(BF)


def rest_kernel(
    first, blocks, lists_ref, mix_ref, qt_ref, kw_ref, vw_ref, ck_ref, cv_ref, bias_ref,
    acc_ref, near_ref, top_ref, den_ref, out_ref, kc_ref, vc_ref, q4_ref, p_ref,
):
    group, tok_rows = qt_ref.shape
    heads = mix_ref.shape[1]
    width = group // heads
    others = FINE_K - 1
    fine = others * FBLK
    mid = 3 * (tok_rows // POOL2)
    far_at = fine + mid
    total = kc_ref.shape[1]
    for slot in range(2):
        kc_ref[slot, fine:] = ck_ref[...]
        vc_ref[slot, :, fine:] = cv_ref[...]
    q4_ref[...] = jnp.zeros_like(q4_ref)
    for index in range(blocks):
        g = first + index
        at = g * FBLK
        slot = index % 2
        biases = []
        for entry in range(others):
            start = pl.multiple_of(lists_ref[entry + 1, g] * FBLK, FBLK)
            kc_ref[slot, entry * FBLK : (entry + 1) * FBLK] = kw_ref[pl.ds(start, FBLK)]
            vc_ref[slot, :, entry * FBLK : (entry + 1) * FBLK] = vw_ref[:, pl.ds(start, FBLK)]
            biases.append(bias_ref[pl.ds(start, FBLK)])
        spread_heads(q4_ref.at[slot], qt_ref, at, heads)
        scores = nn(kc_ref[slot], q4_ref[slot])
        scales, keeps = [], []
        for h in range(heads):
            lanes = slice(h * FBLK, (h + 1) * FBLK)
            parts = [scores[e * FBLK : (e + 1) * FBLK, lanes] + biases[e] for e in range(others)]
            old_top = top_ref[g : g + 1, lanes]
            top = functools.reduce(
                jnp.maximum, [jnp.max(part, axis=0, keepdims=True) for part in parts] + [old_top]
            )
            keep = jnp.exp(old_top - top)
            den = den_ref[g : g + 1, lanes] * keep
            for e, part in enumerate(parts):
                weight = jnp.exp(part - top)
                den = den + jnp.sum(weight, axis=0, keepdims=True)
                p_ref[slot, e * FBLK : (e + 1) * FBLK, lanes] = weight.astype(BF)
            scale = mix_ref[0, h] / den
            scales.append(scale)
            keeps.append(keep * scale)
            relative = den / mix_ref[0, h]
            for level, (low, high) in enumerate(((fine, far_at), (far_at, total))):
                part = scores[low:high, lanes]
                weight = jnp.exp(part - jnp.max(part, axis=0, keepdims=True))
                share = mix_ref[level + 2, h] / jnp.sum(weight, axis=0, keepdims=True) * relative
                p_ref[slot, low:high, lanes] = (weight * share).astype(BF)
        total_out = nn(vc_ref[slot], p_ref[slot])
        rows = []
        for h in range(heads):
            pick = (slice(h * width, (h + 1) * width), slice(h * FBLK, (h + 1) * FBLK))
            mine = (pick[0], slice(at, at + FBLK))
            rows.append(total_out[pick] * scales[h] + acc_ref[mine] * keeps[h] + near_ref[mine])
        out_ref[index * FBLK : (index + 1) * FBLK] = jnp.transpose(
            jnp.concatenate(rows, axis=0)
        ).astype(BF)


def output_kernel(w_ref, *refs):
    out_ref = refs[-1]
    group = w_ref.shape[1]
    head = lax.axis_index("head")
    total = None
    for distance, part in zip((0, 2, 1, 3), refs[:4]):
        start = pl.multiple_of((head ^ distance) * group, group)
        term = nn(part[...], w_ref[pl.ds(start, group)])
        total = term if total is None else total + term
    out_ref[...] = total.astype(BF)


def local(tokens, w_query, w_key, w_value, w_out, level_mix, fine_blocks, order, mask_ids):
    tok_rows, width = tokens.shape
    slabs = lax.axis_size("seq")
    slab, head = lax.axis_index("seq"), lax.axis_index("head")
    group = w_query.shape[1]
    heads = level_mix.shape[1]
    packed = tok_rows - mask_ids.shape[1]
    near, mids, fars = tok_rows // POOL1, tok_rows // POOL2, tok_rows // POOL3
    coarse = 3 * mids + fars * slabs
    step = 3 * mids
    chosen = packed + SUMM_ROWS + near

    shape = jax.ShapeDtypeStruct
    params = pltpu.CompilerParams(vmem_limit_bytes=VMEM_LIMIT)

    def prepare():
        return pl.pallas_call(
            prepare_kernel,
            out_shape=(
                shape((tok_rows, tok_rows), BF),
                shape((tok_rows, tok_rows), BF),
                shape((chosen, tok_rows), BF),
                shape((SUMM_ROWS + near, 128), F32),
                shape((16, SUMM_ROWS + near), F32),
                shape((tok_rows, FBLK), F32),
                shape((2 * group, width), BF),
                shape((width, group), BF),
            ),
            in_specs=vmem_specs(5),
            out_specs=vmem_specs(8),
            compiler_params=params,
            cost_estimate=COST,
            name="prepare",
        )(order, mask_ids, w_query, w_value, w_key)

    def expand(prepared, sources):
        return pl.pallas_call(
            functools.partial(expand_kernel, tok_rows // slabs),
            out_shape=(
                shape((tok_rows, packed), BF),
                shape((packed, tok_rows), BF),
                shape((2 * tok_rows, FBLK), F32),
            ),
            in_specs=vmem_specs(1 + len(sources)),
            out_specs=vmem_specs(3),
            compiler_params=params,
            cost_estimate=COST,
            name="expand",
        )(prepared[5], *sources)

    pieces, prepared, expanded = exchange_tokens(tokens, mask_ids, prepare, expand)
    permute, permute_t, select, f_col, f_row, seen, w_t, w_k = prepared
    spread, spread_t, bias = expanded
    comp, summ, k0, v0, rows_here = pl.pallas_call(
        functools.partial(project_kernel, len(pieces)),
        out_shape=(
            shape((2 * packed, group), BF),
            shape((step, group), BF),
            shape((tok_rows, group), BF),
            shape((group, tok_rows), BF),
            shape((tok_rows, width), BF),
        ),
        in_specs=vmem_specs(len(pieces) + 4),
        out_specs=vmem_specs(5),
        compiler_params=params,
        cost_estimate=COST,
        name="project",
    )(*pieces, w_t, w_k, select, f_col)
    if slabs == 8:
        lined = [summ] + [by_distance(summ, d) for d in (2, 4, 6)]
    comp_before = to_next(comp)

    q_t, v_t, keys, near_k, near_vt = pl.pallas_call(
        order_kernel,
        out_shape=(
            shape((group, tok_rows), BF),
            shape((group, tok_rows), BF),
            shape((tok_rows, group), BF),
            shape((near, group), BF),
            shape((group, near), BF),
        ),
        in_specs=vmem_specs(9),
        out_specs=vmem_specs(5),
        compiler_params=params,
        cost_estimate=COST,
        name="order",
    )(permute, permute_t, select, f_col, f_row, w_t, rows_here, k0, v0)
    blocks = tok_rows // FBLK
    acc, near_out, top, den = pl.pallas_call(
        own_kernel,
        out_shape=(
            shape((group, tok_rows), F32),
            shape((group, tok_rows), F32),
            shape((blocks, heads * FBLK), F32),
            shape((blocks, heads * FBLK), F32),
        ),
        in_specs=smem_specs(1) + vmem_specs(6),
        out_specs=vmem_specs(4),
        scratch_shapes=[
            pltpu.VMEM((2, group, heads * FBLK), BF),
            pltpu.VMEM((2, FBLK + near, heads * FBLK), BF),
        ],
        compiler_params=params,
        cost_estimate=COST,
        name="own",
    )(level_mix, q_t, keys, v_t, near_k, near_vt, seen)

    if slabs == 8:
        places = tuple((index, 0, step, 0) for index in range(4))
        column = stacked(lined, places, group, (top,))
        summaries = [column, by_distance(column, 1)]
    else:
        copies = jnp.broadcast_to(summ[None], (slabs, step, group))
        copies = lax.all_to_all(copies, "seq", split_axis=0, concat_axis=0, tiled=True)
        summaries = [copies.reshape(slabs * step, group)]

    window_k, window_v, coarse_k, coarse_v = pl.pallas_call(
        window_kernel,
        out_shape=(
            shape((2 * tok_rows, group), BF),
            shape((group, 2 * tok_rows), BF),
            shape((coarse, group), BF),
            shape((group, coarse), BF),
        ),
        in_specs=vmem_specs(5 + len(summaries)),
        out_specs=vmem_specs(4),
        scratch_shapes=[pltpu.VMEM((slabs * step, group), BF)],
        compiler_params=params,
        cost_estimate=COST,
        name="window",
    )(keys, v_t, comp_before, spread, spread_t, *summaries)

    total = (FINE_K - 1) * FBLK + coarse
    lists = fine_blocks.T
    parts = PARTS if sum(PARTS) == blocks else (blocks,)
    waiting, out, first = None, None, 0

    def finish(out, attended, third, second, base, after=()):
        fourth = over_head(third, CORE_PAIRS)
        rows = attended.shape[0]
        previous = [] if out is None else [out]
        height = min(2 * FBLK, rows)
        tile = pl.BlockSpec((height, group), lambda i: (i, 0))
        return pl.pallas_call(
            output_kernel,
            grid=(rows // height,),
            out_shape=shape((tok_rows, group), BF),
            in_specs=[pl.BlockSpec((width, group), lambda i: (0, 0))]
            + [tile] * 4
            + [pl.BlockSpec(memory_space=pl.ANY)] * (len(previous) + len(after)),
            out_specs=pl.BlockSpec((height, group), lambda i, base=base * FBLK // height: (i + base, 0)),
            input_output_aliases={5: 0} if previous else {},
            compiler_params=params,
            cost_estimate=COST,
            name="output",
        )(w_out, attended, third, second, fourth, *previous, *after)

    for count in parts:
        attended = pl.pallas_call(
            functools.partial(rest_kernel, first, count),
            out_shape=shape((count * FBLK, group), BF),
            in_specs=smem_specs(2) + vmem_specs(10),
            out_specs=pl.BlockSpec(memory_space=pltpu.VMEM),
            scratch_shapes=[
                pltpu.VMEM((2, total, group), BF),
                pltpu.VMEM((2, group, total), BF),
                pltpu.VMEM((2, group, heads * FBLK), BF),
                pltpu.VMEM((2, total, heads * FBLK), BF),
            ],
            compiler_params=params,
            cost_estimate=COST,
            name="rest",
        )(
            lists, level_mix, q_t, window_k, window_v, coarse_k, coarse_v, bias, acc, near_out, top, den
        )
        third = over_head(attended, X_PAIRS)
        second = over_head(attended, CORE_PAIRS)
        if waiting is not None:
            old, old_third, old_second, old_base = waiting
            old_third, attended = lax.optimization_barrier((old_third, attended))
            out = finish(out, old, old_third, old_second, old_base, [third])
        waiting = (attended, third, second, first)
        first += count
    return finish(out, *waiting)


def solution(mesh):
    placed = (
        P("seq", None),
        P(None, "head"),
        P(None, "head"),
        P(None, "head"),
        P(None, "head"),
        P(None, "head"),
        P("seq", None),
        P("seq", None),
        P("seq", None),
    )
    return jax.shard_map(
        local, mesh=mesh, in_specs=placed, out_specs=P("seq", "head"), check_vma=False
    )
```

```python
import functools

import jax
import jax.numpy as jnp
from jax import lax
from jax.experimental import pallas as pl
from jax.experimental.pallas import tpu as pltpu
from jax.sharding import PartitionSpec as P

FBLK = 128
FINE_K = 4
POOL1 = 8
POOL2 = 64
POOL3 = 512
SUMM_ROWS = 32
CODE_ROWS = 16
BF = jnp.bfloat16
F32 = jnp.float32
I32 = jnp.int32
HIDE = -1e30
VMEM_LIMIT = 24 * 1024 * 1024
LONG_BYTES = 20_000_000
COST = pl.CostEstimate(flops=1, bytes_accessed=1, transcendentals=0)
LONG = pl.CostEstimate(flops=1, bytes_accessed=LONG_BYTES, transcendentals=0)
PARTS = (4, 4)

X_PAIRS = [(0, 2), (2, 0), (1, 3), (3, 1)]
CORE_PAIRS = [(0, 1), (1, 0), (2, 3), (3, 2)]


def nn(a, b):
    return lax.dot_general(a, b, (((1,), (0,)), ((), ())), preferred_element_type=F32)


def nt(a, b):
    return lax.dot_general(a, b, (((1,), (1,)), ((), ())), preferred_element_type=F32)


def iota(shape, axis):
    return lax.broadcasted_iota(I32, shape, axis)


def ones_where(condition):
    return jnp.where(condition, 1.0, 0.0).astype(BF)


def vmem_specs(count):
    return [pl.BlockSpec(memory_space=pltpu.VMEM)] * count


def smem_specs(count):
    return [pl.BlockSpec(memory_space=pltpu.SMEM)] * count


def over_head(block, pairs):
    return lax.ppermute(block, "head", pairs)


def to_next(block):
    return lax.ppermute(block, "seq", [(i, i + 1) for i in range(lax.axis_size("seq") - 1)])


def send_kernel(tokens_ref, mask_ref, *refs):
    outs, own = refs[:-1], refs[-1]
    slab, head = lax.axis_index("seq"), lax.axis_index("head")
    core = head & 1
    rows, width = own.shape
    half = width // 2
    ids = mask_ref[...]
    line = iota((CODE_ROWS, ids.shape[1]), 0)
    code = jnp.where(line == 0, ids >> 5, jnp.where(line == 1, ids & 31, 0)).astype(F32).astype(BF)
    sides = (head >> 1, head >> 1, core, core, core)
    for distance, side, out in zip((7 - core, 5 - core, 3, 2, 1), sides, outs):
        row = pl.multiple_of((slab ^ distance) * rows, rows)
        start = pl.multiple_of(side * half, half)
        out[:rows] = tokens_ref[pl.ds(row, rows), pl.ds(start, half)]
        if out.shape[0] > rows:
            out[rows : rows + CODE_ROWS] = code
    own[...] = tokens_ref[pl.ds(pl.multiple_of(slab * rows, rows), rows)]


def stack_kernel(places, *refs):
    target = refs[-1]
    at = 0
    for source, row, height, column in places:
        target[at : at + height] = refs[source][row : row + height, column : column + target.shape[1]]
        at += height


def stacked(parts, places, width, after=(), cost=COST):
    return pl.pallas_call(
        functools.partial(stack_kernel, places),
        out_shape=jax.ShapeDtypeStruct((sum(place[2] for place in places), width), BF),
        in_specs=vmem_specs(len(parts)) + [pl.BlockSpec(memory_space=pl.ANY)] * len(after),
        out_specs=pl.BlockSpec(memory_space=pltpu.VMEM),
        compiler_params=pltpu.CompilerParams(vmem_limit_bytes=VMEM_LIMIT),
        cost_estimate=cost,
        name="stack",
    )(*parts, *after)


def packed_rows(select, packed, quarter, parts):
    return pl.pallas_call(
        pack_kernel,
        out_shape=jax.ShapeDtypeStruct((packed, quarter), BF),
        in_specs=vmem_specs(1 + len(parts)),
        out_specs=pl.BlockSpec(memory_space=pltpu.VMEM),
        scratch_shapes=[pltpu.VMEM((select.shape[1], quarter), BF)],
        compiler_params=pltpu.CompilerParams(vmem_limit_bytes=VMEM_LIMIT),
        cost_estimate=COST,
        name="pack",
    )(select, *parts)


def by_distance(block, distance):
    return lax.ppermute(block, "seq", [(i, i ^ distance) for i in range(lax.axis_size("seq"))])


def by_core(block, distances):
    heads = lax.axis_size("head")
    pairs = [
        (slab * heads + head, (slab ^ distances[head & 1]) * heads + head)
        for slab in range(lax.axis_size("seq"))
        for head in range(heads)
    ]
    return lax.ppermute(block, ("seq", "head"), pairs)


def exchange_tokens(tokens, mask_ids, prepare, expand):
    tok_rows, width = tokens.shape
    slabs = lax.axis_size("seq")
    rows = tok_rows // slabs
    if slabs != 8:
        quarter = width // 4
        split = tokens.reshape(slabs, rows, width)
        mine = lax.dynamic_slice_in_dim(split, lax.axis_index("head") * quarter, quarter, axis=2)
        first = lax.all_to_all(mine, "seq", split_axis=0, concat_axis=0, tiled=True).reshape(
            tok_rows, quarter
        )
        third = over_head(first, X_PAIRS)
        second = over_head(first, CORE_PAIRS)
        fourth = over_head(third, CORE_PAIRS)
        prepared = prepare()
        halo = to_next(packed_rows(prepared[2], tok_rows - mask_ids.shape[1], quarter, [first]))
        expanded = expand(prepared, [to_next(mask_ids)])
        return [first, third, second, fourth], prepared, expanded, halo
    half = width // 2
    tall = rows + CODE_ROWS
    *blocks, own = pl.pallas_call(
        send_kernel,
        out_shape=(
            jax.ShapeDtypeStruct((tall, half), BF),
            jax.ShapeDtypeStruct((tall, half), BF),
            jax.ShapeDtypeStruct((tall, half), BF),
            jax.ShapeDtypeStruct((tall, half), BF),
            jax.ShapeDtypeStruct((tall, half), BF),
            jax.ShapeDtypeStruct((rows, width), BF),
        ),
        in_specs=vmem_specs(2),
        out_specs=vmem_specs(6),
        compiler_params=pltpu.CompilerParams(vmem_limit_bytes=60 * 1024 * 1024),
        cost_estimate=COST,
        name="send",
    )(tokens, mask_ids)
    routes = ((7, 6), (5, 4), (3, 3), (2, 2), (1, 1))
    one, two, three, four, five = [by_core(block, route) for block, route in zip(blocks, routes)]
    prepared = prepare()
    one, _ = lax.optimization_barrier((one, prepared))
    first_x = over_head(stacked((one,), ((0, 0, rows, 0),), half, (three, four, five)), X_PAIRS)
    two, first_x = lax.optimization_barrier((two, first_x))
    two = stacked((two,), ((0, 0, rows, 0),), half)
    far = [one, two]
    far_core = [over_head(part, CORE_PAIRS) for part in far]
    far_x = [first_x, over_head(two, X_PAIRS)]
    near = [three, four, five]
    near_core = [over_head(part, CORE_PAIRS) for part in near]
    expanded = expand(prepared, [one, far_core[0], three, five])
    halo = packed_rows(
        prepared[2], tok_rows - mask_ids.shape[1], half // 2, far + far_core + near + near_core + [own]
    )
    far_x[1], _, _ = lax.optimization_barrier((far_x[1], expanded, halo))
    halo = to_next(halo)
    far_last = [over_head(part, CORE_PAIRS) for part in far_x]
    return far + far_x + far_core + far_last + near + near_core + [own], prepared, expanded, halo


def column(row, lanes=128):
    return jnp.transpose(jnp.broadcast_to(row.astype(F32), (lanes, row.shape[1]))).astype(I32)


def ranks(ids, tok_rows, lanes=128):
    hidden = column(ids)
    parts = []
    for at in range(0, tok_rows, lanes):
        time = iota((1, lanes), 1) + at
        count = jnp.sum(jnp.where(hidden < time, 1.0, 0.0), axis=0, keepdims=True)
        here = jnp.sum(jnp.where(hidden == time, 1.0, 0.0), axis=0, keepdims=True)
        parts.append(jnp.where(here == 0.0, time - count.astype(I32), -1))
    return jnp.concatenate(parts, axis=1)


def prepare_kernel(
    order_ref, mask_ref, wq_ref, wv_ref, wk_in,
    p_ref, pt_ref, sel_ref, fcol_ref, frow_ref, bias_ref, wt_ref, wk_ref,
):
    slab, slabs = lax.axis_index("seq"), lax.axis_size("seq")
    tok_rows = order_ref.shape[1]
    packed = tok_rows - mask_ref.shape[1]
    flip = (slab ^ 7) * (tok_rows // slabs) if slabs == 8 else 0
    mids = tok_rows // POOL2
    group = wq_ref.shape[1]
    lanes = 128

    place = order_ref[...] ^ flip
    place_column = column(place)
    for at in range(0, tok_rows, lanes):
        p_ref[:, at : at + lanes] = ones_where(place_column == iota((tok_rows, lanes), 1) + at)
        pt_ref[at : at + lanes] = ones_where(iota((lanes, tok_rows), 0) + at == place)
    rank = ranks(mask_ref[...], tok_rows)
    time = jnp.where(rank >= 0, iota((1, tok_rows), 1), -1) + 1
    line = iota((16, tok_rows), 0)
    stack = jnp.where(
        line == 0,
        time >> 5,
        jnp.where(
            line == 1,
            time & 31,
            jnp.where(line == 2, (rank + 1) >> 5, jnp.where(line == 3, (rank + 1) & 31, 0)),
        ),
    )
    moved = nn(stack.astype(F32).astype(BF), p_ref[...]).astype(I32)
    time_here = (moved[0:1] << 5) + moved[1:2] - 1
    rank_here = (moved[2:3] << 5) + moved[3:4] - 1
    for at in range(0, packed, lanes):
        sel_ref[at : at + lanes] = ones_where(iota((lanes, tok_rows), 0) + at == rank_here)
    line = iota((SUMM_ROWS, tok_rows), 0)
    sel_ref[packed : packed + SUMM_ROWS] = ones_where(
        ((time_here >> 6) == line) | (((time_here >> 9) + mids == line) & (time_here >= 0))
    )
    lead = packed + SUMM_ROWS
    near = sel_ref.shape[0] - lead
    sel_ref[lead:] = ones_where((time_here >> 3) == iota((near, tok_rows), 0))
    pools = sel_ref[packed:]
    fcol_ref[...] = 1.0 / jnp.sqrt(jnp.maximum(nn(pools, jnp.ones((tok_rows, lanes), BF)), 1.0))
    frow_ref[...] = 1.0 / jnp.sqrt(jnp.maximum(nt(jnp.ones((16, tok_rows), BF), pools), 1.0))
    bias_ref[...] = jnp.where(column(rank) >= 0, 0.0, HIDE)
    wt_ref[:group] = jnp.transpose(wq_ref[...])
    wt_ref[group:] = jnp.transpose(wv_ref[...])
    wk_ref[...] = wk_in[...]


def mask_before(refs, rows):
    if len(refs) == 1:
        return refs[0][...]
    far, far_core, near_three, near_one = refs
    core = lax.axis_index("head") & 1

    def digits(ref):
        return ref[rows : rows + CODE_ROWS // 2].astype(F32)

    three, one = digits(near_three), digits(near_one)
    seven = jnp.where(core == 0, digits(far), digits(far_core))
    slab = lax.axis_index("seq")
    distance = slab ^ (slab - 1)

    code = jnp.where(distance == 1, one, jnp.where(distance == 3, three, seven)).astype(I32)
    return (code[0:1] << 5) + code[1:2]


def expand_kernel(rows, seen_ref, *refs):
    code_refs, (e_ref, et_ref, bias_ref) = refs[:-3], refs[-3:]
    tok_rows = seen_ref.shape[0]
    rank = ranks(mask_before(code_refs, rows), tok_rows)
    rank = jnp.where(lax.axis_index("seq") > 0, rank, -1)
    rank_column = column(rank)
    bias_ref[:tok_rows] = jnp.where(rank_column >= 0, 0.0, HIDE)
    bias_ref[tok_rows:] = seen_ref[...]
    for at in range(0, et_ref.shape[0], FBLK):
        e_ref[:, at : at + FBLK] = ones_where(rank_column == iota((tok_rows, FBLK), 1) + at)
        et_ref[at : at + FBLK] = ones_where(iota((FBLK, tok_rows), 0) + at == rank)


def assemble(piece_refs, x_ref):
    head = lax.axis_index("head")
    tok_rows, width = x_ref.shape
    if len(piece_refs) == 4:
        quarter = width // 4
        for distance, piece in zip((0, 2, 1, 3), piece_refs):
            start = pl.multiple_of((head ^ distance) * quarter, quarter)
            x_ref[:, pl.ds(start, quarter)] = piece[...]
        return
    far_refs, near_refs, own = piece_refs[:8], piece_refs[8:14], piece_refs[14]
    rows, half = own.shape[0], width // 2
    core, side = head & 1, head >> 1
    for index, piece in enumerate(far_refs):
        turn, crossed = (index // 2) % 2, index // 4
        row = pl.multiple_of((2 * (index % 2) + (core ^ crossed)) * rows, rows)
        start = pl.multiple_of((side ^ turn) * half, half)
        x_ref[pl.ds(row, rows), pl.ds(start, half)] = piece[:rows]
    for index, piece in enumerate(near_refs):
        row = (4 + index % 3) * rows
        start = pl.multiple_of((core ^ (index // 3)) * half, half)
        x_ref[row : row + rows, pl.ds(start, half)] = piece[:rows]
    x_ref[7 * rows :] = own[...]


def pack_kernel(sel_ref, *refs):
    parts, (out_ref, rows_ref) = refs[:-2], refs[-2:]
    packed, quarter = out_ref.shape
    head = lax.axis_index("head")
    if len(parts) == 1:
        rows_ref[...] = parts[0][...]
    else:
        core, side = head & 1, head >> 1
        far_refs, near_refs, own = parts[:4], parts[4:10], parts[10]
        rows = own.shape[0]
        here = pl.ds(pl.multiple_of(core * quarter, quarter), quarter)
        for index, piece in enumerate(far_refs):
            row = pl.multiple_of((2 * (index % 2) + (core ^ (index // 2))) * rows, rows)
            rows_ref[pl.ds(row, rows)] = piece[:rows, here]
        for index in range(3):
            rows_ref[(4 + index) * rows : (5 + index) * rows] = jnp.where(
                core == side, near_refs[index][:rows, here], near_refs[3 + index][:rows, here]
            )
        rows_ref[7 * rows :] = own[:, pl.ds(pl.multiple_of(head * quarter, quarter), quarter)]
    out_ref[...] = nn(sel_ref[:packed], rows_ref[...]).astype(BF)


def project_kernel(count, *refs):
    piece_refs, refs = refs[:count], refs[count:]
    wt_ref, wk_ref, sel_ref, fcol_ref, summ_ref, k_ref, v_ref, x_ref = refs
    assemble(piece_refs, x_ref)
    group = wk_ref.shape[1]
    near = x_ref.shape[0] // POOL1
    lead = sel_ref.shape[0] - near
    x = x_ref[...]
    keys = nn(x, wk_ref[...]).astype(BF)
    k_ref[...] = keys
    vt = nt(wt_ref[group:], x).astype(BF)
    v_ref[...] = vt
    sel = sel_ref[lead - SUMM_ROWS : lead]
    kl = nn(sel, keys)
    vl = nt(vt, sel)
    factor = fcol_ref[:SUMM_ROWS, :1]
    summ_k = kl * factor
    tail = jnp.concatenate(
        [vl, jnp.zeros((group, 128 - SUMM_ROWS), F32)], axis=1
    )
    summ_v = jnp.transpose(tail)[:SUMM_ROWS] * factor
    mids = x_ref.shape[0] // POOL2
    fars = x_ref.shape[0] // POOL3
    summ_ref[:mids] = summ_k[:mids].astype(BF)
    summ_ref[mids : 2 * mids] = summ_v[:mids].astype(BF)
    summ_ref[2 * mids :] = (summ_k[mids:] + pltpu.roll(summ_v[mids:], fars, 0)).astype(BF)


def spread_heads(q4_ref, qt_ref, at, heads):
    width = q4_ref.shape[0] // heads
    for h in range(heads):
        rows = slice(h * width, (h + 1) * width)
        q4_ref[rows, h * FBLK : (h + 1) * FBLK] = qt_ref[rows, at : at + FBLK]


def order_kernel(
    p_ref, pt_ref, sel_ref, fcol_ref, frow_ref, wt_ref, x_ref, k0_ref, v0_ref,
    qt_ref, vt_ref, k_ref, nk_ref, nvt_ref,
):
    group = k_ref.shape[1]
    near = nk_ref.shape[0]
    k0, v0 = k0_ref[...], v0_ref[...]
    q0 = nt(wt_ref[:group], x_ref[...]).astype(BF)
    k_ref[...] = nn(p_ref[...], k0).astype(BF)
    qt_ref[...] = (nn(q0, pt_ref[...]) * 0.125).astype(BF)
    vt_ref[...] = nn(v0, pt_ref[...]).astype(BF)
    pool = sel_ref[sel_ref.shape[0] - near :]
    nk_ref[...] = (nn(pool, k0) * fcol_ref[SUMM_ROWS:, :1]).astype(BF)
    nvt_ref[...] = (nt(v0, pool) * frow_ref[:1, SUMM_ROWS:]).astype(BF)


def own_kernel(
    mix_ref, qt_ref, k_ref, vt_ref, nk_ref, nvt_ref, seen_ref,
    acc_ref, near_ref, top_ref, den_ref, q4_ref, p_ref,
):
    tok_rows, group = k_ref.shape
    heads = mix_ref.shape[1]
    width = group // heads
    q4_ref[...] = jnp.zeros_like(q4_ref)
    same = iota((FBLK, FBLK), 0) == iota((FBLK, FBLK), 1)
    nk, nvt = nk_ref[...], nvt_ref[...]
    for g in range(tok_rows // FBLK):
        at = g * FBLK
        slot = g % 2
        spread_heads(q4_ref.at[slot], qt_ref, at, heads)
        q4 = q4_ref[slot]
        bias = jnp.where(same, 0.0, seen_ref[at : at + FBLK])
        own_scores = nn(k_ref[at : at + FBLK], q4)
        near_scores = nn(nk, q4)
        scales = []
        for h in range(heads):
            lanes = slice(h * FBLK, (h + 1) * FBLK)
            part = own_scores[:, lanes] + bias
            top = jnp.max(part, axis=0, keepdims=True)
            weight = jnp.exp(part - top)
            top_ref[g : g + 1, lanes] = top
            den_ref[g : g + 1, lanes] = jnp.sum(weight, axis=0, keepdims=True)
            p_ref[slot, :FBLK, lanes] = weight.astype(BF)
            part = near_scores[:, lanes]
            weight = jnp.exp(part - jnp.max(part, axis=0, keepdims=True))
            scales.append(mix_ref[1, h] / jnp.sum(weight, axis=0, keepdims=True))
            p_ref[slot, FBLK:, lanes] = weight.astype(BF)
        own_out = nn(vt_ref[:, at : at + FBLK], p_ref[slot, :FBLK])
        near_out = nn(nvt, p_ref[slot, FBLK:])
        for h in range(heads):
            rows, lanes = slice(h * width, (h + 1) * width), slice(h * FBLK, (h + 1) * FBLK)
            acc_ref[rows, at : at + FBLK] = own_out[rows, lanes]
            near_ref[rows, at : at + FBLK] = near_out[rows, lanes] * scales[h]


def window_kernel(k_ref, vt_ref, wt_ref, wk_ref, e_ref, et_ref, *refs):
    halo_refs, refs = refs[:4], refs[4:]
    summ_refs, (kw_ref, vw_ref, ck_ref, cv_ref, all_ref, x_ref) = refs[:-6], refs[-6:]
    tok_rows, group = k_ref.shape
    quarter = x_ref.shape[1] // 4
    head = lax.axis_index("head")
    for distance, part in zip((0, 2, 1, 3), halo_refs):
        start = pl.multiple_of((head ^ distance) * quarter, quarter)
        x_ref[:, pl.ds(start, quarter)] = part[...]
    x = x_ref[...]
    kw_ref[:tok_rows] = nn(e_ref[...], nn(x, wk_ref[...]).astype(BF)).astype(BF)
    kw_ref[tok_rows:] = k_ref[...]
    vw_ref[:, :tok_rows] = nn(nt(wt_ref[group:], x).astype(BF), et_ref[...]).astype(BF)
    vw_ref[:, tok_rows:] = vt_ref[...]
    at = 0
    for part in summ_refs:
        all_ref[at : at + part.shape[0]] = part[...]
        at += part.shape[0]
    slab, slabs = lax.axis_index("seq"), lax.axis_size("seq")
    mids, fars = tok_rows // POOL2, tok_rows // POOL3
    shape = (ck_ref.shape[0], all_ref.shape[0])
    line = iota(shape, 0)
    step = 3 * mids
    turn = line // mids
    far = line - 3 * mids
    shard = slab - 1 + turn
    turned = slab if slabs == 8 else 0
    distance = jnp.where(line < 3 * mids, shard, far // fars) ^ turned
    slot = (distance >> 1) + (distance & 1) * (slabs // 2) if slabs == 8 else distance
    source = slot * step + jnp.where(line < 3 * mids, line - turn * mids, 2 * mids + far % fars)
    source = jnp.where((line >= 3 * mids) | ((shard >= 0) & (shard < slabs)), source, -2 * step)
    gathered = all_ref[...]
    ck_ref[...] = nn(ones_where(source == iota(shape, 1)), gathered).astype(BF)
    values = nn(ones_where(source + jnp.where(line < 3 * mids, mids, fars) == iota(shape, 1)), gathered)
    cv_ref[...] = jnp.transpose(values).astype(BF)


def rest_kernel(
    first, blocks, lists_ref, mix_ref, qt_ref, kw_ref, vw_ref, ck_ref, cv_ref, bias_ref,
    acc_ref, near_ref, top_ref, den_ref, out_ref, kc_ref, vc_ref, q4_ref, p_ref,
):
    group, tok_rows = qt_ref.shape
    heads = mix_ref.shape[1]
    width = group // heads
    others = FINE_K - 1
    fine = others * FBLK
    mid = 3 * (tok_rows // POOL2)
    far_at = fine + mid
    total = kc_ref.shape[1]
    for slot in range(2):
        kc_ref[slot, fine:] = ck_ref[...]
        vc_ref[slot, :, fine:] = cv_ref[...]
    q4_ref[...] = jnp.zeros_like(q4_ref)
    for index in range(blocks):
        g = first + index
        at = g * FBLK
        slot = index % 2
        biases = []
        for entry in range(others):
            start = pl.multiple_of(lists_ref[entry + 1, g] * FBLK, FBLK)
            kc_ref[slot, entry * FBLK : (entry + 1) * FBLK] = kw_ref[pl.ds(start, FBLK)]
            vc_ref[slot, :, entry * FBLK : (entry + 1) * FBLK] = vw_ref[:, pl.ds(start, FBLK)]
            biases.append(bias_ref[pl.ds(start, FBLK)])
        spread_heads(q4_ref.at[slot], qt_ref, at, heads)
        scores = nn(kc_ref[slot], q4_ref[slot])
        scales, keeps = [], []
        for h in range(heads):
            lanes = slice(h * FBLK, (h + 1) * FBLK)
            parts = [scores[e * FBLK : (e + 1) * FBLK, lanes] + biases[e] for e in range(others)]
            old_top = top_ref[g : g + 1, lanes]
            top = functools.reduce(
                jnp.maximum, [jnp.max(part, axis=0, keepdims=True) for part in parts] + [old_top]
            )
            keep = jnp.exp(old_top - top)
            den = den_ref[g : g + 1, lanes] * keep
            for e, part in enumerate(parts):
                weight = jnp.exp(part - top)
                den = den + jnp.sum(weight, axis=0, keepdims=True)
                p_ref[slot, e * FBLK : (e + 1) * FBLK, lanes] = weight.astype(BF)
            scale = mix_ref[0, h] / den
            scales.append(scale)
            keeps.append(keep * scale)
            relative = den / mix_ref[0, h]
            for level, (low, high) in enumerate(((fine, far_at), (far_at, total))):
                part = scores[low:high, lanes]
                weight = jnp.exp(part - jnp.max(part, axis=0, keepdims=True))
                share = mix_ref[level + 2, h] / jnp.sum(weight, axis=0, keepdims=True) * relative
                p_ref[slot, low:high, lanes] = (weight * share).astype(BF)
        total_out = nn(vc_ref[slot], p_ref[slot])
        rows = []
        for h in range(heads):
            pick = (slice(h * width, (h + 1) * width), slice(h * FBLK, (h + 1) * FBLK))
            mine = (pick[0], slice(at, at + FBLK))
            rows.append(total_out[pick] * scales[h] + acc_ref[mine] * keeps[h] + near_ref[mine])
        out_ref[index * FBLK : (index + 1) * FBLK] = jnp.transpose(
            jnp.concatenate(rows, axis=0)
        ).astype(BF)


def output_kernel(w_ref, *refs):
    out_ref = refs[-1]
    group = w_ref.shape[1]
    head = lax.axis_index("head")
    total = None
    for distance, part in zip((0, 2, 1, 3), refs[:4]):
        start = pl.multiple_of((head ^ distance) * group, group)
        term = nn(part[...], w_ref[pl.ds(start, group)])
        total = term if total is None else total + term
    out_ref[...] = total.astype(BF)


def local(tokens, w_query, w_key, w_value, w_out, level_mix, fine_blocks, order, mask_ids):
    tok_rows, width = tokens.shape
    slabs = lax.axis_size("seq")
    slab, head = lax.axis_index("seq"), lax.axis_index("head")
    group = w_query.shape[1]
    heads = level_mix.shape[1]
    packed = tok_rows - mask_ids.shape[1]
    near, mids, fars = tok_rows // POOL1, tok_rows // POOL2, tok_rows // POOL3
    coarse = 3 * mids + fars * slabs
    step = 3 * mids
    chosen = packed + SUMM_ROWS + near

    shape = jax.ShapeDtypeStruct
    params = pltpu.CompilerParams(vmem_limit_bytes=VMEM_LIMIT)

    def prepare():
        return pl.pallas_call(
            prepare_kernel,
            out_shape=(
                shape((tok_rows, tok_rows), BF),
                shape((tok_rows, tok_rows), BF),
                shape((chosen, tok_rows), BF),
                shape((SUMM_ROWS + near, 128), F32),
                shape((16, SUMM_ROWS + near), F32),
                shape((tok_rows, FBLK), F32),
                shape((2 * group, width), BF),
                shape((width, group), BF),
            ),
            in_specs=vmem_specs(5),
            out_specs=vmem_specs(8),
            compiler_params=params,
            cost_estimate=COST,
            name="prepare",
        )(order, mask_ids, w_query, w_value, w_key)

    def expand(prepared, sources):
        return pl.pallas_call(
            functools.partial(expand_kernel, tok_rows // slabs),
            out_shape=(
                shape((tok_rows, packed), BF),
                shape((packed, tok_rows), BF),
                shape((2 * tok_rows, FBLK), F32),
            ),
            in_specs=vmem_specs(1 + len(sources)),
            out_specs=vmem_specs(3),
            compiler_params=params,
            cost_estimate=COST,
            name="expand",
        )(prepared[5], *sources)

    pieces, prepared, expanded, halo = exchange_tokens(tokens, mask_ids, prepare, expand)
    permute, permute_t, select, f_col, f_row, seen, w_t, w_k = prepared
    spread, spread_t, bias = expanded
    summ, k0, v0, rows_here = pl.pallas_call(
        functools.partial(project_kernel, len(pieces)),
        out_shape=(
            shape((step, group), BF),
            shape((tok_rows, group), BF),
            shape((group, tok_rows), BF),
            shape((tok_rows, width), BF),
        ),
        in_specs=vmem_specs(len(pieces) + 4),
        out_specs=vmem_specs(4),
        compiler_params=params,
        cost_estimate=COST,
        name="project",
    )(*pieces, w_t, w_k, select, f_col)
    halo, summ = lax.optimization_barrier((halo, summ))
    halo_x = over_head(halo, X_PAIRS)
    halo_core = over_head(halo, CORE_PAIRS)
    if slabs == 8:
        lined = [summ] + [by_distance(summ, d) for d in (2, 4, 6)]
    else:
        lined = [summ]

    q_t, v_t, keys, near_k, near_vt = pl.pallas_call(
        order_kernel,
        out_shape=(
            shape((group, tok_rows), BF),
            shape((group, tok_rows), BF),
            shape((tok_rows, group), BF),
            shape((near, group), BF),
            shape((group, near), BF),
        ),
        in_specs=vmem_specs(9),
        out_specs=vmem_specs(5),
        compiler_params=params,
        cost_estimate=COST,
        name="order",
    )(permute, permute_t, select, f_col, f_row, w_t, rows_here, k0, v0)
    near_k, halo_x, *lined = lax.optimization_barrier((near_k, halo_x, *lined))
    halo_last = over_head(halo_x, CORE_PAIRS)
    if slabs == 8:
        places = tuple((index, 0, step, 0) for index in range(4))
        column = stacked(lined, places, group)
        column, q_t = lax.optimization_barrier((column, q_t))
        summaries = [column, by_distance(column, 1)]
    else:
        copies = jnp.broadcast_to(summ[None], (slabs, step, group))
        copies = lax.all_to_all(copies, "seq", split_axis=0, concat_axis=0, tiled=True)
        summaries = [copies.reshape(slabs * step, group)]

    blocks = tok_rows // FBLK
    acc, near_out, top, den = pl.pallas_call(
        own_kernel,
        out_shape=(
            shape((group, tok_rows), F32),
            shape((group, tok_rows), F32),
            shape((blocks, heads * FBLK), F32),
            shape((blocks, heads * FBLK), F32),
        ),
        in_specs=smem_specs(1) + vmem_specs(6),
        out_specs=vmem_specs(4),
        scratch_shapes=[
            pltpu.VMEM((2, group, heads * FBLK), BF),
            pltpu.VMEM((2, FBLK + near, heads * FBLK), BF),
        ],
        compiler_params=params,
        cost_estimate=COST,
        name="own",
    )(level_mix, q_t, keys, v_t, near_k, near_vt, seen)

    window_k, window_v, coarse_k, coarse_v = pl.pallas_call(
        window_kernel,
        out_shape=(
            shape((2 * tok_rows, group), BF),
            shape((group, 2 * tok_rows), BF),
            shape((coarse, group), BF),
            shape((group, coarse), BF),
        ),
        in_specs=vmem_specs(10 + len(summaries)),
        out_specs=vmem_specs(4),
        scratch_shapes=[pltpu.VMEM((slabs * step, group), BF), pltpu.VMEM((packed, width), BF)],
        compiler_params=params,
        cost_estimate=COST,
        name="window",
    )(keys, v_t, w_t, w_k, spread, spread_t, halo, halo_x, halo_core, halo_last, *summaries)

    total = (FINE_K - 1) * FBLK + coarse
    lists = fine_blocks.T
    parts = PARTS if sum(PARTS) == blocks else (blocks,)
    waiting, out, first = None, None, 0

    def finish(out, attended, third, second, base, after=()):
        fourth = over_head(third, CORE_PAIRS)
        rows = attended.shape[0]
        previous = [] if out is None else [out]
        height = min(2 * FBLK, rows)
        tile = pl.BlockSpec((height, group), lambda i: (i, 0))
        return pl.pallas_call(
            output_kernel,
            grid=(rows // height,),
            out_shape=shape((tok_rows, group), BF),
            in_specs=[pl.BlockSpec((width, group), lambda i: (0, 0))]
            + [tile] * 4
            + [pl.BlockSpec(memory_space=pl.ANY)] * (len(previous) + len(after)),
            out_specs=pl.BlockSpec((height, group), lambda i, base=base * FBLK // height: (i + base, 0)),
            input_output_aliases={5: 0} if previous else {},
            compiler_params=params,
            cost_estimate=COST,
            name="output",
        )(w_out, attended, third, second, fourth, *previous, *after)

    for count in parts:
        attended = pl.pallas_call(
            functools.partial(rest_kernel, first, count),
            out_shape=shape((count * FBLK, group), BF),
            in_specs=smem_specs(2) + vmem_specs(10),
            out_specs=pl.BlockSpec(memory_space=pltpu.VMEM),
            scratch_shapes=[
                pltpu.VMEM((2, total, group), BF),
                pltpu.VMEM((2, group, total), BF),
                pltpu.VMEM((2, group, heads * FBLK), BF),
                pltpu.VMEM((2, total, heads * FBLK), BF),
            ],
            compiler_params=params,
            cost_estimate=COST,
            name="rest",
        )(
            lists, level_mix, q_t, window_k, window_v, coarse_k, coarse_v, bias, acc, near_out, top, den
        )
        third = over_head(attended, X_PAIRS)
        second = over_head(attended, CORE_PAIRS)
        if waiting is not None:
            old, old_third, old_second, old_base = waiting
            old_third, attended = lax.optimization_barrier((old_third, attended))
            out = finish(out, old, old_third, old_second, old_base, [third])
        waiting = (attended, third, second, first)
        first += count
    return finish(out, *waiting)


def solution(mesh):
    placed = (
        P("seq", None),
        P(None, "head"),
        P(None, "head"),
        P(None, "head"),
        P(None, "head"),
        P(None, "head"),
        P("seq", None),
        P("seq", None),
        P("seq", None),
    )
    return jax.shard_map(
        local, mesh=mesh, in_specs=placed, out_specs=P("seq", "head"), check_vma=False
    )
```

```python
import functools

import jax
import jax.numpy as jnp
from jax import lax
from jax.experimental import pallas as pl
from jax.experimental.pallas import tpu as pltpu
from jax.sharding import PartitionSpec as P

FBLK = 128
FINE_K = 4
POOL1 = 8
POOL2 = 64
POOL3 = 512
SUMM_ROWS = 32
CODE_ROWS = 16
BF = jnp.bfloat16
F32 = jnp.float32
I32 = jnp.int32
HIDE = -1e30
VMEM_LIMIT = 24 * 1024 * 1024
LONG_BYTES = 20_000_000
COST = pl.CostEstimate(flops=1, bytes_accessed=1, transcendentals=0)
LONG = pl.CostEstimate(flops=1, bytes_accessed=LONG_BYTES, transcendentals=0)
PARTS = (4, 4)

X_PAIRS = [(0, 2), (2, 0), (1, 3), (3, 1)]
CORE_PAIRS = [(0, 1), (1, 0), (2, 3), (3, 2)]


def nn(a, b):
    return lax.dot_general(a, b, (((1,), (0,)), ((), ())), preferred_element_type=F32)


def nt(a, b):
    return lax.dot_general(a, b, (((1,), (1,)), ((), ())), preferred_element_type=F32)


def iota(shape, axis):
    return lax.broadcasted_iota(I32, shape, axis)


def ones_where(condition):
    return jnp.where(condition, 1.0, 0.0).astype(BF)


def vmem_specs(count):
    return [pl.BlockSpec(memory_space=pltpu.VMEM)] * count


def smem_specs(count):
    return [pl.BlockSpec(memory_space=pltpu.SMEM)] * count


def over_head(block, pairs):
    return lax.ppermute(block, "head", pairs)


def to_next(block):
    return lax.ppermute(block, "seq", [(i, i + 1) for i in range(lax.axis_size("seq") - 1)])


def send_kernel(tokens_ref, mask_ref, *refs):
    outs, own = refs[:-1], refs[-1]
    slab, head = lax.axis_index("seq"), lax.axis_index("head")
    core = head & 1
    rows, width = own.shape
    half = width // 2
    ids = mask_ref[...]
    line = iota((CODE_ROWS, ids.shape[1]), 0)
    code = jnp.where(line == 0, ids >> 5, jnp.where(line == 1, ids & 31, 0)).astype(F32).astype(BF)
    sides = (head >> 1, head >> 1, core, core, core)
    for distance, side, out in zip((7 - core, 5 - core, 3, 2, 1), sides, outs):
        row = pl.multiple_of((slab ^ distance) * rows, rows)
        start = pl.multiple_of(side * half, half)
        out[:rows] = tokens_ref[pl.ds(row, rows), pl.ds(start, half)]
        if out.shape[0] > rows:
            out[rows : rows + CODE_ROWS] = code
    own[...] = tokens_ref[pl.ds(pl.multiple_of(slab * rows, rows), rows)]


def stack_kernel(places, *refs):
    target = refs[-1]
    at = 0
    for source, row, height, column in places:
        target[at : at + height] = refs[source][row : row + height, column : column + target.shape[1]]
        at += height


def stacked(parts, places, width, after=(), cost=COST):
    return pl.pallas_call(
        functools.partial(stack_kernel, places),
        out_shape=jax.ShapeDtypeStruct((sum(place[2] for place in places), width), BF),
        in_specs=vmem_specs(len(parts)) + [pl.BlockSpec(memory_space=pl.ANY)] * len(after),
        out_specs=pl.BlockSpec(memory_space=pltpu.VMEM),
        compiler_params=pltpu.CompilerParams(vmem_limit_bytes=VMEM_LIMIT),
        cost_estimate=cost,
        name="stack",
    )(*parts, *after)


def by_distance(block, distance):
    return lax.ppermute(block, "seq", [(i, i ^ distance) for i in range(lax.axis_size("seq"))])


def by_core(block, distances):
    heads = lax.axis_size("head")
    pairs = [
        (slab * heads + head, (slab ^ distances[head & 1]) * heads + head)
        for slab in range(lax.axis_size("seq"))
        for head in range(heads)
    ]
    return lax.ppermute(block, ("seq", "head"), pairs)


def exchange_tokens(tokens, mask_ids, prepare, expand):
    tok_rows, width = tokens.shape
    slabs = lax.axis_size("seq")
    rows = tok_rows // slabs
    if slabs != 8:
        quarter = width // 4
        split = tokens.reshape(slabs, rows, width)
        mine = lax.dynamic_slice_in_dim(split, lax.axis_index("head") * quarter, quarter, axis=2)
        first = lax.all_to_all(mine, "seq", split_axis=0, concat_axis=0, tiled=True).reshape(
            tok_rows, quarter
        )
        third = over_head(first, X_PAIRS)
        second = over_head(first, CORE_PAIRS)
        fourth = over_head(third, CORE_PAIRS)
        prepared = prepare()
        return [first, third, second, fourth], prepared, expand(prepared, [to_next(mask_ids)])
    half = width // 2
    tall = rows + CODE_ROWS
    *blocks, own = pl.pallas_call(
        send_kernel,
        out_shape=(
            jax.ShapeDtypeStruct((tall, half), BF),
            jax.ShapeDtypeStruct((tall, half), BF),
            jax.ShapeDtypeStruct((tall, half), BF),
            jax.ShapeDtypeStruct((tall, half), BF),
            jax.ShapeDtypeStruct((tall, half), BF),
            jax.ShapeDtypeStruct((rows, width), BF),
        ),
        in_specs=vmem_specs(2),
        out_specs=vmem_specs(6),
        compiler_params=pltpu.CompilerParams(vmem_limit_bytes=60 * 1024 * 1024),
        cost_estimate=COST,
        name="send",
    )(tokens, mask_ids)
    routes = ((7, 6), (5, 4), (3, 3), (2, 2), (1, 1))
    one, two, three, four, five = [by_core(block, route) for block, route in zip(blocks, routes)]
    prepared = prepare()
    one, _ = lax.optimization_barrier((one, prepared))
    first_x = over_head(stacked((one,), ((0, 0, rows, 0),), half, (three, four, five)), X_PAIRS)
    two, first_x = lax.optimization_barrier((two, first_x))
    two = stacked((two,), ((0, 0, rows, 0),), half)
    far = [one, two]
    far_core = [over_head(part, CORE_PAIRS) for part in far]
    far_x = [first_x, over_head(two, X_PAIRS)]
    near = [three, four, five]
    near_core = [over_head(part, CORE_PAIRS) for part in near]
    expanded = expand(prepared, [one, far_core[0], three, five])
    far_x[1], _ = lax.optimization_barrier((far_x[1], expanded))
    far_last = [over_head(part, CORE_PAIRS) for part in far_x]
    return far + far_x + far_core + far_last + near + near_core + [own], prepared, expanded


def column(row, lanes=128):
    return jnp.transpose(jnp.broadcast_to(row.astype(F32), (lanes, row.shape[1]))).astype(I32)


def ranks(ids, tok_rows, lanes=128):
    hidden = column(ids)
    parts = []
    for at in range(0, tok_rows, lanes):
        time = iota((1, lanes), 1) + at
        count = jnp.sum(jnp.where(hidden < time, 1.0, 0.0), axis=0, keepdims=True)
        here = jnp.sum(jnp.where(hidden == time, 1.0, 0.0), axis=0, keepdims=True)
        parts.append(jnp.where(here == 0.0, time - count.astype(I32), -1))
    return jnp.concatenate(parts, axis=1)


def prepare_kernel(
    order_ref, mask_ref, wq_ref, wv_ref, wk_in,
    p_ref, pt_ref, sel_ref, fcol_ref, frow_ref, bias_ref, wt_ref, wk_ref,
):
    slab, slabs = lax.axis_index("seq"), lax.axis_size("seq")
    tok_rows = order_ref.shape[1]
    packed = tok_rows - mask_ref.shape[1]
    flip = (slab ^ 7) * (tok_rows // slabs) if slabs == 8 else 0
    mids = tok_rows // POOL2
    group = wq_ref.shape[1]
    lanes = 128

    place = order_ref[...] ^ flip
    place_column = column(place)
    for at in range(0, tok_rows, lanes):
        p_ref[:, at : at + lanes] = ones_where(place_column == iota((tok_rows, lanes), 1) + at)
        pt_ref[at : at + lanes] = ones_where(iota((lanes, tok_rows), 0) + at == place)
    rank = ranks(mask_ref[...], tok_rows)
    time = jnp.where(rank >= 0, iota((1, tok_rows), 1), -1) + 1
    line = iota((16, tok_rows), 0)
    stack = jnp.where(
        line == 0,
        time >> 5,
        jnp.where(
            line == 1,
            time & 31,
            jnp.where(line == 2, (rank + 1) >> 5, jnp.where(line == 3, (rank + 1) & 31, 0)),
        ),
    )
    moved = nn(stack.astype(F32).astype(BF), p_ref[...]).astype(I32)
    time_here = (moved[0:1] << 5) + moved[1:2] - 1
    rank_here = (moved[2:3] << 5) + moved[3:4] - 1
    for at in range(0, packed, lanes):
        sel_ref[at : at + lanes] = ones_where(iota((lanes, tok_rows), 0) + at == rank_here)
    line = iota((SUMM_ROWS, tok_rows), 0)
    sel_ref[packed : packed + SUMM_ROWS] = ones_where(
        ((time_here >> 6) == line) | (((time_here >> 9) + mids == line) & (time_here >= 0))
    )
    lead = packed + SUMM_ROWS
    near = sel_ref.shape[0] - lead
    sel_ref[lead:] = ones_where((time_here >> 3) == iota((near, tok_rows), 0))
    pools = sel_ref[packed:]
    fcol_ref[...] = 1.0 / jnp.sqrt(jnp.maximum(nn(pools, jnp.ones((tok_rows, lanes), BF)), 1.0))
    frow_ref[...] = 1.0 / jnp.sqrt(jnp.maximum(nt(jnp.ones((16, tok_rows), BF), pools), 1.0))
    bias_ref[...] = jnp.where(column(rank) >= 0, 0.0, HIDE)
    wt_ref[:group] = jnp.transpose(wq_ref[...])
    wt_ref[group:] = jnp.transpose(wv_ref[...])
    wk_ref[...] = wk_in[...]


def mask_before(refs, rows):
    if len(refs) == 1:
        return refs[0][...]
    far, far_core, near_three, near_one = refs
    core = lax.axis_index("head") & 1

    def digits(ref):
        return ref[rows : rows + CODE_ROWS // 2].astype(F32)

    three, one = digits(near_three), digits(near_one)
    seven = jnp.where(core == 0, digits(far), digits(far_core))
    slab = lax.axis_index("seq")
    distance = slab ^ (slab - 1)

    code = jnp.where(distance == 1, one, jnp.where(distance == 3, three, seven)).astype(I32)
    return (code[0:1] << 5) + code[1:2]


def expand_kernel(rows, seen_ref, *refs):
    code_refs, (e_ref, et_ref, bias_ref) = refs[:-3], refs[-3:]
    tok_rows = seen_ref.shape[0]
    rank = ranks(mask_before(code_refs, rows), tok_rows)
    rank = jnp.where(lax.axis_index("seq") > 0, rank, -1)
    rank_column = column(rank)
    bias_ref[:tok_rows] = jnp.where(rank_column >= 0, 0.0, HIDE)
    bias_ref[tok_rows:] = seen_ref[...]
    for at in range(0, et_ref.shape[0], FBLK):
        e_ref[:, at : at + FBLK] = ones_where(rank_column == iota((tok_rows, FBLK), 1) + at)
        et_ref[at : at + FBLK] = ones_where(iota((FBLK, tok_rows), 0) + at == rank)


def assemble(piece_refs, x_ref):
    head = lax.axis_index("head")
    tok_rows, width = x_ref.shape
    if len(piece_refs) == 4:
        quarter = width // 4
        for distance, piece in zip((0, 2, 1, 3), piece_refs):
            start = pl.multiple_of((head ^ distance) * quarter, quarter)
            x_ref[:, pl.ds(start, quarter)] = piece[...]
        return
    far_refs, near_refs, own = piece_refs[:8], piece_refs[8:14], piece_refs[14]
    rows, half = own.shape[0], width // 2
    core, side = head & 1, head >> 1
    for index, piece in enumerate(far_refs):
        turn, crossed = (index // 2) % 2, index // 4
        row = pl.multiple_of((2 * (index % 2) + (core ^ crossed)) * rows, rows)
        start = pl.multiple_of((side ^ turn) * half, half)
        x_ref[pl.ds(row, rows), pl.ds(start, half)] = piece[:rows]
    for index, piece in enumerate(near_refs):
        row = (4 + index % 3) * rows
        start = pl.multiple_of((core ^ (index // 3)) * half, half)
        x_ref[row : row + rows, pl.ds(start, half)] = piece[:rows]
    x_ref[7 * rows :] = own[...]


def project_kernel(count, *refs):
    piece_refs, refs = refs[:count], refs[count:]
    wt_ref, wk_ref, sel_ref, fcol_ref, comp_ref, summ_ref, k_ref, v_ref, x_ref = refs
    assemble(piece_refs, x_ref)
    group = wk_ref.shape[1]
    packed = comp_ref.shape[0] // 2
    lead = packed + SUMM_ROWS
    x = x_ref[...]
    keys = nn(x, wk_ref[...]).astype(BF)
    k_ref[...] = keys
    vt = nt(wt_ref[group:], x).astype(BF)
    v_ref[...] = vt
    sel = sel_ref[:lead]
    kl = nn(sel, keys)
    vl = nt(vt, sel)
    comp_ref[:packed] = kl[:packed].astype(BF)
    vc = vl[:, :packed].astype(BF)
    for part in range(packed // group):
        comp_ref[packed + part * group : packed + (part + 1) * group] = vc[
            :, part * group : (part + 1) * group
        ]
    factor = fcol_ref[:SUMM_ROWS, :1]
    summ_k = kl[packed:] * factor
    tail = jnp.concatenate(
        [vl[:, packed:], jnp.zeros((group, 128 - SUMM_ROWS), F32)], axis=1
    )
    summ_v = jnp.transpose(tail)[:SUMM_ROWS] * factor
    mids = x_ref.shape[0] // POOL2
    fars = x_ref.shape[0] // POOL3
    summ_ref[:mids] = summ_k[:mids].astype(BF)
    summ_ref[mids : 2 * mids] = summ_v[:mids].astype(BF)
    summ_ref[2 * mids :] = (summ_k[mids:] + pltpu.roll(summ_v[mids:], fars, 0)).astype(BF)


def spread_heads(q4_ref, qt_ref, at, heads):
    width = q4_ref.shape[0] // heads
    for h in range(heads):
        rows = slice(h * width, (h + 1) * width)
        q4_ref[rows, h * FBLK : (h + 1) * FBLK] = qt_ref[rows, at : at + FBLK]


def order_kernel(
    p_ref, pt_ref, sel_ref, fcol_ref, frow_ref, wt_ref, x_ref, k0_ref, v0_ref,
    qt_ref, vt_ref, k_ref, nk_ref, nvt_ref,
):
    group = k_ref.shape[1]
    near = nk_ref.shape[0]
    k0, v0 = k0_ref[...], v0_ref[...]
    q0 = nt(wt_ref[:group], x_ref[...]).astype(BF)
    k_ref[...] = nn(p_ref[...], k0).astype(BF)
    qt_ref[...] = (nn(q0, pt_ref[...]) * 0.125).astype(BF)
    vt_ref[...] = nn(v0, pt_ref[...]).astype(BF)
    pool = sel_ref[sel_ref.shape[0] - near :]
    nk_ref[...] = (nn(pool, k0) * fcol_ref[SUMM_ROWS:, :1]).astype(BF)
    nvt_ref[...] = (nt(v0, pool) * frow_ref[:1, SUMM_ROWS:]).astype(BF)


def own_kernel(
    mix_ref, qt_ref, k_ref, vt_ref, nk_ref, nvt_ref, seen_ref,
    acc_ref, near_ref, top_ref, den_ref, q4_ref, p_ref,
):
    tok_rows, group = k_ref.shape
    heads = mix_ref.shape[1]
    width = group // heads
    q4_ref[...] = jnp.zeros_like(q4_ref)
    same = iota((FBLK, FBLK), 0) == iota((FBLK, FBLK), 1)
    nk, nvt = nk_ref[...], nvt_ref[...]
    for g in range(tok_rows // FBLK):
        at = g * FBLK
        slot = g % 2
        spread_heads(q4_ref.at[slot], qt_ref, at, heads)
        q4 = q4_ref[slot]
        bias = jnp.where(same, 0.0, seen_ref[at : at + FBLK])
        own_scores = nn(k_ref[at : at + FBLK], q4)
        near_scores = nn(nk, q4)
        scales = []
        for h in range(heads):
            lanes = slice(h * FBLK, (h + 1) * FBLK)
            part = own_scores[:, lanes] + bias
            top = jnp.max(part, axis=0, keepdims=True)
            weight = jnp.exp(part - top)
            top_ref[g : g + 1, lanes] = top
            den_ref[g : g + 1, lanes] = jnp.sum(weight, axis=0, keepdims=True)
            p_ref[slot, :FBLK, lanes] = weight.astype(BF)
            part = near_scores[:, lanes]
            weight = jnp.exp(part - jnp.max(part, axis=0, keepdims=True))
            scales.append(mix_ref[1, h] / jnp.sum(weight, axis=0, keepdims=True))
            p_ref[slot, FBLK:, lanes] = weight.astype(BF)
        own_out = nn(vt_ref[:, at : at + FBLK], p_ref[slot, :FBLK])
        near_out = nn(nvt, p_ref[slot, FBLK:])
        for h in range(heads):
            rows, lanes = slice(h * width, (h + 1) * width), slice(h * FBLK, (h + 1) * FBLK)
            acc_ref[rows, at : at + FBLK] = own_out[rows, lanes]
            near_ref[rows, at : at + FBLK] = near_out[rows, lanes] * scales[h]


def window_kernel(k_ref, vt_ref, comp_ref, e_ref, et_ref, *refs):
    summ_refs, (kw_ref, vw_ref, ck_ref, cv_ref, all_ref) = refs[:-5], refs[-5:]
    tok_rows, group = k_ref.shape
    packed = e_ref.shape[1]
    kw_ref[:tok_rows] = nn(e_ref[...], comp_ref[:packed]).astype(BF)
    kw_ref[tok_rows:] = k_ref[...]
    prev = None
    for part in range(packed // group):
        term = nn(
            comp_ref[packed + part * group : packed + (part + 1) * group],
            et_ref[part * group : (part + 1) * group],
        )
        prev = term if prev is None else prev + term
    vw_ref[:, :tok_rows] = prev.astype(BF)
    vw_ref[:, tok_rows:] = vt_ref[...]
    at = 0
    for part in summ_refs:
        all_ref[at : at + part.shape[0]] = part[...]
        at += part.shape[0]
    slab, slabs = lax.axis_index("seq"), lax.axis_size("seq")
    mids, fars = tok_rows // POOL2, tok_rows // POOL3
    shape = (ck_ref.shape[0], all_ref.shape[0])
    line = iota(shape, 0)
    step = 3 * mids
    turn = line // mids
    far = line - 3 * mids
    shard = slab - 1 + turn
    turned = slab if slabs == 8 else 0
    distance = jnp.where(line < 3 * mids, shard, far // fars) ^ turned
    slot = (distance >> 1) + (distance & 1) * (slabs // 2) if slabs == 8 else distance
    source = slot * step + jnp.where(line < 3 * mids, line - turn * mids, 2 * mids + far % fars)
    source = jnp.where((line >= 3 * mids) | ((shard >= 0) & (shard < slabs)), source, -2 * step)
    gathered = all_ref[...]
    ck_ref[...] = nn(ones_where(source == iota(shape, 1)), gathered).astype(BF)
    values = nn(ones_where(source + jnp.where(line < 3 * mids, mids, fars) == iota(shape, 1)), gathered)
    cv_ref[...] = jnp.transpose(values).astype(BF)


def rest_kernel(
    first, blocks, lists_ref, mix_ref, qt_ref, kw_ref, vw_ref, ck_ref, cv_ref, bias_ref,
    acc_ref, near_ref, top_ref, den_ref, out_ref, kc_ref, vc_ref, q4_ref, p_ref,
):
    group, tok_rows = qt_ref.shape
    heads = mix_ref.shape[1]
    width = group // heads
    others = FINE_K - 1
    fine = others * FBLK
    mid = 3 * (tok_rows // POOL2)
    far_at = fine + mid
    total = kc_ref.shape[1]
    for slot in range(2):
        kc_ref[slot, fine:] = ck_ref[...]
        vc_ref[slot, :, fine:] = cv_ref[...]
    q4_ref[...] = jnp.zeros_like(q4_ref)
    for index in range(blocks):
        g = first + index
        at = g * FBLK
        slot = index % 2
        biases = []
        for entry in range(others):
            start = pl.multiple_of(lists_ref[entry + 1, g] * FBLK, FBLK)
            kc_ref[slot, entry * FBLK : (entry + 1) * FBLK] = kw_ref[pl.ds(start, FBLK)]
            vc_ref[slot, :, entry * FBLK : (entry + 1) * FBLK] = vw_ref[:, pl.ds(start, FBLK)]
            biases.append(bias_ref[pl.ds(start, FBLK)])
        spread_heads(q4_ref.at[slot], qt_ref, at, heads)
        scores = nn(kc_ref[slot], q4_ref[slot])
        scales, keeps = [], []
        for h in range(heads):
            lanes = slice(h * FBLK, (h + 1) * FBLK)
            parts = [scores[e * FBLK : (e + 1) * FBLK, lanes] + biases[e] for e in range(others)]
            old_top = top_ref[g : g + 1, lanes]
            top = functools.reduce(
                jnp.maximum, [jnp.max(part, axis=0, keepdims=True) for part in parts] + [old_top]
            )
            keep = jnp.exp(old_top - top)
            den = den_ref[g : g + 1, lanes] * keep
            for e, part in enumerate(parts):
                weight = jnp.exp(part - top)
                den = den + jnp.sum(weight, axis=0, keepdims=True)
                p_ref[slot, e * FBLK : (e + 1) * FBLK, lanes] = weight.astype(BF)
            scale = mix_ref[0, h] / den
            scales.append(scale)
            keeps.append(keep * scale)
            relative = den / mix_ref[0, h]
            for level, (low, high) in enumerate(((fine, far_at), (far_at, total))):
                part = scores[low:high, lanes]
                weight = jnp.exp(part - jnp.max(part, axis=0, keepdims=True))
                share = mix_ref[level + 2, h] / jnp.sum(weight, axis=0, keepdims=True) * relative
                p_ref[slot, low:high, lanes] = (weight * share).astype(BF)
        total_out = nn(vc_ref[slot], p_ref[slot])
        rows = []
        for h in range(heads):
            pick = (slice(h * width, (h + 1) * width), slice(h * FBLK, (h + 1) * FBLK))
            mine = (pick[0], slice(at, at + FBLK))
            rows.append(total_out[pick] * scales[h] + acc_ref[mine] * keeps[h] + near_ref[mine])
        out_ref[index * FBLK : (index + 1) * FBLK] = jnp.transpose(
            jnp.concatenate(rows, axis=0)
        ).astype(BF)


def output_kernel(w_ref, *refs):
    out_ref = refs[-1]
    group = w_ref.shape[1]
    head = lax.axis_index("head")
    total = None
    for distance, part in zip((0, 2, 1, 3), refs[:4]):
        start = pl.multiple_of((head ^ distance) * group, group)
        term = nn(part[...], w_ref[pl.ds(start, group)])
        total = term if total is None else total + term
    out_ref[...] = total.astype(BF)


def local(tokens, w_query, w_key, w_value, w_out, level_mix, fine_blocks, order, mask_ids):
    tok_rows, width = tokens.shape
    slabs = lax.axis_size("seq")
    slab, head = lax.axis_index("seq"), lax.axis_index("head")
    group = w_query.shape[1]
    heads = level_mix.shape[1]
    packed = tok_rows - mask_ids.shape[1]
    near, mids, fars = tok_rows // POOL1, tok_rows // POOL2, tok_rows // POOL3
    coarse = 3 * mids + fars * slabs
    step = 3 * mids
    chosen = packed + SUMM_ROWS + near

    shape = jax.ShapeDtypeStruct
    params = pltpu.CompilerParams(vmem_limit_bytes=VMEM_LIMIT)

    def prepare():
        return pl.pallas_call(
            prepare_kernel,
            out_shape=(
                shape((tok_rows, tok_rows), BF),
                shape((tok_rows, tok_rows), BF),
                shape((chosen, tok_rows), BF),
                shape((SUMM_ROWS + near, 128), F32),
                shape((16, SUMM_ROWS + near), F32),
                shape((tok_rows, FBLK), F32),
                shape((2 * group, width), BF),
                shape((width, group), BF),
            ),
            in_specs=vmem_specs(5),
            out_specs=vmem_specs(8),
            compiler_params=params,
            cost_estimate=COST,
            name="prepare",
        )(order, mask_ids, w_query, w_value, w_key)

    def expand(prepared, sources):
        return pl.pallas_call(
            functools.partial(expand_kernel, tok_rows // slabs),
            out_shape=(
                shape((tok_rows, packed), BF),
                shape((packed, tok_rows), BF),
                shape((2 * tok_rows, FBLK), F32),
            ),
            in_specs=vmem_specs(1 + len(sources)),
            out_specs=vmem_specs(3),
            compiler_params=params,
            cost_estimate=COST,
            name="expand",
        )(prepared[5], *sources)

    pieces, prepared, expanded = exchange_tokens(tokens, mask_ids, prepare, expand)
    permute, permute_t, select, f_col, f_row, seen, w_t, w_k = prepared
    spread, spread_t, bias = expanded
    comp, summ, k0, v0, rows_here = pl.pallas_call(
        functools.partial(project_kernel, len(pieces)),
        out_shape=(
            shape((2 * packed, group), BF),
            shape((step, group), BF),
            shape((tok_rows, group), BF),
            shape((group, tok_rows), BF),
            shape((tok_rows, width), BF),
        ),
        in_specs=vmem_specs(len(pieces) + 4),
        out_specs=vmem_specs(5),
        compiler_params=params,
        cost_estimate=COST,
        name="project",
    )(*pieces, w_t, w_k, select, f_col)
    if slabs == 8:
        lined = [summ] + [by_distance(summ, d) for d in (2, 4, 6)]
    comp_before = to_next(comp)

    q_t, v_t, keys, near_k, near_vt = pl.pallas_call(
        order_kernel,
        out_shape=(
            shape((group, tok_rows), BF),
            shape((group, tok_rows), BF),
            shape((tok_rows, group), BF),
            shape((near, group), BF),
            shape((group, near), BF),
        ),
        in_specs=vmem_specs(9),
        out_specs=vmem_specs(5),
        compiler_params=params,
        cost_estimate=COST,
        name="order",
    )(permute, permute_t, select, f_col, f_row, w_t, rows_here, k0, v0)
    blocks = tok_rows // FBLK
    acc, near_out, top, den = pl.pallas_call(
        own_kernel,
        out_shape=(
            shape((group, tok_rows), F32),
            shape((group, tok_rows), F32),
            shape((blocks, heads * FBLK), F32),
            shape((blocks, heads * FBLK), F32),
        ),
        in_specs=smem_specs(1) + vmem_specs(6),
        out_specs=vmem_specs(4),
        scratch_shapes=[
            pltpu.VMEM((2, group, heads * FBLK), BF),
            pltpu.VMEM((2, FBLK + near, heads * FBLK), BF),
        ],
        compiler_params=params,
        cost_estimate=COST,
        name="own",
    )(level_mix, q_t, keys, v_t, near_k, near_vt, seen)

    if slabs == 8:
        places = tuple((index, 0, step, 0) for index in range(4))
        column = stacked(lined, places, group, (top,))
        summaries = [column, by_distance(column, 1)]
    else:
        copies = jnp.broadcast_to(summ[None], (slabs, step, group))
        copies = lax.all_to_all(copies, "seq", split_axis=0, concat_axis=0, tiled=True)
        summaries = [copies.reshape(slabs * step, group)]

    window_k, window_v, coarse_k, coarse_v = pl.pallas_call(
        window_kernel,
        out_shape=(
            shape((2 * tok_rows, group), BF),
            shape((group, 2 * tok_rows), BF),
            shape((coarse, group), BF),
            shape((group, coarse), BF),
        ),
        in_specs=vmem_specs(5 + len(summaries)),
        out_specs=vmem_specs(4),
        scratch_shapes=[pltpu.VMEM((slabs * step, group), BF)],
        compiler_params=params,
        cost_estimate=COST,
        name="window",
    )(keys, v_t, comp_before, spread, spread_t, *summaries)

    total = (FINE_K - 1) * FBLK + coarse
    lists = fine_blocks.T
    parts = PARTS if sum(PARTS) == blocks else (blocks,)
    waiting, out, first = None, None, 0

    def finish(out, attended, third, second, base, after=()):
        fourth = over_head(third, CORE_PAIRS)
        rows = attended.shape[0]
        previous = [] if out is None else [out]
        height = min(2 * FBLK, rows)
        tile = pl.BlockSpec((height, group), lambda i: (i, 0))
        return pl.pallas_call(
            output_kernel,
            grid=(rows // height,),
            out_shape=shape((tok_rows, group), BF),
            in_specs=[pl.BlockSpec((width, group), lambda i: (0, 0))]
            + [tile] * 4
            + [pl.BlockSpec(memory_space=pl.ANY)] * (len(previous) + len(after)),
            out_specs=pl.BlockSpec((height, group), lambda i, base=base * FBLK // height: (i + base, 0)),
            input_output_aliases={5: 0} if previous else {},
            compiler_params=params,
            cost_estimate=COST,
            name="output",
        )(w_out, attended, third, second, fourth, *previous, *after)

    for count in parts:
        attended = pl.pallas_call(
            functools.partial(rest_kernel, first, count),
            out_shape=shape((count * FBLK, group), BF),
            in_specs=smem_specs(2) + vmem_specs(10),
            out_specs=pl.BlockSpec(memory_space=pltpu.VMEM),
            scratch_shapes=[
                pltpu.VMEM((2, total, group), BF),
                pltpu.VMEM((2, group, total), BF),
                pltpu.VMEM((2, group, heads * FBLK), BF),
                pltpu.VMEM((2, total, heads * FBLK), BF),
            ],
            compiler_params=params,
            cost_estimate=COST,
            name="rest",
        )(
            lists, level_mix, q_t, window_k, window_v, coarse_k, coarse_v, bias, acc, near_out, top, den
        )
        third = over_head(attended, X_PAIRS)
        second = over_head(attended, CORE_PAIRS)
        if waiting is not None:
            old, old_third, old_second, old_base = waiting
            old_third, attended = lax.optimization_barrier((old_third, attended))
            out = finish(out, old, old_third, old_second, old_base, [third])
        waiting = (attended, third, second, first)
        first += count
    return finish(out, *waiting)


def solution(mesh):
    placed = (
        P("seq", None),
        P(None, "head"),
        P(None, "head"),
        P(None, "head"),
        P(None, "head"),
        P(None, "head"),
        P("seq", None),
        P("seq", None),
        P("seq", None),
    )
    return jax.shard_map(
        local, mesh=mesh, in_specs=placed, out_specs=P("seq", "head"), check_vma=False
    )
```

```python
import functools

import jax
import jax.numpy as jnp
from jax import lax
from jax.experimental import pallas as pl
from jax.experimental.pallas import tpu as pltpu
from jax.sharding import PartitionSpec as P

FBLK = 128
FINE_K = 4
POOL1 = 8
POOL2 = 64
POOL3 = 512
SUMM_ROWS = 32
CODE_ROWS = 16
BF = jnp.bfloat16
F32 = jnp.float32
I32 = jnp.int32
HIDE = -1e30
VMEM_LIMIT = 24 * 1024 * 1024
LONG_BYTES = 20_000_000
COST = pl.CostEstimate(flops=1, bytes_accessed=1, transcendentals=0)
LONG = pl.CostEstimate(flops=1, bytes_accessed=LONG_BYTES, transcendentals=0)
PARTS = (4, 4)

X_PAIRS = [(0, 2), (2, 0), (1, 3), (3, 1)]
CORE_PAIRS = [(0, 1), (1, 0), (2, 3), (3, 2)]


def nn(a, b):
    return lax.dot_general(a, b, (((1,), (0,)), ((), ())), preferred_element_type=F32)


def nt(a, b):
    return lax.dot_general(a, b, (((1,), (1,)), ((), ())), preferred_element_type=F32)


def iota(shape, axis):
    return lax.broadcasted_iota(I32, shape, axis)


def ones_where(condition):
    return jnp.where(condition, 1.0, 0.0).astype(BF)


def vmem_specs(count):
    return [pl.BlockSpec(memory_space=pltpu.VMEM)] * count


def smem_specs(count):
    return [pl.BlockSpec(memory_space=pltpu.SMEM)] * count


def over_head(block, pairs):
    return lax.ppermute(block, "head", pairs)


def to_next(block):
    return lax.ppermute(block, "seq", [(i, i + 1) for i in range(lax.axis_size("seq") - 1)])


def send_kernel(tokens_ref, mask_ref, *refs):
    outs, own = refs[:-1], refs[-1]
    slab, head = lax.axis_index("seq"), lax.axis_index("head")
    core = head & 1
    rows, width = own.shape
    half = width // 2
    ids = mask_ref[...]
    line = iota((CODE_ROWS, ids.shape[1]), 0)
    code = jnp.where(line == 0, ids >> 5, jnp.where(line == 1, ids & 31, 0)).astype(F32).astype(BF)
    sides = (head >> 1, head >> 1, core, core, core)
    for distance, side, out in zip((7 - core, 5 - core, 3, 2, 1), sides, outs):
        row = pl.multiple_of((slab ^ distance) * rows, rows)
        start = pl.multiple_of(side * half, half)
        out[:rows] = tokens_ref[pl.ds(row, rows), pl.ds(start, half)]
        if out.shape[0] > rows:
            out[rows : rows + CODE_ROWS] = code
    own[...] = tokens_ref[pl.ds(pl.multiple_of(slab * rows, rows), rows)]


def stack_kernel(places, *refs):
    target = refs[-1]
    at = 0
    for source, row, height, column in places:
        target[at : at + height] = refs[source][row : row + height, column : column + target.shape[1]]
        at += height


def stacked(parts, places, width, after=(), cost=COST):
    return pl.pallas_call(
        functools.partial(stack_kernel, places),
        out_shape=jax.ShapeDtypeStruct((sum(place[2] for place in places), width), BF),
        in_specs=vmem_specs(len(parts)) + [pl.BlockSpec(memory_space=pl.ANY)] * len(after),
        out_specs=pl.BlockSpec(memory_space=pltpu.VMEM),
        compiler_params=pltpu.CompilerParams(vmem_limit_bytes=VMEM_LIMIT),
        cost_estimate=cost,
        name="stack",
    )(*parts, *after)


def by_distance(block, distance):
    return lax.ppermute(block, "seq", [(i, i ^ distance) for i in range(lax.axis_size("seq"))])


def by_core(block, distances):
    heads = lax.axis_size("head")
    pairs = [
        (slab * heads + head, (slab ^ distances[head & 1]) * heads + head)
        for slab in range(lax.axis_size("seq"))
        for head in range(heads)
    ]
    return lax.ppermute(block, ("seq", "head"), pairs)


def exchange_tokens(tokens, mask_ids, prepare, expand):
    tok_rows, width = tokens.shape
    slabs = lax.axis_size("seq")
    rows = tok_rows // slabs
    if slabs != 8:
        quarter = width // 4
        split = tokens.reshape(slabs, rows, width)
        mine = lax.dynamic_slice_in_dim(split, lax.axis_index("head") * quarter, quarter, axis=2)
        first = lax.all_to_all(mine, "seq", split_axis=0, concat_axis=0, tiled=True).reshape(
            tok_rows, quarter
        )
        third = over_head(first, X_PAIRS)
        second = over_head(first, CORE_PAIRS)
        fourth = over_head(third, CORE_PAIRS)
        prepared = prepare()
        return [first, third, second, fourth], prepared, expand(prepared, [to_next(mask_ids)])
    half = width // 2
    tall = rows + CODE_ROWS
    *blocks, own = pl.pallas_call(
        send_kernel,
        out_shape=(
            jax.ShapeDtypeStruct((tall, half), BF),
            jax.ShapeDtypeStruct((tall, half), BF),
            jax.ShapeDtypeStruct((tall, half), BF),
            jax.ShapeDtypeStruct((tall, half), BF),
            jax.ShapeDtypeStruct((tall, half), BF),
            jax.ShapeDtypeStruct((rows, width), BF),
        ),
        in_specs=vmem_specs(2),
        out_specs=vmem_specs(6),
        compiler_params=pltpu.CompilerParams(vmem_limit_bytes=VMEM_LIMIT),
        cost_estimate=COST,
        name="send",
    )(tokens, mask_ids)
    routes = ((7, 6), (5, 4), (3, 3), (2, 2), (1, 1))
    one, two, three, four, five = [by_core(block, route) for block, route in zip(blocks, routes)]
    prepared = prepare()
    one, _ = lax.optimization_barrier((one, prepared))
    first_x = over_head(stacked((one,), ((0, 0, rows, 0),), half, (three, four, five)), X_PAIRS)
    two, first_x = lax.optimization_barrier((two, first_x))
    two = stacked((two,), ((0, 0, rows, 0),), half)
    far = [one, two]
    far_core = [over_head(part, CORE_PAIRS) for part in far]
    far_x = [first_x, over_head(two, X_PAIRS)]
    near = [three, four, five]
    near_core = [over_head(part, CORE_PAIRS) for part in near]
    expanded = expand(prepared, [one, far_core[0], three, five])
    far_x[1], _ = lax.optimization_barrier((far_x[1], expanded))
    far_last = [over_head(part, CORE_PAIRS) for part in far_x]
    return far + far_x + far_core + far_last + near + near_core + [own], prepared, expanded


def column(row, lanes=128):
    return jnp.transpose(jnp.broadcast_to(row.astype(F32), (lanes, row.shape[1]))).astype(I32)


def ranks(ids, tok_rows, lanes=128):
    hidden = column(ids)
    parts = []
    for at in range(0, tok_rows, lanes):
        time = iota((1, lanes), 1) + at
        count = jnp.sum(jnp.where(hidden < time, 1.0, 0.0), axis=0, keepdims=True)
        here = jnp.sum(jnp.where(hidden == time, 1.0, 0.0), axis=0, keepdims=True)
        parts.append(jnp.where(here == 0.0, time - count.astype(I32), -1))
    return jnp.concatenate(parts, axis=1)


def prepare_kernel(
    order_ref, mask_ref, wq_ref, wv_ref, wk_in,
    p_ref, pt_ref, sel_ref, fcol_ref, frow_ref, bias_ref, wt_ref, wk_ref,
):
    slab, slabs = lax.axis_index("seq"), lax.axis_size("seq")
    tok_rows = order_ref.shape[1]
    packed = tok_rows - mask_ref.shape[1]
    flip = (slab ^ 7) * (tok_rows // slabs) if slabs == 8 else 0
    mids = tok_rows // POOL2
    group = wq_ref.shape[1]
    lanes = 128

    place = order_ref[...] ^ flip
    place_column = column(place)
    for at in range(0, tok_rows, lanes):
        p_ref[:, at : at + lanes] = ones_where(place_column == iota((tok_rows, lanes), 1) + at)
        pt_ref[at : at + lanes] = ones_where(iota((lanes, tok_rows), 0) + at == place)
    rank = ranks(mask_ref[...], tok_rows)
    time = jnp.where(rank >= 0, iota((1, tok_rows), 1), -1) + 1
    line = iota((16, tok_rows), 0)
    stack = jnp.where(
        line == 0,
        time >> 5,
        jnp.where(
            line == 1,
            time & 31,
            jnp.where(line == 2, (rank + 1) >> 5, jnp.where(line == 3, (rank + 1) & 31, 0)),
        ),
    )
    moved = nn(stack.astype(F32).astype(BF), p_ref[...]).astype(I32)
    time_here = (moved[0:1] << 5) + moved[1:2] - 1
    rank_here = (moved[2:3] << 5) + moved[3:4] - 1
    for at in range(0, packed, lanes):
        sel_ref[at : at + lanes] = ones_where(iota((lanes, tok_rows), 0) + at == rank_here)
    line = iota((SUMM_ROWS, tok_rows), 0)
    sel_ref[packed : packed + SUMM_ROWS] = ones_where(
        ((time_here >> 6) == line) | (((time_here >> 9) + mids == line) & (time_here >= 0))
    )
    lead = packed + SUMM_ROWS
    near = sel_ref.shape[0] - lead
    sel_ref[lead:] = ones_where((time_here >> 3) == iota((near, tok_rows), 0))
    pools = sel_ref[packed:]
    fcol_ref[...] = 1.0 / jnp.sqrt(jnp.maximum(nn(pools, jnp.ones((tok_rows, lanes), BF)), 1.0))
    frow_ref[...] = 1.0 / jnp.sqrt(jnp.maximum(nt(jnp.ones((16, tok_rows), BF), pools), 1.0))
    bias_ref[...] = jnp.where(column(rank) >= 0, 0.0, HIDE)
    wt_ref[:group] = jnp.transpose(wq_ref[...])
    wt_ref[group:] = jnp.transpose(wv_ref[...])
    wk_ref[...] = wk_in[...]


def mask_before(refs, rows):
    if len(refs) == 1:
        return refs[0][...]
    far, far_core, near_three, near_one = refs
    core = lax.axis_index("head") & 1

    def digits(ref):
        return ref[rows : rows + CODE_ROWS // 2].astype(F32)

    three, one = digits(near_three), digits(near_one)
    seven = jnp.where(core == 0, digits(far), digits(far_core))
    slab = lax.axis_index("seq")
    distance = slab ^ (slab - 1)

    code = jnp.where(distance == 1, one, jnp.where(distance == 3, three, seven)).astype(I32)
    return (code[0:1] << 5) + code[1:2]


def expand_kernel(rows, seen_ref, *refs):
    code_refs, (e_ref, et_ref, bias_ref) = refs[:-3], refs[-3:]
    tok_rows = seen_ref.shape[0]
    rank = ranks(mask_before(code_refs, rows), tok_rows)
    rank = jnp.where(lax.axis_index("seq") > 0, rank, -1)
    rank_column = column(rank)
    bias_ref[:tok_rows] = jnp.where(rank_column >= 0, 0.0, HIDE)
    bias_ref[tok_rows:] = seen_ref[...]
    for at in range(0, et_ref.shape[0], FBLK):
        e_ref[:, at : at + FBLK] = ones_where(rank_column == iota((tok_rows, FBLK), 1) + at)
        et_ref[at : at + FBLK] = ones_where(iota((FBLK, tok_rows), 0) + at == rank)


def assemble(piece_refs, x_ref):
    head = lax.axis_index("head")
    tok_rows, width = x_ref.shape
    if len(piece_refs) == 4:
        quarter = width // 4
        for distance, piece in zip((0, 2, 1, 3), piece_refs):
            start = pl.multiple_of((head ^ distance) * quarter, quarter)
            x_ref[:, pl.ds(start, quarter)] = piece[...]
        return
    far_refs, near_refs, own = piece_refs[:8], piece_refs[8:14], piece_refs[14]
    rows, half = own.shape[0], width // 2
    core, side = head & 1, head >> 1
    for index, piece in enumerate(far_refs):
        turn, crossed = (index // 2) % 2, index // 4
        row = pl.multiple_of((2 * (index % 2) + (core ^ crossed)) * rows, rows)
        start = pl.multiple_of((side ^ turn) * half, half)
        x_ref[pl.ds(row, rows), pl.ds(start, half)] = piece[:rows]
    for index, piece in enumerate(near_refs):
        row = (4 + index % 3) * rows
        start = pl.multiple_of((core ^ (index // 3)) * half, half)
        x_ref[row : row + rows, pl.ds(start, half)] = piece[:rows]
    x_ref[7 * rows :] = own[...]


def project_kernel(count, *refs):
    piece_refs, refs = refs[:count], refs[count:]
    wt_ref, wk_ref, sel_ref, fcol_ref, comp_ref, summ_ref, k_ref, v_ref, x_ref = refs
    assemble(piece_refs, x_ref)
    group = wk_ref.shape[1]
    packed = comp_ref.shape[0] // 2
    lead = packed + SUMM_ROWS
    x = x_ref[...]
    keys = nn(x, wk_ref[...]).astype(BF)
    k_ref[...] = keys
    vt = nt(wt_ref[group:], x).astype(BF)
    v_ref[...] = vt
    sel = sel_ref[:lead]
    kl = nn(sel, keys)
    vl = nt(vt, sel)
    comp_ref[:packed] = kl[:packed].astype(BF)
    vc = vl[:, :packed].astype(BF)
    for part in range(packed // group):
        comp_ref[packed + part * group : packed + (part + 1) * group] = vc[
            :, part * group : (part + 1) * group
        ]
    factor = fcol_ref[:SUMM_ROWS, :1]
    summ_k = kl[packed:] * factor
    tail = jnp.concatenate(
        [vl[:, packed:], jnp.zeros((group, 128 - SUMM_ROWS), F32)], axis=1
    )
    summ_v = jnp.transpose(tail)[:SUMM_ROWS] * factor
    mids = x_ref.shape[0] // POOL2
    fars = x_ref.shape[0] // POOL3
    summ_ref[:mids] = summ_k[:mids].astype(BF)
    summ_ref[mids : 2 * mids] = summ_v[:mids].astype(BF)
    summ_ref[2 * mids :] = (summ_k[mids:] + pltpu.roll(summ_v[mids:], fars, 0)).astype(BF)


def spread_heads(q4_ref, qt_ref, at, heads):
    width = q4_ref.shape[0] // heads
    for h in range(heads):
        rows = slice(h * width, (h + 1) * width)
        q4_ref[rows, h * FBLK : (h + 1) * FBLK] = qt_ref[rows, at : at + FBLK]


def order_kernel(
    p_ref, pt_ref, sel_ref, fcol_ref, frow_ref, wt_ref, x_ref, k0_ref, v0_ref,
    qt_ref, vt_ref, k_ref, nk_ref, nvt_ref,
):
    group = k_ref.shape[1]
    near = nk_ref.shape[0]
    k0, v0 = k0_ref[...], v0_ref[...]
    q0 = nt(wt_ref[:group], x_ref[...]).astype(BF)
    k_ref[...] = nn(p_ref[...], k0).astype(BF)
    qt_ref[...] = (nn(q0, pt_ref[...]) * 0.125).astype(BF)
    vt_ref[...] = nn(v0, pt_ref[...]).astype(BF)
    pool = sel_ref[sel_ref.shape[0] - near :]
    nk_ref[...] = (nn(pool, k0) * fcol_ref[SUMM_ROWS:, :1]).astype(BF)
    nvt_ref[...] = (nt(v0, pool) * frow_ref[:1, SUMM_ROWS:]).astype(BF)


def own_kernel(
    mix_ref, qt_ref, k_ref, vt_ref, nk_ref, nvt_ref, seen_ref,
    acc_ref, near_ref, top_ref, den_ref, q4_ref, p_ref,
):
    tok_rows, group = k_ref.shape
    heads = mix_ref.shape[1]
    width = group // heads
    q4_ref[...] = jnp.zeros_like(q4_ref)
    same = iota((FBLK, FBLK), 0) == iota((FBLK, FBLK), 1)
    nk, nvt = nk_ref[...], nvt_ref[...]
    for g in range(tok_rows // FBLK):
        at = g * FBLK
        slot = g % 2
        spread_heads(q4_ref.at[slot], qt_ref, at, heads)
        q4 = q4_ref[slot]
        bias = jnp.where(same, 0.0, seen_ref[at : at + FBLK])
        own_scores = nn(k_ref[at : at + FBLK], q4)
        near_scores = nn(nk, q4)
        scales = []
        for h in range(heads):
            lanes = slice(h * FBLK, (h + 1) * FBLK)
            part = own_scores[:, lanes] + bias
            top = jnp.max(part, axis=0, keepdims=True)
            weight = jnp.exp(part - top)
            top_ref[g : g + 1, lanes] = top
            den_ref[g : g + 1, lanes] = jnp.sum(weight, axis=0, keepdims=True)
            p_ref[slot, :FBLK, lanes] = weight.astype(BF)
            part = near_scores[:, lanes]
            weight = jnp.exp(part - jnp.max(part, axis=0, keepdims=True))
            scales.append(mix_ref[1, h] / jnp.sum(weight, axis=0, keepdims=True))
            p_ref[slot, FBLK:, lanes] = weight.astype(BF)
        own_out = nn(vt_ref[:, at : at + FBLK], p_ref[slot, :FBLK])
        near_out = nn(nvt, p_ref[slot, FBLK:])
        for h in range(heads):
            rows, lanes = slice(h * width, (h + 1) * width), slice(h * FBLK, (h + 1) * FBLK)
            acc_ref[rows, at : at + FBLK] = own_out[rows, lanes]
            near_ref[rows, at : at + FBLK] = near_out[rows, lanes] * scales[h]


def window_kernel(k_ref, vt_ref, comp_ref, e_ref, et_ref, *refs):
    summ_refs, (kw_ref, vw_ref, ck_ref, cv_ref, all_ref) = refs[:-5], refs[-5:]
    tok_rows, group = k_ref.shape
    packed = e_ref.shape[1]
    kw_ref[:tok_rows] = nn(e_ref[...], comp_ref[:packed]).astype(BF)
    kw_ref[tok_rows:] = k_ref[...]
    prev = None
    for part in range(packed // group):
        term = nn(
            comp_ref[packed + part * group : packed + (part + 1) * group],
            et_ref[part * group : (part + 1) * group],
        )
        prev = term if prev is None else prev + term
    vw_ref[:, :tok_rows] = prev.astype(BF)
    vw_ref[:, tok_rows:] = vt_ref[...]
    at = 0
    for part in summ_refs:
        all_ref[at : at + part.shape[0]] = part[...]
        at += part.shape[0]
    slab, slabs = lax.axis_index("seq"), lax.axis_size("seq")
    mids, fars = tok_rows // POOL2, tok_rows // POOL3
    shape = (ck_ref.shape[0], all_ref.shape[0])
    line = iota(shape, 0)
    step = 3 * mids
    turn = line // mids
    far = line - 3 * mids
    shard = slab - 1 + turn
    turned = slab if slabs == 8 else 0
    distance = jnp.where(line < 3 * mids, shard, far // fars) ^ turned
    slot = (distance >> 1) + (distance & 1) * (slabs // 2) if slabs == 8 else distance
    source = slot * step + jnp.where(line < 3 * mids, line - turn * mids, 2 * mids + far % fars)
    source = jnp.where((line >= 3 * mids) | ((shard >= 0) & (shard < slabs)), source, -2 * step)
    gathered = all_ref[...]
    ck_ref[...] = nn(ones_where(source == iota(shape, 1)), gathered).astype(BF)
    values = nn(ones_where(source + jnp.where(line < 3 * mids, mids, fars) == iota(shape, 1)), gathered)
    cv_ref[...] = jnp.transpose(values).astype(BF)


def rest_kernel(
    first, blocks, lists_ref, mix_ref, qt_ref, kw_ref, vw_ref, ck_ref, cv_ref, bias_ref,
    acc_ref, near_ref, top_ref, den_ref, out_ref, kc_ref, vc_ref, q4_ref, p_ref,
):
    group, tok_rows = qt_ref.shape
    heads = mix_ref.shape[1]
    width = group // heads
    others = FINE_K - 1
    fine = others * FBLK
    mid = 3 * (tok_rows // POOL2)
    far_at = fine + mid
    total = kc_ref.shape[1]
    for slot in range(2):
        kc_ref[slot, fine:] = ck_ref[...]
        vc_ref[slot, :, fine:] = cv_ref[...]
    q4_ref[...] = jnp.zeros_like(q4_ref)
    for index in range(blocks):
        g = first + index
        at = g * FBLK
        slot = index % 2
        biases = []
        for entry in range(others):
            start = pl.multiple_of(lists_ref[entry + 1, g] * FBLK, FBLK)
            kc_ref[slot, entry * FBLK : (entry + 1) * FBLK] = kw_ref[pl.ds(start, FBLK)]
            vc_ref[slot, :, entry * FBLK : (entry + 1) * FBLK] = vw_ref[:, pl.ds(start, FBLK)]
            biases.append(bias_ref[pl.ds(start, FBLK)])
        spread_heads(q4_ref.at[slot], qt_ref, at, heads)
        scores = nn(kc_ref[slot], q4_ref[slot])
        scales, keeps = [], []
        for h in range(heads):
            lanes = slice(h * FBLK, (h + 1) * FBLK)
            parts = [scores[e * FBLK : (e + 1) * FBLK, lanes] + biases[e] for e in range(others)]
            old_top = top_ref[g : g + 1, lanes]
            top = functools.reduce(
                jnp.maximum, [jnp.max(part, axis=0, keepdims=True) for part in parts] + [old_top]
            )
            keep = jnp.exp(old_top - top)
            den = den_ref[g : g + 1, lanes] * keep
            for e, part in enumerate(parts):
                weight = jnp.exp(part - top)
                den = den + jnp.sum(weight, axis=0, keepdims=True)
                p_ref[slot, e * FBLK : (e + 1) * FBLK, lanes] = weight.astype(BF)
            scale = mix_ref[0, h] / den
            scales.append(scale)
            keeps.append(keep * scale)
            relative = den / mix_ref[0, h]
            for level, (low, high) in enumerate(((fine, far_at), (far_at, total))):
                part = scores[low:high, lanes]
                weight = jnp.exp(part - jnp.max(part, axis=0, keepdims=True))
                share = mix_ref[level + 2, h] / jnp.sum(weight, axis=0, keepdims=True) * relative
                p_ref[slot, low:high, lanes] = (weight * share).astype(BF)
        total_out = nn(vc_ref[slot], p_ref[slot])
        rows = []
        for h in range(heads):
            pick = (slice(h * width, (h + 1) * width), slice(h * FBLK, (h + 1) * FBLK))
            mine = (pick[0], slice(at, at + FBLK))
            rows.append(total_out[pick] * scales[h] + acc_ref[mine] * keeps[h] + near_ref[mine])
        out_ref[index * FBLK : (index + 1) * FBLK] = jnp.transpose(
            jnp.concatenate(rows, axis=0)
        ).astype(BF)


def output_kernel(w_ref, *refs):
    out_ref = refs[-1]
    group = w_ref.shape[1]
    head = lax.axis_index("head")
    total = None
    for distance, part in zip((0, 2, 1, 3), refs[:4]):
        start = pl.multiple_of((head ^ distance) * group, group)
        term = nn(part[...], w_ref[pl.ds(start, group)])
        total = term if total is None else total + term
    out_ref[...] = total.astype(BF)


def local(tokens, w_query, w_key, w_value, w_out, level_mix, fine_blocks, order, mask_ids):
    tok_rows, width = tokens.shape
    slabs = lax.axis_size("seq")
    slab, head = lax.axis_index("seq"), lax.axis_index("head")
    group = w_query.shape[1]
    heads = level_mix.shape[1]
    packed = tok_rows - mask_ids.shape[1]
    near, mids, fars = tok_rows // POOL1, tok_rows // POOL2, tok_rows // POOL3
    coarse = 3 * mids + fars * slabs
    step = 3 * mids
    chosen = packed + SUMM_ROWS + near

    shape = jax.ShapeDtypeStruct
    params = pltpu.CompilerParams(vmem_limit_bytes=VMEM_LIMIT)

    def prepare():
        return pl.pallas_call(
            prepare_kernel,
            out_shape=(
                shape((tok_rows, tok_rows), BF),
                shape((tok_rows, tok_rows), BF),
                shape((chosen, tok_rows), BF),
                shape((SUMM_ROWS + near, 128), F32),
                shape((16, SUMM_ROWS + near), F32),
                shape((tok_rows, FBLK), F32),
                shape((2 * group, width), BF),
                shape((width, group), BF),
            ),
            in_specs=vmem_specs(5),
            out_specs=vmem_specs(8),
            compiler_params=params,
            cost_estimate=COST,
            name="prepare",
        )(order, mask_ids, w_query, w_value, w_key)

    def expand(prepared, sources):
        return pl.pallas_call(
            functools.partial(expand_kernel, tok_rows // slabs),
            out_shape=(
                shape((tok_rows, packed), BF),
                shape((packed, tok_rows), BF),
                shape((2 * tok_rows, FBLK), F32),
            ),
            in_specs=vmem_specs(1 + len(sources)),
            out_specs=vmem_specs(3),
            compiler_params=params,
            cost_estimate=COST,
            name="expand",
        )(prepared[5], *sources)

    pieces, prepared, expanded = exchange_tokens(tokens, mask_ids, prepare, expand)
    permute, permute_t, select, f_col, f_row, seen, w_t, w_k = prepared
    spread, spread_t, bias = expanded
    comp, summ, k0, v0, rows_here = pl.pallas_call(
        functools.partial(project_kernel, len(pieces)),
        out_shape=(
            shape((2 * packed, group), BF),
            shape((step, group), BF),
            shape((tok_rows, group), BF),
            shape((group, tok_rows), BF),
            shape((tok_rows, width), BF),
        ),
        in_specs=vmem_specs(len(pieces) + 4),
        out_specs=vmem_specs(5),
        compiler_params=params,
        cost_estimate=COST,
        name="project",
    )(*pieces, w_t, w_k, select, f_col)
    if slabs == 8:
        lined = [summ] + [by_distance(summ, d) for d in (2, 4, 6)]
    comp_before = to_next(comp)

    q_t, v_t, keys, near_k, near_vt = pl.pallas_call(
        order_kernel,
        out_shape=(
            shape((group, tok_rows), BF),
            shape((group, tok_rows), BF),
            shape((tok_rows, group), BF),
            shape((near, group), BF),
            shape((group, near), BF),
        ),
        in_specs=vmem_specs(9),
        out_specs=vmem_specs(5),
        compiler_params=params,
        cost_estimate=COST,
        name="order",
    )(permute, permute_t, select, f_col, f_row, w_t, rows_here, k0, v0)
    blocks = tok_rows // FBLK
    acc, near_out, top, den = pl.pallas_call(
        own_kernel,
        out_shape=(
            shape((group, tok_rows), F32),
            shape((group, tok_rows), F32),
            shape((blocks, heads * FBLK), F32),
            shape((blocks, heads * FBLK), F32),
        ),
        in_specs=smem_specs(1) + vmem_specs(6),
        out_specs=vmem_specs(4),
        scratch_shapes=[
            pltpu.VMEM((2, group, heads * FBLK), BF),
            pltpu.VMEM((2, FBLK + near, heads * FBLK), BF),
        ],
        compiler_params=params,
        cost_estimate=COST,
        name="own",
    )(level_mix, q_t, keys, v_t, near_k, near_vt, seen)

    if slabs == 8:
        places = tuple((index, 0, step, 0) for index in range(4))
        column = stacked(lined, places, group, (top,))
        summaries = [column, by_distance(column, 1)]
    else:
        copies = jnp.broadcast_to(summ[None], (slabs, step, group))
        copies = lax.all_to_all(copies, "seq", split_axis=0, concat_axis=0, tiled=True)
        summaries = [copies.reshape(slabs * step, group)]

    window_k, window_v, coarse_k, coarse_v = pl.pallas_call(
        window_kernel,
        out_shape=(
            shape((2 * tok_rows, group), BF),
            shape((group, 2 * tok_rows), BF),
            shape((coarse, group), BF),
            shape((group, coarse), BF),
        ),
        in_specs=vmem_specs(5 + len(summaries)),
        out_specs=vmem_specs(4),
        scratch_shapes=[pltpu.VMEM((slabs * step, group), BF)],
        compiler_params=params,
        cost_estimate=COST,
        name="window",
    )(keys, v_t, comp_before, spread, spread_t, *summaries)

    total = (FINE_K - 1) * FBLK + coarse
    lists = fine_blocks.T
    parts = PARTS if sum(PARTS) == blocks else (blocks,)
    waiting, out, first = None, None, 0

    def finish(out, attended, third, second, base, after=()):
        fourth = over_head(third, CORE_PAIRS)
        rows = attended.shape[0]
        previous = [] if out is None else [out]
        height = min(2 * FBLK, rows)
        tile = pl.BlockSpec((height, group), lambda i: (i, 0))
        return pl.pallas_call(
            output_kernel,
            grid=(rows // height,),
            out_shape=shape((tok_rows, group), BF),
            in_specs=[pl.BlockSpec((width, group), lambda i: (0, 0))]
            + [tile] * 4
            + [pl.BlockSpec(memory_space=pl.ANY)] * (len(previous) + len(after)),
            out_specs=pl.BlockSpec((height, group), lambda i, base=base * FBLK // height: (i + base, 0)),
            input_output_aliases={5: 0} if previous else {},
            compiler_params=params,
            cost_estimate=COST,
            name="output",
        )(w_out, attended, third, second, fourth, *previous, *after)

    for count in parts:
        attended = pl.pallas_call(
            functools.partial(rest_kernel, first, count),
            out_shape=shape((count * FBLK, group), BF),
            in_specs=smem_specs(2) + vmem_specs(10),
            out_specs=pl.BlockSpec(memory_space=pltpu.VMEM),
            scratch_shapes=[
                pltpu.VMEM((2, total, group), BF),
                pltpu.VMEM((2, group, total), BF),
                pltpu.VMEM((2, group, heads * FBLK), BF),
                pltpu.VMEM((2, total, heads * FBLK), BF),
            ],
            compiler_params=params,
            cost_estimate=COST,
            name="rest",
        )(
            lists, level_mix, q_t, window_k, window_v, coarse_k, coarse_v, bias, acc, near_out, top, den
        )
        third = over_head(attended, X_PAIRS)
        second = over_head(attended, CORE_PAIRS)
        if waiting is not None:
            old, old_third, old_second, old_base = waiting
            old_third, attended = lax.optimization_barrier((old_third, attended))
            out = finish(out, old, old_third, old_second, old_base, [third])
        waiting = (attended, third, second, first)
        first += count
    return finish(out, *waiting)


def solution(mesh):
    placed = (
        P("seq", None),
        P(None, "head"),
        P(None, "head"),
        P(None, "head"),
        P(None, "head"),
        P(None, "head"),
        P("seq", None),
        P("seq", None),
        P("seq", None),
    )
    return jax.shard_map(
        local, mesh=mesh, in_specs=placed, out_specs=P("seq", "head"), check_vma=False
    )
```
